32 devices in a mesh: dp: 16 (over z, x, core), tensor: 2 (over y).
Axes of the slice: x: 2, y: 2, z: 4, core: 2. Of those that a mesh axis runs over, the one named last changes fastest.
Arguments:
- tokens: bfloat16 [1024, 16, 1152], P('tensor', 'dp'), may hold values from -6 to 6
- cond: bfloat16 [16, 1152], P('dp'), may hold values from -6 to 6
- mod_weight: bfloat16 [1152, 6912], P('dp'), may hold values from -0.1875 to 0.1875
- mod_bias: bfloat16 [6912], replicated, may hold values from -3 to 3
- query_key_value_weight: bfloat16 [1152, 3, 1152], P('dp', None, 'tensor'), may hold values from -0.1875 to 0.1875
- qkv_bias: bfloat16 [2, 1152], P(None, 'tensor'), may hold values from -3 to 3
- attention_out_weight: bfloat16 [1152, 1152], P('tensor', 'dp'), may hold values from -1.5 to 1.5
- attention_out_bias: bfloat16 [1152], replicated, may hold values from -3 to 3
- first_hidden_weight: bfloat16 [1152, 4608], P('dp', 'tensor'), may hold values from -0.1875 to 0.1875
- first_hidden_bias: bfloat16 [4608], P('tensor'), may hold values from -3 to 3
- second_hidden_weight: bfloat16 [4608, 1152], P('tensor', 'dp'), may hold values from -0.09375 to 0.09375
- second_hidden_bias: bfloat16 [1152], replicated, may hold values from -3 to 3
- out_grad: bfloat16 [1024, 16, 1152], P('tensor', 'dp'), may hold values from -6 to 6
Outputs:
- output: bfloat16 [1024, 16, 1152], P('tensor', 'dp')
- tokens_grad: bfloat16 [1024, 16, 1152], P('tensor', 'dp')
- cond_grad: float32 [16, 1152], P('dp')
- mod_weight_grad: float32 [1152, 6912], P('dp')
- mod_bias_grad: float32 [6912], replicated
- qkv_weight_grad: float32 [1152, 3, 1152], P('dp', None, 'tensor')
- qkv_bias_grad: float32 [2, 1152], P(None, 'tensor')
- proj_weight_grad: float32 [1152, 1152], P('tensor', 'dp')
- proj_bias_grad: float32 [1152], replicated
- fc1_weight_grad: float32 [1152, 4608], P('dp', 'tensor')
- fc1_bias_grad: float32 [4608], P('tensor')
- fc2_weight_grad: float32 [4608, 1152], P('tensor', 'dp')
- fc2_bias_grad: float32 [1152], replicated
The draws below stay inside these ranges and needn't reach their ends.
All inputs are finite; a program needn't handle non-finite values.
Results may differ from the reference program's by a relative error of at most 0.02.
The reference program's roundings to bfloat16 on the way count: a program that leaves them out, or rounds other values in their place, can miss the bound.
Values may be sent and summed in bfloat16 or wider, within the bound.
A program may use at most 256 MiB of HBM per device.

```python
import jax
import jax.numpy as jnp
from jax import lax

D = 1152
HEADS = 16
FF = 4608
SEQ = 1024
HD = 72
LATENTS = 16


def spiked(entries, stream_key, source, target, blocks, factor):
    def block_of(position):
        return (jnp.arange(entries.shape[position]) // (entries.shape[position] // blocks)).reshape((-1,) + (1,) * (entries.ndim - 1 - position))

    one_side = jax.random.permutation(stream_key, blocks)[block_of(target)]
    second = (block_of(target) + blocks // 2) % blocks
    return jnp.where((block_of(source) == one_side) | (block_of(source) == second), factor * entries, entries)


def block_levels(own_key, shape, cuts, low, largest):
    def one(axis_at, parts):
        heights = jax.random.uniform(jax.random.fold_in(jax.random.fold_in(own_key, 6), axis_at), (parts,), jnp.float32, low / len(cuts), largest / len(cuts))
        return jnp.repeat(jnp.exp(heights), shape[axis_at] // parts).reshape((-1,) + (1,) * (len(shape) - axis_at - 1))

    loudness = one(*cuts[0])
    for cut in cuts[1:]:
        loudness = loudness * one(*cut)
    return loudness


def noise(stream_key, extent, scale, limit, split=(), held_as=jnp.bfloat16):
    gain = block_levels(stream_key, extent, split, -0.22, 0.18) if split else 1.0
    drawn = jax.random.normal(stream_key, extent, jnp.float32) * scale * gain
    return jnp.minimum(jnp.maximum(drawn, -limit), limit).astype(held_as)


def noise_with(key, extent, scale, reach, shards, heavy, kind=jnp.bfloat16):
    array = scale * jax.random.normal(key, extent, jnp.float32)
    if shards:
        array = array * block_levels(key, extent, shards, -0.22, 0.18)
    return jnp.clip(spiked(array, jax.random.fold_in(key, 3), *heavy), -reach, reach).astype(kind)


def setup_inputs(seed: int = 0) -> dict:
    key_of = jax.random.split(jax.random.key(seed), 14)
    return {
        "tokens": noise_with(key_of[0], (SEQ, LATENTS, D), 1.0, 6.0, ((0, 2), (1, 16)), (1, 2, 16, 2.0)),
        "cond": noise(key_of[1], (LATENTS, D), 1.0, 6.0, ((0, 16),)),
        "mod_weight": noise(key_of[2], (D, 6 * D), D ** -0.5, 0.1875, ((0, 16),)),
        "mod_bias": noise(key_of[3], (6 * D,), 0.5, 3.0),
        "query_key_value_weight": noise(key_of[4], (D, 3, D), D ** -0.5, 0.1875, ((0, 16), (2, 2))),
        "qkv_bias": noise(key_of[5], (2, D), 0.5, 3.0, ((1, 2),)),
        "attention_out_weight": noise(key_of[6], (D, D), (HD // 4) ** -0.5, 1.5, ((0, 2), (1, 16))),
        "attention_out_bias": noise(key_of[7], (D,), 0.5, 3.0),
        "first_hidden_weight": noise(key_of[8], (D, FF), D ** -0.5, 0.1875, ((0, 16), (1, 2))),
        "first_hidden_bias": noise(key_of[9], (FF,), 0.5, 3.0, ((0, 2),)),
        "second_hidden_weight": noise(key_of[10], (FF, D), FF ** -0.5, 0.09375, ((0, 2), (1, 16))),
        "second_hidden_bias": noise(key_of[11], (D,), 0.5, 3.0),
        "out_grad": noise_with(key_of[12], (SEQ, LATENTS, D), 1.0, 6.0, ((0, 2), (1, 16)), (1, 2, 16, 2.0)),
    }


@jax.custom_vjp
def low(v):
    return lax.optimization_barrier(v.astype(jnp.bfloat16)).astype(jnp.float32)

@jax.custom_vjp
def low_back(v):
    return v

def low_keep(v):
    return (low(v), None)

def low_pass(kept, grad):
    return (grad,)

def back_keep(v):
    return (v, None)

def back_low(kept, grad):
    return (low(grad),)
low.defvjp(low_keep, low_pass)
low_back.defvjp(back_keep, back_low)
exact_precision = lax.Precision.HIGHEST

def modulate(hidden, shifts, scales):
    center = hidden - lax.optimization_barrier(jnp.mean(hidden, axis=-1, keepdims=True))
    spread = lax.optimization_barrier(jnp.mean(center * center, axis=-1, keepdims=True))
    return center * lax.rsqrt(spread + 1e-06) * (1.0 + scales) + shifts

def attend(packed):
    queries = packed[:, 0]
    keys_all = packed[:, 1]
    values_all = packed[:, 2]
    scores = low_back(jnp.einsum('qhe,khe->hqk', queries, keys_all, precision=exact_precision) * HD ** (-0.5))
    probs = jax.nn.softmax(scores, axis=-1)
    mixture = jnp.einsum('hqk,khe->qhe', low(probs), values_all, precision=exact_precision)
    return mixture.reshape(SEQ, D)

def forward(tokens, cond, mod_weight, mod_bias, query_key_value_weight, qkv_bias, attention_out_weight, attention_out_bias, first_hidden_weight, first_hidden_bias, second_hidden_weight, second_hidden_bias):
    silu_low = low(jax.nn.silu(cond))
    modulation = low_back(jnp.dot(silu_low, mod_weight, precision=exact_precision) + mod_bias)
    pieces = modulation.reshape(LATENTS, 6, D)
    attention_normalized = low(modulate(tokens, pieces[:, 0], pieces[:, 1]))
    query_key_value_shift = jnp.stack([qkv_bias[0], jnp.zeros_like(qkv_bias[0]), qkv_bias[1]])
    projected_output = jnp.einsum('xni,imk->xnmk', attention_normalized, query_key_value_weight, precision=exact_precision) + query_key_value_shift
    projected_output = low(low_back(projected_output))
    packed = jnp.moveaxis(projected_output, 1, 0).reshape(LATENTS, SEQ, 3, HEADS, HD)
    attention_result = lax.map(jax.checkpoint(attend), packed)
    attention_result = low(low_back(jnp.moveaxis(attention_result, 0, 1)))
    attention_branch = low_back(jnp.einsum('vjq,qz->vjz', attention_result, attention_out_weight, precision=exact_precision) + attention_out_bias)
    resid_mid = tokens + pieces[:, 2] * attention_branch
    feedforward_normalized = low(modulate(resid_mid, pieces[:, 3], pieces[:, 4]))
    before_activation = low_back(jnp.einsum('gco,oq->gcq', feedforward_normalized, first_hidden_weight, precision=exact_precision) + first_hidden_bias)
    gelu_activated = low(jax.nn.gelu(before_activation, approximate=True))
    feedforward_branch = low_back(jnp.einsum('cmo,oz->cmz', gelu_activated, second_hidden_weight, precision=exact_precision) + second_hidden_bias)
    return resid_mid + pieces[:, 5] * feedforward_branch

def reference(tokens, cond, mod_weight, mod_bias, query_key_value_weight, qkv_bias, attention_out_weight, attention_out_bias, first_hidden_weight, first_hidden_bias, second_hidden_weight, second_hidden_bias, out_grad):
    inputs = tuple((operand.astype(jnp.float32) for operand in (tokens, cond, mod_weight, mod_bias, query_key_value_weight, qkv_bias, attention_out_weight, attention_out_bias, first_hidden_weight, first_hidden_bias, second_hidden_weight, second_hidden_bias)))
    output, pullback = jax.vjp(forward, *inputs)
    grads = pullback(out_grad.astype(jnp.float32))
    return (output.astype(jnp.bfloat16), grads[0].astype(jnp.bfloat16), grads[1], grads[2], grads[3], grads[4], grads[5], grads[6], grads[7], grads[8], grads[9], grads[10], grads[11])
```

```python
import functools

import jax
import jax.numpy as jnp
from jax import lax
from jax.experimental import pallas as pl
from jax.experimental.pallas import tpu as pltpu
from jax.sharding import PartitionSpec as P

HEADS = 16
MESH = pl.DeviceIdType.MESH
AXES = ("dp", "tensor")
F32 = jnp.float32
BF16 = jnp.bfloat16


def modulate(hidden, shifts, scales):
    center = hidden - jnp.mean(hidden, axis=-1, keepdims=True)
    spread = jnp.mean(center * center, axis=-1, keepdims=True)
    return center * lax.rsqrt(spread + 1e-06) * (1.0 + scales) + shifts


def gelu_tanh(values):
    return jax.nn.gelu(values, approximate=True)


def attend_forward(packed):
    queries = packed[:, 0]
    keys_all = packed[:, 1]
    values_all = packed[:, 2]
    seq_len = packed.shape[0]
    scaling = packed.shape[3] ** (-0.5)
    block_rows = min(512, seq_len)
    results = []
    log_parts = []
    for offset in range(0, seq_len, block_rows):
        query_block = queries[offset : offset + block_rows]
        scores = (
            jnp.einsum("qhe,khe->hqk", query_block, keys_all, preferred_element_type=jnp.float32)
            * scaling
        )
        highest = jnp.max(scores, axis=-1, keepdims=True)
        weights = jnp.exp(scores - highest)
        row_total = jnp.sum(weights, axis=-1, keepdims=True)
        prob_low = (weights / row_total).astype(jnp.bfloat16)
        mixture = jnp.einsum(
            "hqk,khe->qhe", prob_low, values_all, preferred_element_type=jnp.float32
        )
        results.append(mixture.reshape(block_rows, -1))
        log_parts.append((highest + jnp.log(row_total))[..., 0])
    return (jnp.concatenate(results, 0).astype(jnp.bfloat16), jnp.concatenate(log_parts, 1))


def attend_backward(inputs):
    packed, grad_out, log_totals = inputs
    queries = packed[:, 0]
    keys_all = packed[:, 1]
    values_all = packed[:, 2]
    seq_len = packed.shape[0]
    scaling = packed.shape[3] ** (-0.5)
    block_rows = min(512, seq_len)
    query_grads = []
    key_grad = jnp.zeros(keys_all.shape, jnp.float32)
    value_grad = jnp.zeros(values_all.shape, jnp.float32)
    for offset in range(0, seq_len, block_rows):
        query_block = queries[offset : offset + block_rows]
        grad_block = grad_out[offset : offset + block_rows]
        scores = (
            jnp.einsum("qhe,khe->hqk", query_block, keys_all, preferred_element_type=jnp.float32)
            * scaling
        )
        probs = jnp.exp(scores - log_totals[:, offset : offset + block_rows, None])
        prob_low = probs.astype(jnp.bfloat16)
        prob_grad = jnp.einsum(
            "qhe,khe->hqk", grad_block, values_all, preferred_element_type=jnp.float32
        )
        inner = jnp.sum(probs * prob_grad, axis=-1, keepdims=True)
        score_grad = (probs * (prob_grad - inner)).astype(jnp.bfloat16)
        query_grads.append(
            jnp.einsum("hqk,khe->qhe", score_grad, keys_all, preferred_element_type=jnp.float32)
            * scaling
        )
        key_grad = (
            key_grad
            + jnp.einsum(
                "hqk,qhe->khe", score_grad, query_block, preferred_element_type=jnp.float32
            )
            * scaling
        )
        value_grad = value_grad + jnp.einsum(
            "hqk,qhe->khe", prob_low, grad_block, preferred_element_type=jnp.float32
        )
    return jnp.stack([jnp.concatenate(query_grads, 0), key_grad, value_grad], 1).astype(
        jnp.bfloat16
    )


def on_device_general(
    tokens,
    cond,
    mod_weight,
    mod_bias,
    query_key_value_weight,
    qkv_bias,
    attention_out_weight,
    attention_out_bias,
    first_hidden_weight,
    first_hidden_bias,
    second_hidden_weight,
    second_hidden_bias,
    out_grad,
):
    w_mod, w_qkv, w_proj, w_fc1, w_fc2 = (
        lax.all_gather(mod_weight, "dp", axis=0, tiled=True),
        lax.all_gather(query_key_value_weight, "dp", axis=0, tiled=True),
        lax.all_gather(attention_out_weight, "dp", axis=1, tiled=True),
        lax.all_gather(first_hidden_weight, "dp", axis=0, tiled=True),
        lax.all_gather(second_hidden_weight, "dp", axis=1, tiled=True),
    )
    seq_local, latents, width = tokens.shape
    columns = query_key_value_weight.shape[2]
    head_size = width // HEADS
    heads_here = columns // head_size
    local_rows = seq_local * latents
    cond_wide = cond.astype(jnp.float32)
    silu_cond, silu_back = jax.vjp(jax.nn.silu, cond_wide)
    silu_low = silu_cond.astype(jnp.bfloat16)
    modulation = jnp.dot(silu_low, w_mod, preferred_element_type=jnp.float32) + mod_bias.astype(
        jnp.float32
    )
    pieces = modulation.reshape(latents, 6, width)
    hidden_in = tokens.astype(jnp.float32)
    attention_normalized, norm_a_back = jax.vjp(modulate, hidden_in, pieces[:, 0], pieces[:, 1])
    gathered_a = lax.all_gather(
        attention_normalized.astype(jnp.bfloat16), "tensor", axis=0, tiled=True
    )
    seq_len = gathered_a.shape[0]
    total_rows = seq_len * latents
    rows_a = gathered_a.reshape(total_rows, width)
    qkv_flat = w_qkv.reshape(width, 3 * columns)
    zero_row = jnp.zeros((columns,), jnp.float32)
    query_key_value_shift = jnp.stack(
        [qkv_bias[0].astype(jnp.float32), zero_row, qkv_bias[1].astype(jnp.float32)]
    )
    projected_output = (
        jnp.dot(rows_a, qkv_flat, preferred_element_type=jnp.float32).reshape(
            seq_len, latents, 3, columns
        )
        + query_key_value_shift
    )
    packed = jnp.moveaxis(projected_output.astype(jnp.bfloat16), 1, 0).reshape(
        latents, seq_len, 3, heads_here, head_size
    )
    attention_result, log_totals = lax.map(attend_forward, packed)
    attended_rows = jnp.moveaxis(attention_result, 0, 1).reshape(total_rows, columns)
    summed_a = lax.psum_scatter(
        jnp.dot(attended_rows, w_proj, preferred_element_type=jnp.float32).astype(jnp.bfloat16),
        "tensor",
        scatter_dimension=0,
        tiled=True,
    ).astype(jnp.float32)
    attention_branch = summed_a.reshape(seq_local, latents, width) + attention_out_bias.astype(
        jnp.float32
    )
    resid_mid = hidden_in + pieces[:, 2] * attention_branch
    feedforward_normalized, norm_m_back = jax.vjp(modulate, resid_mid, pieces[:, 3], pieces[:, 4])
    gathered_m = lax.all_gather(
        feedforward_normalized.astype(jnp.bfloat16), "tensor", axis=0, tiled=True
    )
    rows_m = gathered_m.reshape(total_rows, width)
    before_activation = jnp.dot(
        rows_m, w_fc1, preferred_element_type=jnp.float32
    ) + first_hidden_bias.astype(jnp.float32)
    gelu_activated, gelu_back = jax.vjp(gelu_tanh, before_activation)
    act_low = gelu_activated.astype(jnp.bfloat16)
    summed_m = lax.psum_scatter(
        jnp.dot(act_low, w_fc2, preferred_element_type=jnp.float32).astype(jnp.bfloat16),
        "tensor",
        scatter_dimension=0,
        tiled=True,
    ).astype(jnp.float32)
    feedforward_branch = summed_m.reshape(seq_local, latents, width) + second_hidden_bias.astype(
        jnp.float32
    )
    output = (resid_mid + pieces[:, 5] * feedforward_branch).astype(jnp.bfloat16)
    grad_out = out_grad.astype(jnp.float32)
    gate_m_grad = jnp.sum(grad_out * feedforward_branch, axis=0)
    grad_m_low = (grad_out * pieces[:, 5]).astype(jnp.bfloat16)
    grad_m_rows = lax.all_gather(grad_m_low, "tensor", axis=0, tiled=True).reshape(
        total_rows, width
    )
    fc2_bias_grad = jnp.sum(grad_m_rows, axis=0, dtype=jnp.float32)
    fc2_weight_grad = jnp.einsum(
        "rf,rd->fd", act_low, grad_m_rows, preferred_element_type=jnp.float32
    )
    act_grad = jnp.einsum("rd,fd->rf", grad_m_rows, w_fc2, preferred_element_type=jnp.float32)
    pre_grad = gelu_back(act_grad)[0].astype(jnp.bfloat16)
    fc1_bias_grad = jnp.sum(pre_grad, axis=0, dtype=jnp.float32)
    fc1_weight_grad = jnp.einsum("rd,rf->df", rows_m, pre_grad, preferred_element_type=jnp.float32)
    normed_m_grad = (
        lax.psum_scatter(
            jnp.einsum("rf,df->rd", pre_grad, w_fc1, preferred_element_type=jnp.float32).astype(
                jnp.bfloat16
            ),
            "tensor",
            scatter_dimension=0,
            tiled=True,
        )
        .astype(jnp.float32)
        .reshape(seq_local, latents, width)
    )
    resid_part, shift_m_grad, scale_m_grad = norm_m_back(normed_m_grad)
    resid_grad = grad_out + resid_part
    gate_a_grad = jnp.sum(resid_grad * attention_branch, axis=0)
    grad_a_low = (resid_grad * pieces[:, 2]).astype(jnp.bfloat16)
    grad_a_flat = grad_a_low.reshape(local_rows, width)
    proj_bias_part = jnp.sum(grad_a_flat, axis=0, dtype=jnp.float32)
    grad_a_rows = lax.all_gather(grad_a_low, "tensor", axis=0, tiled=True).reshape(
        total_rows, width
    )
    proj_weight_grad = jnp.einsum(
        "rc,rd->cd", attended_rows, grad_a_rows, preferred_element_type=jnp.float32
    )
    attended_grad = jnp.einsum(
        "rd,cd->rc", grad_a_rows, w_proj, preferred_element_type=jnp.float32
    ).astype(jnp.bfloat16)
    grad_packed = jnp.moveaxis(attended_grad.reshape(seq_len, latents, heads_here, head_size), 1, 0)
    qkv_grad_packed = lax.map(attend_backward, (packed, grad_packed, log_totals))
    qkv_grad_rows = jnp.moveaxis(qkv_grad_packed, 0, 1).reshape(total_rows, 3 * columns)
    bias_sums = jnp.sum(qkv_grad_rows.reshape(total_rows, 3, columns), axis=0, dtype=jnp.float32)
    qkv_bias_grad = jnp.stack([bias_sums[0], bias_sums[2]])
    qkv_weight_grad = jnp.einsum(
        "rd,rc->dc", rows_a, qkv_grad_rows, preferred_element_type=jnp.float32
    ).reshape(width, 3, columns)
    normed_a_grad = (
        lax.psum_scatter(
            jnp.einsum(
                "rc,dc->rd", qkv_grad_rows, qkv_flat, preferred_element_type=jnp.float32
            ).astype(jnp.bfloat16),
            "tensor",
            scatter_dimension=0,
            tiled=True,
        )
        .astype(jnp.float32)
        .reshape(seq_local, latents, width)
    )
    input_part, shift_a_grad, scale_a_grad = norm_a_back(normed_a_grad)
    tokens_grad = (resid_grad + input_part).astype(jnp.bfloat16)
    partial_mod = jnp.stack(
        [shift_a_grad, scale_a_grad, gate_a_grad, shift_m_grad, scale_m_grad, gate_m_grad], 1
    ).reshape(latents, 6 * width)
    mod_summed, proj_bias_grad = (
        lax.psum(partial_mod.astype(jnp.bfloat16), "tensor").astype(jnp.float32),
        lax.psum(proj_bias_part.astype(jnp.bfloat16), "tensor").astype(jnp.float32),
    )
    mod_grad_low = mod_summed.astype(jnp.bfloat16)
    silu_grad = jnp.einsum("le,de->ld", mod_grad_low, w_mod, preferred_element_type=jnp.float32)
    cond_grad = silu_back(silu_grad)[0]
    silu_every, mod_every = (
        lax.all_gather(silu_low, "dp", axis=0, tiled=True),
        lax.all_gather(mod_grad_low, "dp", axis=0, tiled=True),
    )
    owned_rows = mod_weight.shape[0]
    silu_owned = lax.dynamic_slice_in_dim(
        silu_every, lax.axis_index("dp") * owned_rows, owned_rows, 1
    )
    mod_weight_grad = jnp.einsum(
        "ld,le->de", silu_owned, mod_every, preferred_element_type=jnp.float32
    )
    mod_bias_grad = jnp.sum(mod_every, axis=0, dtype=jnp.float32)
    qkv_weight_grad, proj_weight_grad, fc1_weight_grad, fc2_weight_grad = (
        lax.psum_scatter(
            qkv_weight_grad.astype(jnp.bfloat16), "dp", scatter_dimension=0, tiled=True
        ).astype(jnp.float32),
        lax.psum_scatter(
            proj_weight_grad.astype(jnp.bfloat16), "dp", scatter_dimension=1, tiled=True
        ).astype(jnp.float32),
        lax.psum_scatter(
            fc1_weight_grad.astype(jnp.bfloat16), "dp", scatter_dimension=0, tiled=True
        ).astype(jnp.float32),
        lax.psum_scatter(
            fc2_weight_grad.astype(jnp.bfloat16), "dp", scatter_dimension=1, tiled=True
        ).astype(jnp.float32),
    )
    qkv_bias_grad, proj_bias_grad, fc1_bias_grad, fc2_bias_grad = lax.psum(
        (qkv_bias_grad, proj_bias_grad, fc1_bias_grad, fc2_bias_grad), "dp"
    )
    return (
        output,
        tokens_grad,
        cond_grad,
        mod_weight_grad,
        mod_bias_grad,
        qkv_weight_grad,
        qkv_bias_grad,
        proj_weight_grad,
        proj_bias_grad,
        fc1_weight_grad,
        fc1_bias_grad,
        fc2_weight_grad,
        fc2_bias_grad,
    )


def place():
    d = lax.axis_index("dp")
    y = lax.axis_index("tensor")
    return d, d // 4, (d // 2) % 2, d % 2, y


def neighbours(pos):
    d, z, x, c, y = pos
    sib = (z * 4 + x * 2 + (1 - c), y)
    xn = (z * 4 + (1 - x) * 2 + c, y)
    yn = (d, 1 - y)
    return sib, xn, yn


def z_peer(pos, k):
    d, z, x, c, y = pos
    return (((z + k) % 4) * 4 + x * 2 + c, y)


def greet(peers):
    sem = pltpu.get_barrier_semaphore()
    for peer in peers:
        pl.semaphore_signal(sem, inc=1, device_id=peer, device_id_type=MESH)
    pl.semaphore_wait(sem, len(peers))


def chip_peers(pos):
    return list(neighbours(pos)) + [z_peer(pos, k) for k in (1, 2, 3)]


def remote(src, dst, send, recv, peer):
    return pltpu.make_async_remote_copy(
        src_ref=src, dst_ref=dst, send_sem=send, recv_sem=recv, device_id=peer, device_id_type=MESH
    )


GATHER_RECV = 17
GATHER_SEND = 17


class Gather:
    def __init__(self, shard, full, cols, recv, send, pos):
        self.shard, self.full, self.cols = shard, full, cols
        self.recv, self.send, self.pos = recv, send, pos
        self.sib, self.xn, self.yn = neighbours(pos)
        self.home = pos[3] == pos[4]
        self.away = pos[3] != pos[4]

    def rows(self, b, n):
        if self.cols is None:
            return self.full.at[pl.ds(b, n)]
        return self.full.at[pl.ds(b, n), :, pl.ds(*self.cols)]

    def own(self):
        if self.cols is None:
            return self.shard
        return self.shard.at[:, :, pl.ds(*self.cols)]

    def copy(self, b, n, peer, s, r):
        ref = self.rows(b, n)
        return remote(ref, ref, self.send.at[s], self.recv.at[r], peer)

    def stay(self):
        return pltpu.make_async_copy(self.own(), self.rows(self.pos[0], 1), self.send.at[16])

    def join(self):
        d = self.pos[0]

        @pl.when(self.away)
        def _():
            remote(
                self.own(), self.rows(d, 1), self.send.at[15], self.recv.at[16], self.sib
            ).start()

        @pl.when(self.home)
        def _():
            self.stay().start()

    def spread(self):
        d, z, x, c, y = self.pos
        q = z * 2 + x

        @pl.when(self.home)
        def _():
            self.stay().wait()
            self.copy(2 * q + 1 - c, 1, self.sib, 15, 16).wait_recv()
            for k in (2, 1, 3):
                self.copy(2 * q, 2, z_peer(self.pos, k), k - 1, q).start()
            self.copy(2 * q, 2, self.xn, 3, q).start()
            self.copy(2 * q, 2, self.yn, 4, q).start()

    def from_z(self, k):
        d, z, x, c, y = self.pos
        q = ((z + k) % 4) * 2 + x

        @pl.when(self.home)
        def _():
            self.copy(2 * q, 2, self.xn, 0, q).wait_recv()
            self.copy(2 * q, 2, self.xn, 3 + 2 * k, q).start()
            self.copy(2 * q, 2, self.yn, 4 + 2 * k, q).start()

    def cross(self, k):
        d, z, x, c, y = self.pos
        zz = (z + k) % 4

        @pl.when(self.home)
        def _():
            q = zz * 2 + 1 - x
            self.copy(2 * q, 2, self.xn, 0, q).wait_recv()
            self.copy(2 * q, 1, self.yn, 11 + k, 8 + zz).start()

        @pl.when(self.away)
        def _():
            q = zz * 2 + x
            self.copy(2 * q, 2, self.xn, 0, q).wait_recv()
            self.copy(2 * q + 1, 1, self.xn, 11 + k, 12 + zz).start()

    def finish(self):
        d, z, x, c, y = self.pos

        @pl.when(self.home)
        def _():
            for i in range(11):
                self.copy(0, 2, self.xn, i, 0).wait_send()
            for k in range(4):
                self.copy(0, 1, self.yn, 11 + k, 8).wait_send()

        @pl.when(self.away)
        def _():
            for k in range(4):
                zz = (z + k) % 4
                q = zz * 2 + 1 - x
                self.copy(2 * q, 1, self.yn, 0, 8 + zz).wait_recv()
                self.copy(2 * q + 1, 1, self.xn, 0, 12 + zz).wait_recv()
            self.copy(0, 1, self.sib, 15, 16).wait_send()
            for k in range(4):
                self.copy(0, 1, self.xn, 11 + k, 12).wait_send()


def gather_events(parts):
    events = [p.join for p in parts] + [p.spread for p in parts]
    for p in parts:
        events += [functools.partial(p.from_z, k) for k in (1, 2, 3)]
    for p in parts:
        events += [functools.partial(p.cross, k) for k in range(4)]
    return events + [p.finish for p in parts]


def gather_parts(shards, fulls, chunks, recv, send, pos):
    return [
        Gather(shards[g], fulls[g], cols, recv.at[i], send.at[i], pos)
        for i, (g, cols) in enumerate(chunks)
    ]


def gather_kernel(chunks, count, *refs):
    shards, fulls = refs[:count], refs[count : 2 * count]
    recv, send = refs[2 * count :]
    pos = place()
    greet(chip_peers(pos))
    for event in gather_events(gather_parts(shards, fulls, chunks, recv, send, pos)):
        event()


def gather_sems(chunks):
    n = len(chunks)
    return [
        pltpu.SemaphoreType.DMA((n, GATHER_RECV)),
        pltpu.SemaphoreType.DMA((n, GATHER_SEND)),
    ]


def gather_weights(shards, chunks, collective_id):
    count = len(shards)
    anywhere = pl.BlockSpec(memory_space=pl.ANY)
    return pl.pallas_call(
        functools.partial(gather_kernel, chunks, count),
        out_shape=[jax.ShapeDtypeStruct((16,) + s.shape[1:], s.dtype) for s in shards],
        in_specs=[anywhere] * count,
        out_specs=[anywhere] * count,
        scratch_shapes=gather_sems(chunks),
        compiler_params=pltpu.CompilerParams(
            collective_id=collective_id, has_side_effects=True
        ),
    )(*shards)


REDUCE_RECV = 24
REDUCE_SEND = 17


class Reduce:
    def __init__(self, grad, land, spare, out, recv, send, pos, cols):
        self.grad, self.land, self.spare, self.out = grad, land, spare, out
        self.recv, self.send, self.pos, self.cols = recv, send, pos, pl.ds(*cols)
        self.sib, self.xn, self.yn = neighbours(pos)
        self.home = pos[3] == pos[4]
        self.away = pos[3] != pos[4]

    def rows(self, b, n=1):
        return self.grad.at[pl.ds(b, n), :, self.cols]

    def copy(self, src, slot, n, r, s, peer):
        return remote(src, self.land.at[pl.ds(slot, n)], self.send.at[s], self.recv.at[r], peer)

    def arrive(self, slot, n, r):
        self.copy(self.land.at[pl.ds(slot, n)], slot, n, r, 0, self.xn).wait_recv()

    def add(self, b, *slots):
        total = self.grad[b, :, self.cols].astype(F32)
        for slot in slots:
            total = total + self.land[slot].astype(F32)
        self.grad[b, :, self.cols] = total.astype(BF16)

    def first(self):
        d, z, x, c, y = self.pos

        def over_y(column, sem):
            def step(k, _):
                zz = lax.rem(z + 1 + k, 4)
                q = zz * 2 + column
                self.copy(self.rows(2 * q), q, 1, q, sem + k, self.yn).start()
                return 0

            lax.fori_loop(0, 4, step, 0)

        def over_x(k, _):
            zz = lax.rem(z + 1 + k, 4)
            b = zz * 4 + (1 - x) * 2 + 1
            self.copy(self.rows(b), 8 + zz, 1, 8 + zz, 8 + k, self.xn).start()
            return 0

        @pl.when(self.away)
        def _():
            over_y(1 - x, 0)

        lax.fori_loop(0, 4, over_x, 0)

        @pl.when(self.away)
        def _():
            over_y(x, 4)

    def second(self):
        d, z, x, c, y = self.pos

        @pl.when(self.home)
        def _():
            def step(k, _):
                zz = lax.rem(z + 1 + k, 4)
                q = zz * 2 + 1 - x
                self.arrive(q, 1, q)
                self.add(2 * q, q)
                self.copy(self.rows(2 * q), 12 + zz, 1, 12 + zz, k, self.xn).start()
                return 0

            lax.fori_loop(0, 4, step, 0)

        def step(k, _):
            zz = lax.rem(z + 1 + k, 4)
            q = zz * 2 + x
            self.arrive(8 + zz, 1, 8 + zz)
            self.add(2 * q + 1, 8 + zz)

            @pl.when(self.away)
            def _():
                self.copy(self.rows(2 * q + 1), 16 + zz, 1, 16 + zz, 12 + k, self.yn).start()

            return 0

        lax.fori_loop(0, 4, step, 0)

    def third(self):
        d, z, x, c, y = self.pos

        @pl.when(self.home)
        def _():
            def step(k, _):
                zz = lax.rem(z + 1 + k, 4)
                q = zz * 2 + x
                self.arrive(q, 1, q)
                self.arrive(12 + zz, 1, 12 + zz)
                self.add(2 * q, q, 12 + zz)
                self.arrive(16 + zz, 1, 16 + zz)
                self.add(2 * q + 1, 16 + zz)
                peer = (zz * 4 + x * 2 + c, y)
                self.copy(self.rows(2 * q, 2), 20 + 2 * k, 2, 20 + k, 4 + k, peer).start()
                return 0

            lax.fori_loop(0, 3, step, 0)

    def hand_over(self):
        return remote(
            self.spare, self.out.at[:, self.cols], self.send.at[16], self.recv.at[23], self.sib
        )

    def fourth(self):
        d, z, x, c, y = self.pos

        @pl.when(self.home)
        def _():
            q = z * 2 + x
            self.arrive(q, 1, q)
            self.arrive(12 + z, 1, 12 + z)
            self.arrive(16 + z, 1, 16 + z)
            for k in range(3):
                self.arrive(20 + 2 * k, 2, 20 + k)
            low = self.grad[2 * q, :, self.cols].astype(F32)
            for slot in (q, 12 + z, 20, 22, 24):
                low = low + self.land[slot].astype(F32)
            high = self.grad[2 * q + 1, :, self.cols].astype(F32)
            for slot in (16 + z, 21, 23, 25):
                high = high + self.land[slot].astype(F32)

            @pl.when(c == 0)
            def _():
                self.out[:, self.cols] = low
                self.spare[...] = high

            @pl.when(c == 1)
            def _():
                self.out[:, self.cols] = high
                self.spare[...] = low

            self.hand_over().start()

    def finish(self):
        one, two = self.rows(0), self.rows(0, 2)

        @pl.when(self.home)
        def _():
            for k in range(4):
                self.copy(one, 0, 1, 0, k, self.xn).wait_send()
            for k in range(3):
                self.copy(two, 0, 2, 0, 4 + k, self.xn).wait_send()
            self.hand_over().wait_send()

        @pl.when(self.away)
        def _():
            for k in range(8):
                self.copy(one, 0, 1, 0, k, self.yn).wait_send()
            for k in range(4):
                self.copy(one, 0, 1, 0, 12 + k, self.yn).wait_send()
            self.hand_over().wait_recv()

        for k in range(4):
            self.copy(one, 0, 1, 0, 8 + k, self.xn).wait_send()


def reduce_events(parts):
    n = len(parts)
    events = [parts[0].first]
    for i in range(n + 2):
        if i + 1 < n:
            events.append(parts[i + 1].first)
        if i < n:
            events.append(parts[i].second)
        if 0 <= i - 1 < n:
            events.append(parts[i - 1].third)
        if 0 <= i - 2 < n:
            events.append(parts[i - 2].fourth)
    return events + [p.finish for p in parts]


def reduce_kernel(chunks, count, *refs):
    n = len(chunks)
    grads, outs = refs[:count], refs[count : 2 * count]
    lands, spares = refs[2 * count : 2 * count + n], refs[2 * count + n : 2 * count + 2 * n]
    recv, send = refs[2 * count + 2 * n :]
    pos = place()
    greet(chip_peers(pos))
    parts = [
        Reduce(grads[g], lands[i], spares[i], outs[g], recv.at[i], send.at[i], pos, cols)
        for i, (g, cols) in enumerate(chunks)
    ]
    for event in reduce_events(parts):
        event()


def reduce_scratch(chunks):
    n = len(chunks)
    return (
        [pltpu.VMEM((26, 72, cols[1]), BF16) for _, cols in chunks]
        + [pltpu.VMEM((72, cols[1]), F32) for _, cols in chunks]
        + [pltpu.SemaphoreType.DMA((n, REDUCE_RECV)), pltpu.SemaphoreType.DMA((n, REDUCE_SEND))]
    )


def reduce_grads(grads, chunks, collective_id):
    count = len(grads)
    vmem = pl.BlockSpec(memory_space=pltpu.VMEM)
    return pl.pallas_call(
        functools.partial(reduce_kernel, chunks, count),
        out_shape=[jax.ShapeDtypeStruct(g.shape[1:], F32) for g in grads],
        in_specs=[vmem] * count,
        out_specs=[vmem] * count,
        scratch_shapes=reduce_scratch(chunks),
        compiler_params=pltpu.CompilerParams(
            collective_id=collective_id, has_side_effects=True, vmem_limit_bytes=63000 * 1024
        ),
    )(*grads)


def mod_forward_kernel(
    piece_ref, w_ref, bias_ref, mod_ref, silu_ref, part, land, mine, other, s1, r1, s2, r2, s3
):
    pos = place()
    d, z, x, c, y = pos
    sib = neighbours(pos)[0]
    greet([((d + k) % 16, y) for k in range(1, 16)])

    def piece(k):
        to = (d + k) % 16
        return remote(piece_ref.at[to], silu_ref.at[d], s1.at[k], r1.at[d], (to, y))

    def piece_in(k):
        src = (d + k) % 16
        return remote(piece_ref.at[src], silu_ref.at[src], s1.at[k], r1.at[src], (src, y))

    for k in range(1, 16):
        piece(k).start()
    silu_ref[d] = piece_ref[d]
    for k in range(1, 16):
        piece_in(k).wait_recv()
    rows = jnp.concatenate(
        [silu_ref[2 * q + y].astype(F32)[0:1, :] for q in range(8)], axis=0
    ).astype(BF16)[:, :72]
    width = w_ref.shape[1] // 6
    for j in range(6):
        cols = slice(j * width, (j + 1) * width)
        value = jnp.dot(rows, w_ref[:, cols], preferred_element_type=F32)
        for q in range(8):
            part[q, :, cols] = value[q : q + 1, :]
    me = z * 2 + x

    def send_part(k):
        q = (me + k) % 8
        return remote(part.at[q], land.at[me], s2.at[k], r2.at[me], (q * 2 + c, y))

    def part_in(k):
        q = (me + k) % 8
        return remote(part.at[q], land.at[q], s2.at[k], r2.at[q], (q * 2 + c, y))

    for k in range(1, 8):
        send_part(k).start()
    land[me] = part[me]
    for k in range(1, 8):
        part_in(k).wait_recv()
    total = land[0]
    for q in range(1, 8):
        total = total + land[q]
    mine[...] = total
    swap = remote(mine, other, s3.at[0], s3.at[1], sib)
    swap.start()
    for k in range(1, 16):
        piece(k).wait_send()
    for k in range(1, 8):
        send_part(k).wait_send()
    swap.wait()
    mod_ref[...] = mine[...] + other[...] + bias_ref[...]


def mod_forward(pieces, w_mod, bias, collective_id):
    vmem = pl.BlockSpec(memory_space=pltpu.VMEM)
    n = w_mod.shape[1]
    return pl.pallas_call(
        mod_forward_kernel,
        out_shape=[jax.ShapeDtypeStruct((1, n), F32), jax.ShapeDtypeStruct((16, 8, 128), BF16)],
        in_specs=[vmem] * 3,
        out_specs=[vmem] * 2,
        scratch_shapes=[
            pltpu.VMEM((8, 1, n), F32),
            pltpu.VMEM((8, 1, n), F32),
            pltpu.VMEM((1, n), F32),
            pltpu.VMEM((1, n), F32),
            pltpu.SemaphoreType.DMA((16,)),
            pltpu.SemaphoreType.DMA((16,)),
            pltpu.SemaphoreType.DMA((8,)),
            pltpu.SemaphoreType.DMA((8,)),
            pltpu.SemaphoreType.DMA((2,)),
        ],
        compiler_params=pltpu.CompilerParams(
            collective_id=collective_id, has_side_effects=True, vmem_limit_bytes=40 * 2**20
        ),
    )(pieces, w_mod, bias)


def mod_backward_kernel(
    v1_ref, v2_ref, v3_ref, silu_ref, w_ref,
    mwg_ref, mbg_ref, sg_ref, v2_out, v3_out,
    v1_in, v2_in, mods, b2, b3, sgp, s0, s1, r1, s2, r2, s3, r3, s4, r4,
):
    pos = place()
    d, z, x, c, y = pos
    sib = neighbours(pos)[0]
    lin = d * 2 + y
    greet([(((lin + k) % 32) // 2, (lin + k) % 2) for k in range(1, 32)])
    me = (z * 2 + x) * 2 + y
    a = remote(v1_ref, v1_in, s0.at[0], s0.at[1], sib)
    b = remote(v2_ref, v2_in, s0.at[2], s0.at[3], sib)
    a.start()
    b.start()

    @pl.when(y == c)
    def _():
        b3[me] = v3_ref[...]

    sgp[...] = jnp.zeros_like(sgp)

    def send3(q, core):
        s = q * 2 + core
        return remote(v3_ref, b3.at[me], s3.at[s], r3.at[me], (s, c))

    for q in range(8):
        for core in range(2):

            @pl.when(jnp.logical_or(d != q * 2 + core, y != c))
            def _():
                send3(q, core).start()

    a.wait()
    b.wait()
    mods[me] = (v1_ref[...] + v1_in[...]).astype(BF16)
    b2[me] = v2_ref[...] + v2_in[...]

    def chip(k):
        m = (me + k) % 16
        return m, ((m // 2) * 2 + c, m % 2)

    for k in range(1, 16):
        m, peer = chip(k)
        remote(mods.at[me], mods.at[me], s1.at[k], r1.at[me], peer).start()
        remote(b2.at[me], b2.at[me], s2.at[k], r2.at[me], peer).start()
    for k in range(1, 16):
        m, peer = chip(k)
        remote(mods.at[m], mods.at[m], s1.at[k], r1.at[m], peer).wait_recv()
    every = jnp.concatenate([mods[i].astype(F32) for i in range(16)], axis=0)
    mbg_ref[...] = jnp.sum(every, axis=0, keepdims=True)
    every = every.astype(BF16)
    grad = lax.dot_general(
        every, w_ref[...], (((1,), (1,)), ((), ())), preferred_element_type=F32
    )
    for i in range(16):
        sgp[i, 0:1, :72] = grad[i : i + 1, :]

    def send4(k):
        m = (d + k) % 16
        return remote(sgp.at[m], sg_ref.at[d], s4.at[k], r4.at[d], (m, y))

    for k in range(1, 16):
        send4(k).start()
    sg_ref[d] = sgp[d]
    owned = jnp.concatenate([silu_ref[i].astype(F32)[0:1, :] for i in range(16)], axis=0)
    owned = owned.astype(BF16)[:, :72]
    width = w_ref.shape[1] // 6
    for j in range(6):
        cols = slice(j * width, (j + 1) * width)
        mwg_ref[:, cols] = lax.dot_general(
            owned, every[:, cols], (((0,), (0,)), ((), ())), preferred_element_type=F32
        )
    for k in range(1, 16):
        m, peer = chip(k)
        remote(b2.at[m], b2.at[m], s2.at[k], r2.at[m], peer).wait_recv()
    total = b2[0]
    for i in range(1, 16):
        total = total + b2[i]
    v2_out[...] = total

    def arrive3(i, guard):
        @pl.when(guard)
        def _():
            remote(v3_ref, b3.at[i], s3.at[0], r3.at[i], sib).wait_recv()

    for i in range(16):
        arrive3(i, jnp.logical_or(i != me, y != c))
    total = b3[0]
    for i in range(1, 16):
        total = total + b3[i]
    v3_out[...] = total
    for k in range(1, 16):
        m = (d + k) % 16
        remote(sgp.at[m], sg_ref.at[m], s4.at[k], r4.at[m], (m, y)).wait_recv()
    for q in range(8):
        for core in range(2):

            @pl.when(jnp.logical_or(d != q * 2 + core, y != c))
            def _():
                send3(q, core).wait_send()

    for k in range(1, 16):
        m, peer = chip(k)
        remote(mods.at[me], mods.at[me], s1.at[k], r1.at[me], peer).wait_send()
        remote(b2.at[me], b2.at[me], s2.at[k], r2.at[me], peer).wait_send()
        send4(k).wait_send()


def mod_backward(v1, v2, v3, silu, w_mod, collective_id):
    vmem = pl.BlockSpec(memory_space=pltpu.VMEM)
    n = w_mod.shape[1]
    n2, n3 = v2.shape[1], v3.shape[1]
    dma = pltpu.SemaphoreType.DMA((16,))
    return pl.pallas_call(
        mod_backward_kernel,
        out_shape=[
            jax.ShapeDtypeStruct((72, n), F32),
            jax.ShapeDtypeStruct((1, n), F32),
            jax.ShapeDtypeStruct((16, 8, 128), F32),
            jax.ShapeDtypeStruct((1, n2), F32),
            jax.ShapeDtypeStruct((1, n3), F32),
        ],
        in_specs=[vmem] * 5,
        out_specs=[vmem] * 5,
        scratch_shapes=[
            pltpu.VMEM((1, n), F32),
            pltpu.VMEM((1, n2), F32),
            pltpu.VMEM((16, 1, n), BF16),
            pltpu.VMEM((16, 1, n2), F32),
            pltpu.VMEM((16, 1, n3), F32),
            pltpu.VMEM((16, 8, 128), F32),
            pltpu.SemaphoreType.DMA((4,)),
        ]
        + [dma] * 8,
        compiler_params=pltpu.CompilerParams(
            collective_id=collective_id, has_side_effects=True, vmem_limit_bytes=40 * 2**20
        ),
    )(v1, v2, v3, silu, w_mod)


def index_of(z, x, c, y):
    return ((z * 2 + x) * 2 + c) * 2 + y


def core_pairs():
    return [
        (index_of(z, x, c, y), index_of(z, x, 1 - c, y))
        for z in range(4)
        for x in range(2)
        for c in range(2)
        for y in range(2)
    ]


def latent_pairs():
    return [
        (index_of(z, x, c, y), index_of(z, x, y, c))
        for z in range(4)
        for x in range(2)
        for c in range(2)
        for y in range(2)
        if c != y
    ]


def trade(value):
    moved = lax.ppermute(value, AXES, latent_pairs())
    home = lax.axis_index("dp") % 2 == lax.axis_index("tensor")
    return jnp.where(home, value, moved)


def both_halves(value):
    return jnp.concatenate([value, lax.ppermute(value, AXES, core_pairs())], axis=0)


def own_sum(partial):
    n = partial.shape[0] // 2
    moved = lax.ppermute(partial[n:].astype(BF16), AXES, core_pairs())
    return partial[:n] + moved.astype(F32)


def columns(n, step):
    return [(i, min(step, n - i)) for i in range(0, n, step)]


def on_device_chip(
    tokens,
    cond,
    mod_weight,
    mod_bias,
    query_key_value_weight,
    qkv_bias,
    attention_out_weight,
    attention_out_bias,
    first_hidden_weight,
    first_hidden_bias,
    second_hidden_weight,
    second_hidden_bias,
    out_grad,
):
    half, _, width = tokens.shape
    owned, _, cols = query_key_value_weight.shape
    head_size = width // HEADS
    heads_here = cols // head_size
    hidden = first_hidden_weight.shape[1]

    silu_cond, silu_back = jax.vjp(jax.nn.silu, cond.astype(F32))
    pieces = jnp.pad(
        silu_cond.astype(BF16).reshape(16, 1, owned), ((0, 0), (0, 7), (0, 128 - owned))
    )
    modulation, silu_owned = mod_forward(pieces, mod_weight, mod_bias.astype(F32)[None], 1)
    shift_a, scale_a, gate_a, shift_m, scale_m, gate_m = [
        modulation[:, i * width : (i + 1) * width] for i in range(6)
    ]

    bias_rows = jnp.concatenate([qkv_bias.reshape(-1), first_hidden_bias]).reshape(-1, width)
    carried = trade(jnp.concatenate([tokens.reshape(half, width), bias_rows], axis=0))
    tokens_here = carried[:half].astype(F32)
    biases = carried[half:].reshape(-1)
    q_bias, v_bias, fc1_bias = biases[:cols], biases[cols : 2 * cols], biases[2 * cols :]
    grad_out = trade(out_grad.reshape(half, width)).astype(F32)

    s_qkv = query_key_value_weight.reshape(1, owned, 3 * cols)
    s_proj = attention_out_weight.T.reshape(1, owned, cols)
    s_fc1 = first_hidden_weight.reshape(1, owned, hidden)
    s_fc2 = second_hidden_weight.T.reshape(1, owned, hidden)
    (w_qkv,) = gather_weights([s_qkv], [(0, (0, 896)), (0, (896, 832))], 2)
    w_qkv = w_qkv.reshape(width, 3 * cols)
    chunks = [(0, None)] + [(g, p) for g in (1, 2) for p in columns(hidden, 1152)]
    w_proj, w_fc1, w_fc2 = gather_weights([s_proj, s_fc1, s_fc2], chunks, 3)
    w_proj, w_fc1, w_fc2 = (w.reshape(width, -1) for w in (w_proj, w_fc1, w_fc2))

    normed_a, norm_a_back = jax.vjp(modulate, tokens_here, shift_a, scale_a)
    rows_a = both_halves(normed_a.astype(BF16))
    qkv_shift = jnp.concatenate([q_bias, jnp.zeros_like(q_bias), v_bias]).astype(F32)
    qkv = (jnp.dot(rows_a, w_qkv, preferred_element_type=F32) + qkv_shift).astype(BF16)
    packed = qkv.reshape(2 * half, 3, heads_here, head_size)
    attended, log_totals = attend_forward(packed)
    branch_a = own_sum(
        jnp.einsum("rc,dc->rd", attended, w_proj, preferred_element_type=F32)
    ) + attention_out_bias.astype(F32)
    resid_mid = tokens_here + gate_a * branch_a

    normed_m, norm_m_back = jax.vjp(modulate, resid_mid, shift_m, scale_m)
    rows_m = both_halves(normed_m.astype(BF16))
    preact = jnp.dot(rows_m, w_fc1, preferred_element_type=F32) + fc1_bias.astype(F32)
    activated, gelu_back = jax.vjp(gelu_tanh, preact)
    act_low = activated.astype(BF16)
    branch_m = own_sum(
        jnp.einsum("rf,df->rd", act_low, w_fc2, preferred_element_type=F32)
    ) + second_hidden_bias.astype(F32)
    output = (resid_mid + gate_m * branch_m).astype(BF16)

    gate_m_grad = jnp.sum(grad_out * branch_m, axis=0)
    grad_m_own = (grad_out * gate_m).astype(BF16)
    fc2_bias_part = jnp.sum(grad_m_own, axis=0, dtype=F32)
    grad_m = both_halves(grad_m_own)
    fc2_grad = jnp.einsum("rd,rf->df", grad_m, act_low, preferred_element_type=F32).astype(BF16)
    act_grad = jnp.dot(grad_m, w_fc2, preferred_element_type=F32)
    pre_grad = gelu_back(act_grad)[0].astype(BF16)
    fc1_bias_part = jnp.sum(pre_grad, axis=0, dtype=F32)
    fc1_grad = jnp.einsum("rd,rf->df", rows_m, pre_grad, preferred_element_type=F32).astype(BF16)
    normed_m_grad = own_sum(
        jnp.einsum("rf,df->rd", pre_grad, w_fc1, preferred_element_type=F32)
    )
    resid_part, shift_m_grad, scale_m_grad = norm_m_back(normed_m_grad)
    resid_grad = grad_out + resid_part

    gate_a_grad = jnp.sum(resid_grad * branch_a, axis=0)
    grad_a_own = (resid_grad * gate_a).astype(BF16)
    proj_bias_part = jnp.sum(grad_a_own, axis=0, dtype=F32)
    grad_a = both_halves(grad_a_own)
    proj_grad = jnp.einsum("rd,rc->dc", grad_a, attended, preferred_element_type=F32).astype(BF16)
    attended_grad = jnp.dot(grad_a, w_proj, preferred_element_type=F32).astype(BF16)
    qkv_grad = attend_backward(
        (packed, attended_grad.reshape(2 * half, heads_here, head_size), log_totals)
    ).reshape(2 * half, 3 * cols)
    qkv_bias_part = jnp.sum(qkv_grad, axis=0, dtype=F32)
    qkv_bias_part = jnp.concatenate([qkv_bias_part[:cols], qkv_bias_part[2 * cols :]])
    qkv_wgrad = jnp.einsum("rd,rc->dc", rows_a, qkv_grad, preferred_element_type=F32).astype(BF16)
    normed_a_grad = own_sum(
        jnp.einsum("rc,dc->rd", qkv_grad, w_qkv, preferred_element_type=F32)
    )
    input_part, shift_a_grad, scale_a_grad = norm_a_back(normed_a_grad)
    tokens_grad = (resid_grad + input_part).astype(BF16)

    chunks = [(g, p) for g in (0, 1) for p in columns(hidden, 768)] + [(2, (0, cols))]
    fc2_out, fc1_out, proj_out = reduce_grads(
        [g.reshape(16, owned, -1) for g in (fc2_grad, fc1_grad, proj_grad)], chunks, 4
    )
    (qkv_out,) = reduce_grads(
        [qkv_wgrad.reshape(16, owned, -1)], [(0, (0, 640)), (0, (640, 640)), (0, (1280, 448))], 5
    )

    mod_part = jnp.concatenate(
        [
            shift_a_grad.reshape(1, -1),
            scale_a_grad.reshape(1, -1),
            gate_a_grad.reshape(1, -1),
            shift_m_grad.reshape(1, -1),
            scale_m_grad.reshape(1, -1),
            gate_m_grad.reshape(1, -1),
        ],
        axis=1,
    )
    wide_part = jnp.concatenate([fc2_bias_part, proj_bias_part])[None]
    half_part = jnp.concatenate([fc1_bias_part, qkv_bias_part])[None]
    mod_weight_grad, mod_bias_grad, silu_grad, wide, narrow = mod_backward(
        mod_part, wide_part, half_part, silu_owned, mod_weight, 6
    )
    cond_grad = silu_back(silu_grad[:, 0, :owned].reshape(1, width))[0]
    return (
        trade(output).reshape(half, 1, width),
        trade(tokens_grad).reshape(half, 1, width),
        cond_grad,
        mod_weight_grad,
        mod_bias_grad[0],
        qkv_out.reshape(owned, 3, cols),
        narrow[0, hidden:].reshape(2, cols),
        proj_out.T,
        wide[0, width:],
        fc1_out,
        narrow[0, :hidden],
        fc2_out.T,
        wide[0, :width],
    )


def solution(mesh):
    shape = dict(mesh.shape)
    body = on_device_chip if shape == {"dp": 16, "tensor": 2} else on_device_general
    return jax.shard_map(
        body,
        mesh=mesh,
        in_specs=(
            P("tensor", "dp", None),
            P("dp", None),
            P("dp", None),
            P(),
            P("dp", None, "tensor"),
            P(None, "tensor"),
            P("tensor", "dp"),
            P(),
            P("dp", "tensor"),
            P("tensor"),
            P("tensor", "dp"),
            P(),
            P("tensor", "dp", None),
        ),
        out_specs=(
            P("tensor", "dp", None),
            P("tensor", "dp", None),
            P("dp", None),
            P("dp", None),
            P(),
            P("dp", None, "tensor"),
            P(None, "tensor"),
            P("tensor", "dp"),
            P(),
            P("dp", "tensor"),
            P("tensor"),
            P("tensor", "dp"),
            P(),
        ),
        check_vma=False,
    )
```

```python
import functools
import math

import jax
import jax.numpy as jnp
from jax import lax
from jax.experimental import pallas as pl
from jax.experimental.pallas import tpu as pltpu
from jax.sharding import PartitionSpec as P

HEADS = 16
MESH = pl.DeviceIdType.MESH
AXES = ("dp", "tensor")
F32 = jnp.float32
BF16 = jnp.bfloat16


def modulate(hidden, shifts, scales):
    center = hidden - jnp.mean(hidden, axis=-1, keepdims=True)
    spread = jnp.mean(center * center, axis=-1, keepdims=True)
    return center * lax.rsqrt(spread + 1e-06) * (1.0 + scales) + shifts


def gelu_tanh(values):
    return jax.nn.gelu(values, approximate=True)


def attend_forward(packed):
    queries = packed[:, 0]
    keys_all = packed[:, 1]
    values_all = packed[:, 2]
    seq_len = packed.shape[0]
    scaling = packed.shape[3] ** (-0.5)
    block_rows = min(512, seq_len)
    results = []
    log_parts = []
    for offset in range(0, seq_len, block_rows):
        query_block = queries[offset : offset + block_rows]
        scores = (
            jnp.einsum("qhe,khe->hqk", query_block, keys_all, preferred_element_type=jnp.float32)
            * scaling
        )
        highest = jnp.max(scores, axis=-1, keepdims=True)
        weights = jnp.exp(scores - highest)
        row_total = jnp.sum(weights, axis=-1, keepdims=True)
        prob_low = (weights / row_total).astype(jnp.bfloat16)
        mixture = jnp.einsum(
            "hqk,khe->qhe", prob_low, values_all, preferred_element_type=jnp.float32
        )
        results.append(mixture.reshape(block_rows, -1))
        log_parts.append((highest + jnp.log(row_total))[..., 0])
    return (jnp.concatenate(results, 0).astype(jnp.bfloat16), jnp.concatenate(log_parts, 1))


def attend_backward(inputs):
    packed, grad_out, log_totals = inputs
    queries = packed[:, 0]
    keys_all = packed[:, 1]
    values_all = packed[:, 2]
    seq_len = packed.shape[0]
    scaling = packed.shape[3] ** (-0.5)
    block_rows = min(512, seq_len)
    query_grads = []
    key_grad = jnp.zeros(keys_all.shape, jnp.float32)
    value_grad = jnp.zeros(values_all.shape, jnp.float32)
    for offset in range(0, seq_len, block_rows):
        query_block = queries[offset : offset + block_rows]
        grad_block = grad_out[offset : offset + block_rows]
        scores = (
            jnp.einsum("qhe,khe->hqk", query_block, keys_all, preferred_element_type=jnp.float32)
            * scaling
        )
        probs = jnp.exp(scores - log_totals[:, offset : offset + block_rows, None])
        prob_low = probs.astype(jnp.bfloat16)
        prob_grad = jnp.einsum(
            "qhe,khe->hqk", grad_block, values_all, preferred_element_type=jnp.float32
        )
        inner = jnp.sum(probs * prob_grad, axis=-1, keepdims=True)
        score_grad = (probs * (prob_grad - inner)).astype(jnp.bfloat16)
        query_grads.append(
            jnp.einsum("hqk,khe->qhe", score_grad, keys_all, preferred_element_type=jnp.float32)
            * scaling
        )
        key_grad = (
            key_grad
            + jnp.einsum(
                "hqk,qhe->khe", score_grad, query_block, preferred_element_type=jnp.float32
            )
            * scaling
        )
        value_grad = value_grad + jnp.einsum(
            "hqk,qhe->khe", prob_low, grad_block, preferred_element_type=jnp.float32
        )
    return jnp.stack([jnp.concatenate(query_grads, 0), key_grad, value_grad], 1).astype(
        jnp.bfloat16
    )


def on_device_general(
    tokens,
    cond,
    mod_weight,
    mod_bias,
    query_key_value_weight,
    qkv_bias,
    attention_out_weight,
    attention_out_bias,
    first_hidden_weight,
    first_hidden_bias,
    second_hidden_weight,
    second_hidden_bias,
    out_grad,
):
    w_mod, w_qkv, w_proj, w_fc1, w_fc2 = (
        lax.all_gather(mod_weight, "dp", axis=0, tiled=True),
        lax.all_gather(query_key_value_weight, "dp", axis=0, tiled=True),
        lax.all_gather(attention_out_weight, "dp", axis=1, tiled=True),
        lax.all_gather(first_hidden_weight, "dp", axis=0, tiled=True),
        lax.all_gather(second_hidden_weight, "dp", axis=1, tiled=True),
    )
    seq_local, latents, width = tokens.shape
    columns = query_key_value_weight.shape[2]
    head_size = width // HEADS
    heads_here = columns // head_size
    local_rows = seq_local * latents
    cond_wide = cond.astype(jnp.float32)
    silu_cond, silu_back = jax.vjp(jax.nn.silu, cond_wide)
    silu_low = silu_cond.astype(jnp.bfloat16)
    modulation = jnp.dot(silu_low, w_mod, preferred_element_type=jnp.float32) + mod_bias.astype(
        jnp.float32
    )
    pieces = modulation.reshape(latents, 6, width)
    hidden_in = tokens.astype(jnp.float32)
    attention_normalized, norm_a_back = jax.vjp(modulate, hidden_in, pieces[:, 0], pieces[:, 1])
    gathered_a = lax.all_gather(
        attention_normalized.astype(jnp.bfloat16), "tensor", axis=0, tiled=True
    )
    seq_len = gathered_a.shape[0]
    total_rows = seq_len * latents
    rows_a = gathered_a.reshape(total_rows, width)
    qkv_flat = w_qkv.reshape(width, 3 * columns)
    zero_row = jnp.zeros((columns,), jnp.float32)
    query_key_value_shift = jnp.stack(
        [qkv_bias[0].astype(jnp.float32), zero_row, qkv_bias[1].astype(jnp.float32)]
    )
    projected_output = (
        jnp.dot(rows_a, qkv_flat, preferred_element_type=jnp.float32).reshape(
            seq_len, latents, 3, columns
        )
        + query_key_value_shift
    )
    packed = jnp.moveaxis(projected_output.astype(jnp.bfloat16), 1, 0).reshape(
        latents, seq_len, 3, heads_here, head_size
    )
    attention_result, log_totals = lax.map(attend_forward, packed)
    attended_rows = jnp.moveaxis(attention_result, 0, 1).reshape(total_rows, columns)
    summed_a = lax.psum_scatter(
        jnp.dot(attended_rows, w_proj, preferred_element_type=jnp.float32).astype(jnp.bfloat16),
        "tensor",
        scatter_dimension=0,
        tiled=True,
    ).astype(jnp.float32)
    attention_branch = summed_a.reshape(seq_local, latents, width) + attention_out_bias.astype(
        jnp.float32
    )
    resid_mid = hidden_in + pieces[:, 2] * attention_branch
    feedforward_normalized, norm_m_back = jax.vjp(modulate, resid_mid, pieces[:, 3], pieces[:, 4])
    gathered_m = lax.all_gather(
        feedforward_normalized.astype(jnp.bfloat16), "tensor", axis=0, tiled=True
    )
    rows_m = gathered_m.reshape(total_rows, width)
    before_activation = jnp.dot(
        rows_m, w_fc1, preferred_element_type=jnp.float32
    ) + first_hidden_bias.astype(jnp.float32)
    gelu_activated, gelu_back = jax.vjp(gelu_tanh, before_activation)
    act_low = gelu_activated.astype(jnp.bfloat16)
    summed_m = lax.psum_scatter(
        jnp.dot(act_low, w_fc2, preferred_element_type=jnp.float32).astype(jnp.bfloat16),
        "tensor",
        scatter_dimension=0,
        tiled=True,
    ).astype(jnp.float32)
    feedforward_branch = summed_m.reshape(seq_local, latents, width) + second_hidden_bias.astype(
        jnp.float32
    )
    output = (resid_mid + pieces[:, 5] * feedforward_branch).astype(jnp.bfloat16)
    grad_out = out_grad.astype(jnp.float32)
    gate_m_grad = jnp.sum(grad_out * feedforward_branch, axis=0)
    grad_m_low = (grad_out * pieces[:, 5]).astype(jnp.bfloat16)
    grad_m_rows = lax.all_gather(grad_m_low, "tensor", axis=0, tiled=True).reshape(
        total_rows, width
    )
    fc2_bias_grad = jnp.sum(grad_m_rows, axis=0, dtype=jnp.float32)
    fc2_weight_grad = jnp.einsum(
        "rf,rd->fd", act_low, grad_m_rows, preferred_element_type=jnp.float32
    )
    act_grad = jnp.einsum("rd,fd->rf", grad_m_rows, w_fc2, preferred_element_type=jnp.float32)
    pre_grad = gelu_back(act_grad)[0].astype(jnp.bfloat16)
    fc1_bias_grad = jnp.sum(pre_grad, axis=0, dtype=jnp.float32)
    fc1_weight_grad = jnp.einsum("rd,rf->df", rows_m, pre_grad, preferred_element_type=jnp.float32)
    normed_m_grad = (
        lax.psum_scatter(
            jnp.einsum("rf,df->rd", pre_grad, w_fc1, preferred_element_type=jnp.float32).astype(
                jnp.bfloat16
            ),
            "tensor",
            scatter_dimension=0,
            tiled=True,
        )
        .astype(jnp.float32)
        .reshape(seq_local, latents, width)
    )
    resid_part, shift_m_grad, scale_m_grad = norm_m_back(normed_m_grad)
    resid_grad = grad_out + resid_part
    gate_a_grad = jnp.sum(resid_grad * attention_branch, axis=0)
    grad_a_low = (resid_grad * pieces[:, 2]).astype(jnp.bfloat16)
    grad_a_flat = grad_a_low.reshape(local_rows, width)
    proj_bias_part = jnp.sum(grad_a_flat, axis=0, dtype=jnp.float32)
    grad_a_rows = lax.all_gather(grad_a_low, "tensor", axis=0, tiled=True).reshape(
        total_rows, width
    )
    proj_weight_grad = jnp.einsum(
        "rc,rd->cd", attended_rows, grad_a_rows, preferred_element_type=jnp.float32
    )
    attended_grad = jnp.einsum(
        "rd,cd->rc", grad_a_rows, w_proj, preferred_element_type=jnp.float32
    ).astype(jnp.bfloat16)
    grad_packed = jnp.moveaxis(attended_grad.reshape(seq_len, latents, heads_here, head_size), 1, 0)
    qkv_grad_packed = lax.map(attend_backward, (packed, grad_packed, log_totals))
    qkv_grad_rows = jnp.moveaxis(qkv_grad_packed, 0, 1).reshape(total_rows, 3 * columns)
    bias_sums = jnp.sum(qkv_grad_rows.reshape(total_rows, 3, columns), axis=0, dtype=jnp.float32)
    qkv_bias_grad = jnp.stack([bias_sums[0], bias_sums[2]])
    qkv_weight_grad = jnp.einsum(
        "rd,rc->dc", rows_a, qkv_grad_rows, preferred_element_type=jnp.float32
    ).reshape(width, 3, columns)
    normed_a_grad = (
        lax.psum_scatter(
            jnp.einsum(
                "rc,dc->rd", qkv_grad_rows, qkv_flat, preferred_element_type=jnp.float32
            ).astype(jnp.bfloat16),
            "tensor",
            scatter_dimension=0,
            tiled=True,
        )
        .astype(jnp.float32)
        .reshape(seq_local, latents, width)
    )
    input_part, shift_a_grad, scale_a_grad = norm_a_back(normed_a_grad)
    tokens_grad = (resid_grad + input_part).astype(jnp.bfloat16)
    partial_mod = jnp.stack(
        [shift_a_grad, scale_a_grad, gate_a_grad, shift_m_grad, scale_m_grad, gate_m_grad], 1
    ).reshape(latents, 6 * width)
    mod_summed, proj_bias_grad = (
        lax.psum(partial_mod.astype(jnp.bfloat16), "tensor").astype(jnp.float32),
        lax.psum(proj_bias_part.astype(jnp.bfloat16), "tensor").astype(jnp.float32),
    )
    mod_grad_low = mod_summed.astype(jnp.bfloat16)
    silu_grad = jnp.einsum("le,de->ld", mod_grad_low, w_mod, preferred_element_type=jnp.float32)
    cond_grad = silu_back(silu_grad)[0]
    silu_every, mod_every = (
        lax.all_gather(silu_low, "dp", axis=0, tiled=True),
        lax.all_gather(mod_grad_low, "dp", axis=0, tiled=True),
    )
    owned_rows = mod_weight.shape[0]
    silu_owned = lax.dynamic_slice_in_dim(
        silu_every, lax.axis_index("dp") * owned_rows, owned_rows, 1
    )
    mod_weight_grad = jnp.einsum(
        "ld,le->de", silu_owned, mod_every, preferred_element_type=jnp.float32
    )
    mod_bias_grad = jnp.sum(mod_every, axis=0, dtype=jnp.float32)
    qkv_weight_grad, proj_weight_grad, fc1_weight_grad, fc2_weight_grad = (
        lax.psum_scatter(
            qkv_weight_grad.astype(jnp.bfloat16), "dp", scatter_dimension=0, tiled=True
        ).astype(jnp.float32),
        lax.psum_scatter(
            proj_weight_grad.astype(jnp.bfloat16), "dp", scatter_dimension=1, tiled=True
        ).astype(jnp.float32),
        lax.psum_scatter(
            fc1_weight_grad.astype(jnp.bfloat16), "dp", scatter_dimension=0, tiled=True
        ).astype(jnp.float32),
        lax.psum_scatter(
            fc2_weight_grad.astype(jnp.bfloat16), "dp", scatter_dimension=1, tiled=True
        ).astype(jnp.float32),
    )
    qkv_bias_grad, proj_bias_grad, fc1_bias_grad, fc2_bias_grad = lax.psum(
        (qkv_bias_grad, proj_bias_grad, fc1_bias_grad, fc2_bias_grad), "dp"
    )
    return (
        output,
        tokens_grad,
        cond_grad,
        mod_weight_grad,
        mod_bias_grad,
        qkv_weight_grad,
        qkv_bias_grad,
        proj_weight_grad,
        proj_bias_grad,
        fc1_weight_grad,
        fc1_bias_grad,
        fc2_weight_grad,
        fc2_bias_grad,
    )


def place():
    d = lax.axis_index("dp")
    y = lax.axis_index("tensor")
    return d, d // 4, (d // 2) % 2, d % 2, y


def neighbours(pos):
    d, z, x, c, y = pos
    sib = (z * 4 + x * 2 + (1 - c), y)
    xn = (z * 4 + (1 - x) * 2 + c, y)
    yn = (d, 1 - y)
    return sib, xn, yn


def z_peer(pos, k):
    d, z, x, c, y = pos
    return (((z + k) % 4) * 4 + x * 2 + c, y)


def greet(peers):
    sem = pltpu.get_barrier_semaphore()
    for peer in peers:
        pl.semaphore_signal(sem, inc=1, device_id=peer, device_id_type=MESH)
    pl.semaphore_wait(sem, len(peers))


def chip_peers(pos):
    d, z, x, c, y = pos
    across = [(z * 4 + x * 2 + 1 - c, 1 - y)]
    return list(neighbours(pos)) + across + [z_peer(pos, k) for k in (1, 2, 3)]


def remote(src, dst, send, recv, peer):
    return pltpu.make_async_remote_copy(
        src_ref=src, dst_ref=dst, send_sem=send, recv_sem=recv, device_id=peer, device_id_type=MESH
    )


GATHER_RECV = 24
GATHER_SEND = 28


class Gather:
    def __init__(self, shard, full, relay, cols, recv, send, pos):
        self.shard, self.full, self.relay, self.cols = shard, full, relay, cols
        self.recv, self.send, self.pos = recv, send, pos
        d, z, x, c, y = pos
        self.sib, self.xn, _ = neighbours(pos)
        self.far = (z * 4 + x * 2 + y, 1 - y)
        self.home, self.away = c == y, c != y

    def part(self, ref, b):
        if self.cols is None:
            return ref.at[pl.ds(b, 1)]
        return ref.at[pl.ds(b, 1), :, pl.ds(*self.cols)]

    def move(self, src, dst, s, r, peer):
        return remote(src, dst, self.send.at[s], self.recv.at[r], peer)

    def came(self, r):
        block = self.part(self.full, 0)
        self.move(block, block, 0, r, self.sib).wait_recv()

    def stay(self):
        return pltpu.make_async_copy(
            self.part(self.shard, 0), self.part(self.full, self.pos[0]), self.send.at[27]
        )

    def start(self):
        d, z, x, c, y = self.pos
        q = z * 2 + x
        own = self.part(self.shard, 0)

        @pl.when(self.home)
        def _():
            for k in (2, 1, 3):
                self.move(own, self.part(self.full, d), k, q, z_peer(self.pos, k)).start()
            self.move(own, self.part(self.full, d), 4, q, self.xn).start()
            self.move(own, self.part(self.full, d), 8, 8 + q, self.far).start()
            self.stay().start()

        @pl.when(self.away)
        def _():
            for k in (2, 1, 3):
                self.move(own, self.part(self.relay, q), k, q, z_peer(self.pos, k)).start()
            self.move(own, self.part(self.full, d), 8, 16 + q, self.far).start()
            self.move(own, self.part(self.relay, q), 4, q, self.xn).start()
            self.move(own, self.part(self.full, d), 16, 8 + q, self.sib).start()

    def from_z(self, k):
        d, z, x, c, y = self.pos
        q = ((z + k) % 4) * 2 + x
        dst = self.part(self.full, 2 * q + c)

        @pl.when(self.home)
        def _():
            self.came(q)
            self.move(dst, dst, 4 + k, q, self.xn).start()
            self.move(dst, dst, 8 + k, 8 + q, self.far).start()

        @pl.when(self.away)
        def _():
            self.came(q)
            src = self.part(self.relay, q)
            self.move(src, dst, 8 + k, 16 + q, self.far).start()
            self.move(src, src, 4 + k, q, self.xn).start()
            self.move(src, dst, 16 + k, 8 + q, self.sib).start()

    def from_x(self, k):
        d, z, x, c, y = self.pos
        q = ((z + k) % 4) * 2 + 1 - x
        dst = self.part(self.full, 2 * q + c)

        @pl.when(self.home)
        def _():
            self.came(q)
            self.move(dst, dst, 12 + k, 8 + q, self.far).start()

        @pl.when(self.away)
        def _():
            self.came(q)
            self.move(self.part(self.relay, q), dst, 20 + k, 8 + q, self.sib).start()

    def from_y(self, k):
        d, z, x, c, y = self.pos
        q = ((z + k) % 4) * 2 + x

        @pl.when(self.away)
        def _():
            block = self.part(self.full, 2 * q + 1 - c)
            self.came(16 + q)
            self.move(block, block, 12 + k, 16 + q, self.xn).start()

    def finish(self):
        d, z, x, c, y = self.pos
        block = self.part(self.full, 0)

        @pl.when(self.home)
        def _():
            self.stay().wait()
            for q in range(8):
                self.came(8 + q)
            for s in list(range(1, 16)):
                self.move(block, block, s, 0, self.sib).wait_send()

        @pl.when(self.away)
        def _():
            for q in range(8):
                self.came(8 + q)
            for k in range(4):
                self.came(16 + ((z + k) % 4) * 2 + 1 - x)
            for s in list(range(1, 24)):
                self.move(block, block, s, 0, self.sib).wait_send()


def gather_events(parts):
    events = [p.start for p in parts]
    for p in parts:
        for k in (1, 2, 3):
            events.append(functools.partial(p.from_z, k))
    late = []
    for p in parts:
        for k in range(4):
            late.append(functools.partial(p.from_x, k))
            late.append(functools.partial(p.from_y, k))
    return events + late + [p.finish for p in parts]


def gather_parts(shards, fulls, relays, chunks, recv, send, pos):
    return [
        Gather(shards[g], fulls[g], relays[g], cols, recv.at[i], send.at[i], pos)
        for i, (g, cols) in enumerate(chunks)
    ]


def gather_kernel(chunks, count, *refs):
    shards, fulls, relays = (refs[i * count : (i + 1) * count] for i in range(3))
    recv, send = refs[3 * count :]
    pos = place()
    greet(chip_peers(pos))
    for event in gather_events(gather_parts(shards, fulls, relays, chunks, recv, send, pos)):
        event()


def gather_sems(chunks):
    n = len(chunks)
    return [
        pltpu.SemaphoreType.DMA((n, GATHER_RECV)),
        pltpu.SemaphoreType.DMA((n, GATHER_SEND)),
    ]


def gather_shapes(shards):
    return [jax.ShapeDtypeStruct((16,) + s.shape[1:], s.dtype) for s in shards] + [
        jax.ShapeDtypeStruct((8,) + s.shape[1:], s.dtype) for s in shards
    ]


def gather_weights(shards, chunks, collective_id):
    count = len(shards)
    anywhere = pl.BlockSpec(memory_space=pl.ANY)
    return pl.pallas_call(
        functools.partial(gather_kernel, chunks, count),
        out_shape=gather_shapes(shards),
        in_specs=[anywhere] * count,
        out_specs=[anywhere] * (2 * count),
        scratch_shapes=gather_sems(chunks),
        compiler_params=pltpu.CompilerParams(
            collective_id=collective_id, has_side_effects=True
        ),
    )(*shards)[:count]


REDUCE_RECV = 27
REDUCE_SEND = 23


class Reduce:
    def __init__(self, grad, land, out, recv, send, pos, cols):
        self.grad, self.land, self.out = grad, land, out
        self.recv, self.send, self.pos, self.cols = recv, send, pos, pl.ds(*cols)
        d, z, x, c, y = pos
        self.sib, self.xn, self.yn = neighbours(pos)
        self.home, self.away = c == y, c != y

    def rows(self, b):
        return self.grad.at[pl.ds(b, 1), :, self.cols]

    def slot(self, i):
        return self.land.at[pl.ds(i, 1)]

    def push(self, src, slot, s, peer):
        return remote(src, self.slot(slot), self.send.at[s], self.recv.at[slot], peer)

    def came(self, slot):
        self.push(self.slot(slot), slot, 0, self.sib).wait_recv()

    def value(self, i):
        return self.land[i].astype(F32)

    def first(self):
        d, z, x, c, y = self.pos

        @pl.when(self.away)
        def _():
            for column, base in ((1 - x, 0), (x, 4)):

                def step(k, _):
                    q = lax.rem(z + 1 + k, 4) * 2 + column
                    self.push(self.rows(2 * q + c), q, base + k, self.yn).start()
                    self.push(self.rows(2 * q + 1 - c), 15 + q, 8 + base + k, self.sib).start()
                    return 0

                lax.fori_loop(0, 4, step, 0)

        @pl.when(self.home)
        def _():
            for column, base in ((1 - x, 0), (x, 4)):

                def step(k, _):
                    q = lax.rem(z + 1 + k, 4) * 2 + column
                    self.push(self.rows(2 * q + 1 - c), q, base + k, self.sib).start()
                    return 0

                lax.fori_loop(0, 4, step, 0)

    def second(self):
        d, z, x, c, y = self.pos

        @pl.when(self.away)
        def _():
            def step(k, _):
                zz = lax.rem(z + 1 + k, 4)
                q = zz * 2 + 1 - x
                self.came(q)
                self.push(self.slot(q), 8 + zz, 16 + k, self.xn).start()
                return 0

            lax.fori_loop(0, 4, step, 0)

        @pl.when(self.home)
        def _():
            def over_x(k, _):
                zz = lax.rem(z + 1 + k, 4)
                q = zz * 2 + 1 - x
                self.came(15 + q)
                self.push(self.slot(15 + q), 23 + zz, 15 + k, self.xn).start()
                return 0

            lax.fori_loop(0, 4, over_x, 0)

            def step(k, _):
                zz = lax.rem(z + 1 + k, 4)
                q = zz * 2 + 1 - x
                b = 2 * q + c
                self.came(q)
                total = self.grad[b, :, self.cols].astype(F32) + self.value(q)
                self.grad[b, :, self.cols] = total.astype(BF16)
                self.push(self.rows(b), 8 + zz, 8 + k, self.xn).start()
                return 0

            lax.fori_loop(0, 4, step, 0)

    def third(self):
        d, z, x, c, y = self.pos

        @pl.when(self.home)
        def _():
            def far(k, _):
                zz = lax.rem(z + 1 + k, 4)
                q = zz * 2 + x
                self.came(15 + q)
                self.came(23 + zz)
                self.land[15 + q] = (self.value(15 + q) + self.value(23 + zz)).astype(BF16)
                self.push(self.slot(15 + q), 15 + zz, 19 + k, self.yn).start()
                return 0

            lax.fori_loop(0, 4, far, 0)

            def step(k, _):
                zz = lax.rem(z + 1 + k, 4)
                q = zz * 2 + x
                b = 2 * q + c
                self.came(q)
                self.came(8 + zz)
                total = self.grad[b, :, self.cols].astype(F32)
                total = total + self.value(q) + self.value(8 + zz)
                self.grad[b, :, self.cols] = total.astype(BF16)
                self.push(self.rows(b), 12 + k, 12 + k, (zz * 4 + x * 2 + c, y)).start()
                return 0

            lax.fori_loop(0, 3, step, 0)

    def fourth(self):
        d, z, x, c, y = self.pos

        @pl.when(self.away)
        def _():
            def step(k, _):
                zz = lax.rem(z + 1 + k, 4)
                q = zz * 2 + x
                self.came(q)
                self.came(8 + zz)
                self.came(15 + zz)
                total = self.value(q) + self.value(8 + zz) + self.value(15 + zz)
                self.land[q] = total.astype(BF16)
                self.push(self.slot(q), 12 + k, 20 + k, (zz * 4 + x * 2 + c, y)).start()
                return 0

            lax.fori_loop(0, 3, step, 0)

    def fifth(self):
        d, z, x, c, y = self.pos
        q = z * 2 + x
        self.came(q)
        self.came(8 + z)
        for k in range(3):
            self.came(12 + k)
        total = self.value(q) + self.value(8 + z)
        total = total + self.value(12) + self.value(13) + self.value(14)

        @pl.when(self.home)
        def _():
            self.out[:, self.cols] = total + self.grad[d, :, self.cols].astype(F32)

        @pl.when(self.away)
        def _():
            self.came(15 + z)
            self.out[:, self.cols] = total + self.value(15 + z)

    def finish(self):
        block = self.slot(0)
        for s in range(REDUCE_SEND):
            self.push(block, 0, s, self.sib).wait_send()


def reduce_events(parts):
    n = len(parts)
    stages = (Reduce.first, Reduce.second, Reduce.third, Reduce.fourth, Reduce.fifth)
    events = [parts[0].first]
    for i in range(n + 3):
        if i + 1 < n:
            events.append(parts[i + 1].first)
        for lag, stage in enumerate(stages[1:]):
            if 0 <= i - lag < n:
                events.append(functools.partial(stage, parts[i - lag]))
    return events + [p.finish for p in parts]


def reduce_kernel(chunks, count, *refs):
    n = len(chunks)
    grads, outs = refs[:count], refs[count : 2 * count]
    lands, (recv, send) = refs[2 * count : 2 * count + n], refs[2 * count + n :]
    pos = place()
    greet(chip_peers(pos))
    parts = [
        Reduce(grads[g], lands[i], outs[g], recv.at[i], send.at[i], pos, cols)
        for i, (g, cols) in enumerate(chunks)
    ]
    for event in reduce_events(parts):
        event()


def reduce_scratch(chunks):
    n = len(chunks)
    return [pltpu.VMEM((27, 72, cols[1]), BF16) for _, cols in chunks] + [
        pltpu.SemaphoreType.DMA((n, REDUCE_RECV)),
        pltpu.SemaphoreType.DMA((n, REDUCE_SEND)),
    ]


def reduce_grads(grads, chunks, collective_id):
    count = len(grads)
    vmem = pl.BlockSpec(memory_space=pltpu.VMEM)
    return pl.pallas_call(
        functools.partial(reduce_kernel, chunks, count),
        out_shape=[jax.ShapeDtypeStruct(g.shape[1:], F32) for g in grads],
        in_specs=[vmem] * count,
        out_specs=[vmem] * count,
        scratch_shapes=reduce_scratch(chunks),
        compiler_params=pltpu.CompilerParams(
            collective_id=collective_id, has_side_effects=True, vmem_limit_bytes=63000 * 1024
        ),
    )(*grads)


def mod_forward_kernel(
    piece_ref, w_ref, bias_ref, mod_ref, silu_ref, part, land, mine, other, s1, r1, s2, r2, s3
):
    pos = place()
    d, z, x, c, y = pos
    sib = neighbours(pos)[0]
    greet([((d + k) % 16, y) for k in range(1, 16)])

    def piece(k):
        to = (d + k) % 16
        return remote(piece_ref.at[to], silu_ref.at[d], s1.at[k], r1.at[d], (to, y))

    def piece_in(k):
        src = (d + k) % 16
        return remote(piece_ref.at[src], silu_ref.at[src], s1.at[k], r1.at[src], (src, y))

    for k in range(1, 16):
        piece(k).start()
    silu_ref[d] = piece_ref[d]
    for k in range(1, 16):
        piece_in(k).wait_recv()
    rows = jnp.concatenate(
        [silu_ref[2 * q + y].astype(F32)[0:1, :] for q in range(8)], axis=0
    ).astype(BF16)[:, :72]
    width = w_ref.shape[1] // 6
    for j in range(6):
        cols = slice(j * width, (j + 1) * width)
        value = jnp.dot(rows, w_ref[:, cols], preferred_element_type=F32)
        for q in range(8):
            part[q, :, cols] = value[q : q + 1, :]
    me = z * 2 + x

    def send_part(k):
        q = (me + k) % 8
        return remote(part.at[q], land.at[me], s2.at[k], r2.at[me], (q * 2 + c, y))

    def part_in(k):
        q = (me + k) % 8
        return remote(part.at[q], land.at[q], s2.at[k], r2.at[q], (q * 2 + c, y))

    for k in range(1, 8):
        send_part(k).start()
    land[me] = part[me]
    for k in range(1, 8):
        part_in(k).wait_recv()
    total = land[0]
    for q in range(1, 8):
        total = total + land[q]
    mine[...] = total
    swap = remote(mine, other, s3.at[0], s3.at[1], sib)
    swap.start()
    for k in range(1, 16):
        piece(k).wait_send()
    for k in range(1, 8):
        send_part(k).wait_send()
    swap.wait()
    mod_ref[...] = mine[...] + other[...] + bias_ref[...]


def mod_forward(pieces, w_mod, bias, collective_id):
    vmem = pl.BlockSpec(memory_space=pltpu.VMEM)
    n = w_mod.shape[1]
    return pl.pallas_call(
        mod_forward_kernel,
        out_shape=[jax.ShapeDtypeStruct((1, n), F32), jax.ShapeDtypeStruct((16, 8, 128), BF16)],
        in_specs=[vmem] * 3,
        out_specs=[vmem] * 2,
        scratch_shapes=[
            pltpu.VMEM((8, 1, n), F32),
            pltpu.VMEM((8, 1, n), F32),
            pltpu.VMEM((1, n), F32),
            pltpu.VMEM((1, n), F32),
            pltpu.SemaphoreType.DMA((16,)),
            pltpu.SemaphoreType.DMA((16,)),
            pltpu.SemaphoreType.DMA((8,)),
            pltpu.SemaphoreType.DMA((8,)),
            pltpu.SemaphoreType.DMA((2,)),
        ],
        compiler_params=pltpu.CompilerParams(
            collective_id=collective_id, has_side_effects=True, vmem_limit_bytes=40 * 2**20
        ),
    )(pieces, w_mod, bias)


def mod_backward_kernel(
    v1_ref, v2_ref, v3_ref, silu_ref, w_ref,
    mwg_ref, mbg_ref, sg_ref, v2_out, v3_out,
    v1_in, v2_in, mods, b2, b3, sgp, s0, s1, r1, s2, r2, s3, r3, s4, r4,
):
    pos = place()
    d, z, x, c, y = pos
    sib = neighbours(pos)[0]
    lin = d * 2 + y
    greet([(((lin + k) % 32) // 2, (lin + k) % 2) for k in range(1, 32)])
    me = (z * 2 + x) * 2 + y
    a = remote(v1_ref, v1_in, s0.at[0], s0.at[1], sib)
    b = remote(v2_ref, v2_in, s0.at[2], s0.at[3], sib)
    a.start()
    b.start()

    @pl.when(y == c)
    def _():
        b3[me] = v3_ref[...]

    sgp[...] = jnp.zeros_like(sgp)

    def send3(q, core):
        s = q * 2 + core
        return remote(v3_ref, b3.at[me], s3.at[s], r3.at[me], (s, c))

    for q in range(8):
        for core in range(2):

            @pl.when(jnp.logical_or(d != q * 2 + core, y != c))
            def _():
                send3(q, core).start()

    a.wait()
    b.wait()
    mods[me] = (v1_ref[...] + v1_in[...]).astype(BF16)
    b2[me] = v2_ref[...] + v2_in[...]

    def chip(k):
        m = (me + k) % 16
        return m, ((m // 2) * 2 + c, m % 2)

    for k in range(1, 16):
        m, peer = chip(k)
        remote(mods.at[me], mods.at[me], s1.at[k], r1.at[me], peer).start()
        remote(b2.at[me], b2.at[me], s2.at[k], r2.at[me], peer).start()
    for k in range(1, 16):
        m, peer = chip(k)
        remote(mods.at[m], mods.at[m], s1.at[k], r1.at[m], peer).wait_recv()
    every = jnp.concatenate([mods[i].astype(F32) for i in range(16)], axis=0)
    mbg_ref[...] = jnp.sum(every, axis=0, keepdims=True)
    every = every.astype(BF16)
    grad = lax.dot_general(
        every, w_ref[...], (((1,), (1,)), ((), ())), preferred_element_type=F32
    )
    for i in range(16):
        sgp[i, 0:1, :72] = grad[i : i + 1, :]

    def send4(k):
        m = (d + k) % 16
        return remote(sgp.at[m], sg_ref.at[d], s4.at[k], r4.at[d], (m, y))

    for k in range(1, 16):
        send4(k).start()
    sg_ref[d] = sgp[d]
    owned = jnp.concatenate([silu_ref[i].astype(F32)[0:1, :] for i in range(16)], axis=0)
    owned = owned.astype(BF16)[:, :72]
    width = w_ref.shape[1] // 6
    for j in range(6):
        cols = slice(j * width, (j + 1) * width)
        mwg_ref[:, cols] = lax.dot_general(
            owned, every[:, cols], (((0,), (0,)), ((), ())), preferred_element_type=F32
        )
    for k in range(1, 16):
        m, peer = chip(k)
        remote(b2.at[m], b2.at[m], s2.at[k], r2.at[m], peer).wait_recv()
    total = b2[0]
    for i in range(1, 16):
        total = total + b2[i]
    v2_out[...] = total

    def arrive3(i, guard):
        @pl.when(guard)
        def _():
            remote(v3_ref, b3.at[i], s3.at[0], r3.at[i], sib).wait_recv()

    for i in range(16):
        arrive3(i, jnp.logical_or(i != me, y != c))
    total = b3[0]
    for i in range(1, 16):
        total = total + b3[i]
    v3_out[...] = total
    for k in range(1, 16):
        m = (d + k) % 16
        remote(sgp.at[m], sg_ref.at[m], s4.at[k], r4.at[m], (m, y)).wait_recv()
    for q in range(8):
        for core in range(2):

            @pl.when(jnp.logical_or(d != q * 2 + core, y != c))
            def _():
                send3(q, core).wait_send()

    for k in range(1, 16):
        m, peer = chip(k)
        remote(mods.at[me], mods.at[me], s1.at[k], r1.at[me], peer).wait_send()
        remote(b2.at[me], b2.at[me], s2.at[k], r2.at[me], peer).wait_send()
        send4(k).wait_send()


def mod_backward(v1, v2, v3, silu, w_mod, collective_id):
    vmem = pl.BlockSpec(memory_space=pltpu.VMEM)
    n = w_mod.shape[1]
    n2, n3 = v2.shape[1], v3.shape[1]
    dma = pltpu.SemaphoreType.DMA((16,))
    return pl.pallas_call(
        mod_backward_kernel,
        out_shape=[
            jax.ShapeDtypeStruct((72, n), F32),
            jax.ShapeDtypeStruct((1, n), F32),
            jax.ShapeDtypeStruct((16, 8, 128), F32),
            jax.ShapeDtypeStruct((1, n2), F32),
            jax.ShapeDtypeStruct((1, n3), F32),
        ],
        in_specs=[vmem] * 5,
        out_specs=[vmem] * 5,
        scratch_shapes=[
            pltpu.VMEM((1, n), F32),
            pltpu.VMEM((1, n2), F32),
            pltpu.VMEM((16, 1, n), BF16),
            pltpu.VMEM((16, 1, n2), F32),
            pltpu.VMEM((16, 1, n3), F32),
            pltpu.VMEM((16, 8, 128), F32),
            pltpu.SemaphoreType.DMA((4,)),
        ]
        + [dma] * 8,
        compiler_params=pltpu.CompilerParams(
            collective_id=collective_id, has_side_effects=True, vmem_limit_bytes=40 * 2**20
        ),
    )(v1, v2, v3, silu, w_mod)


def index_of(z, x, c, y):
    return ((z * 2 + x) * 2 + c) * 2 + y


def core_pairs():
    return [
        (index_of(z, x, c, y), index_of(z, x, 1 - c, y))
        for z in range(4)
        for x in range(2)
        for c in range(2)
        for y in range(2)
    ]


def latent_pairs():
    return [
        (index_of(z, x, c, y), index_of(z, x, y, c))
        for z in range(4)
        for x in range(2)
        for c in range(2)
        for y in range(2)
        if c != y
    ]


def trade(value):
    moved = lax.ppermute(value, AXES, latent_pairs())
    home = lax.axis_index("dp") % 2 == lax.axis_index("tensor")
    return jnp.where(home, value, moved)


def both_halves(value):
    return jnp.concatenate([value, lax.ppermute(value, AXES, core_pairs())], axis=0)


def own_sum(partial):
    n = partial.shape[0] // 2
    moved = lax.ppermute(partial[n:].astype(BF16), AXES, core_pairs())
    return partial[:n] + moved.astype(F32)


def columns(n, step):
    return [(i, min(step, n - i)) for i in range(0, n, step)]


def on_device_chip(
    tokens,
    cond,
    mod_weight,
    mod_bias,
    query_key_value_weight,
    qkv_bias,
    attention_out_weight,
    attention_out_bias,
    first_hidden_weight,
    first_hidden_bias,
    second_hidden_weight,
    second_hidden_bias,
    out_grad,
):
    half, _, width = tokens.shape
    owned, _, cols = query_key_value_weight.shape
    head_size = width // HEADS
    heads_here = cols // head_size
    hidden = first_hidden_weight.shape[1]

    silu_cond, silu_back = jax.vjp(jax.nn.silu, cond.astype(F32))
    pieces = jnp.pad(
        silu_cond.astype(BF16).reshape(16, 1, owned), ((0, 0), (0, 7), (0, 128 - owned))
    )
    modulation, silu_owned = mod_forward(pieces, mod_weight, mod_bias.astype(F32)[None], 1)
    shift_a, scale_a, gate_a, shift_m, scale_m, gate_m = [
        modulation[:, i * width : (i + 1) * width] for i in range(6)
    ]

    bias_rows = jnp.concatenate([qkv_bias.reshape(-1), first_hidden_bias]).reshape(-1, width)
    carried = trade(jnp.concatenate([tokens.reshape(half, width), bias_rows], axis=0))
    tokens_here = carried[:half].astype(F32)
    biases = carried[half:].reshape(-1)
    q_bias, v_bias, fc1_bias = biases[:cols], biases[cols : 2 * cols], biases[2 * cols :]
    grad_out = trade(out_grad.reshape(half, width)).astype(F32)

    s_qkv = query_key_value_weight.reshape(1, owned, 3 * cols)
    s_proj = attention_out_weight.T.reshape(1, owned, cols)
    s_fc1 = first_hidden_weight.reshape(1, owned, hidden)
    s_fc2 = second_hidden_weight.T.reshape(1, owned, hidden)
    (w_qkv,) = gather_weights([s_qkv], [(0, (0, 896)), (0, (896, 832))], 2)
    w_qkv = w_qkv.reshape(width, 3 * cols)
    chunks = [(0, None)] + [(g, p) for g in (1, 2) for p in columns(hidden, 1152)]
    w_proj, w_fc1, w_fc2 = gather_weights([s_proj, s_fc1, s_fc2], chunks, 3)
    w_proj, w_fc1, w_fc2 = (w.reshape(width, -1) for w in (w_proj, w_fc1, w_fc2))

    normed_a, norm_a_back = jax.vjp(modulate, tokens_here, shift_a, scale_a)
    rows_a = both_halves(normed_a.astype(BF16))
    qkv_shift = jnp.concatenate([q_bias, jnp.zeros_like(q_bias), v_bias]).astype(F32)
    qkv = (jnp.dot(rows_a, w_qkv, preferred_element_type=F32) + qkv_shift).astype(BF16)
    packed = qkv.reshape(2 * half, 3, heads_here, head_size)
    attended, log_totals = attend_forward(packed)
    branch_a = own_sum(
        jnp.einsum("rc,dc->rd", attended, w_proj, preferred_element_type=F32)
    ) + attention_out_bias.astype(F32)
    resid_mid = tokens_here + gate_a * branch_a

    normed_m, norm_m_back = jax.vjp(modulate, resid_mid, shift_m, scale_m)
    rows_m = both_halves(normed_m.astype(BF16))
    preact = jnp.dot(rows_m, w_fc1, preferred_element_type=F32) + fc1_bias.astype(F32)
    activated, gelu_back = jax.vjp(gelu_tanh, preact)
    act_low = activated.astype(BF16)
    branch_m = own_sum(
        jnp.einsum("rf,df->rd", act_low, w_fc2, preferred_element_type=F32)
    ) + second_hidden_bias.astype(F32)
    output = (resid_mid + gate_m * branch_m).astype(BF16)

    gate_m_grad = jnp.sum(grad_out * branch_m, axis=0)
    grad_m_own = (grad_out * gate_m).astype(BF16)
    fc2_bias_part = jnp.sum(grad_m_own, axis=0, dtype=F32)
    grad_m = both_halves(grad_m_own)
    fc2_grad = jnp.einsum("rd,rf->df", grad_m, act_low, preferred_element_type=F32).astype(BF16)
    act_grad = jnp.dot(grad_m, w_fc2, preferred_element_type=F32)
    pre_grad = gelu_back(act_grad)[0].astype(BF16)
    fc1_bias_part = jnp.sum(pre_grad, axis=0, dtype=F32)
    fc1_grad = jnp.einsum("rd,rf->df", rows_m, pre_grad, preferred_element_type=F32).astype(BF16)
    normed_m_grad = own_sum(
        jnp.einsum("rf,df->rd", pre_grad, w_fc1, preferred_element_type=F32)
    )
    resid_part, shift_m_grad, scale_m_grad = norm_m_back(normed_m_grad)
    resid_grad = grad_out + resid_part

    gate_a_grad = jnp.sum(resid_grad * branch_a, axis=0)
    grad_a_own = (resid_grad * gate_a).astype(BF16)
    proj_bias_part = jnp.sum(grad_a_own, axis=0, dtype=F32)
    grad_a = both_halves(grad_a_own)
    proj_grad = jnp.einsum("rd,rc->dc", grad_a, attended, preferred_element_type=F32).astype(BF16)
    attended_grad = jnp.dot(grad_a, w_proj, preferred_element_type=F32).astype(BF16)
    qkv_grad = attend_backward(
        (packed, attended_grad.reshape(2 * half, heads_here, head_size), log_totals)
    ).reshape(2 * half, 3 * cols)
    qkv_bias_part = jnp.sum(qkv_grad, axis=0, dtype=F32)
    qkv_bias_part = jnp.concatenate([qkv_bias_part[:cols], qkv_bias_part[2 * cols :]])
    qkv_wgrad = jnp.einsum("rd,rc->dc", rows_a, qkv_grad, preferred_element_type=F32).astype(BF16)
    normed_a_grad = own_sum(
        jnp.einsum("rc,dc->rd", qkv_grad, w_qkv, preferred_element_type=F32)
    )
    input_part, shift_a_grad, scale_a_grad = norm_a_back(normed_a_grad)
    tokens_grad = (resid_grad + input_part).astype(BF16)

    chunks = [(g, p) for g in (0, 1) for p in columns(hidden, 768)] + [(2, (0, cols))]
    fc2_out, fc1_out, proj_out = reduce_grads(
        [g.reshape(16, owned, -1) for g in (fc2_grad, fc1_grad, proj_grad)], chunks, 4
    )
    (qkv_out,) = reduce_grads(
        [qkv_wgrad.reshape(16, owned, -1)], [(0, (0, 640)), (0, (640, 640)), (0, (1280, 448))], 5
    )

    mod_part = jnp.concatenate(
        [
            shift_a_grad.reshape(1, -1),
            scale_a_grad.reshape(1, -1),
            gate_a_grad.reshape(1, -1),
            shift_m_grad.reshape(1, -1),
            scale_m_grad.reshape(1, -1),
            gate_m_grad.reshape(1, -1),
        ],
        axis=1,
    )
    wide_part = jnp.concatenate([fc2_bias_part, proj_bias_part])[None]
    half_part = jnp.concatenate([fc1_bias_part, qkv_bias_part])[None]
    mod_weight_grad, mod_bias_grad, silu_grad, wide, narrow = mod_backward(
        mod_part, wide_part, half_part, silu_owned, mod_weight, 6
    )
    cond_grad = silu_back(silu_grad[:, 0, :owned].reshape(1, width))[0]
    return (
        trade(output).reshape(half, 1, width),
        trade(tokens_grad).reshape(half, 1, width),
        cond_grad,
        mod_weight_grad,
        mod_bias_grad[0],
        qkv_out.reshape(owned, 3, cols),
        narrow[0, hidden:].reshape(2, cols),
        proj_out.T,
        wide[0, width:],
        fc1_out,
        narrow[0, :hidden],
        fc2_out.T,
        wide[0, :width],
    )


def solution(mesh):
    shape = dict(mesh.shape)
    body = on_device_chip if shape == {"dp": 16, "tensor": 2} else on_device_general
    return jax.shard_map(
        body,
        mesh=mesh,
        in_specs=(
            P("tensor", "dp", None),
            P("dp", None),
            P("dp", None),
            P(),
            P("dp", None, "tensor"),
            P(None, "tensor"),
            P("tensor", "dp"),
            P(),
            P("dp", "tensor"),
            P("tensor"),
            P("tensor", "dp"),
            P(),
            P("tensor", "dp", None),
        ),
        out_specs=(
            P("tensor", "dp", None),
            P("tensor", "dp", None),
            P("dp", None),
            P("dp", None),
            P(),
            P("dp", None, "tensor"),
            P(None, "tensor"),
            P("tensor", "dp"),
            P(),
            P("dp", "tensor"),
            P("tensor"),
            P("tensor", "dp"),
            P(),
        ),
        check_vma=False,
    )
```

```python
import functools
import math

import jax
import jax.numpy as jnp
from jax import lax
from jax.experimental import pallas as pl
from jax.experimental.pallas import tpu as pltpu
from jax.sharding import PartitionSpec as P

HEADS = 16
MESH = pl.DeviceIdType.MESH
AXES = ("dp", "tensor")
F32 = jnp.float32
BF16 = jnp.bfloat16


def modulate(hidden, shifts, scales):
    center = hidden - jnp.mean(hidden, axis=-1, keepdims=True)
    spread = jnp.mean(center * center, axis=-1, keepdims=True)
    return center * lax.rsqrt(spread + 1e-06) * (1.0 + scales) + shifts


def gelu_tanh(values):
    return jax.nn.gelu(values, approximate=True)


def attend_forward(packed):
    queries = packed[:, 0]
    keys_all = packed[:, 1]
    values_all = packed[:, 2]
    seq_len = packed.shape[0]
    scaling = packed.shape[3] ** (-0.5)
    block_rows = min(512, seq_len)
    results = []
    log_parts = []
    for offset in range(0, seq_len, block_rows):
        query_block = queries[offset : offset + block_rows]
        scores = (
            jnp.einsum("qhe,khe->hqk", query_block, keys_all, preferred_element_type=jnp.float32)
            * scaling
        )
        highest = jnp.max(scores, axis=-1, keepdims=True)
        weights = jnp.exp(scores - highest)
        row_total = jnp.sum(weights, axis=-1, keepdims=True)
        prob_low = (weights / row_total).astype(jnp.bfloat16)
        mixture = jnp.einsum(
            "hqk,khe->qhe", prob_low, values_all, preferred_element_type=jnp.float32
        )
        results.append(mixture.reshape(block_rows, -1))
        log_parts.append((highest + jnp.log(row_total))[..., 0])
    return (jnp.concatenate(results, 0).astype(jnp.bfloat16), jnp.concatenate(log_parts, 1))


def attend_backward(inputs):
    packed, grad_out, log_totals = inputs
    queries = packed[:, 0]
    keys_all = packed[:, 1]
    values_all = packed[:, 2]
    seq_len = packed.shape[0]
    scaling = packed.shape[3] ** (-0.5)
    block_rows = min(512, seq_len)
    query_grads = []
    key_grad = jnp.zeros(keys_all.shape, jnp.float32)
    value_grad = jnp.zeros(values_all.shape, jnp.float32)
    for offset in range(0, seq_len, block_rows):
        query_block = queries[offset : offset + block_rows]
        grad_block = grad_out[offset : offset + block_rows]
        scores = (
            jnp.einsum("qhe,khe->hqk", query_block, keys_all, preferred_element_type=jnp.float32)
            * scaling
        )
        probs = jnp.exp(scores - log_totals[:, offset : offset + block_rows, None])
        prob_low = probs.astype(jnp.bfloat16)
        prob_grad = jnp.einsum(
            "qhe,khe->hqk", grad_block, values_all, preferred_element_type=jnp.float32
        )
        inner = jnp.sum(probs * prob_grad, axis=-1, keepdims=True)
        score_grad = (probs * (prob_grad - inner)).astype(jnp.bfloat16)
        query_grads.append(
            jnp.einsum("hqk,khe->qhe", score_grad, keys_all, preferred_element_type=jnp.float32)
            * scaling
        )
        key_grad = (
            key_grad
            + jnp.einsum(
                "hqk,qhe->khe", score_grad, query_block, preferred_element_type=jnp.float32
            )
            * scaling
        )
        value_grad = value_grad + jnp.einsum(
            "hqk,qhe->khe", prob_low, grad_block, preferred_element_type=jnp.float32
        )
    return jnp.stack([jnp.concatenate(query_grads, 0), key_grad, value_grad], 1).astype(
        jnp.bfloat16
    )


def on_device_general(
    tokens,
    cond,
    mod_weight,
    mod_bias,
    query_key_value_weight,
    qkv_bias,
    attention_out_weight,
    attention_out_bias,
    first_hidden_weight,
    first_hidden_bias,
    second_hidden_weight,
    second_hidden_bias,
    out_grad,
):
    w_mod, w_qkv, w_proj, w_fc1, w_fc2 = (
        lax.all_gather(mod_weight, "dp", axis=0, tiled=True),
        lax.all_gather(query_key_value_weight, "dp", axis=0, tiled=True),
        lax.all_gather(attention_out_weight, "dp", axis=1, tiled=True),
        lax.all_gather(first_hidden_weight, "dp", axis=0, tiled=True),
        lax.all_gather(second_hidden_weight, "dp", axis=1, tiled=True),
    )
    seq_local, latents, width = tokens.shape
    columns = query_key_value_weight.shape[2]
    head_size = width // HEADS
    heads_here = columns // head_size
    local_rows = seq_local * latents
    cond_wide = cond.astype(jnp.float32)
    silu_cond, silu_back = jax.vjp(jax.nn.silu, cond_wide)
    silu_low = silu_cond.astype(jnp.bfloat16)
    modulation = jnp.dot(silu_low, w_mod, preferred_element_type=jnp.float32) + mod_bias.astype(
        jnp.float32
    )
    pieces = modulation.reshape(latents, 6, width)
    hidden_in = tokens.astype(jnp.float32)
    attention_normalized, norm_a_back = jax.vjp(modulate, hidden_in, pieces[:, 0], pieces[:, 1])
    gathered_a = lax.all_gather(
        attention_normalized.astype(jnp.bfloat16), "tensor", axis=0, tiled=True
    )
    seq_len = gathered_a.shape[0]
    total_rows = seq_len * latents
    rows_a = gathered_a.reshape(total_rows, width)
    qkv_flat = w_qkv.reshape(width, 3 * columns)
    zero_row = jnp.zeros((columns,), jnp.float32)
    query_key_value_shift = jnp.stack(
        [qkv_bias[0].astype(jnp.float32), zero_row, qkv_bias[1].astype(jnp.float32)]
    )
    projected_output = (
        jnp.dot(rows_a, qkv_flat, preferred_element_type=jnp.float32).reshape(
            seq_len, latents, 3, columns
        )
        + query_key_value_shift
    )
    packed = jnp.moveaxis(projected_output.astype(jnp.bfloat16), 1, 0).reshape(
        latents, seq_len, 3, heads_here, head_size
    )
    attention_result, log_totals = lax.map(attend_forward, packed)
    attended_rows = jnp.moveaxis(attention_result, 0, 1).reshape(total_rows, columns)
    summed_a = lax.psum_scatter(
        jnp.dot(attended_rows, w_proj, preferred_element_type=jnp.float32).astype(jnp.bfloat16),
        "tensor",
        scatter_dimension=0,
        tiled=True,
    ).astype(jnp.float32)
    attention_branch = summed_a.reshape(seq_local, latents, width) + attention_out_bias.astype(
        jnp.float32
    )
    resid_mid = hidden_in + pieces[:, 2] * attention_branch
    feedforward_normalized, norm_m_back = jax.vjp(modulate, resid_mid, pieces[:, 3], pieces[:, 4])
    gathered_m = lax.all_gather(
        feedforward_normalized.astype(jnp.bfloat16), "tensor", axis=0, tiled=True
    )
    rows_m = gathered_m.reshape(total_rows, width)
    before_activation = jnp.dot(
        rows_m, w_fc1, preferred_element_type=jnp.float32
    ) + first_hidden_bias.astype(jnp.float32)
    gelu_activated, gelu_back = jax.vjp(gelu_tanh, before_activation)
    act_low = gelu_activated.astype(jnp.bfloat16)
    summed_m = lax.psum_scatter(
        jnp.dot(act_low, w_fc2, preferred_element_type=jnp.float32).astype(jnp.bfloat16),
        "tensor",
        scatter_dimension=0,
        tiled=True,
    ).astype(jnp.float32)
    feedforward_branch = summed_m.reshape(seq_local, latents, width) + second_hidden_bias.astype(
        jnp.float32
    )
    output = (resid_mid + pieces[:, 5] * feedforward_branch).astype(jnp.bfloat16)
    grad_out = out_grad.astype(jnp.float32)
    gate_m_grad = jnp.sum(grad_out * feedforward_branch, axis=0)
    grad_m_low = (grad_out * pieces[:, 5]).astype(jnp.bfloat16)
    grad_m_rows = lax.all_gather(grad_m_low, "tensor", axis=0, tiled=True).reshape(
        total_rows, width
    )
    fc2_bias_grad = jnp.sum(grad_m_rows, axis=0, dtype=jnp.float32)
    fc2_weight_grad = jnp.einsum(
        "rf,rd->fd", act_low, grad_m_rows, preferred_element_type=jnp.float32
    )
    act_grad = jnp.einsum("rd,fd->rf", grad_m_rows, w_fc2, preferred_element_type=jnp.float32)
    pre_grad = gelu_back(act_grad)[0].astype(jnp.bfloat16)
    fc1_bias_grad = jnp.sum(pre_grad, axis=0, dtype=jnp.float32)
    fc1_weight_grad = jnp.einsum("rd,rf->df", rows_m, pre_grad, preferred_element_type=jnp.float32)
    normed_m_grad = (
        lax.psum_scatter(
            jnp.einsum("rf,df->rd", pre_grad, w_fc1, preferred_element_type=jnp.float32).astype(
                jnp.bfloat16
            ),
            "tensor",
            scatter_dimension=0,
            tiled=True,
        )
        .astype(jnp.float32)
        .reshape(seq_local, latents, width)
    )
    resid_part, shift_m_grad, scale_m_grad = norm_m_back(normed_m_grad)
    resid_grad = grad_out + resid_part
    gate_a_grad = jnp.sum(resid_grad * attention_branch, axis=0)
    grad_a_low = (resid_grad * pieces[:, 2]).astype(jnp.bfloat16)
    grad_a_flat = grad_a_low.reshape(local_rows, width)
    proj_bias_part = jnp.sum(grad_a_flat, axis=0, dtype=jnp.float32)
    grad_a_rows = lax.all_gather(grad_a_low, "tensor", axis=0, tiled=True).reshape(
        total_rows, width
    )
    proj_weight_grad = jnp.einsum(
        "rc,rd->cd", attended_rows, grad_a_rows, preferred_element_type=jnp.float32
    )
    attended_grad = jnp.einsum(
        "rd,cd->rc", grad_a_rows, w_proj, preferred_element_type=jnp.float32
    ).astype(jnp.bfloat16)
    grad_packed = jnp.moveaxis(attended_grad.reshape(seq_len, latents, heads_here, head_size), 1, 0)
    qkv_grad_packed = lax.map(attend_backward, (packed, grad_packed, log_totals))
    qkv_grad_rows = jnp.moveaxis(qkv_grad_packed, 0, 1).reshape(total_rows, 3 * columns)
    bias_sums = jnp.sum(qkv_grad_rows.reshape(total_rows, 3, columns), axis=0, dtype=jnp.float32)
    qkv_bias_grad = jnp.stack([bias_sums[0], bias_sums[2]])
    qkv_weight_grad = jnp.einsum(
        "rd,rc->dc", rows_a, qkv_grad_rows, preferred_element_type=jnp.float32
    ).reshape(width, 3, columns)
    normed_a_grad = (
        lax.psum_scatter(
            jnp.einsum(
                "rc,dc->rd", qkv_grad_rows, qkv_flat, preferred_element_type=jnp.float32
            ).astype(jnp.bfloat16),
            "tensor",
            scatter_dimension=0,
            tiled=True,
        )
        .astype(jnp.float32)
        .reshape(seq_local, latents, width)
    )
    input_part, shift_a_grad, scale_a_grad = norm_a_back(normed_a_grad)
    tokens_grad = (resid_grad + input_part).astype(jnp.bfloat16)
    partial_mod = jnp.stack(
        [shift_a_grad, scale_a_grad, gate_a_grad, shift_m_grad, scale_m_grad, gate_m_grad], 1
    ).reshape(latents, 6 * width)
    mod_summed, proj_bias_grad = (
        lax.psum(partial_mod.astype(jnp.bfloat16), "tensor").astype(jnp.float32),
        lax.psum(proj_bias_part.astype(jnp.bfloat16), "tensor").astype(jnp.float32),
    )
    mod_grad_low = mod_summed.astype(jnp.bfloat16)
    silu_grad = jnp.einsum("le,de->ld", mod_grad_low, w_mod, preferred_element_type=jnp.float32)
    cond_grad = silu_back(silu_grad)[0]
    silu_every, mod_every = (
        lax.all_gather(silu_low, "dp", axis=0, tiled=True),
        lax.all_gather(mod_grad_low, "dp", axis=0, tiled=True),
    )
    owned_rows = mod_weight.shape[0]
    silu_owned = lax.dynamic_slice_in_dim(
        silu_every, lax.axis_index("dp") * owned_rows, owned_rows, 1
    )
    mod_weight_grad = jnp.einsum(
        "ld,le->de", silu_owned, mod_every, preferred_element_type=jnp.float32
    )
    mod_bias_grad = jnp.sum(mod_every, axis=0, dtype=jnp.float32)
    qkv_weight_grad, proj_weight_grad, fc1_weight_grad, fc2_weight_grad = (
        lax.psum_scatter(
            qkv_weight_grad.astype(jnp.bfloat16), "dp", scatter_dimension=0, tiled=True
        ).astype(jnp.float32),
        lax.psum_scatter(
            proj_weight_grad.astype(jnp.bfloat16), "dp", scatter_dimension=1, tiled=True
        ).astype(jnp.float32),
        lax.psum_scatter(
            fc1_weight_grad.astype(jnp.bfloat16), "dp", scatter_dimension=0, tiled=True
        ).astype(jnp.float32),
        lax.psum_scatter(
            fc2_weight_grad.astype(jnp.bfloat16), "dp", scatter_dimension=1, tiled=True
        ).astype(jnp.float32),
    )
    qkv_bias_grad, proj_bias_grad, fc1_bias_grad, fc2_bias_grad = lax.psum(
        (qkv_bias_grad, proj_bias_grad, fc1_bias_grad, fc2_bias_grad), "dp"
    )
    return (
        output,
        tokens_grad,
        cond_grad,
        mod_weight_grad,
        mod_bias_grad,
        qkv_weight_grad,
        qkv_bias_grad,
        proj_weight_grad,
        proj_bias_grad,
        fc1_weight_grad,
        fc1_bias_grad,
        fc2_weight_grad,
        fc2_bias_grad,
    )


def place():
    d = lax.axis_index("dp")
    y = lax.axis_index("tensor")
    return d, d // 4, (d // 2) % 2, d % 2, y


def neighbours(pos):
    d, z, x, c, y = pos
    sib = (z * 4 + x * 2 + (1 - c), y)
    xn = (z * 4 + (1 - x) * 2 + c, y)
    yn = (d, 1 - y)
    return sib, xn, yn


def z_peer(pos, k):
    d, z, x, c, y = pos
    return (((z + k) % 4) * 4 + x * 2 + c, y)


def greet(peers):
    sem = pltpu.get_barrier_semaphore()
    for peer in peers:
        pl.semaphore_signal(sem, inc=1, device_id=peer, device_id_type=MESH)
    pl.semaphore_wait(sem, len(peers))


def chip_peers(pos):
    d, z, x, c, y = pos
    across = [(z * 4 + x * 2 + 1 - c, 1 - y)]
    return list(neighbours(pos)) + across + [z_peer(pos, k) for k in (1, 2, 3)]


def remote(src, dst, send, recv, peer):
    return pltpu.make_async_remote_copy(
        src_ref=src, dst_ref=dst, send_sem=send, recv_sem=recv, device_id=peer, device_id_type=MESH
    )


GATHER_RECV = 24
GATHER_SEND = 28


class Gather:
    def __init__(self, shard, full, relay, cols, recv, send, pos):
        self.shard, self.full, self.relay, self.cols = shard, full, relay, cols
        self.recv, self.send, self.pos = recv, send, pos
        d, z, x, c, y = pos
        self.sib, self.xn, _ = neighbours(pos)
        self.far = (z * 4 + x * 2 + y, 1 - y)
        self.home, self.away = c == y, c != y

    def part(self, ref, b):
        if self.cols is None:
            return ref.at[pl.ds(b, 1)]
        return ref.at[pl.ds(b, 1), :, pl.ds(*self.cols)]

    def move(self, src, dst, s, r, peer):
        return remote(src, dst, self.send.at[s], self.recv.at[r], peer)

    def came(self, r):
        block = self.part(self.full, 0)
        self.move(block, block, 0, r, self.sib).wait_recv()

    def stay(self):
        return pltpu.make_async_copy(
            self.part(self.shard, 0), self.part(self.full, self.pos[0]), self.send.at[27]
        )

    def start(self):
        d, z, x, c, y = self.pos
        q = z * 2 + x
        own = self.part(self.shard, 0)

        @pl.when(self.home)
        def _():
            for k in (2, 1, 3):
                self.move(own, self.part(self.full, d), k, q, z_peer(self.pos, k)).start()
            self.move(own, self.part(self.full, d), 4, q, self.xn).start()
            self.move(own, self.part(self.full, d), 8, 8 + q, self.far).start()
            self.stay().start()

        @pl.when(self.away)
        def _():
            for k in (2, 1, 3):
                self.move(own, self.part(self.relay, q), k, q, z_peer(self.pos, k)).start()
            self.move(own, self.part(self.full, d), 8, 16 + q, self.far).start()
            self.move(own, self.part(self.relay, q), 4, q, self.xn).start()
            self.move(own, self.part(self.full, d), 16, 8 + q, self.sib).start()

    def from_z(self, k):
        d, z, x, c, y = self.pos
        q = ((z + k) % 4) * 2 + x
        dst = self.part(self.full, 2 * q + c)

        @pl.when(self.home)
        def _():
            self.came(q)
            self.move(dst, dst, 4 + k, q, self.xn).start()
            self.move(dst, dst, 8 + k, 8 + q, self.far).start()

        @pl.when(self.away)
        def _():
            self.came(q)
            src = self.part(self.relay, q)
            self.move(src, dst, 8 + k, 16 + q, self.far).start()
            self.move(src, src, 4 + k, q, self.xn).start()
            self.move(src, dst, 16 + k, 8 + q, self.sib).start()

    def from_x(self, k):
        d, z, x, c, y = self.pos
        q = ((z + k) % 4) * 2 + 1 - x
        dst = self.part(self.full, 2 * q + c)

        @pl.when(self.home)
        def _():
            self.came(q)
            self.move(dst, dst, 12 + k, 8 + q, self.far).start()

        @pl.when(self.away)
        def _():
            self.came(q)
            self.move(self.part(self.relay, q), dst, 20 + k, 8 + q, self.sib).start()

    def from_y(self, k):
        d, z, x, c, y = self.pos
        q = ((z + k) % 4) * 2 + x

        @pl.when(self.away)
        def _():
            block = self.part(self.full, 2 * q + 1 - c)
            self.came(16 + q)
            self.move(block, block, 12 + k, 16 + q, self.xn).start()

    def ready(self):
        d, z, x, c, y = self.pos
        for q in range(8):
            self.came(8 + q)

        @pl.when(self.home)
        def _():
            self.stay().wait()

        @pl.when(self.away)
        def _():
            for k in range(4):
                self.came(16 + ((z + k) % 4) * 2 + 1 - x)

    def finish(self):
        block = self.part(self.full, 0)
        for s in range(1, 16):
            self.move(block, block, s, 0, self.sib).wait_send()

        @pl.when(self.away)
        def _():
            for s in range(16, 24):
                self.move(block, block, s, 0, self.sib).wait_send()

    def early(self):
        return [functools.partial(self.from_z, k) for k in (1, 2, 3)]

    def late(self):
        steps = []
        for k in range(4):
            steps += [functools.partial(self.from_x, k), functools.partial(self.from_y, k)]
        return steps + [self.ready]


def gather_events(parts, lead=2):
    n = len(parts)
    events = [p.start for p in parts[:lead]]
    for i in range(n + 1):
        if i < n:
            events += parts[i].early()
        if i + lead < n:
            events.append(parts[i + lead].start)
        if i > 0:
            events += parts[i - 1].late()
    return events


def gather_parts(shards, fulls, relays, chunks, recv, send, pos):
    return [
        Gather(shards[g], fulls[g], relays[g], cols, recv.at[i], send.at[i], pos)
        for i, (g, cols) in enumerate(chunks)
    ]


def gather_kernel(chunks, count, *refs):
    shards, fulls, relays = (refs[i * count : (i + 1) * count] for i in range(3))
    recv, send = refs[3 * count :]
    pos = place()
    greet(chip_peers(pos))
    parts = gather_parts(shards, fulls, relays, chunks, recv, send, pos)
    for event in gather_events(parts) + [p.finish for p in parts]:
        event()


def gather_sems(chunks):
    n = len(chunks)
    return [
        pltpu.SemaphoreType.DMA((n, GATHER_RECV)),
        pltpu.SemaphoreType.DMA((n, GATHER_SEND)),
    ]


def gather_shapes(shards):
    return [jax.ShapeDtypeStruct((16,) + s.shape[1:], s.dtype) for s in shards] + [
        jax.ShapeDtypeStruct((8,) + s.shape[1:], s.dtype) for s in shards
    ]


def gather_weights(shards, chunks, collective_id):
    count = len(shards)
    anywhere = pl.BlockSpec(memory_space=pl.ANY)
    return pl.pallas_call(
        functools.partial(gather_kernel, chunks, count),
        out_shape=gather_shapes(shards),
        in_specs=[anywhere] * count,
        out_specs=[anywhere] * (2 * count),
        scratch_shapes=gather_sems(chunks),
        compiler_params=pltpu.CompilerParams(
            collective_id=collective_id, has_side_effects=True
        ),
    )(*shards)[:count]


REDUCE_RECV = 27
REDUCE_SEND = 23


class Reduce:
    def __init__(self, grad, land, out, recv, send, pos, cols):
        self.grad, self.land, self.out = grad, land, out
        self.recv, self.send, self.pos, self.cols = recv, send, pos, pl.ds(*cols)
        d, z, x, c, y = pos
        self.sib, self.xn, self.yn = neighbours(pos)
        self.home, self.away = c == y, c != y

    def rows(self, b):
        return self.grad.at[pl.ds(b, 1), :, self.cols]

    def slot(self, i):
        return self.land.at[pl.ds(i, 1)]

    def push(self, src, slot, s, peer):
        return remote(src, self.slot(slot), self.send.at[s], self.recv.at[slot], peer)

    def came(self, slot):
        self.push(self.slot(slot), slot, 0, self.sib).wait_recv()

    def value(self, i):
        return self.land[i].astype(F32)

    def first(self):
        d, z, x, c, y = self.pos

        @pl.when(self.away)
        def _():
            for column, base in ((1 - x, 0), (x, 4)):

                def step(k, _):
                    q = lax.rem(z + 1 + k, 4) * 2 + column
                    self.push(self.rows(2 * q + c), q, base + k, self.yn).start()
                    self.push(self.rows(2 * q + 1 - c), 15 + q, 8 + base + k, self.sib).start()
                    return 0

                lax.fori_loop(0, 4, step, 0)

        @pl.when(self.home)
        def _():
            for column, base in ((1 - x, 0), (x, 4)):

                def step(k, _):
                    q = lax.rem(z + 1 + k, 4) * 2 + column
                    self.push(self.rows(2 * q + 1 - c), q, base + k, self.sib).start()
                    return 0

                lax.fori_loop(0, 4, step, 0)

    def second(self):
        d, z, x, c, y = self.pos

        @pl.when(self.away)
        def _():
            def step(k, _):
                zz = lax.rem(z + 1 + k, 4)
                q = zz * 2 + 1 - x
                self.came(q)
                self.push(self.slot(q), 8 + zz, 16 + k, self.xn).start()
                return 0

            lax.fori_loop(0, 4, step, 0)

        @pl.when(self.home)
        def _():
            def over_x(k, _):
                zz = lax.rem(z + 1 + k, 4)
                q = zz * 2 + 1 - x
                self.came(15 + q)
                self.push(self.slot(15 + q), 23 + zz, 15 + k, self.xn).start()
                return 0

            lax.fori_loop(0, 4, over_x, 0)

            def step(k, _):
                zz = lax.rem(z + 1 + k, 4)
                q = zz * 2 + 1 - x
                b = 2 * q + c
                self.came(q)
                total = self.grad[b, :, self.cols].astype(F32) + self.value(q)
                self.grad[b, :, self.cols] = total.astype(BF16)
                self.push(self.rows(b), 8 + zz, 8 + k, self.xn).start()
                return 0

            lax.fori_loop(0, 4, step, 0)

    def third(self):
        d, z, x, c, y = self.pos

        @pl.when(self.home)
        def _():
            def far(k, _):
                zz = lax.rem(z + 1 + k, 4)
                q = zz * 2 + x
                self.came(15 + q)
                self.came(23 + zz)
                self.land[15 + q] = (self.value(15 + q) + self.value(23 + zz)).astype(BF16)
                self.push(self.slot(15 + q), 15 + zz, 19 + k, self.yn).start()
                return 0

            lax.fori_loop(0, 4, far, 0)

            def step(k, _):
                zz = lax.rem(z + 1 + k, 4)
                q = zz * 2 + x
                b = 2 * q + c
                self.came(q)
                self.came(8 + zz)
                total = self.grad[b, :, self.cols].astype(F32)
                total = total + self.value(q) + self.value(8 + zz)
                self.grad[b, :, self.cols] = total.astype(BF16)
                self.push(self.rows(b), 12 + k, 12 + k, (zz * 4 + x * 2 + c, y)).start()
                return 0

            lax.fori_loop(0, 3, step, 0)

    def fourth(self):
        d, z, x, c, y = self.pos

        @pl.when(self.away)
        def _():
            def step(k, _):
                zz = lax.rem(z + 1 + k, 4)
                q = zz * 2 + x
                self.came(q)
                self.came(8 + zz)
                self.came(15 + zz)
                total = self.value(q) + self.value(8 + zz) + self.value(15 + zz)
                self.land[q] = total.astype(BF16)
                self.push(self.slot(q), 12 + k, 20 + k, (zz * 4 + x * 2 + c, y)).start()
                return 0

            lax.fori_loop(0, 3, step, 0)

    def fifth(self):
        d, z, x, c, y = self.pos
        q = z * 2 + x
        self.came(q)
        self.came(8 + z)
        for k in range(3):
            self.came(12 + k)
        total = self.value(q) + self.value(8 + z)
        total = total + self.value(12) + self.value(13) + self.value(14)

        @pl.when(self.home)
        def _():
            self.out[:, self.cols] = total + self.grad[d, :, self.cols].astype(F32)

        @pl.when(self.away)
        def _():
            self.came(15 + z)
            self.out[:, self.cols] = total + self.value(15 + z)

    def finish(self):
        block = self.slot(0)
        for s in range(REDUCE_SEND):
            self.push(block, 0, s, self.sib).wait_send()


def reduce_events(parts):
    n = len(parts)
    stages = (Reduce.first, Reduce.second, Reduce.third, Reduce.fourth, Reduce.fifth)
    events = [parts[0].first]
    for i in range(n + 3):
        if i + 1 < n:
            events.append(parts[i + 1].first)
        for lag, stage in enumerate(stages[1:]):
            if 0 <= i - lag < n:
                events.append(functools.partial(stage, parts[i - lag]))
    return events + [p.finish for p in parts]


def reduce_kernel(chunks, count, *refs):
    n = len(chunks)
    grads, outs = refs[:count], refs[count : 2 * count]
    lands, (recv, send) = refs[2 * count : 2 * count + n], refs[2 * count + n :]
    pos = place()
    greet(chip_peers(pos))
    parts = [
        Reduce(grads[g], lands[i], outs[g], recv.at[i], send.at[i], pos, cols)
        for i, (g, cols) in enumerate(chunks)
    ]
    for event in reduce_events(parts):
        event()


def reduce_scratch(chunks):
    n = len(chunks)
    return [pltpu.VMEM((27, 72, cols[1]), BF16) for _, cols in chunks] + [
        pltpu.SemaphoreType.DMA((n, REDUCE_RECV)),
        pltpu.SemaphoreType.DMA((n, REDUCE_SEND)),
    ]


def reduce_grads(grads, chunks, collective_id):
    count = len(grads)
    vmem = pl.BlockSpec(memory_space=pltpu.VMEM)
    return pl.pallas_call(
        functools.partial(reduce_kernel, chunks, count),
        out_shape=[jax.ShapeDtypeStruct(g.shape[1:], F32) for g in grads],
        in_specs=[vmem] * count,
        out_specs=[vmem] * count,
        scratch_shapes=reduce_scratch(chunks),
        compiler_params=pltpu.CompilerParams(
            collective_id=collective_id, has_side_effects=True, vmem_limit_bytes=63000 * 1024
        ),
    )(*grads)


class Pump:
    def __init__(self, events):
        self.events, self.next = list(events), 0

    def run(self, count=None):
        stop = len(self.events) if count is None else min(len(self.events), self.next + count)
        for event in self.events[self.next : stop]:
            event()
        self.next = stop

    def loop(self, steps, body, first=0, every=1, count=None):
        todo = self.events[self.next :][: len(range(first, steps, every))]
        todo = todo if count is None else todo[:count]
        self.next += len(todo)

        def step(i, _):
            for j, event in enumerate(todo):
                pl.when(i == first + j * every)(event)
            body(i)
            return 0

        lax.fori_loop(0, steps, step, 0)


def first_kernel(
    chunks, piece_ref, w_ref, bias_ref, shard, mod_ref, silu_ref, full, relay,
    part, land, mine, other, s1, r1, s2, r2, s3, recv, send,
):
    pos = place()
    d, z, x, c, y = pos
    sib, _, yn = neighbours(pos)
    far = (z * 4 + x * 2 + 1 - c, 1 - y)
    greet([((d + k) % 16, y) for k in range(1, 16)] + [yn, far])

    def piece(k):
        to = (d + k) % 16
        return remote(piece_ref.at[to], silu_ref.at[d], s1.at[k], r1.at[d], (to, y))

    def piece_in(k):
        src = (d + k) % 16
        return remote(piece_ref.at[src], silu_ref.at[src], s1.at[k], r1.at[src], (src, y))

    for k in range(1, 16):
        piece(k).start()
    parts = gather_parts([shard], [full], [relay], chunks, recv, send, pos)
    pump = Pump(gather_events(parts))
    pump.run(2)
    silu_ref[d] = piece_ref[d]
    for k in range(1, 16):
        piece_in(k).wait_recv()
    rows = jnp.concatenate(
        [silu_ref[2 * q + y].astype(F32)[0:1, :] for q in range(8)], axis=0
    ).astype(BF16)[:, :72]
    width = w_ref.shape[1] // 6
    for j in range(6):
        cols = slice(j * width, (j + 1) * width)
        value = jnp.dot(rows, w_ref[:, cols], preferred_element_type=F32)
        for q in range(8):
            part[q, :, cols] = value[q : q + 1, :]
    me = z * 2 + x

    def send_part(k):
        q = (me + k) % 8
        return remote(part.at[q], land.at[me], s2.at[k], r2.at[me], (q * 2 + c, y))

    def part_in(k):
        q = (me + k) % 8
        return remote(part.at[q], land.at[q], s2.at[k], r2.at[q], (q * 2 + c, y))

    for k in range(1, 8):
        send_part(k).start()
    land[me] = part[me]
    pump.run(6)
    for k in range(1, 8):
        part_in(k).wait_recv()
    total = land[0]
    for q in range(1, 8):
        total = total + land[q]
    mine[...] = total
    swap = remote(mine, other, s3.at[0], s3.at[1], sib)
    swap.start()
    pump.run(3)
    for k in range(1, 16):
        piece(k).wait_send()
    for k in range(1, 8):
        send_part(k).wait_send()
    swap.wait()
    mod_ref[...] = mine[...] + other[...] + bias_ref[...]
    pump.run()
    for p in parts:
        p.finish()


def first_stage(pieces, w_mod, bias, shard, chunks, collective_id):
    vmem, anywhere = pl.BlockSpec(memory_space=pltpu.VMEM), pl.BlockSpec(memory_space=pl.ANY)
    n = w_mod.shape[1]
    return pl.pallas_call(
        functools.partial(first_kernel, chunks),
        out_shape=[jax.ShapeDtypeStruct((1, n), F32), jax.ShapeDtypeStruct((16, 8, 128), BF16)]
        + gather_shapes([shard]),
        in_specs=[vmem] * 3 + [anywhere],
        out_specs=[vmem] * 2 + [anywhere] * 2,
        scratch_shapes=[
            pltpu.VMEM((8, 1, n), F32),
            pltpu.VMEM((8, 1, n), F32),
            pltpu.VMEM((1, n), F32),
            pltpu.VMEM((1, n), F32),
            pltpu.SemaphoreType.DMA((16,)),
            pltpu.SemaphoreType.DMA((16,)),
            pltpu.SemaphoreType.DMA((8,)),
            pltpu.SemaphoreType.DMA((8,)),
            pltpu.SemaphoreType.DMA((2,)),
        ]
        + gather_sems(chunks),
        compiler_params=pltpu.CompilerParams(
            collective_id=collective_id, has_side_effects=True, vmem_limit_bytes=40 * 2**20
        ),
    )(pieces, w_mod, bias, shard)[:3]


def flat(value):
    return value.reshape(-1, value.shape[-1])


def product(a, b, ca, cb):
    return lax.dot_general(a, b, (((ca,), (cb,)), ((), ())), preferred_element_type=F32)


def last_kernel(
    rows_ref, dqkv_ref, wqkv_ref, tokens_ref, resid_ref, scale_ref, parts_ref, wide_ref, half_ref,
    silu_ref, w_ref,
    tgrad_ref, qkv_out, mwg_ref, mbg_ref, sg_ref, wide_out, half_out,
    grad, ngrad, sent, got, v1, v1_in, v2_in, mods, b2, b3, sgp, land0, land1, land2,
    s0, s1, r1, s2, r2, s3, r3, s4, r4, recv, send,
):
    pos = place()
    d, z, x, c, y = pos
    sib = neighbours(pos)[0]
    lin = d * 2 + y
    half, width = tokens_ref.shape
    heads = dqkv_ref.shape[0] // 3
    greet([(((lin + k) % 32) // 2, (lin + k) % 2) for k in range(1, 32)])
    me = (z * 2 + x) * 2 + y

    @pl.when(y == c)
    def _():
        b3[me] = half_ref[...]

    sgp[...] = jnp.zeros_like(sgp)

    def send3(q, core):
        s = q * 2 + core
        return remote(half_ref, b3.at[me], s3.at[s], r3.at[me], (s, c))

    def each3(action):
        for q in range(8):
            for core in range(2):
                pl.when(jnp.logical_or(d != q * 2 + core, y != c))(
                    functools.partial(action, q, core)
                )

    n = dqkv_ref.shape[1] * heads
    reducers = [
        Reduce(grad.at[j], land, qkv_out.at[j], recv.at[j], send.at[j], pos, (0, n))
        for j, land in enumerate((land0, land1, land2))
    ]

    def weight_grad(j, _):
        value = product(rows_ref[...], flat(dqkv_ref[pl.ds(j * heads, heads)]), 0, 1)
        grad[j] = value.reshape(grad.shape[1:]).astype(BF16)
        for i, reducer in enumerate(reducers):
            pl.when(j == i)(reducer.first)
        pl.when(j == 2)(reducers[0].second)
        return 0

    lax.fori_loop(0, 3, weight_grad, 0)
    each3(lambda q, core: send3(q, core).start())
    pump = Pump(reduce_events(reducers)[:-3])
    pump.events = [e for e in pump.events if e not in [r.first for r in reducers]][1:]

    tile = half // 2
    swap = remote(sent, got, s0.at[4], s0.at[5], sib)

    def into_norm(i):
        cols = pl.ds(pl.multiple_of(i * tile, tile), tile)
        return product(flat(dqkv_ref[:, :, cols]), wqkv_ref[...], 0, 1)

    def other_rows(i, _):
        sent[pl.ds(pl.multiple_of(i * tile, tile), tile), :] = into_norm(i + 2).astype(BF16)
        return 0

    def own_rows(i, _):
        ngrad[pl.ds(pl.multiple_of(i * tile, tile), tile), :] = into_norm(i)
        return 0

    lax.fori_loop(0, 2, other_rows, 0)
    swap.start()
    pump.run(1)
    lax.fori_loop(0, 2, own_rows, 0)
    swap.wait()
    piece = half // 4
    scale = 1.0 + scale_ref[...]

    def norm_back(i, sums):
        part = pl.ds(pl.multiple_of(i * piece, piece), piece)
        value = tokens_ref[part, :].astype(F32)
        center = value - jnp.mean(value, axis=-1, keepdims=True)
        rate = lax.rsqrt(jnp.mean(center * center, axis=-1, keepdims=True) + 1e-06)
        normed = center * rate
        g = ngrad[part, :] + got[part, :].astype(F32)
        e = g * scale
        inner = jnp.mean(e * normed, axis=-1, keepdims=True)
        back = rate * (e - jnp.mean(e, axis=-1, keepdims=True) - normed * inner)
        tgrad_ref[part, :] = (resid_ref[part, :] + back).astype(BF16)
        return (
            sums[0] + jnp.sum(g, axis=0, keepdims=True),
            sums[1] + jnp.sum(g * normed, axis=0, keepdims=True),
        )

    zero = jnp.zeros((1, width), F32)
    shift_sum, scale_sum = lax.fori_loop(0, 4, norm_back, (zero, zero))
    v1[:, :width] = shift_sum
    v1[:, width : 2 * width] = scale_sum
    v1[:, 2 * width :] = parts_ref[...]

    a = remote(v1, v1_in, s0.at[0], s0.at[1], sib)
    b = remote(wide_ref, v2_in, s0.at[2], s0.at[3], sib)
    a.start()
    b.start()
    pump.run(1)
    a.wait()
    b.wait()
    mods[me] = (v1[...] + v1_in[...]).astype(BF16)
    b2[me] = wide_ref[...] + v2_in[...]

    def chip(k):
        m = (me + k) % 16
        return m, ((m // 2) * 2 + c, m % 2)

    def to_chip(buf, send, recv, k):
        return remote(buf.at[me], buf.at[me], send.at[k], recv.at[me], chip(k)[1])

    def from_chip(buf, send, recv, k):
        m, peer = chip(k)
        return remote(buf.at[m], buf.at[m], send.at[k], recv.at[m], peer)

    both = ((mods, s1, r1), (b2, s2, r2))
    for k in range(1, 16):
        for buf in both:
            to_chip(*buf, k).start()
    pump.run(3)
    for k in range(1, 16):
        from_chip(*both[0], k).wait_recv()
    every = jnp.concatenate([mods[i].astype(F32) for i in range(16)], axis=0)
    mbg_ref[...] = jnp.sum(every, axis=0, keepdims=True)
    every = every.astype(BF16)
    back = product(every, w_ref[...], 1, 1)
    for i in range(16):
        sgp[i, 0:1, :72] = back[i : i + 1, :]

    def send4(k):
        m = (d + k) % 16
        return remote(sgp.at[m], sg_ref.at[d], s4.at[k], r4.at[d], (m, y))

    for k in range(1, 16):
        send4(k).start()
    sg_ref[d] = sgp[d]
    pump.run(2)
    owned = jnp.concatenate([silu_ref[i].astype(F32)[0:1, :] for i in range(16)], axis=0)
    owned = owned.astype(BF16)[:, :72]
    for j in range(6):
        cols = slice(j * width, (j + 1) * width)
        mwg_ref[:, cols] = product(owned, every[:, cols], 0, 0)
    for k in range(1, 16):
        from_chip(*both[1], k).wait_recv()
    total = b2[0]
    for i in range(1, 16):
        total = total + b2[i]
    wide_out[...] = total

    def arrive3(i):
        remote(half_ref, b3.at[i], s3.at[0], r3.at[i], sib).wait_recv()

    for i in range(16):
        pl.when(jnp.logical_or(i != me, y != c))(functools.partial(arrive3, i))
    total = b3[0]
    for i in range(1, 16):
        total = total + b3[i]
    half_out[...] = total
    for k in range(1, 16):
        m = (d + k) % 16
        remote(sgp.at[m], sg_ref.at[m], s4.at[k], r4.at[m], (m, y)).wait_recv()
    pump.run()
    for reducer in reducers:
        reducer.finish()
    each3(lambda q, core: send3(q, core).wait_send())
    for k in range(1, 16):
        for buf in both:
            to_chip(*buf, k).wait_send()
        send4(k).wait_send()


def last_stage(rows, dqkv, w_qkv, tokens, resid, scale, parts, wide, halves, silu, w_mod, collective_id):
    vmem = pl.BlockSpec(memory_space=pltpu.VMEM)
    n = w_mod.shape[1]
    n2, n3 = wide.shape[1], halves.shape[1]
    half, width = tokens.shape
    cols = dqkv.shape[0] * dqkv.shape[1] // 3
    dma = pltpu.SemaphoreType.DMA((16,))
    shape = jax.ShapeDtypeStruct
    return pl.pallas_call(
        last_kernel,
        out_shape=[
            shape((half, width), BF16),
            shape((3, 72, cols), F32),
            shape((72, n), F32),
            shape((1, n), F32),
            shape((16, 8, 128), F32),
            shape((1, n2), F32),
            shape((1, n3), F32),
        ],
        in_specs=[vmem] * 11,
        out_specs=[vmem] * 7,
        scratch_shapes=[
            pltpu.VMEM((3, 16, 72, cols), BF16),
            pltpu.VMEM((half, width), F32),
            pltpu.VMEM((half, width), BF16),
            pltpu.VMEM((half, width), BF16),
            pltpu.VMEM((1, n), F32),
            pltpu.VMEM((1, n), F32),
            pltpu.VMEM((1, n2), F32),
            pltpu.VMEM((16, 1, n), BF16),
            pltpu.VMEM((16, 1, n2), F32),
            pltpu.VMEM((16, 1, n3), F32),
            pltpu.VMEM((16, 8, 128), F32),
        ]
        + [pltpu.VMEM((27, 72, cols), BF16)] * 3
        + [pltpu.SemaphoreType.DMA((6,))]
        + [dma] * 8
        + [
            pltpu.SemaphoreType.DMA((3, REDUCE_RECV)),
            pltpu.SemaphoreType.DMA((3, REDUCE_SEND)),
        ],
        compiler_params=pltpu.CompilerParams(
            collective_id=collective_id, has_side_effects=True, vmem_limit_bytes=63000 * 1024
        ),
    )(rows, dqkv, w_qkv, tokens, resid, scale, parts, wide, halves, silu, w_mod)


LOG2E = math.log2(math.e)


def attention_step(qkv, out, lse, block, scale):
    heads, blocks = qkv.shape[0] // 3, qkv.shape[2] // block
    factor = scale * LOG2E

    def body(i):
        h = i // blocks
        cols = pl.ds(pl.multiple_of((i % blocks) * block, block), block)
        scores = product(qkv[heads + h], qkv[h, :, cols], 0, 0)
        top = jnp.max(scores, axis=0, keepdims=True)
        probs = jnp.exp2((scores - top) * factor)
        total = jnp.sum(probs, axis=0, keepdims=True)
        mixed = product(qkv[2 * heads + h], probs.astype(BF16), 1, 0)
        out[h, :, cols] = (mixed / total).astype(BF16)
        lse[h, :, cols] = top * factor + jnp.log2(total)

    return heads * blocks, body


GELU = math.sqrt(2 / math.pi)


def gelu_and_slope(v):
    square = v * v
    t = jnp.tanh(v * (GELU + GELU * 0.044715 * square))
    half = 0.5 * (1.0 + t)
    return v * half, half + 0.5 * v * (1.0 - t * t) * (GELU + GELU * 3 * 0.044715 * square)


def forward_kernel(
    chunks, block, scale, qkv, tokens, vecs, fc1_bias, grad_m, s_proj, s_fc1, s_fc2,
    out, lse, branch, resid, rows, act, slope, fc2_grad,
    w_proj, w_fc1, w_fc2, relay_proj, relay_1, relay_2,
    proj_here, fc1_here, sent, got, sems, recv, send,
):
    pos = place()
    sib = neighbours(pos)[0]
    half, width = tokens.shape
    greet(chip_peers(pos))
    parts = gather_parts(
        [s_proj, s_fc1, s_fc2],
        [w_proj, w_fc1, w_fc2],
        [relay_proj, relay_1, relay_2],
        chunks,
        recv,
        send,
        pos,
    )
    first = [i for i, (g, _) in enumerate(chunks) if g < 2]
    events = gather_events(parts, 3)
    pump = Pump(events)
    pump.run(3)
    steps, body = attention_step(qkv, out, lse, block, scale)
    pump.loop(steps, body, first=2)
    pump.run(events.index(parts[0].ready) + 1 - pump.next)

    load = pltpu.make_async_copy(w_proj, proj_here, sems.at[0])
    load.start()
    load.wait()
    tile = half // 2
    swap = remote(sent, got, sems.at[1], sems.at[2], sib)

    def project(i):
        cols = pl.ds(pl.multiple_of(i * tile, tile), tile)
        heads = flat(out[:, :, cols])
        return product(heads, flat(proj_here[...]), 0, 1)

    def other_rows(i, _):
        sent[pl.ds(pl.multiple_of(i * tile, tile), tile), :] = project(i + 2).astype(BF16)
        return 0

    def own_rows(i, _):
        branch[pl.ds(pl.multiple_of(i * tile, tile), tile), :] = project(i) + vecs[3:4, :]
        return 0

    lax.fori_loop(0, 2, other_rows, 0)
    swap.start()
    lax.fori_loop(0, 2, own_rows, 0)
    pump.run(4)
    swap.wait()
    share = remote(rows.at[:half], rows.at[half:], sems.at[3], sems.at[4], sib)
    piece = half // 4

    def norm(i, _):
        part = pl.ds(pl.multiple_of(i * piece, piece), piece)
        total = branch[part, :] + got[part, :].astype(F32)
        branch[part, :] = total
        mid = tokens[part, :].astype(F32) + vecs[0:1, :] * total
        resid[part, :] = mid
        center = mid - jnp.mean(mid, axis=-1, keepdims=True)
        spread = jnp.mean(center * center, axis=-1, keepdims=True)
        normed = center * lax.rsqrt(spread + 1e-06) * (1.0 + vecs[2:3, :]) + vecs[1:2, :]
        rows[part, :] = normed.astype(BF16)
        return 0

    lax.fori_loop(0, 4, norm, 0)
    share.start()
    pump.run(events.index(parts[first[-1]].ready) + 1 - pump.next)

    load = pltpu.make_async_copy(w_fc1, fc1_here, sems.at[0])
    load.start()
    load.wait()
    share.wait()
    n = 256

    def hidden(i):
        cols = pl.ds(pl.multiple_of(i * n, n), n)
        weight = flat(fc1_here[:, :, cols])
        value, rate = gelu_and_slope(product(rows[...], weight, 1, 0) + fc1_bias[:, cols])
        act[:, cols] = value.astype(BF16)
        slope[:, cols] = rate.astype(BF16)

    pump.loop(act.shape[1] // n, hidden)

    def weight_grad(i):
        cols = pl.ds(pl.multiple_of(i * n, n), n)
        value = product(grad_m[...], act[:, cols], 0, 0)
        fc2_grad[:, :, cols] = value.reshape(fc2_grad.shape[:2] + (n,)).astype(BF16)

    pump.loop(act.shape[1] // n, weight_grad)
    pump.run()
    for p in parts:
        p.finish()


def forward_stage(qkv, tokens, vecs, fc1_bias, grad_m, shards, chunks, collective_id, block=512):
    heads, size, count = qkv.shape[0] // 3, qkv.shape[1], qkv.shape[2]
    half, width = tokens.shape
    owned, cols = shards[0].shape[1:]
    hidden = shards[1].shape[2]
    vmem, anywhere = pl.BlockSpec(memory_space=pltpu.VMEM), pl.BlockSpec(memory_space=pl.ANY)
    shape = jax.ShapeDtypeStruct
    return pl.pallas_call(
        functools.partial(forward_kernel, chunks, block, size**-0.5),
        out_shape=[
            shape((heads, size, count), BF16),
            shape((heads, 1, count), F32),
            shape((half, width), F32),
            shape((half, width), F32),
            shape((count, width), BF16),
            shape((count, hidden), BF16),
            shape((count, hidden), BF16),
            shape((16, owned, hidden), BF16),
        ]
        + gather_shapes(shards),
        in_specs=[vmem] * 5 + [anywhere] * 3,
        out_specs=[vmem] * 8 + [anywhere] * 6,
        scratch_shapes=[
            pltpu.VMEM((16, owned, cols), BF16),
            pltpu.VMEM((16, owned, hidden), BF16),
            pltpu.VMEM((half, width), BF16),
            pltpu.VMEM((half, width), BF16),
            pltpu.SemaphoreType.DMA((5,)),
        ]
        + gather_sems(chunks),
        compiler_params=pltpu.CompilerParams(
            collective_id=collective_id, has_side_effects=True, vmem_limit_bytes=63000 * 1024
        ),
    )(qkv, tokens, vecs, fc1_bias, grad_m, *shards)[:11]


def attention_back_step(qkv, grad, out, lse, result, key_sum, value_sum, block, scale):
    heads, blocks = qkv.shape[0] // 3, qkv.shape[2] // block
    factor = scale * LOG2E

    def body(i):
        h, j = i // blocks, i % blocks
        cols = pl.ds(pl.multiple_of(j * block, block), block)
        queries, keys, values = qkv[h, :, cols], qkv[heads + h], qkv[2 * heads + h]
        grads = grad[h, :, cols]
        inner = jnp.sum(out[h, :, cols].astype(F32) * grads.astype(F32), axis=0, keepdims=True)
        probs = jnp.exp2(product(keys, queries, 0, 0) * factor - lse[h, :, cols])
        score_grad = (probs * (product(values, grads, 0, 0) - inner)).astype(BF16)
        value_part = product(grads, probs.astype(BF16), 1, 1)
        key_part = product(queries, score_grad, 1, 1)
        result[h, :, cols] = (product(keys, score_grad, 1, 0) * scale).astype(BF16)

        @pl.when(j == 0)
        def _():
            key_sum[...] = key_part
            value_sum[...] = value_part

        @pl.when(j > 0)
        def _():
            key_sum[...] += key_part
            value_sum[...] += value_part

        @pl.when(j == blocks - 1)
        def _():
            result[heads + h] = (key_sum[...] * scale).astype(BF16)
            result[2 * heads + h] = value_sum[...].astype(BF16)

    return heads * blocks, body


def attention_backward_kernel(chunks, count, block, scale, qkv, grad, out, lse, *refs):
    n = len(chunks)
    grads, result, outs = refs[:count], refs[count], refs[count + 1 : 2 * count + 1]
    key_sum, value_sum = refs[2 * count + 1 : 2 * count + 3]
    rest = refs[2 * count + 3 :]
    lands, (recv, send) = rest[:n], rest[n:]
    pos = place()
    greet(chip_peers(pos))
    parts = [
        Reduce(grads[g], lands[i], outs[g], recv.at[i], send.at[i], pos, cols)
        for i, (g, cols) in enumerate(chunks)
    ]
    steps, body = attention_back_step(
        qkv, grad, out, lse, result, key_sum, value_sum, block, scale
    )
    pump = Pump(reduce_events(parts))
    pump.run(2)
    pump.loop(steps, body, first=4, every=4)
    pump.run()


def attention_backward(qkv, grad, out, lse, grads, chunks, collective_id, block=512):
    count = len(grads)
    heads, size, tokens = qkv.shape[0] // 3, qkv.shape[1], qkv.shape[2]
    vmem = pl.BlockSpec(memory_space=pltpu.VMEM)
    return pl.pallas_call(
        functools.partial(attention_backward_kernel, chunks, count, block, size**-0.5),
        out_shape=[jax.ShapeDtypeStruct(qkv.shape, BF16)]
        + [jax.ShapeDtypeStruct(g.shape[1:], F32) for g in grads],
        in_specs=[vmem] * (4 + count),
        out_specs=[vmem] * (1 + count),
        scratch_shapes=[pltpu.VMEM((size, tokens), F32)] * 2 + reduce_scratch(chunks),
        compiler_params=pltpu.CompilerParams(
            collective_id=collective_id, has_side_effects=True, vmem_limit_bytes=63000 * 1024
        ),
    )(qkv, grad, out, lse, *grads)


def index_of(z, x, c, y):
    return ((z * 2 + x) * 2 + c) * 2 + y


def core_pairs():
    return [
        (index_of(z, x, c, y), index_of(z, x, 1 - c, y))
        for z in range(4)
        for x in range(2)
        for c in range(2)
        for y in range(2)
    ]


def latent_pairs():
    return [
        (index_of(z, x, c, y), index_of(z, x, y, c))
        for z in range(4)
        for x in range(2)
        for c in range(2)
        for y in range(2)
        if c != y
    ]


def trade(value):
    moved = lax.ppermute(value, AXES, latent_pairs())
    home = lax.axis_index("dp") % 2 == lax.axis_index("tensor")
    return jnp.where(home, value, moved)


def both_halves(value):
    return jnp.concatenate([value, lax.ppermute(value, AXES, core_pairs())], axis=0)


def own_sum(partial):
    n = partial.shape[0] // 2
    moved = lax.ppermute(partial[n:].astype(BF16), AXES, core_pairs())
    return partial[:n] + moved.astype(F32)


def columns(n, step):
    return [(i, min(step, n - i)) for i in range(0, n, step)]


def on_device_chip(
    tokens,
    cond,
    mod_weight,
    mod_bias,
    query_key_value_weight,
    qkv_bias,
    attention_out_weight,
    attention_out_bias,
    first_hidden_weight,
    first_hidden_bias,
    second_hidden_weight,
    second_hidden_bias,
    out_grad,
):
    half, _, width = tokens.shape
    owned, _, cols = query_key_value_weight.shape
    head_size = width // HEADS
    heads_here = cols // head_size
    hidden = first_hidden_weight.shape[1]

    silu_cond, silu_back = jax.vjp(jax.nn.silu, cond.astype(F32))
    pieces = jnp.pad(
        silu_cond.astype(BF16).reshape(16, 1, owned), ((0, 0), (0, 7), (0, 128 - owned))
    )
    s_qkv = query_key_value_weight.reshape(1, owned, 3 * cols)
    modulation, silu_owned, w_qkv = first_stage(
        pieces, mod_weight, mod_bias.astype(F32)[None], s_qkv, [(0, p) for p in columns(3 * cols, 896)], 2
    )
    w_qkv = w_qkv.reshape(width, 3 * cols)
    shift_a, scale_a, gate_a, shift_m, scale_m, gate_m = [
        modulation[:, i * width : (i + 1) * width] for i in range(6)
    ]

    bias_rows = jnp.concatenate([qkv_bias.reshape(-1), first_hidden_bias]).reshape(-1, width)
    carried = trade(jnp.concatenate([tokens.reshape(half, width), bias_rows], axis=0))
    tokens_here = carried[:half].astype(F32)
    biases = carried[half:].reshape(-1)
    q_bias, v_bias, fc1_bias = biases[:cols], biases[cols : 2 * cols], biases[2 * cols :]
    grad_out = trade(out_grad.reshape(half, width)).astype(F32)

    s_proj = attention_out_weight.T.reshape(1, owned, cols)
    s_fc1 = first_hidden_weight.reshape(1, owned, hidden)
    s_fc2 = second_hidden_weight.T.reshape(1, owned, hidden)
    chunks = [(0, None)] + [(g, p) for g in (1, 2) for p in columns(hidden, 1152)]

    normed_a = modulate(tokens_here, shift_a, scale_a)
    rows_a = both_halves(normed_a.astype(BF16))
    qkv_shift = jnp.concatenate([q_bias, jnp.zeros_like(q_bias), v_bias]).astype(F32)
    qkv = product(w_qkv, rows_a, 0, 1) + qkv_shift[:, None]
    qkv = qkv.astype(BF16).reshape(3 * heads_here, head_size, 2 * half)
    grad_m_own = (grad_out * gate_m).astype(BF16)
    fc2_bias_part = jnp.sum(grad_m_own, axis=0, dtype=F32)
    grad_m = both_halves(grad_m_own)
    vecs = jnp.concatenate([gate_a, shift_m, scale_m, attention_out_bias.astype(F32)[None]])
    (
        attended,
        log_totals,
        branch_a,
        resid_mid,
        rows_m,
        act_low,
        slope,
        fc2_grad,
        w_proj,
        w_fc1,
        w_fc2,
    ) = forward_stage(
        qkv,
        carried[:half],
        vecs,
        fc1_bias.astype(F32)[None],
        grad_m,
        [s_proj, s_fc1, s_fc2],
        chunks,
        3,
    )
    w_proj, w_fc1, w_fc2 = (w.reshape(width, -1) for w in (w_proj, w_fc1, w_fc2))
    attended_rows = attended.reshape(cols, 2 * half)
    _, norm_m_back = jax.vjp(modulate, resid_mid, shift_m, scale_m)
    branch_m = own_sum(
        jnp.einsum("rf,df->rd", act_low, w_fc2, preferred_element_type=F32)
    ) + second_hidden_bias.astype(F32)
    output = (resid_mid + gate_m * branch_m).astype(BF16)

    gate_m_grad = jnp.sum(grad_out * branch_m, axis=0)
    act_grad = jnp.dot(grad_m, w_fc2, preferred_element_type=F32)
    pre_grad = (act_grad * slope.astype(F32)).astype(BF16)
    fc1_bias_part = jnp.sum(pre_grad, axis=0, dtype=F32)
    fc1_grad = jnp.einsum("rd,rf->df", rows_m, pre_grad, preferred_element_type=F32).astype(BF16)
    normed_m_grad = own_sum(
        jnp.einsum("rf,df->rd", pre_grad, w_fc1, preferred_element_type=F32)
    )
    resid_part, shift_m_grad, scale_m_grad = norm_m_back(normed_m_grad)
    resid_grad = grad_out + resid_part

    gate_a_grad = jnp.sum(resid_grad * branch_a, axis=0)
    grad_a_own = (resid_grad * gate_a).astype(BF16)
    proj_bias_part = jnp.sum(grad_a_own, axis=0, dtype=F32)
    grad_a = both_halves(grad_a_own)
    proj_grad = product(grad_a, attended_rows, 0, 1).astype(BF16)
    attended_grad = product(w_proj, grad_a, 0, 1).astype(BF16)
    chunks = [(g, p) for g in (0, 1) for p in columns(hidden, 768)] + [(2, (0, cols))]
    qkv_grad, fc2_out, fc1_out, proj_out = attention_backward(
        qkv,
        attended_grad.reshape(attended.shape),
        attended,
        log_totals,
        [fc2_grad, fc1_grad.reshape(16, owned, -1), proj_grad.reshape(16, owned, -1)],
        chunks,
        4,
    )
    qkv_bias_part = jnp.sum(qkv_grad, axis=2, dtype=F32)
    half_part = jnp.concatenate(
        [
            fc1_bias_part,
            qkv_bias_part[:heads_here].reshape(-1),
            qkv_bias_part[2 * heads_here :].reshape(-1),
        ]
    )[None]
    mod_part = jnp.concatenate(
        [
            gate_a_grad.reshape(1, -1),
            shift_m_grad.reshape(1, -1),
            scale_m_grad.reshape(1, -1),
            gate_m_grad.reshape(1, -1),
        ],
        axis=1,
    )
    wide_part = jnp.concatenate([fc2_bias_part, proj_bias_part])[None]
    tokens_grad, qkv_out, mod_weight_grad, mod_bias_grad, silu_grad, wide, narrow = last_stage(
        rows_a,
        qkv_grad,
        w_qkv,
        carried[:half],
        resid_grad,
        scale_a,
        mod_part,
        wide_part,
        half_part,
        silu_owned,
        mod_weight,
        6,
    )
    cond_grad = silu_back(silu_grad[:, 0, :owned].reshape(1, width))[0]
    return (
        trade(output).reshape(half, 1, width),
        trade(tokens_grad).reshape(half, 1, width),
        cond_grad,
        mod_weight_grad,
        mod_bias_grad[0],
        jnp.moveaxis(qkv_out, 0, 1),
        narrow[0, hidden:].reshape(2, cols),
        proj_out.T,
        wide[0, width:],
        fc1_out,
        narrow[0, :hidden],
        fc2_out.T,
        wide[0, :width],
    )


def solution(mesh):
    shape = dict(mesh.shape)
    body = on_device_chip if shape == {"dp": 16, "tensor": 2} else on_device_general
    return jax.shard_map(
        body,
        mesh=mesh,
        in_specs=(
            P("tensor", "dp", None),
            P("dp", None),
            P("dp", None),
            P(),
            P("dp", None, "tensor"),
            P(None, "tensor"),
            P("tensor", "dp"),
            P(),
            P("dp", "tensor"),
            P("tensor"),
            P("tensor", "dp"),
            P(),
            P("tensor", "dp", None),
        ),
        out_specs=(
            P("tensor", "dp", None),
            P("tensor", "dp", None),
            P("dp", None),
            P("dp", None),
            P(),
            P("dp", None, "tensor"),
            P(None, "tensor"),
            P("tensor", "dp"),
            P(),
            P("dp", "tensor"),
            P("tensor"),
            P("tensor", "dp"),
            P(),
        ),
        check_vma=False,
    )
```

```python
import functools
import math

import jax
import jax.numpy as jnp
from jax import lax
from jax.experimental import pallas as pl
from jax.experimental.pallas import tpu as pltpu
from jax.sharding import PartitionSpec as P

HEADS = 16
MESH = pl.DeviceIdType.MESH
AXES = ("dp", "tensor")
F32 = jnp.float32
BF16 = jnp.bfloat16


def modulate(hidden, shifts, scales):
    center = hidden - jnp.mean(hidden, axis=-1, keepdims=True)
    spread = jnp.mean(center * center, axis=-1, keepdims=True)
    return center * lax.rsqrt(spread + 1e-06) * (1.0 + scales) + shifts


def gelu_tanh(values):
    return jax.nn.gelu(values, approximate=True)


def attend_forward(packed):
    queries = packed[:, 0]
    keys_all = packed[:, 1]
    values_all = packed[:, 2]
    seq_len = packed.shape[0]
    scaling = packed.shape[3] ** (-0.5)
    block_rows = min(512, seq_len)
    results = []
    log_parts = []
    for offset in range(0, seq_len, block_rows):
        query_block = queries[offset : offset + block_rows]
        scores = (
            jnp.einsum("qhe,khe->hqk", query_block, keys_all, preferred_element_type=jnp.float32)
            * scaling
        )
        highest = jnp.max(scores, axis=-1, keepdims=True)
        weights = jnp.exp(scores - highest)
        row_total = jnp.sum(weights, axis=-1, keepdims=True)
        prob_low = (weights / row_total).astype(jnp.bfloat16)
        mixture = jnp.einsum(
            "hqk,khe->qhe", prob_low, values_all, preferred_element_type=jnp.float32
        )
        results.append(mixture.reshape(block_rows, -1))
        log_parts.append((highest + jnp.log(row_total))[..., 0])
    return (jnp.concatenate(results, 0).astype(jnp.bfloat16), jnp.concatenate(log_parts, 1))


def attend_backward(inputs):
    packed, grad_out, log_totals = inputs
    queries = packed[:, 0]
    keys_all = packed[:, 1]
    values_all = packed[:, 2]
    seq_len = packed.shape[0]
    scaling = packed.shape[3] ** (-0.5)
    block_rows = min(512, seq_len)
    query_grads = []
    key_grad = jnp.zeros(keys_all.shape, jnp.float32)
    value_grad = jnp.zeros(values_all.shape, jnp.float32)
    for offset in range(0, seq_len, block_rows):
        query_block = queries[offset : offset + block_rows]
        grad_block = grad_out[offset : offset + block_rows]
        scores = (
            jnp.einsum("qhe,khe->hqk", query_block, keys_all, preferred_element_type=jnp.float32)
            * scaling
        )
        probs = jnp.exp(scores - log_totals[:, offset : offset + block_rows, None])
        prob_low = probs.astype(jnp.bfloat16)
        prob_grad = jnp.einsum(
            "qhe,khe->hqk", grad_block, values_all, preferred_element_type=jnp.float32
        )
        inner = jnp.sum(probs * prob_grad, axis=-1, keepdims=True)
        score_grad = (probs * (prob_grad - inner)).astype(jnp.bfloat16)
        query_grads.append(
            jnp.einsum("hqk,khe->qhe", score_grad, keys_all, preferred_element_type=jnp.float32)
            * scaling
        )
        key_grad = (
            key_grad
            + jnp.einsum(
                "hqk,qhe->khe", score_grad, query_block, preferred_element_type=jnp.float32
            )
            * scaling
        )
        value_grad = value_grad + jnp.einsum(
            "hqk,qhe->khe", prob_low, grad_block, preferred_element_type=jnp.float32
        )
    return jnp.stack([jnp.concatenate(query_grads, 0), key_grad, value_grad], 1).astype(
        jnp.bfloat16
    )


def on_device_general(
    tokens,
    cond,
    mod_weight,
    mod_bias,
    query_key_value_weight,
    qkv_bias,
    attention_out_weight,
    attention_out_bias,
    first_hidden_weight,
    first_hidden_bias,
    second_hidden_weight,
    second_hidden_bias,
    out_grad,
):
    w_mod, w_qkv, w_proj, w_fc1, w_fc2 = (
        lax.all_gather(mod_weight, "dp", axis=0, tiled=True),
        lax.all_gather(query_key_value_weight, "dp", axis=0, tiled=True),
        lax.all_gather(attention_out_weight, "dp", axis=1, tiled=True),
        lax.all_gather(first_hidden_weight, "dp", axis=0, tiled=True),
        lax.all_gather(second_hidden_weight, "dp", axis=1, tiled=True),
    )
    seq_local, latents, width = tokens.shape
    columns = query_key_value_weight.shape[2]
    head_size = width // HEADS
    heads_here = columns // head_size
    local_rows = seq_local * latents
    cond_wide = cond.astype(jnp.float32)
    silu_cond, silu_back = jax.vjp(jax.nn.silu, cond_wide)
    silu_low = silu_cond.astype(jnp.bfloat16)
    modulation = jnp.dot(silu_low, w_mod, preferred_element_type=jnp.float32) + mod_bias.astype(
        jnp.float32
    )
    pieces = modulation.reshape(latents, 6, width)
    hidden_in = tokens.astype(jnp.float32)
    attention_normalized, norm_a_back = jax.vjp(modulate, hidden_in, pieces[:, 0], pieces[:, 1])
    gathered_a = lax.all_gather(
        attention_normalized.astype(jnp.bfloat16), "tensor", axis=0, tiled=True
    )
    seq_len = gathered_a.shape[0]
    total_rows = seq_len * latents
    rows_a = gathered_a.reshape(total_rows, width)
    qkv_flat = w_qkv.reshape(width, 3 * columns)
    zero_row = jnp.zeros((columns,), jnp.float32)
    query_key_value_shift = jnp.stack(
        [qkv_bias[0].astype(jnp.float32), zero_row, qkv_bias[1].astype(jnp.float32)]
    )
    projected_output = (
        jnp.dot(rows_a, qkv_flat, preferred_element_type=jnp.float32).reshape(
            seq_len, latents, 3, columns
        )
        + query_key_value_shift
    )
    packed = jnp.moveaxis(projected_output.astype(jnp.bfloat16), 1, 0).reshape(
        latents, seq_len, 3, heads_here, head_size
    )
    attention_result, log_totals = lax.map(attend_forward, packed)
    attended_rows = jnp.moveaxis(attention_result, 0, 1).reshape(total_rows, columns)
    summed_a = lax.psum_scatter(
        jnp.dot(attended_rows, w_proj, preferred_element_type=jnp.float32).astype(jnp.bfloat16),
        "tensor",
        scatter_dimension=0,
        tiled=True,
    ).astype(jnp.float32)
    attention_branch = summed_a.reshape(seq_local, latents, width) + attention_out_bias.astype(
        jnp.float32
    )
    resid_mid = hidden_in + pieces[:, 2] * attention_branch
    feedforward_normalized, norm_m_back = jax.vjp(modulate, resid_mid, pieces[:, 3], pieces[:, 4])
    gathered_m = lax.all_gather(
        feedforward_normalized.astype(jnp.bfloat16), "tensor", axis=0, tiled=True
    )
    rows_m = gathered_m.reshape(total_rows, width)
    before_activation = jnp.dot(
        rows_m, w_fc1, preferred_element_type=jnp.float32
    ) + first_hidden_bias.astype(jnp.float32)
    gelu_activated, gelu_back = jax.vjp(gelu_tanh, before_activation)
    act_low = gelu_activated.astype(jnp.bfloat16)
    summed_m = lax.psum_scatter(
        jnp.dot(act_low, w_fc2, preferred_element_type=jnp.float32).astype(jnp.bfloat16),
        "tensor",
        scatter_dimension=0,
        tiled=True,
    ).astype(jnp.float32)
    feedforward_branch = summed_m.reshape(seq_local, latents, width) + second_hidden_bias.astype(
        jnp.float32
    )
    output = (resid_mid + pieces[:, 5] * feedforward_branch).astype(jnp.bfloat16)
    grad_out = out_grad.astype(jnp.float32)
    gate_m_grad = jnp.sum(grad_out * feedforward_branch, axis=0)
    grad_m_low = (grad_out * pieces[:, 5]).astype(jnp.bfloat16)
    grad_m_rows = lax.all_gather(grad_m_low, "tensor", axis=0, tiled=True).reshape(
        total_rows, width
    )
    fc2_bias_grad = jnp.sum(grad_m_rows, axis=0, dtype=jnp.float32)
    fc2_weight_grad = jnp.einsum(
        "rf,rd->fd", act_low, grad_m_rows, preferred_element_type=jnp.float32
    )
    act_grad = jnp.einsum("rd,fd->rf", grad_m_rows, w_fc2, preferred_element_type=jnp.float32)
    pre_grad = gelu_back(act_grad)[0].astype(jnp.bfloat16)
    fc1_bias_grad = jnp.sum(pre_grad, axis=0, dtype=jnp.float32)
    fc1_weight_grad = jnp.einsum("rd,rf->df", rows_m, pre_grad, preferred_element_type=jnp.float32)
    normed_m_grad = (
        lax.psum_scatter(
            jnp.einsum("rf,df->rd", pre_grad, w_fc1, preferred_element_type=jnp.float32).astype(
                jnp.bfloat16
            ),
            "tensor",
            scatter_dimension=0,
            tiled=True,
        )
        .astype(jnp.float32)
        .reshape(seq_local, latents, width)
    )
    resid_part, shift_m_grad, scale_m_grad = norm_m_back(normed_m_grad)
    resid_grad = grad_out + resid_part
    gate_a_grad = jnp.sum(resid_grad * attention_branch, axis=0)
    grad_a_low = (resid_grad * pieces[:, 2]).astype(jnp.bfloat16)
    grad_a_flat = grad_a_low.reshape(local_rows, width)
    proj_bias_part = jnp.sum(grad_a_flat, axis=0, dtype=jnp.float32)
    grad_a_rows = lax.all_gather(grad_a_low, "tensor", axis=0, tiled=True).reshape(
        total_rows, width
    )
    proj_weight_grad = jnp.einsum(
        "rc,rd->cd", attended_rows, grad_a_rows, preferred_element_type=jnp.float32
    )
    attended_grad = jnp.einsum(
        "rd,cd->rc", grad_a_rows, w_proj, preferred_element_type=jnp.float32
    ).astype(jnp.bfloat16)
    grad_packed = jnp.moveaxis(attended_grad.reshape(seq_len, latents, heads_here, head_size), 1, 0)
    qkv_grad_packed = lax.map(attend_backward, (packed, grad_packed, log_totals))
    qkv_grad_rows = jnp.moveaxis(qkv_grad_packed, 0, 1).reshape(total_rows, 3 * columns)
    bias_sums = jnp.sum(qkv_grad_rows.reshape(total_rows, 3, columns), axis=0, dtype=jnp.float32)
    qkv_bias_grad = jnp.stack([bias_sums[0], bias_sums[2]])
    qkv_weight_grad = jnp.einsum(
        "rd,rc->dc", rows_a, qkv_grad_rows, preferred_element_type=jnp.float32
    ).reshape(width, 3, columns)
    normed_a_grad = (
        lax.psum_scatter(
            jnp.einsum(
                "rc,dc->rd", qkv_grad_rows, qkv_flat, preferred_element_type=jnp.float32
            ).astype(jnp.bfloat16),
            "tensor",
            scatter_dimension=0,
            tiled=True,
        )
        .astype(jnp.float32)
        .reshape(seq_local, latents, width)
    )
    input_part, shift_a_grad, scale_a_grad = norm_a_back(normed_a_grad)
    tokens_grad = (resid_grad + input_part).astype(jnp.bfloat16)
    partial_mod = jnp.stack(
        [shift_a_grad, scale_a_grad, gate_a_grad, shift_m_grad, scale_m_grad, gate_m_grad], 1
    ).reshape(latents, 6 * width)
    mod_summed, proj_bias_grad = (
        lax.psum(partial_mod.astype(jnp.bfloat16), "tensor").astype(jnp.float32),
        lax.psum(proj_bias_part.astype(jnp.bfloat16), "tensor").astype(jnp.float32),
    )
    mod_grad_low = mod_summed.astype(jnp.bfloat16)
    silu_grad = jnp.einsum("le,de->ld", mod_grad_low, w_mod, preferred_element_type=jnp.float32)
    cond_grad = silu_back(silu_grad)[0]
    silu_every, mod_every = (
        lax.all_gather(silu_low, "dp", axis=0, tiled=True),
        lax.all_gather(mod_grad_low, "dp", axis=0, tiled=True),
    )
    owned_rows = mod_weight.shape[0]
    silu_owned = lax.dynamic_slice_in_dim(
        silu_every, lax.axis_index("dp") * owned_rows, owned_rows, 1
    )
    mod_weight_grad = jnp.einsum(
        "ld,le->de", silu_owned, mod_every, preferred_element_type=jnp.float32
    )
    mod_bias_grad = jnp.sum(mod_every, axis=0, dtype=jnp.float32)
    qkv_weight_grad, proj_weight_grad, fc1_weight_grad, fc2_weight_grad = (
        lax.psum_scatter(
            qkv_weight_grad.astype(jnp.bfloat16), "dp", scatter_dimension=0, tiled=True
        ).astype(jnp.float32),
        lax.psum_scatter(
            proj_weight_grad.astype(jnp.bfloat16), "dp", scatter_dimension=1, tiled=True
        ).astype(jnp.float32),
        lax.psum_scatter(
            fc1_weight_grad.astype(jnp.bfloat16), "dp", scatter_dimension=0, tiled=True
        ).astype(jnp.float32),
        lax.psum_scatter(
            fc2_weight_grad.astype(jnp.bfloat16), "dp", scatter_dimension=1, tiled=True
        ).astype(jnp.float32),
    )
    qkv_bias_grad, proj_bias_grad, fc1_bias_grad, fc2_bias_grad = lax.psum(
        (qkv_bias_grad, proj_bias_grad, fc1_bias_grad, fc2_bias_grad), "dp"
    )
    return (
        output,
        tokens_grad,
        cond_grad,
        mod_weight_grad,
        mod_bias_grad,
        qkv_weight_grad,
        qkv_bias_grad,
        proj_weight_grad,
        proj_bias_grad,
        fc1_weight_grad,
        fc1_bias_grad,
        fc2_weight_grad,
        fc2_bias_grad,
    )


def place():
    d = lax.axis_index("dp")
    y = lax.axis_index("tensor")
    return d, d // 4, (d // 2) % 2, d % 2, y


def neighbours(pos):
    d, z, x, c, y = pos
    sib = (z * 4 + x * 2 + (1 - c), y)
    xn = (z * 4 + (1 - x) * 2 + c, y)
    yn = (d, 1 - y)
    return sib, xn, yn


def z_peer(pos, k):
    d, z, x, c, y = pos
    return (((z + k) % 4) * 4 + x * 2 + c, y)


def greet(peers):
    sem = pltpu.get_barrier_semaphore()
    for peer in peers:
        pl.semaphore_signal(sem, inc=1, device_id=peer, device_id_type=MESH)
    pl.semaphore_wait(sem, len(peers))


def chip_peers(pos):
    d, z, x, c, y = pos
    across = [(z * 4 + x * 2 + 1 - c, 1 - y)]
    return list(neighbours(pos)) + across + [z_peer(pos, k) for k in (1, 2, 3)]


def remote(src, dst, send, recv, peer):
    return pltpu.make_async_remote_copy(
        src_ref=src, dst_ref=dst, send_sem=send, recv_sem=recv, device_id=peer, device_id_type=MESH
    )


GATHER_RECV = 24
GATHER_SEND = 32


class Gather:
    def __init__(self, shard, full, relay, cols, wide, recv, send, pos):
        self.wide = wide
        self.shard, self.full, self.relay, self.cols = shard, full, relay, cols
        self.recv, self.send, self.pos = recv, send, pos
        d, z, x, c, y = pos
        self.sib, self.xn, _ = neighbours(pos)
        self.far = (z * 4 + x * 2 + y, 1 - y)
        self.home, self.away = c == y, c != y

    def part(self, ref, b):
        if self.cols is None:
            return ref.at[pl.ds(b, 1)]
        return ref.at[pl.ds(b, 1), :, pl.ds(*self.cols)]

    def move(self, src, dst, s, r, peer):
        return remote(src, dst, self.send.at[s], self.recv.at[r], peer)

    def came(self, r):
        block = self.part(self.full, 0)
        self.move(block, block, 0, r, self.sib).wait_recv()

    def stay(self):
        return pltpu.make_async_copy(
            self.part(self.shard, 0), self.part(self.full, self.pos[0]), self.send.at[31]
        )

    def start(self):
        d, z, x, c, y = self.pos
        q = z * 2 + x
        own = self.part(self.shard, 0)

        @pl.when(self.home)
        def _():
            for k in (2, 1, 3):
                self.move(own, self.part(self.full, d), k, q, z_peer(self.pos, k)).start()
            self.move(own, self.part(self.full, d), 4, q, self.xn).start()
            self.move(own, self.part(self.full, d), 8, 8 + q, self.far).start()
            self.stay().start()

        @pl.when(self.away)
        def _():
            for k in (2, 1, 3):
                self.move(own, self.part(self.relay, q), k, q, z_peer(self.pos, k)).start()
            self.move(own, self.part(self.full, d), 8, 16 + q, self.far).start()
            self.move(own, self.part(self.relay, q), 4, q, self.xn).start()
            self.move(own, self.part(self.full, d), 16, 8 + q, self.sib).start()

    def from_z(self, k):
        d, z, x, c, y = self.pos
        q = ((z + k) % 4) * 2 + x
        dst = self.part(self.full, 2 * q + c)

        @pl.when(self.home)
        def _():
            self.came(q)
            self.move(dst, dst, 4 + k, q, self.xn).start()
            self.move(dst, dst, 8 + k, 8 + q, self.far).start()

        @pl.when(self.away)
        def _():
            self.came(q)
            src = self.part(self.relay, q)
            self.move(src, dst, 8 + k, 16 + q, self.far).start()
            self.move(src, src, 4 + k, q, self.xn).start()
            self.move(src, dst, 16 + k, 8 + q, self.sib).start()

    def from_x(self, k):
        d, z, x, c, y = self.pos
        q = ((z + k) % 4) * 2 + 1 - x
        dst = self.part(self.full, 2 * q + c)

        @pl.when(self.home)
        def _():
            self.came(q)
            if not self.wide:
                self.move(dst, dst, 12 + k, 8 + q, self.far).start()

        @pl.when(self.away)
        def _():
            self.came(q)
            self.move(self.part(self.relay, q), dst, 20 + k, 8 + q, self.sib).start()

    def from_y(self, k):
        d, z, x, c, y = self.pos
        q = ((z + k) % 4) * 2 + x

        @pl.when(self.away)
        def _():
            block = self.part(self.full, 2 * q + 1 - c)
            self.came(16 + q)
            self.move(block, block, 12 + k, 16 + q, self.xn).start()
            if self.wide:
                block = self.part(self.full, 2 * q + c)
                self.came(8 + q)
                self.move(block, block, 24 + k, 8 + q, self.xn).start()

    def ready(self):
        d, z, x, c, y = self.pos

        @pl.when(self.home)
        def _():
            for q in range(8):
                self.came(8 + q)
            self.stay().wait()

        @pl.when(self.away)
        def _():
            for k in range(4):
                q = ((z + k) % 4) * 2
                self.came(16 + q + 1 - x)
                self.came(8 + q + 1 - x)
                if not self.wide:
                    self.came(8 + q + x)

    def finish(self):
        block = self.part(self.full, 0)
        for s in range(1, 12):
            self.move(block, block, s, 0, self.sib).wait_send()

        @pl.when(self.home)
        def _():
            if not self.wide:
                for s in range(12, 16):
                    self.move(block, block, s, 0, self.sib).wait_send()

        @pl.when(self.away)
        def _():
            for s in range(12, 28 if self.wide else 24):
                self.move(block, block, s, 0, self.sib).wait_send()

    def early(self):
        return [functools.partial(self.from_z, k) for k in (1, 2, 3)]

    def late(self):
        steps = []
        for k in range(4):
            steps += [functools.partial(self.from_x, k), functools.partial(self.from_y, k)]
        return steps + [self.ready]


def gather_events(parts, lead=2):
    n = len(parts)
    events = [p.start for p in parts[:lead]]
    for i in range(n + 1):
        if i < n:
            events += parts[i].early()
        if i + lead < n:
            events.append(parts[i + lead].start)
        if i > 0:
            events += parts[i - 1].late()
    return events


def gather_parts(shards, fulls, relays, chunks, recv, send, pos):
    return [
        Gather(shards[g], fulls[g], relays[g], cols, wide, recv.at[i], send.at[i], pos)
        for i, (g, cols, wide) in enumerate(chunks)
    ]


def gather_sems(chunks):
    n = len(chunks)
    return [
        pltpu.SemaphoreType.DMA((n, GATHER_RECV)),
        pltpu.SemaphoreType.DMA((n, GATHER_SEND)),
    ]


def gather_shapes(shards):
    return [jax.ShapeDtypeStruct((16,) + s.shape[1:], s.dtype) for s in shards] + [
        jax.ShapeDtypeStruct((8,) + s.shape[1:], s.dtype) for s in shards
    ]


REDUCE_RECV = 27
REDUCE_SEND = 23


class Reduce:
    def __init__(self, grad, land, out, recv, send, pos, cols):
        self.grad, self.land, self.out = grad, land, out
        self.recv, self.send, self.pos, self.cols = recv, send, pos, pl.ds(*cols)
        d, z, x, c, y = pos
        self.sib, self.xn, self.yn = neighbours(pos)
        self.home, self.away = c == y, c != y

    def rows(self, b):
        return self.grad.at[pl.ds(b, 1), :, self.cols]

    def slot(self, i):
        return self.land.at[pl.ds(i, 1)]

    def push(self, src, slot, s, peer):
        return remote(src, self.slot(slot), self.send.at[s], self.recv.at[slot], peer)

    def came(self, slot):
        self.push(self.slot(slot), slot, 0, self.sib).wait_recv()

    def value(self, i):
        return self.land[i].astype(F32)

    def first(self):
        d, z, x, c, y = self.pos

        @pl.when(self.away)
        def _():
            for column, base in ((1 - x, 0), (x, 4)):

                def step(k, _):
                    q = lax.rem(z + 1 + k, 4) * 2 + column
                    self.push(self.rows(2 * q + c), q, base + k, self.yn).start()
                    self.push(self.rows(2 * q + 1 - c), 15 + q, 8 + base + k, self.sib).start()
                    return 0

                lax.fori_loop(0, 4, step, 0)

        @pl.when(self.home)
        def _():
            for column, base in ((1 - x, 0), (x, 4)):

                def step(k, _):
                    q = lax.rem(z + 1 + k, 4) * 2 + column
                    self.push(self.rows(2 * q + 1 - c), q, base + k, self.sib).start()
                    return 0

                lax.fori_loop(0, 4, step, 0)

    def second(self, k):
        d, z, x, c, y = self.pos
        zz = (z + 1 + k) % 4
        q = zz * 2 + 1 - x

        @pl.when(self.away)
        def _():
            self.came(q)
            self.push(self.slot(q), 8 + zz, 16 + k, self.xn).start()

        @pl.when(self.home)
        def _():
            self.came(15 + q)
            self.push(self.slot(15 + q), 23 + zz, 15 + k, self.xn).start()
            b = 2 * q + c
            self.came(q)
            total = self.grad[b, :, self.cols].astype(F32) + self.value(q)
            self.grad[b, :, self.cols] = total.astype(BF16)
            self.push(self.rows(b), 8 + zz, 8 + k, self.xn).start()

    def third(self, k):
        d, z, x, c, y = self.pos
        zz = (z + 1 + k) % 4
        q = zz * 2 + x

        @pl.when(self.home)
        def _():
            self.came(15 + q)
            self.came(23 + zz)
            self.land[15 + q] = (self.value(15 + q) + self.value(23 + zz)).astype(BF16)
            self.push(self.slot(15 + q), 15 + zz, 19 + k, self.yn).start()
            if k < 3:
                b = 2 * q + c
                self.came(q)
                self.came(8 + zz)
                total = self.grad[b, :, self.cols].astype(F32)
                total = total + self.value(q) + self.value(8 + zz)
                self.grad[b, :, self.cols] = total.astype(BF16)
                self.push(self.rows(b), 12 + k, 12 + k, (zz * 4 + x * 2 + c, y)).start()

    def fourth(self, k):
        d, z, x, c, y = self.pos
        zz = (z + 1 + k) % 4
        q = zz * 2 + x

        @pl.when(self.away)
        def _():
            self.came(q)
            self.came(8 + zz)
            self.came(15 + zz)
            total = self.value(q) + self.value(8 + zz) + self.value(15 + zz)
            self.land[q] = total.astype(BF16)
            self.push(self.slot(q), 12 + k, 20 + k, (zz * 4 + x * 2 + c, y)).start()

    def fifth(self):
        d, z, x, c, y = self.pos
        q = z * 2 + x
        self.came(q)
        self.came(8 + z)
        for k in range(3):
            self.came(12 + k)
        total = self.value(q) + self.value(8 + z)
        total = total + self.value(12) + self.value(13) + self.value(14)

        @pl.when(self.home)
        def _():
            self.out[:, self.cols] = total + self.grad[d, :, self.cols].astype(F32)

        @pl.when(self.away)
        def _():
            self.came(15 + z)
            self.out[:, self.cols] = total + self.value(15 + z)

    def finish(self):
        block = self.slot(0)
        for s in range(REDUCE_SEND):
            self.push(block, 0, s, self.sib).wait_send()


def reduce_events(parts, lead=1):
    n = len(parts)
    events = [p.first for p in parts[:lead]]
    for i in range(n + 3):
        if i + lead < n:
            events.append(parts[i + lead].first)
        for k in range(4):
            if i < n:
                events.append(functools.partial(parts[i].second, k))
            if 0 <= i - 1 < n:
                events.append(functools.partial(parts[i - 1].third, k))
            if 0 <= i - 2 < n and k < 3:
                events.append(functools.partial(parts[i - 2].fourth, k))
        if 0 <= i - 3 < n:
            events.append(parts[i - 3].fifth)
    return events


def reduce_scratch(chunks):
    n = len(chunks)
    return [pltpu.VMEM((27, 72, cols[1]), BF16) for _, cols in chunks] + [
        pltpu.SemaphoreType.DMA((n, REDUCE_RECV)),
        pltpu.SemaphoreType.DMA((n, REDUCE_SEND)),
    ]


class Pump:
    def __init__(self, events):
        self.events, self.next = list(events), 0

    def run(self, count=None):
        stop = len(self.events)
        if count is not None:
            stop = min(stop, self.next + max(0, count))
        for event in self.events[self.next : stop]:
            event()
        self.next = stop

    def loop(self, steps, body, count=0):
        todo = self.events[self.next :][:count]
        self.next += len(todo)

        def step(i, _):
            for j, event in enumerate(todo):
                pl.when(i == j * steps // count)(event)
            body(i)
            return 0

        lax.fori_loop(0, steps, step, 0)


def flat(value):
    return value.reshape(-1, value.shape[-1])


def product(a, b, ca, cb):
    return lax.dot_general(a, b, (((ca,), (cb,)), ((), ())), preferred_element_type=F32)


def last_kernel(
    rows_ref, dqkv_ref, wqkv_ref, tokens_ref, resid_ref, scale_ref, parts_ref, wide_ref, half_ref,
    silu_ref, w_ref,
    tgrad_ref, qkv_out, mwg_ref, mbg_ref, sg_ref, wide_out, half_out,
    grad, ngrad, sent, got, v1, v1_in, v2_in, mods, b2, b3, sgp, land0, land1, land2,
    s0, s1, r1, s2, r2, s3, r3, s4, r4, recv, send,
):
    pos = place()
    d, z, x, c, y = pos
    sib = neighbours(pos)[0]
    lin = d * 2 + y
    half, width = tokens_ref.shape
    heads = dqkv_ref.shape[0] // 3
    greet([(((lin + k) % 32) // 2, (lin + k) % 2) for k in range(1, 32)])
    me = (z * 2 + x) * 2 + y

    @pl.when(y == c)
    def _():
        b3[me] = half_ref[...]

    sgp[...] = jnp.zeros_like(sgp)

    def send3(q, core):
        s = q * 2 + core
        return remote(half_ref, b3.at[me], s3.at[s], r3.at[me], (s, c))

    def each3(action):
        for q in range(8):
            for core in range(2):
                pl.when(jnp.logical_or(d != q * 2 + core, y != c))(
                    functools.partial(action, q, core)
                )

    n = dqkv_ref.shape[1] * heads
    reducers = [
        Reduce(grad.at[j], land, qkv_out.at[j], recv.at[j], send.at[j], pos, (0, n))
        for j, land in enumerate((land0, land1, land2))
    ]

    def weight_grad(j, _):
        value = product(rows_ref[...], flat(dqkv_ref[pl.ds(j * heads, heads)]), 0, 1)
        grad[j] = value.reshape(grad.shape[1:]).astype(BF16)
        for i, reducer in enumerate(reducers):
            pl.when(j == i)(reducer.first)
        return 0

    lax.fori_loop(0, 3, weight_grad, 0)
    each3(lambda q, core: send3(q, core).start())
    pump = Pump(reduce_events(reducers, 3)[3:])

    tile = half // 2
    swap = remote(sent, got, s0.at[4], s0.at[5], sib)

    def into_norm(i):
        cols = pl.ds(pl.multiple_of(i * tile, tile), tile)
        return product(flat(dqkv_ref[:, :, cols]), wqkv_ref[...], 0, 1)

    def other_rows(i, _):
        sent[pl.ds(pl.multiple_of(i * tile, tile), tile), :] = into_norm(i + 2).astype(BF16)
        return 0

    def own_rows(i, _):
        ngrad[pl.ds(pl.multiple_of(i * tile, tile), tile), :] = into_norm(i)
        return 0

    lax.fori_loop(0, 2, other_rows, 0)
    swap.start()
    pump.run(1)
    lax.fori_loop(0, 2, own_rows, 0)
    swap.wait()
    piece = half // 4
    scale = 1.0 + scale_ref[...]

    def norm_back(i, sums):
        part = pl.ds(pl.multiple_of(i * piece, piece), piece)
        value = tokens_ref[part, :].astype(F32)
        center = value - jnp.mean(value, axis=-1, keepdims=True)
        rate = lax.rsqrt(jnp.mean(center * center, axis=-1, keepdims=True) + 1e-06)
        normed = center * rate
        g = ngrad[part, :] + got[part, :].astype(F32)
        e = g * scale
        inner = jnp.mean(e * normed, axis=-1, keepdims=True)
        back = rate * (e - jnp.mean(e, axis=-1, keepdims=True) - normed * inner)
        tgrad_ref[part, :] = (resid_ref[part, :] + back).astype(BF16)
        return (
            sums[0] + jnp.sum(g, axis=0, keepdims=True),
            sums[1] + jnp.sum(g * normed, axis=0, keepdims=True),
        )

    zero = jnp.zeros((1, width), F32)
    shift_sum, scale_sum = lax.fori_loop(0, 4, norm_back, (zero, zero))
    v1[:, :width] = shift_sum
    v1[:, width : 2 * width] = scale_sum
    v1[:, 2 * width :] = parts_ref[...]

    a = remote(v1, v1_in, s0.at[0], s0.at[1], sib)
    b = remote(wide_ref, v2_in, s0.at[2], s0.at[3], sib)
    a.start()
    b.start()
    pump.run(1)
    a.wait()
    b.wait()
    mods[me] = (v1[...] + v1_in[...]).astype(BF16)
    b2[me] = wide_ref[...] + v2_in[...]

    def chip(k):
        m = (me + k) % 16
        return m, ((m // 2) * 2 + c, m % 2)

    def to_chip(buf, send, recv, k):
        return remote(buf.at[me], buf.at[me], send.at[k], recv.at[me], chip(k)[1])

    def from_chip(buf, send, recv, k):
        m, peer = chip(k)
        return remote(buf.at[m], buf.at[m], send.at[k], recv.at[m], peer)

    both = ((mods, s1, r1), (b2, s2, r2))
    for k in range(1, 16):
        for buf in both:
            to_chip(*buf, k).start()
    pump.run(3)
    for k in range(1, 16):
        from_chip(*both[0], k).wait_recv()
    every = jnp.concatenate([mods[i].astype(F32) for i in range(16)], axis=0)
    mbg_ref[...] = jnp.sum(every, axis=0, keepdims=True)
    every = every.astype(BF16)
    back = product(every, w_ref[...], 1, 1)
    for i in range(16):
        sgp[i, 0:1, :72] = back[i : i + 1, :]

    def send4(k):
        m = (d + k) % 16
        return remote(sgp.at[m], sg_ref.at[d], s4.at[k], r4.at[d], (m, y))

    for k in range(1, 16):
        send4(k).start()
    sg_ref[d] = sgp[d]
    pump.run(2)
    owned = jnp.concatenate([silu_ref[i].astype(F32)[0:1, :] for i in range(16)], axis=0)
    owned = owned.astype(BF16)[:, :72]
    for j in range(6):
        cols = slice(j * width, (j + 1) * width)
        mwg_ref[:, cols] = product(owned, every[:, cols], 0, 0)
    for k in range(1, 16):
        from_chip(*both[1], k).wait_recv()
    total = b2[0]
    for i in range(1, 16):
        total = total + b2[i]
    wide_out[...] = total

    def arrive3(i):
        remote(half_ref, b3.at[i], s3.at[0], r3.at[i], sib).wait_recv()

    for i in range(16):
        pl.when(jnp.logical_or(i != me, y != c))(functools.partial(arrive3, i))
    total = b3[0]
    for i in range(1, 16):
        total = total + b3[i]
    half_out[...] = total
    for k in range(1, 16):
        m = (d + k) % 16
        remote(sgp.at[m], sg_ref.at[m], s4.at[k], r4.at[m], (m, y)).wait_recv()
    pump.run()
    for reducer in reducers:
        reducer.finish()
    each3(lambda q, core: send3(q, core).wait_send())
    for k in range(1, 16):
        for buf in both:
            to_chip(*buf, k).wait_send()
        send4(k).wait_send()


def last_stage(rows, dqkv, w_qkv, tokens, resid, scale, parts, wide, halves, silu, w_mod, collective_id):
    vmem = pl.BlockSpec(memory_space=pltpu.VMEM)
    n = w_mod.shape[1]
    n2, n3 = wide.shape[1], halves.shape[1]
    half, width = tokens.shape
    cols = dqkv.shape[0] * dqkv.shape[1] // 3
    dma = pltpu.SemaphoreType.DMA((16,))
    shape = jax.ShapeDtypeStruct
    return pl.pallas_call(
        last_kernel,
        out_shape=[
            shape((half, width), BF16),
            shape((3, 72, cols), F32),
            shape((72, n), F32),
            shape((1, n), F32),
            shape((16, 8, 128), F32),
            shape((1, n2), F32),
            shape((1, n3), F32),
        ],
        in_specs=[vmem] * 11,
        out_specs=[vmem] * 7,
        scratch_shapes=[
            pltpu.VMEM((3, 16, 72, cols), BF16),
            pltpu.VMEM((half, width), F32),
            pltpu.VMEM((half, width), BF16),
            pltpu.VMEM((half, width), BF16),
            pltpu.VMEM((1, n), F32),
            pltpu.VMEM((1, n), F32),
            pltpu.VMEM((1, n2), F32),
            pltpu.VMEM((16, 1, n), BF16),
            pltpu.VMEM((16, 1, n2), F32),
            pltpu.VMEM((16, 1, n3), F32),
            pltpu.VMEM((16, 8, 128), F32),
        ]
        + [pltpu.VMEM((27, 72, cols), BF16)] * 3
        + [pltpu.SemaphoreType.DMA((6,))]
        + [dma] * 8
        + [
            pltpu.SemaphoreType.DMA((3, REDUCE_RECV)),
            pltpu.SemaphoreType.DMA((3, REDUCE_SEND)),
        ],
        compiler_params=pltpu.CompilerParams(
            collective_id=collective_id, has_side_effects=True, vmem_limit_bytes=63000 * 1024
        ),
    )(rows, dqkv, w_qkv, tokens, resid, scale, parts, wide, halves, silu, w_mod)


LOG2E = math.log2(math.e)


def attention_step(qkv, out, lse, block, scale):
    heads, blocks = qkv.shape[0] // 3, qkv.shape[2] // block
    factor = scale * LOG2E

    def body(i):
        h = i // blocks
        cols = pl.ds(pl.multiple_of((i % blocks) * block, block), block)
        scores = product(qkv[heads + h], qkv[h, :, cols], 0, 0)
        top = jnp.max(scores, axis=0, keepdims=True)
        probs = jnp.exp2((scores - top) * factor)
        total = jnp.sum(probs, axis=0, keepdims=True)
        mixed = product(qkv[2 * heads + h], probs.astype(BF16), 1, 0)
        out[h, :, cols] = (mixed / total).astype(BF16)
        lse[h, :, cols] = top * factor + jnp.log2(total)

    return heads * blocks, body


GELU = math.sqrt(2 / math.pi)


def gelu_and_slope(v):
    square = v * v
    t = jnp.tanh(v * (GELU + GELU * 0.044715 * square))
    half = 0.5 * (1.0 + t)
    return v * half, half + 0.5 * v * (1.0 - t * t) * (GELU + GELU * 3 * 0.044715 * square)


def forward_kernel(
    chunks, block, scale,
    piece_ref, w_mod, mod_bias, proj_bias, small_in, tokens_in, grad_in,
    s_qkv, s_proj, s_fc1, s_fc2,
    mod, silu_ref, fc2_bias_grad,
    rows_a_out, qkv_out, attended_out, lse_out, branch_out, resid_out, rows_out, act_out,
    slope_out, fc2_grad_out, grad_m_out, tokens_out, grad_out,
    w_qkv, w_proj, w_fc1, w_fc2, relay_qkv, relay_proj, relay_1, relay_2,
    part, land, mine, other, small, tokens, out_grad,
    rows_a, qkv, out, lse, branch, resid, rows, act, slope, fc2_grad, grad_m,
    qkv_here, proj_here, weight_here, sent, got,
    s1, r1, s2, r2, sems, out_sems, recv, send,
):
    pos = place()
    d, z, x, c, y = pos
    sib, _, yn = neighbours(pos)
    far = (z * 4 + x * 2 + 1 - c, 1 - y)
    half, width = tokens.shape
    home, away = c == y, c != y
    greet([((d + k) % 16, y) for k in range(1, 16)] + [yn, far])

    stores = []

    def store(src, dst):
        copy = pltpu.make_async_copy(src, dst, out_sems.at[len(stores)])
        copy.start()
        stores.append(copy)

    def swapped(src, dst, i):
        there = remote(src, dst, sems.at[i], sems.at[i + 1], far)
        here = pltpu.make_async_copy(src, dst, sems.at[i + 1])

        def start():
            pl.when(away)(lambda: there.start())
            pl.when(home)(lambda: here.start())

        def wait():
            pl.when(away)(lambda: there.wait())
            pl.when(home)(lambda: here.wait())

        return start, wait

    def piece(k):
        to = (d + k) % 16
        return remote(piece_ref.at[to], silu_ref.at[d], s1.at[k], r1.at[d], (to, y))

    def piece_in(k):
        src = (d + k) % 16
        return remote(piece_ref.at[src], silu_ref.at[src], s1.at[k], r1.at[src], (src, y))

    for k in range(1, 16):
        piece(k).start()
    small_start, small_wait = swapped(small_in, small, 7)
    tokens_start, tokens_wait = swapped(tokens_in, tokens, 9)
    grad_start, grad_wait = swapped(grad_in, out_grad, 11)
    small_start()
    tokens_start()
    parts = gather_parts(
        [s_qkv, s_proj, s_fc1, s_fc2],
        [w_qkv, w_proj, w_fc1, w_fc2],
        [relay_qkv, relay_proj, relay_1, relay_2],
        chunks,
        recv,
        send,
        pos,
    )
    last_of = {g: parts[i].ready for i, (g, _, _) in enumerate(chunks)}
    events = gather_events(parts)
    pump = Pump(events)

    def until_ready(g):
        pump.run(events.index(last_of[g]) + 1 - pump.next)

    pump.run(2)
    silu_ref[d] = piece_ref[d]
    for k in range(1, 16):
        piece_in(k).wait_recv()
    some = jnp.concatenate(
        [silu_ref[2 * q + y].astype(F32)[0:1, :] for q in range(8)], axis=0
    ).astype(BF16)[:, :72]
    for j in range(6):
        cols = slice(j * width, (j + 1) * width)
        value = jnp.dot(some, w_mod[:, cols], preferred_element_type=F32)
        for q in range(8):
            part[q, :, cols] = value[q : q + 1, :]
    me = z * 2 + x

    def send_part(k):
        q = (me + k) % 8
        return remote(part.at[q], land.at[me], s2.at[k], r2.at[me], (q * 2 + c, y))

    def part_in(k):
        q = (me + k) % 8
        return remote(part.at[q], land.at[q], s2.at[k], r2.at[q], (q * 2 + c, y))

    for k in range(1, 8):
        send_part(k).start()
    land[me] = part[me]
    pump.run(4)
    for k in range(1, 8):
        part_in(k).wait_recv()
    total = land[0]
    for q in range(1, 8):
        total = total + land[q]
    mine[...] = total
    swap = remote(mine, other, sems.at[13], sems.at[14], sib)
    swap.start()
    pump.run(3)
    for k in range(1, 16):
        piece(k).wait_send()
    for k in range(1, 8):
        send_part(k).wait_send()
    swap.wait()
    mod[...] = mine[...] + other[...] + mod_bias[...]
    shift_a, scale_a, gate_a, shift_m, scale_m, gate_m = [
        mod[:, i * width : (i + 1) * width] for i in range(6)
    ]
    small_wait()
    tokens_wait()

    tall = half // 4

    def norm_rows(value, shift, scale_up):
        center = value - jnp.mean(value, axis=-1, keepdims=True)
        spread = jnp.mean(center * center, axis=-1, keepdims=True)
        normed = center * lax.rsqrt(spread + 1e-06) * (1.0 + scale_up) + shift
        return normed.astype(BF16)

    def first_norm(i, _):
        own = pl.ds(pl.multiple_of(i * tall, tall), tall)
        rows_a[own, :] = norm_rows(tokens[own, :].astype(F32), shift_a, scale_a)
        return 0

    lax.fori_loop(0, 4, first_norm, 0)
    share = remote(rows_a.at[:half], rows_a.at[half:], sems.at[5], sems.at[6], sib)
    share.start()
    until_ready(0)
    heads = qkv.shape[0] // 3
    cols = heads * qkv.shape[1]
    load = pltpu.make_async_copy(w_qkv, qkv_here, sems.at[0])
    load.start()
    grad_start()
    pump.run(2)
    load.wait()
    share.wait()
    store(rows_a, rows_a_out)
    store(tokens, tokens_out)
    row = lax.broadcasted_iota(jnp.int32, (8, 2 * half), 0)
    for j in range(3):
        weight = flat(qkv_here[:, :, j * cols : (j + 1) * cols])
        value = product(weight, rows_a[...], 0, 1)
        if j != 1:
            pick = jnp.where(row == j // 2, 1.0, 0.0).astype(BF16)
            value = value + product(small[:, :cols], pick, 0, 0)
        value = value.reshape((heads,) + qkv.shape[1:])
        qkv[pl.ds(j * heads, heads)] = value.astype(BF16)
        pump.run(2)
    store(qkv, qkv_out)
    steps, body = attention_step(qkv, out, lse, block, scale)
    pump.loop(steps, body, 16)
    store(out, attended_out)
    store(lse, lse_out)
    until_ready(1)

    load = pltpu.make_async_copy(w_proj, proj_here, sems.at[0])
    load.start()
    load.wait()
    tile = half // 2
    swap = remote(sent, got, sems.at[1], sems.at[2], sib)

    def project(i):
        cols = pl.ds(pl.multiple_of(i * tile, tile), tile)
        return product(flat(out[:, :, cols]), flat(proj_here[...]), 0, 1)

    def other_rows(i, _):
        sent[pl.ds(pl.multiple_of(i * tile, tile), tile), :] = project(i + 2).astype(BF16)
        return 0

    def own_rows(i, _):
        branch[pl.ds(pl.multiple_of(i * tile, tile), tile), :] = project(i) + proj_bias[...]
        return 0

    lax.fori_loop(0, 2, other_rows, 0)
    swap.start()
    lax.fori_loop(0, 2, own_rows, 0)
    pump.run(2)
    grad_wait()
    store(out_grad, grad_out)

    def gated(i, total):
        own = pl.ds(pl.multiple_of(i * tall, tall), tall)
        value = (out_grad[own, :].astype(F32) * gate_m).astype(BF16)
        grad_m[own, :] = value
        return total + jnp.sum(value.astype(F32), axis=0, keepdims=True)

    fc2_bias_grad[...] = lax.fori_loop(0, 4, gated, jnp.zeros((1, width), F32))
    share_m = remote(grad_m.at[:half], grad_m.at[half:], sems.at[15], sems.at[16], sib)
    share_m.start()
    swap.wait()
    share = remote(rows.at[:half], rows.at[half:], sems.at[3], sems.at[4], sib)

    def norm(i, _):
        own = pl.ds(pl.multiple_of(i * tall, tall), tall)
        total = branch[own, :] + got[own, :].astype(F32)
        branch[own, :] = total
        mid = tokens[own, :].astype(F32) + gate_a * total
        resid[own, :] = mid
        rows[own, :] = norm_rows(mid, shift_m, scale_m)
        return 0

    lax.fori_loop(0, 4, norm, 0)
    share.start()
    store(branch, branch_out)
    store(resid, resid_out)
    until_ready(2)

    load = pltpu.make_async_copy(w_fc1, weight_here, sems.at[0])
    load.start()
    load.wait()
    share.wait()
    store(rows, rows_out)
    n = 256
    hidden_steps = act.shape[1] // n

    def hidden(i):
        cols = pl.ds(pl.multiple_of(i * n, n), n)
        bias = small[:, cols].astype(F32)[2:3, :]
        value, rate = gelu_and_slope(
            product(rows[...], flat(weight_here[:, :, cols]), 1, 0) + bias
        )
        act[:, cols] = value.astype(BF16)
        slope[:, cols] = rate.astype(BF16)

    pump.loop(hidden_steps, hidden, hidden_steps)
    store(act, act_out)
    store(slope, slope_out)
    share_m.wait()
    store(grad_m, grad_m_out)

    def weight_grad(i):
        cols = pl.ds(pl.multiple_of(i * n, n), n)
        value = product(grad_m[...], act[:, cols], 0, 0)
        fc2_grad[:, :, cols] = value.reshape(fc2_grad.shape[:2] + (n,)).astype(BF16)

    pump.loop(hidden_steps, weight_grad, hidden_steps)
    store(fc2_grad, fc2_grad_out)
    pump.run()
    for p in parts:
        p.finish()
    for copy in stores:
        copy.wait()


def forward_stage(
    pieces, w_mod, mod_bias, proj_bias, small, tokens, out_grad, shards, size, chunks,
    collective_id, block=512,
):
    half, width = tokens.shape
    count = 2 * half
    owned, cols = shards[1].shape[1:]
    heads = cols // size
    hidden = shards[2].shape[2]
    n = w_mod.shape[1]
    vmem, anywhere = pl.BlockSpec(memory_space=pltpu.VMEM), pl.BlockSpec(memory_space=pl.ANY)
    shape, dma = jax.ShapeDtypeStruct, pltpu.SemaphoreType.DMA
    kept = [
        ((count, width), BF16),
        ((3 * heads, size, count), BF16),
        ((heads, size, count), BF16),
        ((heads, 1, count), F32),
        ((half, width), F32),
        ((half, width), F32),
        ((count, width), BF16),
        ((count, hidden), BF16),
        ((count, hidden), BF16),
        ((16, owned, hidden), BF16),
        ((count, width), BF16),
    ]
    swap = ((half, width), BF16)
    return pl.pallas_call(
        functools.partial(forward_kernel, chunks, block, size**-0.5),
        out_shape=[shape((1, n), F32), shape((16, 8, 128), BF16), shape((1, width), F32)]
        + [shape(*k) for k in kept + [swap, swap]]
        + gather_shapes(shards),
        in_specs=[vmem] * 5 + [anywhere] * 6,
        out_specs=[vmem] * 3 + [anywhere] * 21,
        scratch_shapes=[
            pltpu.VMEM((8, 1, n), F32),
            pltpu.VMEM((8, 1, n), F32),
            pltpu.VMEM((1, n), F32),
            pltpu.VMEM((1, n), F32),
            pltpu.VMEM(small.shape, BF16),
            pltpu.VMEM(*swap),
            pltpu.VMEM(*swap),
        ]
        + [pltpu.VMEM(*k) for k in kept]
        + [
            pltpu.VMEM((16, owned, 3 * cols), BF16),
            pltpu.VMEM((16, owned, cols), BF16),
            pltpu.VMEM((16, owned, hidden), BF16),
            pltpu.VMEM(*swap),
            pltpu.VMEM(*swap),
            dma((16,)),
            dma((16,)),
            dma((8,)),
            dma((8,)),
            dma((17,)),
            dma((13,)),
        ]
        + gather_sems(chunks),
        compiler_params=pltpu.CompilerParams(
            collective_id=collective_id, has_side_effects=True, vmem_limit_bytes=64500 * 1024
        ),
    )(pieces, w_mod, mod_bias, proj_bias, small, tokens, out_grad, *shards)[:20]


def attention_back_step(qkv, grad, out, lse, result, key_sum, value_sum, block, scale):
    heads, blocks = qkv.shape[0] // 3, qkv.shape[2] // block
    factor = scale * LOG2E

    def body(i):
        h, j = i // blocks, i % blocks
        cols = pl.ds(pl.multiple_of(j * block, block), block)
        queries, keys, values = qkv[h, :, cols], qkv[heads + h], qkv[2 * heads + h]
        grads = grad[h, :, cols]
        inner = jnp.sum(out[h, :, cols].astype(F32) * grads.astype(F32), axis=0, keepdims=True)
        probs = jnp.exp2(product(keys, queries, 0, 0) * factor - lse[h, :, cols])
        score_grad = (probs * (product(values, grads, 0, 0) - inner)).astype(BF16)
        value_part = product(grads, probs.astype(BF16), 1, 1)
        key_part = product(queries, score_grad, 1, 1)
        result[h, :, cols] = (product(keys, score_grad, 1, 0) * scale).astype(BF16)

        @pl.when(j == 0)
        def _():
            key_sum[...] = key_part
            value_sum[...] = value_part

        @pl.when(j > 0)
        def _():
            key_sum[...] += key_part
            value_sum[...] += value_part

        @pl.when(j == blocks - 1)
        def _():
            result[heads + h] = (key_sum[...] * scale).astype(BF16)
            result[2 * heads + h] = value_sum[...].astype(BF16)

    return heads * blocks, body


def loader(sems):
    count = iter(range(64))

    def load(src, dst):
        copy = pltpu.make_async_copy(src, dst, sems.at[next(count)])
        copy.start()
        return copy.wait

    return load


def hidden_back_kernel(
    chunks, bias, grad_m_in, act_in, slope_in, rows_in, fc2_grad_in, w_fc2, w_fc1,
    fc1_bias_grad, fc2_out, fc1_grad_out, branch_out, ngrad_out,
    grad_m, act, slope, rows, fc2_grad, fc1_grad, branch, ngrad,
    weight, pre_grad, sent1, got1, sent2, got2, *rest,
):
    n = len(chunks)
    lands, (sems, load_sems, recv, send) = rest[:n], rest[n:]
    pos = place()
    sib = neighbours(pos)[0]
    half, width = branch.shape
    hidden = act.shape[1]
    load = loader(load_sems)
    grad_ready = load(fc2_grad_in, fc2_grad)
    weight_ready = load(w_fc2, weight)
    m_ready = load(grad_m_in, grad_m)
    slope_ready = load(slope_in, slope)
    act_ready = load(act_in, act)
    rows_ready = load(rows_in, rows)
    greet(chip_peers(pos))
    parts = [
        Reduce(fc2_grad, lands[i], fc2_out, recv.at[i], send.at[i], pos, cols)
        for i, cols in enumerate(chunks)
    ]
    pump = Pump(reduce_events(parts))
    grad_ready()
    pump.run(2)
    weight_ready()
    m_ready()
    slope_ready()
    tile = 256

    def into_hidden(i):
        cols = pl.ds(pl.multiple_of(i * tile, tile), tile)
        value = product(grad_m[...], flat(weight[:, :, cols]), 1, 0)
        value = (value * slope[:, cols].astype(F32)).astype(BF16)
        pre_grad[:, cols] = value
        fc1_bias_grad[:, cols] = jnp.sum(value.astype(F32), axis=0, keepdims=True)

    pump.loop(hidden // tile, into_hidden, 9)

    def out_of_hidden(source, sent, own, extra):
        def body(i):
            turn = lax.rem(i + 2, 4)
            part = pl.ds(pl.multiple_of(turn * tile, tile), tile)
            value = product(source[part, :], flat(weight[...]), 1, 1)

            @pl.when(i < 2)
            def _():
                sent[pl.ds(pl.multiple_of(i * tile, tile), tile), :] = value.astype(BF16)

            @pl.when(i >= 2)
            def _():
                own[part, :] = value + extra

        return body

    swap1 = remote(sent1, got1, sems.at[1], sems.at[2], sib)
    swap2 = remote(sent2, got2, sems.at[3], sems.at[4], sib)
    act_ready()
    pump.loop(4, out_of_hidden(act, sent1, branch, bias[...]), 8)
    swap1.start()
    weight_ready = load(w_fc1, weight)
    pump.run(2)
    weight_ready()
    pump.loop(4, out_of_hidden(pre_grad, sent2, ngrad, 0.0), 8)
    swap2.start()

    def join(own, got):
        def body(i, _):
            part = pl.ds(pl.multiple_of(i * tile, tile), tile)
            own[part, :] += got[part, :].astype(F32)
            return 0

        lax.fori_loop(0, half // tile, body, 0)

    swap1.wait()
    join(branch, got1)
    stored = [load(branch, branch_out)]
    rows_ready()

    def weight_grad(i):
        cols = pl.ds(pl.multiple_of(i * tile, tile), tile)
        value = product(rows[...], pre_grad[:, cols], 0, 0)
        fc1_grad[:, :, cols] = value.reshape(fc1_grad.shape[:2] + (tile,)).astype(BF16)

    pump.loop(hidden // tile, weight_grad, 9)
    stored.append(load(fc1_grad, fc1_grad_out))
    swap2.wait()
    join(ngrad, got2)
    stored.append(load(ngrad, ngrad_out))
    pump.run()
    for p in parts:
        p.finish()
    for wait in stored:
        wait()


def hidden_back(bias, grad_m, act, slope, rows, fc2_grad, w_fc2, w_fc1, chunks, collective_id):
    vmem, anywhere = pl.BlockSpec(memory_space=pltpu.VMEM), pl.BlockSpec(memory_space=pl.ANY)
    shape = jax.ShapeDtypeStruct
    count, width = grad_m.shape
    half, hidden = count // 2, act.shape[1]
    swap = pltpu.VMEM((half, width), BF16)
    sums = pltpu.VMEM((half, width), F32)
    land = reduce_scratch([(0, cols) for cols in chunks])
    return pl.pallas_call(
        functools.partial(hidden_back_kernel, chunks),
        out_shape=[
            shape((1, hidden), F32),
            shape(fc2_grad.shape[1:], F32),
            shape(fc2_grad.shape, BF16),
            shape((half, width), F32),
            shape((half, width), F32),
        ],
        in_specs=[vmem] + [anywhere] * 7,
        out_specs=[vmem] * 2 + [anywhere] * 3,
        scratch_shapes=[
            pltpu.VMEM((count, width), BF16),
            pltpu.VMEM((count, hidden), BF16),
            pltpu.VMEM((count, hidden), BF16),
            pltpu.VMEM((count, width), BF16),
            pltpu.VMEM(fc2_grad.shape, BF16),
            pltpu.VMEM(fc2_grad.shape, BF16),
            sums,
            sums,
            pltpu.VMEM(fc2_grad.shape, BF16),
            pltpu.VMEM((count, hidden), BF16),
            swap,
            swap,
            swap,
            swap,
        ]
        + land[: len(chunks)]
        + [pltpu.SemaphoreType.DMA((5,)), pltpu.SemaphoreType.DMA((12,))]
        + land[len(chunks) :],
        compiler_params=pltpu.CompilerParams(
            collective_id=collective_id, has_side_effects=True, vmem_limit_bytes=64500 * 1024
        ),
    )(bias, grad_m, act, slope, rows, fc2_grad, w_fc2, w_fc1)


def norm_back_rows(value, g, scale_up):
    center = value - jnp.mean(value, axis=-1, keepdims=True)
    rate = lax.rsqrt(jnp.mean(center * center, axis=-1, keepdims=True) + 1e-06)
    normed = center * rate
    e = g * scale_up
    inner = jnp.mean(e * normed, axis=-1, keepdims=True)
    return rate * (e - jnp.mean(e, axis=-1, keepdims=True) - normed * inner), normed


def row_sum(value):
    return jnp.sum(value, axis=0, keepdims=True)


def attention_back_kernel(
    chunks, block, scale, vecs, resid_in, ngrad_in, out_grad_in, branch_in, w_proj_in, qkv_in,
    out_in, lse_in, fc1_grad_in,
    sums, fc1_out, proj_out, resid_grad_out, result_out,
    resid, ngrad, out_grad, branch, w_proj, qkv, out, lse, fc1_grad, resid_grad, result,
    rows, grad, proj_grad, key_sum, value_sum, *rest,
):
    n = len(chunks)
    lands, (sems, load_sems, recv, send) = rest[:n], rest[n:]
    pos = place()
    sib = neighbours(pos)[0]
    half, width = resid.shape
    load = loader(load_sems)
    first = [load(fc1_grad_in, fc1_grad)]
    norm_ready = [
        load(*pair)
        for pair in ((ngrad_in, ngrad), (resid_in, resid), (out_grad_in, out_grad), (branch_in, branch))
    ]
    late = [load(w_proj_in, w_proj), load(out_in, out), load(qkv_in, qkv), load(lse_in, lse)]
    greet(chip_peers(pos))
    parts = [
        Reduce(
            (fc1_grad, proj_grad)[g],
            lands[i],
            (fc1_out, proj_out)[g],
            recv.at[i],
            send.at[i],
            pos,
            cols,
        )
        for i, (g, cols) in enumerate(chunks)
    ]
    pump = Pump(reduce_events(parts))
    for wait in first:
        wait()
    pump.run(2)
    for wait in norm_ready:
        wait()
    tall = half // 4
    scale_up = 1.0 + vecs[1:2, :]

    def norm(i, total):
        part = pl.ds(pl.multiple_of(i * tall, tall), tall)
        g = ngrad[part, :]
        back, normed = norm_back_rows(resid[part, :], g, scale_up)
        value = out_grad[part, :].astype(F32) + back
        resid_grad[part, :] = value
        low = (value * vecs[0:1, :]).astype(BF16)
        rows[part, :] = low
        terms = (g, g * normed, value * branch[part, :], low.astype(F32))
        return tuple(t + row_sum(v) for t, v in zip(total, terms))

    total = lax.fori_loop(0, 4, norm, (jnp.zeros((1, width), F32),) * 4)
    share = remote(rows.at[:half], rows.at[half:], sems.at[0], sems.at[1], sib)
    share.start()
    stored = [load(resid_grad, resid_grad_out)]
    for i in range(4):
        sums[i : i + 1, :] = total[i]
    pump.run(1)
    for wait in late:
        wait()
    share.wait()
    tile = 256

    def attended(i):
        cols = pl.ds(pl.multiple_of(i * tile, tile), tile)
        value = product(flat(w_proj[...]), rows[cols, :], 0, 1)
        grad[:, :, cols] = value.reshape(grad.shape[:2] + (tile,)).astype(BF16)

    pump.loop(2 * half // tile, attended, 4)
    value = product(rows[...], flat(out[...]), 0, 1)
    proj_grad[...] = value.reshape(proj_grad.shape).astype(BF16)
    steps, body = attention_back_step(
        qkv, grad, out, lse, result, key_sum, value_sum, block, scale
    )
    pump.loop(steps, body, 28)
    stored.append(load(result, result_out))
    pump.run()
    for p in parts:
        p.finish()
    for wait in stored:
        wait()


def attention_back(
    vecs, resid, ngrad, out_grad, branch, w_proj, qkv, out, lse, fc1_grad, chunks, collective_id,
    block=512,
):
    heads, size, count = out.shape
    half, width = resid.shape
    owned, cols = w_proj.shape[1:]
    vmem, anywhere = pl.BlockSpec(memory_space=pltpu.VMEM), pl.BlockSpec(memory_space=pl.ANY)
    shape = jax.ShapeDtypeStruct
    land = reduce_scratch(chunks)
    arrays = (resid, ngrad, out_grad, branch, w_proj, qkv, out, lse, fc1_grad)
    made = [((half, width), F32), (qkv.shape, BF16)]
    return pl.pallas_call(
        functools.partial(attention_back_kernel, chunks, block, size**-0.5),
        out_shape=[
            shape((4, width), F32),
            shape(fc1_grad.shape[1:], F32),
            shape((owned, cols), F32),
        ]
        + [shape(*m) for m in made],
        in_specs=[vmem] + [anywhere] * 9,
        out_specs=[vmem] * 3 + [anywhere] * 2,
        scratch_shapes=[pltpu.VMEM(a.shape, a.dtype) for a in arrays]
        + [pltpu.VMEM(*m) for m in made]
        + [
            pltpu.VMEM((count, width), BF16),
            pltpu.VMEM(out.shape, BF16),
            pltpu.VMEM((16, owned, cols), BF16),
            pltpu.VMEM((size, count), F32),
            pltpu.VMEM((size, count), F32),
        ]
        + land[: len(chunks)]
        + [pltpu.SemaphoreType.DMA((2,)), pltpu.SemaphoreType.DMA((12,))]
        + land[len(chunks) :],
        compiler_params=pltpu.CompilerParams(
            collective_id=collective_id, has_side_effects=True, vmem_limit_bytes=64500 * 1024
        ),
    )(vecs, *arrays)


def index_of(z, x, c, y):
    return ((z * 2 + x) * 2 + c) * 2 + y


def core_pairs():
    return [
        (index_of(z, x, c, y), index_of(z, x, 1 - c, y))
        for z in range(4)
        for x in range(2)
        for c in range(2)
        for y in range(2)
    ]


def latent_pairs():
    return [
        (index_of(z, x, c, y), index_of(z, x, y, c))
        for z in range(4)
        for x in range(2)
        for c in range(2)
        for y in range(2)
        if c != y
    ]


def trade(value):
    moved = lax.ppermute(value, AXES, latent_pairs())
    home = lax.axis_index("dp") % 2 == lax.axis_index("tensor")
    return jnp.where(home, value, moved)


def both_halves(value):
    return jnp.concatenate([value, lax.ppermute(value, AXES, core_pairs())], axis=0)


def own_sum(partial):
    n = partial.shape[0] // 2
    moved = lax.ppermute(partial[n:].astype(BF16), AXES, core_pairs())
    return partial[:n] + moved.astype(F32)


def columns(n, step):
    return [(i, min(step, n - i)) for i in range(0, n, step)]


def on_device_chip(
    tokens,
    cond,
    mod_weight,
    mod_bias,
    query_key_value_weight,
    qkv_bias,
    attention_out_weight,
    attention_out_bias,
    first_hidden_weight,
    first_hidden_bias,
    second_hidden_weight,
    second_hidden_bias,
    out_grad,
):
    half, _, width = tokens.shape
    owned, _, cols = query_key_value_weight.shape
    head_size = width // HEADS
    heads_here = cols // head_size
    hidden = first_hidden_weight.shape[1]

    silu_cond, silu_back = jax.vjp(jax.nn.silu, cond.astype(F32))
    pieces = jnp.pad(
        silu_cond.astype(BF16).reshape(16, 1, owned), ((0, 0), (0, 7), (0, 128 - owned))
    )
    s_qkv = query_key_value_weight.reshape(1, owned, 3 * cols)
    small = jnp.stack(
        [
            jnp.pad(qkv_bias[0], (0, hidden - cols)),
            jnp.pad(qkv_bias[1], (0, hidden - cols)),
            first_hidden_bias,
        ]
    )
    small = jnp.pad(small, ((0, 5), (0, 0)))
    shards = [
        s_qkv,
        attention_out_weight.T.reshape(1, owned, cols),
        first_hidden_weight.reshape(1, owned, hidden),
        second_hidden_weight.T.reshape(1, owned, hidden),
    ]
    chunks = [(0, p, True) for p in columns(3 * cols, 896)] + [(1, None, False)]
    chunks += [(g, p, False) for g in (2, 3) for p in columns(hidden, 1152)]
    (
        modulation,
        silu_owned,
        fc2_bias_part,
        rows_a,
        qkv,
        attended,
        log_totals,
        branch_a,
        resid_mid,
        rows_m,
        act_low,
        slope,
        fc2_grad,
        grad_m,
        tokens_here,
        out_grad_here,
        w_qkv,
        w_proj,
        w_fc1,
        w_fc2,
    ) = forward_stage(
        pieces,
        mod_weight,
        mod_bias.astype(F32)[None],
        attention_out_bias.astype(F32)[None],
        small,
        tokens.reshape(half, width),
        out_grad.reshape(half, width),
        shards,
        head_size,
        chunks,
        2,
    )
    shift_a, scale_a, gate_a, shift_m, scale_m, gate_m = [
        modulation[:, i * width : (i + 1) * width] for i in range(6)
    ]
    grad_out = out_grad_here.astype(F32)

    fc1_bias_part, fc2_out, fc1_grad, branch_m, normed_m_grad = hidden_back(
        second_hidden_bias.astype(F32)[None],
        grad_m,
        act_low,
        slope,
        rows_m,
        fc2_grad,
        w_fc2,
        w_fc1,
        columns(hidden, 768),
        4,
    )
    output = (resid_mid + gate_m * branch_m).astype(BF16)
    gate_m_grad = jnp.sum(grad_out * branch_m, axis=0)
    sums, fc1_out, proj_out, resid_grad, qkv_grad = attention_back(
        jnp.concatenate([gate_a, scale_m]),
        resid_mid,
        normed_m_grad,
        out_grad_here,
        branch_a,
        w_proj,
        qkv,
        attended,
        log_totals,
        fc1_grad,
        [(0, p) for p in columns(hidden, 768)] + [(1, (0, cols))],
        5,
    )
    shift_m_grad, scale_m_grad, gate_a_grad, proj_bias_part = (sums[i] for i in range(4))
    qkv_bias_part = jnp.sum(qkv_grad, axis=2, dtype=F32)
    half_part = jnp.concatenate(
        [
            fc1_bias_part[0],
            qkv_bias_part[:heads_here].reshape(-1),
            qkv_bias_part[2 * heads_here :].reshape(-1),
        ]
    )[None]
    mod_part = jnp.concatenate(
        [
            gate_a_grad.reshape(1, -1),
            shift_m_grad.reshape(1, -1),
            scale_m_grad.reshape(1, -1),
            gate_m_grad.reshape(1, -1),
        ],
        axis=1,
    )
    wide_part = jnp.concatenate([fc2_bias_part[0], proj_bias_part])[None]
    tokens_grad, qkv_out, mod_weight_grad, mod_bias_grad, silu_grad, wide, narrow = last_stage(
        rows_a,
        qkv_grad,
        w_qkv.reshape(width, 3 * cols),
        tokens_here,
        resid_grad,
        scale_a,
        mod_part,
        wide_part,
        half_part,
        silu_owned,
        mod_weight,
        6,
    )
    cond_grad = silu_back(silu_grad[:, 0, :owned].reshape(1, width))[0]
    return (
        trade(output).reshape(half, 1, width),
        trade(tokens_grad).reshape(half, 1, width),
        cond_grad,
        mod_weight_grad,
        mod_bias_grad[0],
        jnp.moveaxis(qkv_out, 0, 1),
        narrow[0, hidden:].reshape(2, cols),
        proj_out.T,
        wide[0, width:],
        fc1_out,
        narrow[0, :hidden],
        fc2_out.T,
        wide[0, :width],
    )


def solution(mesh):
    shape = dict(mesh.shape)
    body = on_device_chip if shape == {"dp": 16, "tensor": 2} else on_device_general
    return jax.shard_map(
        body,
        mesh=mesh,
        in_specs=(
            P("tensor", "dp", None),
            P("dp", None),
            P("dp", None),
            P(),
            P("dp", None, "tensor"),
            P(None, "tensor"),
            P("tensor", "dp"),
            P(),
            P("dp", "tensor"),
            P("tensor"),
            P("tensor", "dp"),
            P(),
            P("tensor", "dp", None),
        ),
        out_specs=(
            P("tensor", "dp", None),
            P("tensor", "dp", None),
            P("dp", None),
            P("dp", None),
            P(),
            P("dp", None, "tensor"),
            P(None, "tensor"),
            P("tensor", "dp"),
            P(),
            P("dp", "tensor"),
            P("tensor"),
            P("tensor", "dp"),
            P(),
        ),
        check_vma=False,
    )
```

```python
import functools
import math

import jax
import jax.numpy as jnp
from jax import lax
from jax.experimental import pallas as pl
from jax.experimental.pallas import tpu as pltpu
from jax.sharding import PartitionSpec as P

HEADS = 16
MESH = pl.DeviceIdType.MESH
AXES = ("dp", "tensor")
F32 = jnp.float32
BF16 = jnp.bfloat16


def modulate(hidden, shifts, scales):
    center = hidden - jnp.mean(hidden, axis=-1, keepdims=True)
    spread = jnp.mean(center * center, axis=-1, keepdims=True)
    return center * lax.rsqrt(spread + 1e-06) * (1.0 + scales) + shifts


def gelu_tanh(values):
    return jax.nn.gelu(values, approximate=True)


def attend_forward(packed):
    queries = packed[:, 0]
    keys_all = packed[:, 1]
    values_all = packed[:, 2]
    seq_len = packed.shape[0]
    scaling = packed.shape[3] ** (-0.5)
    block_rows = min(512, seq_len)
    results = []
    log_parts = []
    for offset in range(0, seq_len, block_rows):
        query_block = queries[offset : offset + block_rows]
        scores = (
            jnp.einsum("qhe,khe->hqk", query_block, keys_all, preferred_element_type=jnp.float32)
            * scaling
        )
        highest = jnp.max(scores, axis=-1, keepdims=True)
        weights = jnp.exp(scores - highest)
        row_total = jnp.sum(weights, axis=-1, keepdims=True)
        prob_low = (weights / row_total).astype(jnp.bfloat16)
        mixture = jnp.einsum(
            "hqk,khe->qhe", prob_low, values_all, preferred_element_type=jnp.float32
        )
        results.append(mixture.reshape(block_rows, -1))
        log_parts.append((highest + jnp.log(row_total))[..., 0])
    return (jnp.concatenate(results, 0).astype(jnp.bfloat16), jnp.concatenate(log_parts, 1))


def attend_backward(inputs):
    packed, grad_out, log_totals = inputs
    queries = packed[:, 0]
    keys_all = packed[:, 1]
    values_all = packed[:, 2]
    seq_len = packed.shape[0]
    scaling = packed.shape[3] ** (-0.5)
    block_rows = min(512, seq_len)
    query_grads = []
    key_grad = jnp.zeros(keys_all.shape, jnp.float32)
    value_grad = jnp.zeros(values_all.shape, jnp.float32)
    for offset in range(0, seq_len, block_rows):
        query_block = queries[offset : offset + block_rows]
        grad_block = grad_out[offset : offset + block_rows]
        scores = (
            jnp.einsum("qhe,khe->hqk", query_block, keys_all, preferred_element_type=jnp.float32)
            * scaling
        )
        probs = jnp.exp(scores - log_totals[:, offset : offset + block_rows, None])
        prob_low = probs.astype(jnp.bfloat16)
        prob_grad = jnp.einsum(
            "qhe,khe->hqk", grad_block, values_all, preferred_element_type=jnp.float32
        )
        inner = jnp.sum(probs * prob_grad, axis=-1, keepdims=True)
        score_grad = (probs * (prob_grad - inner)).astype(jnp.bfloat16)
        query_grads.append(
            jnp.einsum("hqk,khe->qhe", score_grad, keys_all, preferred_element_type=jnp.float32)
            * scaling
        )
        key_grad = (
            key_grad
            + jnp.einsum(
                "hqk,qhe->khe", score_grad, query_block, preferred_element_type=jnp.float32
            )
            * scaling
        )
        value_grad = value_grad + jnp.einsum(
            "hqk,qhe->khe", prob_low, grad_block, preferred_element_type=jnp.float32
        )
    return jnp.stack([jnp.concatenate(query_grads, 0), key_grad, value_grad], 1).astype(
        jnp.bfloat16
    )


def on_device_general(
    tokens,
    cond,
    mod_weight,
    mod_bias,
    query_key_value_weight,
    qkv_bias,
    attention_out_weight,
    attention_out_bias,
    first_hidden_weight,
    first_hidden_bias,
    second_hidden_weight,
    second_hidden_bias,
    out_grad,
):
    w_mod, w_qkv, w_proj, w_fc1, w_fc2 = (
        lax.all_gather(mod_weight, "dp", axis=0, tiled=True),
        lax.all_gather(query_key_value_weight, "dp", axis=0, tiled=True),
        lax.all_gather(attention_out_weight, "dp", axis=1, tiled=True),
        lax.all_gather(first_hidden_weight, "dp", axis=0, tiled=True),
        lax.all_gather(second_hidden_weight, "dp", axis=1, tiled=True),
    )
    seq_local, latents, width = tokens.shape
    columns = query_key_value_weight.shape[2]
    head_size = width // HEADS
    heads_here = columns // head_size
    local_rows = seq_local * latents
    cond_wide = cond.astype(jnp.float32)
    silu_cond, silu_back = jax.vjp(jax.nn.silu, cond_wide)
    silu_low = silu_cond.astype(jnp.bfloat16)
    modulation = jnp.dot(silu_low, w_mod, preferred_element_type=jnp.float32) + mod_bias.astype(
        jnp.float32
    )
    pieces = modulation.reshape(latents, 6, width)
    hidden_in = tokens.astype(jnp.float32)
    attention_normalized, norm_a_back = jax.vjp(modulate, hidden_in, pieces[:, 0], pieces[:, 1])
    gathered_a = lax.all_gather(
        attention_normalized.astype(jnp.bfloat16), "tensor", axis=0, tiled=True
    )
    seq_len = gathered_a.shape[0]
    total_rows = seq_len * latents
    rows_a = gathered_a.reshape(total_rows, width)
    qkv_flat = w_qkv.reshape(width, 3 * columns)
    zero_row = jnp.zeros((columns,), jnp.float32)
    query_key_value_shift = jnp.stack(
        [qkv_bias[0].astype(jnp.float32), zero_row, qkv_bias[1].astype(jnp.float32)]
    )
    projected_output = (
        jnp.dot(rows_a, qkv_flat, preferred_element_type=jnp.float32).reshape(
            seq_len, latents, 3, columns
        )
        + query_key_value_shift
    )
    packed = jnp.moveaxis(projected_output.astype(jnp.bfloat16), 1, 0).reshape(
        latents, seq_len, 3, heads_here, head_size
    )
    attention_result, log_totals = lax.map(attend_forward, packed)
    attended_rows = jnp.moveaxis(attention_result, 0, 1).reshape(total_rows, columns)
    summed_a = lax.psum_scatter(
        jnp.dot(attended_rows, w_proj, preferred_element_type=jnp.float32).astype(jnp.bfloat16),
        "tensor",
        scatter_dimension=0,
        tiled=True,
    ).astype(jnp.float32)
    attention_branch = summed_a.reshape(seq_local, latents, width) + attention_out_bias.astype(
        jnp.float32
    )
    resid_mid = hidden_in + pieces[:, 2] * attention_branch
    feedforward_normalized, norm_m_back = jax.vjp(modulate, resid_mid, pieces[:, 3], pieces[:, 4])
    gathered_m = lax.all_gather(
        feedforward_normalized.astype(jnp.bfloat16), "tensor", axis=0, tiled=True
    )
    rows_m = gathered_m.reshape(total_rows, width)
    before_activation = jnp.dot(
        rows_m, w_fc1, preferred_element_type=jnp.float32
    ) + first_hidden_bias.astype(jnp.float32)
    gelu_activated, gelu_back = jax.vjp(gelu_tanh, before_activation)
    act_low = gelu_activated.astype(jnp.bfloat16)
    summed_m = lax.psum_scatter(
        jnp.dot(act_low, w_fc2, preferred_element_type=jnp.float32).astype(jnp.bfloat16),
        "tensor",
        scatter_dimension=0,
        tiled=True,
    ).astype(jnp.float32)
    feedforward_branch = summed_m.reshape(seq_local, latents, width) + second_hidden_bias.astype(
        jnp.float32
    )
    output = (resid_mid + pieces[:, 5] * feedforward_branch).astype(jnp.bfloat16)
    grad_out = out_grad.astype(jnp.float32)
    gate_m_grad = jnp.sum(grad_out * feedforward_branch, axis=0)
    grad_m_low = (grad_out * pieces[:, 5]).astype(jnp.bfloat16)
    grad_m_rows = lax.all_gather(grad_m_low, "tensor", axis=0, tiled=True).reshape(
        total_rows, width
    )
    fc2_bias_grad = jnp.sum(grad_m_rows, axis=0, dtype=jnp.float32)
    fc2_weight_grad = jnp.einsum(
        "rf,rd->fd", act_low, grad_m_rows, preferred_element_type=jnp.float32
    )
    act_grad = jnp.einsum("rd,fd->rf", grad_m_rows, w_fc2, preferred_element_type=jnp.float32)
    pre_grad = gelu_back(act_grad)[0].astype(jnp.bfloat16)
    fc1_bias_grad = jnp.sum(pre_grad, axis=0, dtype=jnp.float32)
    fc1_weight_grad = jnp.einsum("rd,rf->df", rows_m, pre_grad, preferred_element_type=jnp.float32)
    normed_m_grad = (
        lax.psum_scatter(
            jnp.einsum("rf,df->rd", pre_grad, w_fc1, preferred_element_type=jnp.float32).astype(
                jnp.bfloat16
            ),
            "tensor",
            scatter_dimension=0,
            tiled=True,
        )
        .astype(jnp.float32)
        .reshape(seq_local, latents, width)
    )
    resid_part, shift_m_grad, scale_m_grad = norm_m_back(normed_m_grad)
    resid_grad = grad_out + resid_part
    gate_a_grad = jnp.sum(resid_grad * attention_branch, axis=0)
    grad_a_low = (resid_grad * pieces[:, 2]).astype(jnp.bfloat16)
    grad_a_flat = grad_a_low.reshape(local_rows, width)
    proj_bias_part = jnp.sum(grad_a_flat, axis=0, dtype=jnp.float32)
    grad_a_rows = lax.all_gather(grad_a_low, "tensor", axis=0, tiled=True).reshape(
        total_rows, width
    )
    proj_weight_grad = jnp.einsum(
        "rc,rd->cd", attended_rows, grad_a_rows, preferred_element_type=jnp.float32
    )
    attended_grad = jnp.einsum(
        "rd,cd->rc", grad_a_rows, w_proj, preferred_element_type=jnp.float32
    ).astype(jnp.bfloat16)
    grad_packed = jnp.moveaxis(attended_grad.reshape(seq_len, latents, heads_here, head_size), 1, 0)
    qkv_grad_packed = lax.map(attend_backward, (packed, grad_packed, log_totals))
    qkv_grad_rows = jnp.moveaxis(qkv_grad_packed, 0, 1).reshape(total_rows, 3 * columns)
    bias_sums = jnp.sum(qkv_grad_rows.reshape(total_rows, 3, columns), axis=0, dtype=jnp.float32)
    qkv_bias_grad = jnp.stack([bias_sums[0], bias_sums[2]])
    qkv_weight_grad = jnp.einsum(
        "rd,rc->dc", rows_a, qkv_grad_rows, preferred_element_type=jnp.float32
    ).reshape(width, 3, columns)
    normed_a_grad = (
        lax.psum_scatter(
            jnp.einsum(
                "rc,dc->rd", qkv_grad_rows, qkv_flat, preferred_element_type=jnp.float32
            ).astype(jnp.bfloat16),
            "tensor",
            scatter_dimension=0,
            tiled=True,
        )
        .astype(jnp.float32)
        .reshape(seq_local, latents, width)
    )
    input_part, shift_a_grad, scale_a_grad = norm_a_back(normed_a_grad)
    tokens_grad = (resid_grad + input_part).astype(jnp.bfloat16)
    partial_mod = jnp.stack(
        [shift_a_grad, scale_a_grad, gate_a_grad, shift_m_grad, scale_m_grad, gate_m_grad], 1
    ).reshape(latents, 6 * width)
    mod_summed, proj_bias_grad = (
        lax.psum(partial_mod.astype(jnp.bfloat16), "tensor").astype(jnp.float32),
        lax.psum(proj_bias_part.astype(jnp.bfloat16), "tensor").astype(jnp.float32),
    )
    mod_grad_low = mod_summed.astype(jnp.bfloat16)
    silu_grad = jnp.einsum("le,de->ld", mod_grad_low, w_mod, preferred_element_type=jnp.float32)
    cond_grad = silu_back(silu_grad)[0]
    silu_every, mod_every = (
        lax.all_gather(silu_low, "dp", axis=0, tiled=True),
        lax.all_gather(mod_grad_low, "dp", axis=0, tiled=True),
    )
    owned_rows = mod_weight.shape[0]
    silu_owned = lax.dynamic_slice_in_dim(
        silu_every, lax.axis_index("dp") * owned_rows, owned_rows, 1
    )
    mod_weight_grad = jnp.einsum(
        "ld,le->de", silu_owned, mod_every, preferred_element_type=jnp.float32
    )
    mod_bias_grad = jnp.sum(mod_every, axis=0, dtype=jnp.float32)
    qkv_weight_grad, proj_weight_grad, fc1_weight_grad, fc2_weight_grad = (
        lax.psum_scatter(
            qkv_weight_grad.astype(jnp.bfloat16), "dp", scatter_dimension=0, tiled=True
        ).astype(jnp.float32),
        lax.psum_scatter(
            proj_weight_grad.astype(jnp.bfloat16), "dp", scatter_dimension=1, tiled=True
        ).astype(jnp.float32),
        lax.psum_scatter(
            fc1_weight_grad.astype(jnp.bfloat16), "dp", scatter_dimension=0, tiled=True
        ).astype(jnp.float32),
        lax.psum_scatter(
            fc2_weight_grad.astype(jnp.bfloat16), "dp", scatter_dimension=1, tiled=True
        ).astype(jnp.float32),
    )
    qkv_bias_grad, proj_bias_grad, fc1_bias_grad, fc2_bias_grad = lax.psum(
        (qkv_bias_grad, proj_bias_grad, fc1_bias_grad, fc2_bias_grad), "dp"
    )
    return (
        output,
        tokens_grad,
        cond_grad,
        mod_weight_grad,
        mod_bias_grad,
        qkv_weight_grad,
        qkv_bias_grad,
        proj_weight_grad,
        proj_bias_grad,
        fc1_weight_grad,
        fc1_bias_grad,
        fc2_weight_grad,
        fc2_bias_grad,
    )


def place():
    d = lax.axis_index("dp")
    y = lax.axis_index("tensor")
    return d, d // 4, (d // 2) % 2, d % 2, y


def neighbours(pos):
    d, z, x, c, y = pos
    sib = (z * 4 + x * 2 + (1 - c), y)
    xn = (z * 4 + (1 - x) * 2 + c, y)
    yn = (d, 1 - y)
    return sib, xn, yn


def z_peer(pos, k):
    d, z, x, c, y = pos
    return (((z + k) % 4) * 4 + x * 2 + c, y)


def z_order(z, k):
    return (z, z + 1 - 2 * (z % 2), 2 - z // 2, 3 - 3 * (z // 2))[k]


def greet(peers):
    sem = pltpu.get_barrier_semaphore()
    for peer in peers:
        pl.semaphore_signal(sem, inc=1, device_id=peer, device_id_type=MESH)
    pl.semaphore_wait(sem, len(peers))


def chip_peers(pos):
    d, z, x, c, y = pos
    across = [(z * 4 + x * 2 + 1 - c, 1 - y)]
    return list(neighbours(pos)) + across + [z_peer(pos, k) for k in (1, 2, 3)]


def remote(src, dst, send, recv, peer):
    return pltpu.make_async_remote_copy(
        src_ref=src, dst_ref=dst, send_sem=send, recv_sem=recv, device_id=peer, device_id_type=MESH
    )


Z_SENDS = (1, 2, 3)
GATHER_RECV = 24
GATHER_SEND = 32


class Gather:
    def __init__(self, shard, full, relay, cols, wide, recv, send, pos):
        self.wide = wide
        self.shard, self.full, self.relay, self.cols = shard, full, relay, cols
        self.recv, self.send, self.pos = recv, send, pos
        d, z, x, c, y = pos
        self.sib, self.xn, _ = neighbours(pos)
        self.far = (z * 4 + x * 2 + y, 1 - y)
        self.home, self.away = c == y, c != y

    def part(self, ref, b):
        if self.cols is None:
            return ref.at[pl.ds(b, 1)]
        return ref.at[pl.ds(b, 1), :, pl.ds(*self.cols)]

    def move(self, src, dst, s, r, peer):
        return remote(src, dst, self.send.at[s], self.recv.at[r], peer)

    def came(self, r):
        block = self.part(self.full, 0)
        self.move(block, block, 0, r, self.sib).wait_recv()

    def stay(self):
        return pltpu.make_async_copy(
            self.part(self.shard, 0), self.part(self.full, self.pos[0]), self.send.at[31]
        )

    def start(self):
        d, z, x, c, y = self.pos
        q = z * 2 + x
        own = self.part(self.shard, 0)

        @pl.when(self.home)
        def _():
            for k in Z_SENDS:
                peer = (z_order(z, k) * 4 + x * 2 + c, y)
                self.move(own, self.part(self.full, d), k, q, peer).start()
            self.move(own, self.part(self.full, d), 4, q, self.xn).start()
            self.move(own, self.part(self.full, d), 8, 8 + q, self.far).start()
            self.stay().start()

        @pl.when(self.away)
        def _():
            for k in Z_SENDS:
                peer = (z_order(z, k) * 4 + x * 2 + c, y)
                self.move(own, self.part(self.relay, q), k, q, peer).start()
            self.move(own, self.part(self.full, d), 8, 16 + q, self.far).start()
            self.move(own, self.part(self.relay, q), 4, q, self.xn).start()
            self.move(own, self.part(self.full, d), 16, 8 + q, self.sib).start()

    def from_z(self, k):
        d, z, x, c, y = self.pos
        q = z_order(z, k) * 2 + x
        dst = self.part(self.full, 2 * q + c)

        @pl.when(self.home)
        def _():
            self.came(q)
            self.move(dst, dst, 4 + k, q, self.xn).start()
            self.move(dst, dst, 8 + k, 8 + q, self.far).start()

        @pl.when(self.away)
        def _():
            self.came(q)
            src = self.part(self.relay, q)
            self.move(src, dst, 8 + k, 16 + q, self.far).start()
            self.move(src, src, 4 + k, q, self.xn).start()
            self.move(src, dst, 16 + k, 8 + q, self.sib).start()

    def from_x(self, k):
        d, z, x, c, y = self.pos
        q = z_order(z, k) * 2 + 1 - x
        dst = self.part(self.full, 2 * q + c)

        @pl.when(self.home)
        def _():
            self.came(q)
            if self.wide != 1:
                self.move(dst, dst, 12 + k, 8 + q, self.far).start()

        @pl.when(self.away)
        def _():
            self.came(q)
            if self.wide == 2:
                self.move(self.part(self.relay, q), dst, 12 + k, 16 + q, self.far).start()
            self.move(self.part(self.relay, q), dst, 20 + k, 8 + q, self.sib).start()

    def from_y(self, k):
        d, z, x, c, y = self.pos
        q = z_order(z, k) * 2 + x

        @pl.when(self.away)
        def _():
            block = self.part(self.full, 2 * q + 1 - c)
            if self.wide != 2:
                self.came(16 + q)
                self.move(block, block, 12 + k, 16 + q, self.xn).start()
            if self.wide == 1:
                block = self.part(self.full, 2 * q + c)
                self.came(8 + q)
                self.move(block, block, 24 + k, 8 + q, self.xn).start()

    def ready(self):
        d, z, x, c, y = self.pos

        @pl.when(self.home)
        def _():
            for q in range(8):
                self.came(8 + q)
            self.stay().wait()

        @pl.when(self.away)
        def _():
            for k in range(4):
                q = ((z + k) % 4) * 2
                self.came(16 + q + 1 - x)
                self.came(8 + q + 1 - x)
                if self.wide != 1:
                    self.came(8 + q + x)
                if self.wide == 2:
                    self.came(16 + q + x)

    def finish(self):
        block = self.part(self.full, 0)
        for s in range(1, 12):
            self.move(block, block, s, 0, self.sib).wait_send()

        @pl.when(self.home)
        def _():
            if self.wide != 1:
                for s in range(12, 16):
                    self.move(block, block, s, 0, self.sib).wait_send()

        @pl.when(self.away)
        def _():
            for s in range(12, 28 if self.wide == 1 else 24):
                self.move(block, block, s, 0, self.sib).wait_send()

    def early(self):
        return [functools.partial(self.from_z, k) for k in (1, 2, 3)]

    def late(self):
        steps = []
        for k in range(4):
            steps += [functools.partial(self.from_x, k), functools.partial(self.from_y, k)]
        return steps + [self.ready]


def gather_events(parts, lead=2):
    n = len(parts)
    events = [p.start for p in parts[:lead]]
    for i in range(n + 1):
        if i < n:
            events += parts[i].early()
        if i + lead < n:
            events.append(parts[i + lead].start)
        if i > 0:
            events += parts[i - 1].late()
    return events


def gather_parts(shards, fulls, relays, chunks, recv, send, pos):
    return [
        Gather(shards[g], fulls[g], relays[g], cols, wide, recv.at[i], send.at[i], pos)
        for i, (g, cols, wide) in enumerate(chunks)
    ]


def gather_sems(chunks):
    n = len(chunks)
    return [
        pltpu.SemaphoreType.DMA((n, GATHER_RECV)),
        pltpu.SemaphoreType.DMA((n, GATHER_SEND)),
    ]


def gather_shapes(shards):
    return [jax.ShapeDtypeStruct((16,) + s.shape[1:], s.dtype) for s in shards] + [
        jax.ShapeDtypeStruct((8,) + s.shape[1:], s.dtype) for s in shards
    ]


REDUCE_RECV = 27
REDUCE_SEND = 23


class Reduce:
    def __init__(self, grad, land, out, recv, send, pos, cols):
        self.grad, self.land, self.out = grad, land, out
        self.recv, self.send, self.pos, self.cols = recv, send, pos, pl.ds(*cols)
        d, z, x, c, y = pos
        self.sib, self.xn, self.yn = neighbours(pos)
        self.home, self.away = c == y, c != y

    def rows(self, b):
        return self.grad.at[pl.ds(b, 1), :, self.cols]

    def slot(self, i):
        return self.land.at[pl.ds(i, 1)]

    def push(self, src, slot, s, peer):
        return remote(src, self.slot(slot), self.send.at[s], self.recv.at[slot], peer)

    def came(self, slot):
        self.push(self.slot(slot), slot, 0, self.sib).wait_recv()

    def value(self, i):
        return self.land[i].astype(F32)

    def first(self):
        d, z, x, c, y = self.pos

        @pl.when(self.away)
        def _():
            for column, base in ((1 - x, 0), (x, 4)):

                def step(k, _):
                    q = lax.rem(z + 1 + k, 4) * 2 + column
                    self.push(self.rows(2 * q + c), q, base + k, self.yn).start()
                    self.push(self.rows(2 * q + 1 - c), 15 + q, 8 + base + k, self.sib).start()
                    return 0

                lax.fori_loop(0, 4, step, 0)

        @pl.when(self.home)
        def _():
            for column, base in ((1 - x, 0), (x, 4)):

                def step(k, _):
                    q = lax.rem(z + 1 + k, 4) * 2 + column
                    self.push(self.rows(2 * q + 1 - c), q, base + k, self.sib).start()
                    return 0

                lax.fori_loop(0, 4, step, 0)

    def second(self, k):
        d, z, x, c, y = self.pos
        zz = (z + 1 + k) % 4
        q = zz * 2 + 1 - x

        @pl.when(self.away)
        def _():
            self.came(q)
            self.push(self.slot(q), 8 + zz, 16 + k, self.xn).start()

        @pl.when(self.home)
        def _():
            self.came(15 + q)
            self.push(self.slot(15 + q), 23 + zz, 15 + k, self.xn).start()
            b = 2 * q + c
            self.came(q)
            total = self.grad[b, :, self.cols].astype(F32) + self.value(q)
            self.grad[b, :, self.cols] = total.astype(BF16)
            self.push(self.rows(b), 8 + zz, 8 + k, self.xn).start()

    def third(self, k):
        d, z, x, c, y = self.pos
        zz = (z + 1 + k) % 4
        q = zz * 2 + x

        @pl.when(self.home)
        def _():
            self.came(15 + q)
            self.came(23 + zz)
            self.land[15 + q] = (self.value(15 + q) + self.value(23 + zz)).astype(BF16)
            self.push(self.slot(15 + q), 15 + zz, 19 + k, self.yn).start()
            if k < 3:
                b = 2 * q + c
                self.came(q)
                self.came(8 + zz)
                total = self.grad[b, :, self.cols].astype(F32)
                total = total + self.value(q) + self.value(8 + zz)
                self.grad[b, :, self.cols] = total.astype(BF16)
                self.push(self.rows(b), 12 + k, 12 + k, (zz * 4 + x * 2 + c, y)).start()

    def fourth(self, k):
        d, z, x, c, y = self.pos
        zz = (z + 1 + k) % 4
        q = zz * 2 + x

        @pl.when(self.away)
        def _():
            self.came(q)
            self.came(8 + zz)
            self.came(15 + zz)
            total = self.value(q) + self.value(8 + zz) + self.value(15 + zz)
            self.land[q] = total.astype(BF16)
            self.push(self.slot(q), 12 + k, 20 + k, (zz * 4 + x * 2 + c, y)).start()

    def fifth(self):
        d, z, x, c, y = self.pos
        q = z * 2 + x
        self.came(q)
        self.came(8 + z)
        for k in range(3):
            self.came(12 + k)
        total = self.value(q) + self.value(8 + z)
        total = total + self.value(12) + self.value(13) + self.value(14)

        @pl.when(self.home)
        def _():
            self.out[:, self.cols] = total + self.grad[d, :, self.cols].astype(F32)

        @pl.when(self.away)
        def _():
            self.came(15 + z)
            self.out[:, self.cols] = total + self.value(15 + z)

    def finish(self):
        block = self.slot(0)
        for s in range(REDUCE_SEND):
            self.push(block, 0, s, self.sib).wait_send()


def reduce_events(parts, lead=1):
    n = len(parts)
    events = [p.first for p in parts[:lead]]
    for i in range(n + 3):
        if i + lead < n:
            events.append(parts[i + lead].first)
        for k in range(4):
            if i < n:
                events.append(functools.partial(parts[i].second, k))
            if 0 <= i - 1 < n:
                events.append(functools.partial(parts[i - 1].third, k))
            if 0 <= i - 2 < n and k < 3:
                events.append(functools.partial(parts[i - 2].fourth, k))
        if 0 <= i - 3 < n:
            events.append(parts[i - 3].fifth)
    return events


def reduce_scratch(chunks):
    n = len(chunks)
    return [pltpu.VMEM((27, 72, cols[1]), BF16) for _, cols in chunks] + [
        pltpu.SemaphoreType.DMA((n, REDUCE_RECV)),
        pltpu.SemaphoreType.DMA((n, REDUCE_SEND)),
    ]


class Pump:
    def __init__(self, events):
        self.events, self.next = list(events), 0

    def run(self, count=None):
        stop = len(self.events)
        if count is not None:
            stop = min(stop, self.next + max(0, count))
        for event in self.events[self.next : stop]:
            event()
        self.next = stop

    def loop(self, steps, body, count=0):
        todo = self.events[self.next :][:count]
        self.next += len(todo)

        def step(i, _):
            for j, event in enumerate(todo):
                pl.when(i == j * steps // count)(event)
            body(i)
            return 0

        lax.fori_loop(0, steps, step, 0)


def flat(value):
    return value.reshape(-1, value.shape[-1])


def product(a, b, ca, cb):
    return lax.dot_general(a, b, (((ca,), (cb,)), ((), ())), preferred_element_type=F32)


def loader(sems):
    count = iter(range(64))

    def load(src, dst):
        copy = pltpu.make_async_copy(src, dst, sems.at[next(count)])
        copy.start()
        return copy.wait

    return load


def norm_back_rows(value, g, scale_up):
    center = value - jnp.mean(value, axis=-1, keepdims=True)
    rate = lax.rsqrt(jnp.mean(center * center, axis=-1, keepdims=True) + 1e-06)
    normed = center * rate
    e = g * scale_up
    inner = jnp.mean(e * normed, axis=-1, keepdims=True)
    return rate * (e - jnp.mean(e, axis=-1, keepdims=True) - normed * inner), normed


def row_sum(value):
    return jnp.sum(value, axis=0, keepdims=True)


def last_kernel(
    mod_ref, sums_ref, fc2_bias_ref, fc1_bias_ref, w_ref,
    rows_in, dqkv_in, wqkv_in, tokens_in, resid_in,
    tgrad_ref, qkv_out, sg_ref, mods_a, mods_b, b2, b3,
    rows_ref, dqkv_ref, wqkv_ref, tokens_ref, resid_ref, tsend, half_ref,
    grad, ngrad, sent, got, v1, v1_in, v2, v2_in, sgp, land0, land1, land2,
    load_sems, s0, s1, r1, s2, r2, s3, r3, s4, r4, s5, r5, recv, send,
):
    pos = place()
    d, z, x, c, y = pos
    sib = neighbours(pos)[0]
    far = (z * 4 + x * 2 + 1 - c, 1 - y)
    lin = d * 2 + y
    half, width = tokens_ref.shape
    heads = dqkv_ref.shape[0] // 3
    load = loader(load_sems)
    ready = [load(dqkv_in, dqkv_ref), load(rows_in, rows_ref)]
    ready_late = [
        load(*pair)
        for pair in ((wqkv_in, wqkv_ref), (tokens_in, tokens_ref), (resid_in, resid_ref))
    ]
    greet([(((lin + k) % 32) // 2, (lin + k) % 2) for k in range(1, 32)])
    me = (z * 2 + x) * 2 + y
    sgp[...] = jnp.zeros_like(sgp)
    n = dqkv_ref.shape[1] * heads
    hidden = fc1_bias_ref.shape[1]
    for wait in ready:
        wait()

    half_ref[...] = jnp.zeros_like(half_ref)
    half_ref[:, :hidden] = fc1_bias_ref[...]
    ones = jnp.ones((8, 2 * half), BF16)
    for j, at in ((0, hidden), (2, hidden + (n + 127) // 128 * 128)):
        value = product(ones, flat(dqkv_ref[j * heads : (j + 1) * heads]), 1, 1)
        half_ref[:, at : at + n] = value[0:1, :]

    for i in range(6):
        early = sums_ref[i : i + 1, :] if i < 5 else fc2_bias_ref[...]
        v2[:, i * width : (i + 1) * width] = early
    swap_early = remote(v2, v2_in, s0.at[2], s0.at[3], sib)
    swap_early.start()

    @pl.when(y == c)
    def _():
        b3[me] = half_ref[...]

    def send3(q, core):
        s = q * 2 + core
        return remote(half_ref, b3.at[me], s3.at[s], r3.at[me], (s, c))

    def each3(action):
        for q in range(8):
            for core in range(2):
                pl.when(jnp.logical_or(d != q * 2 + core, y != c))(
                    functools.partial(action, q, core)
                )

    reducers = [
        Reduce(grad.at[j], land, qkv_out.at[j], recv.at[j], send.at[j], pos, (0, n))
        for j, land in enumerate((land0, land1, land2))
    ]

    def weight_grad(j, _):
        value = product(rows_ref[...], flat(dqkv_ref[pl.ds(j * heads, heads)]), 0, 1)
        grad[j] = value.reshape(grad.shape[1:]).astype(BF16)
        for i, reducer in enumerate(reducers):
            pl.when(j == i)(reducer.first)
        return 0

    lax.fori_loop(0, 3, weight_grad, 0)
    each3(lambda q, core: send3(q, core).start())
    pump = Pump(reduce_events(reducers, 3)[3:])

    def chip(k):
        m = (me + k) % 16
        return m, ((m // 2) * 2 + c, m % 2)

    def to_chip(buf, send, recv, k):
        return remote(buf.at[me], buf.at[me], send.at[k], recv.at[me], chip(k)[1])

    def from_chip(buf, send, recv, k):
        m, peer = chip(k)
        return remote(buf.at[m], buf.at[m], send.at[k], recv.at[m], peer)

    last, wide, known = (mods_a, s1, r1), (b2, s2, r2), (mods_b, s5, r5)
    swap_early.wait()
    mods_b[me] = (v2[:, : 4 * width] + v2_in[:, : 4 * width]).astype(BF16)
    b2[me] = v2[:, 4 * width :] + v2_in[:, 4 * width :]
    for k in range(1, 16):
        to_chip(*known, k).start()
        to_chip(*wide, k).start()
    for wait in ready_late:
        wait()

    tile = half // 2
    swap = remote(sent, got, s0.at[4], s0.at[5], sib)

    def into_norm(i):
        cols = pl.ds(pl.multiple_of(i * tile, tile), tile)
        return product(flat(dqkv_ref[:, :, cols]), flat(wqkv_ref[...]), 0, 1)

    def other_rows(i):
        sent[pl.ds(pl.multiple_of(i * tile, tile), tile), :] = into_norm(i + 2).astype(BF16)

    def own_rows(i):
        ngrad[pl.ds(pl.multiple_of(i * tile, tile), tile), :] = into_norm(i)

    pump.loop(2, other_rows, 6)
    swap.start()
    pump.loop(2, own_rows, 6)
    swap.wait()
    piece = half // 4
    scale = 1.0 + mod_ref[:, width : 2 * width]
    v1[...] = jnp.zeros_like(v1)

    def norm_back(i):
        part = pl.ds(pl.multiple_of(i * piece, piece), piece)
        g = ngrad[part, :] + got[part, :].astype(F32)
        back, normed = norm_back_rows(tokens_ref[part, :].astype(F32), g, scale)
        value = (resid_ref[part, :] + back).astype(BF16)

        @pl.when(y == c)
        def _():
            tgrad_ref[part, :] = value

        @pl.when(y != c)
        def _():
            tsend[part, :] = value

        v1[:, :width] += row_sum(g)
        v1[:, width : 2 * width] += row_sum(g * normed)

    pump.loop(4, norm_back, 8)
    trade = remote(tsend, tgrad_ref, s0.at[6], s0.at[7], far)
    pl.when(y != c)(lambda: trade.start())

    swap = remote(v1, v1_in, s0.at[0], s0.at[1], sib)
    swap.start()
    pump.run(2)
    swap.wait()
    mods_a[me] = (v1[...] + v1_in[...]).astype(BF16)
    for k in range(1, 16):
        to_chip(*last, k).start()

    def rows_of(buf):
        return jnp.concatenate([buf[i].astype(F32) for i in range(16)], axis=0)

    def back_of(buf, at):
        every = rows_of(buf).astype(BF16)
        return product(every, w_ref[:, at : at + every.shape[1]], 1, 1)

    pump.run(8)
    for k in range(1, 16):
        from_chip(*known, k).wait_recv()
    back = back_of(mods_b, 2 * width)
    pump.run(2)
    for k in range(1, 16):
        from_chip(*last, k).wait_recv()
    back = back + back_of(mods_a, 0)
    for i in range(16):
        sgp[i, 0:1, :72] = back[i : i + 1, :]

    def send4(k):
        m = (d + k) % 16
        return remote(sgp.at[m], sg_ref.at[d], s4.at[k], r4.at[d], (m, y))

    for k in range(1, 16):
        send4(k).start()
    sg_ref[d] = sgp[d]
    pump.run(4)
    for k in range(1, 16):
        from_chip(*wide, k).wait_recv()

    def arrive3(i):
        remote(half_ref, b3.at[i], s3.at[0], r3.at[i], sib).wait_recv()

    for i in range(16):
        pl.when(jnp.logical_or(i != me, y != c))(functools.partial(arrive3, i))
    for k in range(1, 16):
        m = (d + k) % 16
        remote(sgp.at[m], sg_ref.at[m], s4.at[k], r4.at[m], (m, y)).wait_recv()
    pump.run()
    for reducer in reducers:
        reducer.finish()
    pl.when(y != c)(lambda: trade.wait())
    each3(lambda q, core: send3(q, core).wait_send())
    for k in range(1, 16):
        for buf in (last, wide, known):
            to_chip(*buf, k).wait_send()
        send4(k).wait_send()


def last_stage(
    mod, sums, fc2_bias, fc1_bias, w_mod, rows, dqkv, w_qkv, tokens, resid, collective_id
):
    vmem, anywhere = pl.BlockSpec(memory_space=pltpu.VMEM), pl.BlockSpec(memory_space=pl.ANY)
    n = w_mod.shape[1]
    half, width = tokens.shape
    cols = dqkv.shape[0] * dqkv.shape[1] // 3
    n2, n3 = 2 * width, fc1_bias.shape[1] + 2 * ((cols + 127) // 128 * 128)
    dma = pltpu.SemaphoreType.DMA((16,))
    shape = jax.ShapeDtypeStruct
    loaded = (rows, dqkv, w_qkv, tokens, resid)
    return pl.pallas_call(
        last_kernel,
        out_shape=[
            shape((half, width), BF16),
            shape((3, 72, cols), F32),
            shape((16, 8, 128), F32),
            shape((16, 1, n // 3), BF16),
            shape((16, 1, n - n // 3), BF16),
            shape((16, 1, n2), F32),
            shape((16, 1, n3), F32),
        ],
        in_specs=[vmem] * 5 + [anywhere] * 5,
        out_specs=[vmem] * 7,
        scratch_shapes=[pltpu.VMEM(a.shape, a.dtype) for a in loaded]
        + [
            pltpu.VMEM((half, width), BF16),
            pltpu.VMEM((1, n3), F32),
            pltpu.VMEM((3, 16, 72, cols), BF16),
            pltpu.VMEM((half, width), F32),
            pltpu.VMEM((half, width), BF16),
            pltpu.VMEM((half, width), BF16),
            pltpu.VMEM((1, n // 3), F32),
            pltpu.VMEM((1, n // 3), F32),
            pltpu.VMEM((1, n), F32),
            pltpu.VMEM((1, n), F32),
            pltpu.VMEM((16, 8, 128), F32),
        ]
        + [pltpu.VMEM((27, 72, cols), BF16)] * 3
        + [pltpu.SemaphoreType.DMA((8,)), pltpu.SemaphoreType.DMA((8,))]
        + [dma] * 10
        + [
            pltpu.SemaphoreType.DMA((3, REDUCE_RECV)),
            pltpu.SemaphoreType.DMA((3, REDUCE_SEND)),
        ],
        compiler_params=pltpu.CompilerParams(
            collective_id=collective_id, has_side_effects=True, vmem_limit_bytes=64500 * 1024
        ),
    )(mod, sums, fc2_bias, fc1_bias, w_mod, *loaded)


LOG2E = math.log2(math.e)


def attention_step(qkv, out, lse, block, scale):
    heads, blocks = qkv.shape[0] // 3, qkv.shape[2] // block
    factor = scale * LOG2E

    def body(i):
        h = i // blocks
        cols = pl.ds(pl.multiple_of((i % blocks) * block, block), block)
        scores = product(qkv[heads + h], qkv[h, :, cols], 0, 0)
        top = jnp.max(scores, axis=0, keepdims=True)
        probs = jnp.exp2((scores - top) * factor)
        total = jnp.sum(probs, axis=0, keepdims=True)
        mixed = product(qkv[2 * heads + h], probs.astype(BF16), 1, 0)
        out[h, :, cols] = (mixed / total).astype(BF16)
        lse[h, :, cols] = top * factor + jnp.log2(total)

    return heads * blocks, body


GELU = math.sqrt(2 / math.pi)


def gelu_and_slope(v):
    square = v * v
    t = jnp.tanh(v * (GELU + GELU * 0.044715 * square))
    half = 0.5 * (1.0 + t)
    return v * half, half + 0.5 * v * (1.0 - t * t) * (GELU + GELU * 3 * 0.044715 * square)


def forward_kernel(
    chunks, block, scale,
    piece_ref, w_mod, mod_bias, proj_bias, small_in, tokens_in, grad_in,
    s_qkv, s_proj, s_fc1, s_fc2,
    mod, silu_ref, fc2_bias_grad,
    rows_a_out, qkv_out, attended_out, lse_out, branch_out, resid_out, rows_out, act_out,
    slope_out, fc2_grad_out, grad_m_out, tokens_out, grad_out,
    w_qkv, w_proj, w_fc1, w_fc2, relay_qkv, relay_proj, relay_1, relay_2,
    part, land, mine, other, small, tokens, out_grad,
    rows_a, qkv, out, lse, branch, resid, rows, act, slope, fc2_grad, grad_m,
    qkv_here, proj_here, weight_here, sent, got,
    s1, r1, s2, r2, sems, out_sems, recv, send,
):
    pos = place()
    d, z, x, c, y = pos
    sib, _, yn = neighbours(pos)
    far = (z * 4 + x * 2 + 1 - c, 1 - y)
    half, width = tokens.shape
    home, away = c == y, c != y
    greet([((d + k) % 16, y) for k in range(1, 16)] + [yn, far])

    stores = []

    def store(src, dst):
        copy = pltpu.make_async_copy(src, dst, out_sems.at[len(stores)])
        copy.start()
        stores.append(copy)

    def swapped(src, dst, i):
        there = remote(src, dst, sems.at[i], sems.at[i + 1], far)
        here = pltpu.make_async_copy(src, dst, sems.at[i + 1])

        def start():
            pl.when(away)(lambda: there.start())
            pl.when(home)(lambda: here.start())

        def wait():
            pl.when(away)(lambda: there.wait())
            pl.when(home)(lambda: here.wait())

        return start, wait

    def piece(k):
        to = (d + k) % 16
        return remote(piece_ref.at[to], silu_ref.at[d], s1.at[k], r1.at[d], (to, y))

    def piece_in(k):
        src = (d + k) % 16
        return remote(piece_ref.at[src], silu_ref.at[src], s1.at[k], r1.at[src], (src, y))

    for k in range(1, 16):
        piece(k).start()
    small_start, small_wait = swapped(small_in, small, 7)
    tokens_start, tokens_wait = swapped(tokens_in, tokens, 9)
    grad_start, grad_wait = swapped(grad_in, out_grad, 11)
    small_start()
    tokens_start()
    parts = gather_parts(
        [s_qkv, s_proj, s_fc1, s_fc2],
        [w_qkv, w_proj, w_fc1, w_fc2],
        [relay_qkv, relay_proj, relay_1, relay_2],
        chunks,
        recv,
        send,
        pos,
    )
    last_of = {g: parts[i].ready for i, (g, _, _) in enumerate(chunks)}
    events = gather_events(parts)
    pump = Pump(events)

    def until_ready(g):
        pump.run(events.index(last_of[g]) + 1 - pump.next)

    pump.run(6)
    silu_ref[d] = piece_ref[d]
    for k in range(1, 16):
        piece_in(k).wait_recv()
    some = jnp.concatenate(
        [silu_ref[2 * q + y].astype(F32)[0:1, :] for q in range(8)], axis=0
    ).astype(BF16)[:, :72]
    for j in range(6):
        cols = slice(j * width, (j + 1) * width)
        value = jnp.dot(some, w_mod[:, cols], preferred_element_type=F32)
        for q in range(8):
            part[q, :, cols] = value[q : q + 1, :]
    me = z * 2 + x

    def send_part(k):
        q = (me + k) % 8
        return remote(part.at[q], land.at[me], s2.at[k], r2.at[me], (q * 2 + c, y))

    def part_in(k):
        q = (me + k) % 8
        return remote(part.at[q], land.at[q], s2.at[k], r2.at[q], (q * 2 + c, y))

    for k in range(1, 8):
        send_part(k).start()
    land[me] = part[me]
    pump.run(10)
    for k in range(1, 8):
        part_in(k).wait_recv()
    total = land[0]
    for q in range(1, 8):
        total = total + land[q]
    mine[...] = total
    swap = remote(mine, other, sems.at[13], sems.at[14], sib)
    swap.start()
    pump.run(4)
    for k in range(1, 16):
        piece(k).wait_send()
    for k in range(1, 8):
        send_part(k).wait_send()
    swap.wait()
    mod[...] = mine[...] + other[...] + mod_bias[...]
    shift_a, scale_a, gate_a, shift_m, scale_m, gate_m = [
        mod[:, i * width : (i + 1) * width] for i in range(6)
    ]
    small_wait()
    tokens_wait()

    tall = half // 4

    def norm_rows(value, shift, scale_up):
        center = value - jnp.mean(value, axis=-1, keepdims=True)
        spread = jnp.mean(center * center, axis=-1, keepdims=True)
        normed = center * lax.rsqrt(spread + 1e-06) * (1.0 + scale_up) + shift
        return normed.astype(BF16)

    def first_norm(i, _):
        own = pl.ds(pl.multiple_of(i * tall, tall), tall)
        rows_a[own, :] = norm_rows(tokens[own, :].astype(F32), shift_a, scale_a)
        return 0

    lax.fori_loop(0, 4, first_norm, 0)
    share = remote(rows_a.at[:half], rows_a.at[half:], sems.at[5], sems.at[6], sib)
    share.start()
    until_ready(0)
    heads = qkv.shape[0] // 3
    cols = heads * qkv.shape[1]
    load = pltpu.make_async_copy(w_qkv, qkv_here, sems.at[0])
    load.start()
    grad_start()
    pump.run(2)
    load.wait()
    share.wait()
    store(rows_a, rows_a_out)
    store(tokens, tokens_out)
    row = lax.broadcasted_iota(jnp.int32, (8, 2 * half), 0)
    for j in range(3):
        weight = flat(qkv_here[:, :, j * cols : (j + 1) * cols])
        value = product(weight, rows_a[...], 0, 1)
        if j != 1:
            pick = jnp.where(row == j // 2, 1.0, 0.0).astype(BF16)
            value = value + product(small[:, :cols], pick, 0, 0)
        value = value.reshape((heads,) + qkv.shape[1:])
        qkv[pl.ds(j * heads, heads)] = value.astype(BF16)
        pump.run(2)
    store(qkv, qkv_out)
    steps, body = attention_step(qkv, out, lse, block, scale)
    pump.loop(steps, body, 22)
    store(out, attended_out)
    store(lse, lse_out)
    until_ready(1)

    load = pltpu.make_async_copy(w_proj, proj_here, sems.at[0])
    load.start()
    load.wait()
    tile = half // 2
    swap = remote(sent, got, sems.at[1], sems.at[2], sib)

    def project(i):
        cols = pl.ds(pl.multiple_of(i * tile, tile), tile)
        return product(flat(out[:, :, cols]), flat(proj_here[...]), 0, 1)

    def other_rows(i, _):
        sent[pl.ds(pl.multiple_of(i * tile, tile), tile), :] = project(i + 2).astype(BF16)
        return 0

    def own_rows(i, _):
        branch[pl.ds(pl.multiple_of(i * tile, tile), tile), :] = project(i) + proj_bias[...]
        return 0

    lax.fori_loop(0, 2, other_rows, 0)
    swap.start()
    lax.fori_loop(0, 2, own_rows, 0)
    pump.run(2)
    grad_wait()
    store(out_grad, grad_out)

    def gated(i, total):
        own = pl.ds(pl.multiple_of(i * tall, tall), tall)
        value = (out_grad[own, :].astype(F32) * gate_m).astype(BF16)
        grad_m[own, :] = value
        return total + jnp.sum(value.astype(F32), axis=0, keepdims=True)

    fc2_bias_grad[...] = lax.fori_loop(0, 4, gated, jnp.zeros((1, width), F32))
    share_m = remote(grad_m.at[:half], grad_m.at[half:], sems.at[15], sems.at[16], sib)
    share_m.start()
    swap.wait()
    share = remote(rows.at[:half], rows.at[half:], sems.at[3], sems.at[4], sib)

    def norm(i, _):
        own = pl.ds(pl.multiple_of(i * tall, tall), tall)
        total = branch[own, :] + got[own, :].astype(F32)
        branch[own, :] = total
        mid = tokens[own, :].astype(F32) + gate_a * total
        resid[own, :] = mid
        rows[own, :] = norm_rows(mid, shift_m, scale_m)
        return 0

    lax.fori_loop(0, 4, norm, 0)
    share.start()
    store(branch, branch_out)
    store(resid, resid_out)
    until_ready(2)

    load = pltpu.make_async_copy(w_fc1, weight_here, sems.at[0])
    load.start()
    load.wait()
    share.wait()
    store(rows, rows_out)
    n = 256
    hidden_steps = act.shape[1] // n

    def hidden(i):
        cols = pl.ds(pl.multiple_of(i * n, n), n)
        bias = small[:, cols].astype(F32)[2:3, :]
        value, rate = gelu_and_slope(
            product(rows[...], flat(weight_here[:, :, cols]), 1, 0) + bias
        )
        act[:, cols] = value.astype(BF16)
        slope[:, cols] = rate.astype(BF16)

    pump.loop(hidden_steps, hidden, hidden_steps)
    store(act, act_out)
    store(slope, slope_out)
    share_m.wait()
    store(grad_m, grad_m_out)

    def weight_grad(i):
        cols = pl.ds(pl.multiple_of(i * n, n), n)
        value = product(grad_m[...], act[:, cols], 0, 0)
        fc2_grad[:, :, cols] = value.reshape(fc2_grad.shape[:2] + (n,)).astype(BF16)

    pump.loop(hidden_steps, weight_grad, hidden_steps)
    store(fc2_grad, fc2_grad_out)
    pump.run()
    for p in parts:
        p.finish()
    for copy in stores:
        copy.wait()


def forward_stage(
    pieces, w_mod, mod_bias, proj_bias, small, tokens, out_grad, shards, size, chunks,
    collective_id, block=512,
):
    half, width = tokens.shape
    count = 2 * half
    owned, cols = shards[1].shape[1:]
    heads = cols // size
    hidden = shards[2].shape[2]
    n = w_mod.shape[1]
    vmem, anywhere = pl.BlockSpec(memory_space=pltpu.VMEM), pl.BlockSpec(memory_space=pl.ANY)
    shape, dma = jax.ShapeDtypeStruct, pltpu.SemaphoreType.DMA
    kept = [
        ((count, width), BF16),
        ((3 * heads, size, count), BF16),
        ((heads, size, count), BF16),
        ((heads, 1, count), F32),
        ((half, width), F32),
        ((half, width), F32),
        ((count, width), BF16),
        ((count, hidden), BF16),
        ((count, hidden), BF16),
        ((16, owned, hidden), BF16),
        ((count, width), BF16),
    ]
    swap = ((half, width), BF16)
    return pl.pallas_call(
        functools.partial(forward_kernel, chunks, block, size**-0.5),
        out_shape=[shape((1, n), F32), shape((16, 8, 128), BF16), shape((1, width), F32)]
        + [shape(*k) for k in kept + [swap, swap]]
        + gather_shapes(shards),
        in_specs=[vmem] * 5 + [anywhere] * 6,
        out_specs=[vmem] * 3 + [anywhere] * 21,
        scratch_shapes=[
            pltpu.VMEM((8, 1, n), F32),
            pltpu.VMEM((8, 1, n), F32),
            pltpu.VMEM((1, n), F32),
            pltpu.VMEM((1, n), F32),
            pltpu.VMEM(small.shape, BF16),
            pltpu.VMEM(*swap),
            pltpu.VMEM(*swap),
        ]
        + [pltpu.VMEM(*k) for k in kept]
        + [
            pltpu.VMEM((16, owned, 3 * cols), BF16),
            pltpu.VMEM((16, owned, cols), BF16),
            pltpu.VMEM((16, owned, hidden), BF16),
            pltpu.VMEM(*swap),
            pltpu.VMEM(*swap),
            dma((16,)),
            dma((16,)),
            dma((8,)),
            dma((8,)),
            dma((17,)),
            dma((13,)),
        ]
        + gather_sems(chunks),
        compiler_params=pltpu.CompilerParams(
            collective_id=collective_id, has_side_effects=True, vmem_limit_bytes=64500 * 1024
        ),
    )(pieces, w_mod, mod_bias, proj_bias, small, tokens, out_grad, *shards)[:20]


def attention_back_step(qkv, grad, out, lse, result, key_sum, value_sum, block, scale):
    heads, blocks = qkv.shape[0] // 3, qkv.shape[2] // block
    factor = scale * LOG2E

    def body(i):
        h, j = i // blocks, i % blocks
        cols = pl.ds(pl.multiple_of(j * block, block), block)
        queries, keys, values = qkv[h, :, cols], qkv[heads + h], qkv[2 * heads + h]
        grads = grad[h, :, cols]
        inner = jnp.sum(out[h, :, cols].astype(F32) * grads.astype(F32), axis=0, keepdims=True)
        probs = jnp.exp2(product(keys, queries, 0, 0) * factor - lse[h, :, cols])
        score_grad = (probs * (product(values, grads, 0, 0) - inner)).astype(BF16)
        value_part = product(grads, probs.astype(BF16), 1, 1)
        key_part = product(queries, score_grad, 1, 1)
        result[h, :, cols] = (product(keys, score_grad, 1, 0) * scale).astype(BF16)

        @pl.when(j == 0)
        def _():
            key_sum[...] = key_part
            value_sum[...] = value_part

        @pl.when(j > 0)
        def _():
            key_sum[...] += key_part
            value_sum[...] += value_part

        @pl.when(j == blocks - 1)
        def _():
            result[heads + h] = (key_sum[...] * scale).astype(BF16)
            result[2 * heads + h] = value_sum[...].astype(BF16)

    return heads * blocks, body


def hidden_back_kernel(
    chunks, bias, grad_m_in, act_in, slope_in, rows_in, fc2_grad_in, w_fc2, w_fc1,
    fc1_bias_grad, fc2_out, fc1_grad_out, branch_out, ngrad_out,
    grad_m, act, slope, rows, fc2_grad, fc1_grad, branch, ngrad,
    weight, pre_grad, sent1, got1, sent2, got2, *rest,
):
    n = len(chunks)
    lands, (sems, load_sems, recv, send) = rest[:n], rest[n:]
    pos = place()
    sib = neighbours(pos)[0]
    half, width = branch.shape
    hidden = act.shape[1]
    load = loader(load_sems)
    grad_ready = load(fc2_grad_in, fc2_grad)
    weight_ready = load(w_fc2, weight)
    m_ready = load(grad_m_in, grad_m)
    slope_ready = load(slope_in, slope)
    act_ready = load(act_in, act)
    rows_ready = load(rows_in, rows)
    greet(chip_peers(pos))
    parts = [
        Reduce(fc2_grad, lands[i], fc2_out, recv.at[i], send.at[i], pos, cols)
        for i, cols in enumerate(chunks)
    ]
    pump = Pump(reduce_events(parts))
    grad_ready()
    pump.run(2)
    weight_ready()
    m_ready()
    slope_ready()
    tile = 256

    def into_hidden(i):
        cols = pl.ds(pl.multiple_of(i * tile, tile), tile)
        value = product(grad_m[...], flat(weight[:, :, cols]), 1, 0)
        value = (value * slope[:, cols].astype(F32)).astype(BF16)
        pre_grad[:, cols] = value
        fc1_bias_grad[:, cols] = jnp.sum(value.astype(F32), axis=0, keepdims=True)

    pump.loop(hidden // tile, into_hidden, 9)

    def out_of_hidden(source, sent, own, extra):
        def body(i):
            turn = lax.rem(i + 2, 4)
            part = pl.ds(pl.multiple_of(turn * tile, tile), tile)
            value = product(source[part, :], flat(weight[...]), 1, 1)

            @pl.when(i < 2)
            def _():
                sent[pl.ds(pl.multiple_of(i * tile, tile), tile), :] = value.astype(BF16)

            @pl.when(i >= 2)
            def _():
                own[part, :] = value + extra

        return body

    swap1 = remote(sent1, got1, sems.at[1], sems.at[2], sib)
    swap2 = remote(sent2, got2, sems.at[3], sems.at[4], sib)
    act_ready()
    pump.loop(4, out_of_hidden(act, sent1, branch, bias[...]), 8)
    swap1.start()
    weight_ready = load(w_fc1, weight)
    pump.run(2)
    weight_ready()
    pump.loop(4, out_of_hidden(pre_grad, sent2, ngrad, 0.0), 8)
    swap2.start()

    def join(own, got):
        def body(i, _):
            part = pl.ds(pl.multiple_of(i * tile, tile), tile)
            own[part, :] += got[part, :].astype(F32)
            return 0

        lax.fori_loop(0, half // tile, body, 0)

    swap1.wait()
    join(branch, got1)
    stored = [load(branch, branch_out)]
    rows_ready()

    def weight_grad(i):
        cols = pl.ds(pl.multiple_of(i * tile, tile), tile)
        value = product(rows[...], pre_grad[:, cols], 0, 0)
        fc1_grad[:, :, cols] = value.reshape(fc1_grad.shape[:2] + (tile,)).astype(BF16)

    pump.loop(hidden // tile, weight_grad, 9)
    stored.append(load(fc1_grad, fc1_grad_out))
    swap2.wait()
    join(ngrad, got2)
    stored.append(load(ngrad, ngrad_out))
    pump.run()
    for p in parts:
        p.finish()
    for wait in stored:
        wait()


def hidden_back(bias, grad_m, act, slope, rows, fc2_grad, w_fc2, w_fc1, chunks, collective_id):
    vmem, anywhere = pl.BlockSpec(memory_space=pltpu.VMEM), pl.BlockSpec(memory_space=pl.ANY)
    shape = jax.ShapeDtypeStruct
    count, width = grad_m.shape
    half, hidden = count // 2, act.shape[1]
    swap = pltpu.VMEM((half, width), BF16)
    sums = pltpu.VMEM((half, width), F32)
    land = reduce_scratch([(0, cols) for cols in chunks])
    return pl.pallas_call(
        functools.partial(hidden_back_kernel, chunks),
        out_shape=[
            shape((1, hidden), F32),
            shape(fc2_grad.shape[1:], F32),
            shape(fc2_grad.shape, BF16),
            shape((half, width), F32),
            shape((half, width), F32),
        ],
        in_specs=[vmem] + [anywhere] * 7,
        out_specs=[vmem] * 2 + [anywhere] * 3,
        scratch_shapes=[
            pltpu.VMEM((count, width), BF16),
            pltpu.VMEM((count, hidden), BF16),
            pltpu.VMEM((count, hidden), BF16),
            pltpu.VMEM((count, width), BF16),
            pltpu.VMEM(fc2_grad.shape, BF16),
            pltpu.VMEM(fc2_grad.shape, BF16),
            sums,
            sums,
            pltpu.VMEM(fc2_grad.shape, BF16),
            pltpu.VMEM((count, hidden), BF16),
            swap,
            swap,
            swap,
            swap,
        ]
        + land[: len(chunks)]
        + [pltpu.SemaphoreType.DMA((5,)), pltpu.SemaphoreType.DMA((12,))]
        + land[len(chunks) :],
        compiler_params=pltpu.CompilerParams(
            collective_id=collective_id, has_side_effects=True, vmem_limit_bytes=64500 * 1024
        ),
    )(bias, grad_m, act, slope, rows, fc2_grad, w_fc2, w_fc1)


def attention_back_kernel(
    chunks, block, scale, mod, resid_in, ngrad_in, out_grad_in, branch_in, branch_m_in, w_proj_in,
    qkv_in, out_in, lse_in, fc1_grad_in,
    sums, fc1_out, proj_out, output, resid_grad_out, result_out,
    resid, ngrad, out_grad, branch, branch_m, w_proj, qkv, out, lse, fc1_grad, resid_grad, result,
    rows, grad, proj_grad, key_sum, value_sum, given, *rest,
):
    n = len(chunks)
    lands, (sems, load_sems, recv, send) = rest[:n], rest[n:]
    pos = place()
    sib = neighbours(pos)[0]
    half, width = resid.shape
    d, z, x, c, y = pos
    home, away = c == y, c != y
    far = (z * 4 + x * 2 + 1 - c, 1 - y)
    load = loader(load_sems)
    first = [load(fc1_grad_in, fc1_grad)]
    norm_ready = [
        load(*pair)
        for pair in (
            (ngrad_in, ngrad),
            (resid_in, resid),
            (out_grad_in, out_grad),
            (branch_in, branch),
            (branch_m_in, branch_m),
        )
    ]
    late = [load(w_proj_in, w_proj), load(out_in, out), load(qkv_in, qkv), load(lse_in, lse)]
    greet(chip_peers(pos))
    parts = [
        Reduce(
            (fc1_grad, proj_grad)[g],
            lands[i],
            (fc1_out, proj_out)[g],
            recv.at[i],
            send.at[i],
            pos,
            cols,
        )
        for i, (g, cols) in enumerate(chunks)
    ]
    pump = Pump(reduce_events(parts))
    for wait in first:
        wait()
    pump.run(2)
    for wait in norm_ready:
        wait()
    tall = half // 4
    gate_a, scale_m, gate_m = (mod[:, i * width : (i + 1) * width] for i in (2, 4, 5))
    scale_up = 1.0 + scale_m

    def norm(i, total):
        part = pl.ds(pl.multiple_of(i * tall, tall), tall)
        g = ngrad[part, :]
        mid = resid[part, :]
        back, normed = norm_back_rows(mid, g, scale_up)
        grads = out_grad[part, :].astype(F32)
        value = grads + back
        resid_grad[part, :] = value
        low = (value * gate_a).astype(BF16)
        rows[part, :] = low
        made = (mid + gate_m * branch_m[part, :]).astype(BF16)

        @pl.when(home)
        def _():
            output[part, :] = made

        @pl.when(away)
        def _():
            given[part, :] = made

        terms = (
            value * branch[part, :],
            g,
            g * normed,
            grads * branch_m[part, :],
            low.astype(F32),
        )
        return tuple(t + row_sum(v) for t, v in zip(total, terms))

    total = lax.fori_loop(0, 4, norm, (jnp.zeros((1, width), F32),) * 5)
    share = remote(rows.at[:half], rows.at[half:], sems.at[0], sems.at[1], sib)
    share.start()
    stored = [load(resid_grad, resid_grad_out)]
    trade = remote(given, output, sems.at[2], sems.at[3], far)
    pl.when(away)(lambda: trade.start())
    sums[...] = jnp.zeros_like(sums)
    for i in range(5):
        sums[i : i + 1, :] = total[i]
    pump.run(1)
    for wait in late:
        wait()
    share.wait()
    tile = 256

    def attended(i):
        cols = pl.ds(pl.multiple_of(i * tile, tile), tile)
        value = product(flat(w_proj[...]), rows[cols, :], 0, 1)
        grad[:, :, cols] = value.reshape(grad.shape[:2] + (tile,)).astype(BF16)

    pump.loop(2 * half // tile, attended, 4)
    value = product(rows[...], flat(out[...]), 0, 1)
    proj_grad[...] = value.reshape(proj_grad.shape).astype(BF16)
    steps, body = attention_back_step(
        qkv, grad, out, lse, result, key_sum, value_sum, block, scale
    )
    pump.loop(steps, body, 28)
    stored.append(load(result, result_out))
    pump.run()
    pl.when(away)(lambda: trade.wait())
    for p in parts:
        p.finish()
    for wait in stored:
        wait()


def attention_back(
    mod, resid, ngrad, out_grad, branch, branch_m, w_proj, qkv, out, lse, fc1_grad, chunks,
    collective_id, block=512,
):
    heads, size, count = out.shape
    half, width = resid.shape
    owned, cols = w_proj.shape[1:]
    vmem, anywhere = pl.BlockSpec(memory_space=pltpu.VMEM), pl.BlockSpec(memory_space=pl.ANY)
    shape = jax.ShapeDtypeStruct
    land = reduce_scratch(chunks)
    arrays = (resid, ngrad, out_grad, branch, branch_m, w_proj, qkv, out, lse, fc1_grad)
    made = [((half, width), F32), (qkv.shape, BF16)]
    return pl.pallas_call(
        functools.partial(attention_back_kernel, chunks, block, size**-0.5),
        out_shape=[
            shape((8, width), F32),
            shape(fc1_grad.shape[1:], F32),
            shape((owned, cols), F32),
            shape((half, width), BF16),
        ]
        + [shape(*m) for m in made],
        in_specs=[vmem] + [anywhere] * 10,
        out_specs=[vmem] * 4 + [anywhere] * 2,
        scratch_shapes=[pltpu.VMEM(a.shape, a.dtype) for a in arrays]
        + [pltpu.VMEM(*m) for m in made]
        + [
            pltpu.VMEM((count, width), BF16),
            pltpu.VMEM(out.shape, BF16),
            pltpu.VMEM((16, owned, cols), BF16),
            pltpu.VMEM((size, count), F32),
            pltpu.VMEM((size, count), F32),
            pltpu.VMEM((half, width), BF16),
        ]
        + land[: len(chunks)]
        + [pltpu.SemaphoreType.DMA((4,)), pltpu.SemaphoreType.DMA((12,))]
        + land[len(chunks) :],
        compiler_params=pltpu.CompilerParams(
            collective_id=collective_id, has_side_effects=True, vmem_limit_bytes=64500 * 1024
        ),
    )(mod, *arrays)


def columns(n, step):
    return [(i, min(step, n - i)) for i in range(0, n, step)]


def on_device_chip(
    tokens,
    cond,
    mod_weight,
    mod_bias,
    query_key_value_weight,
    qkv_bias,
    attention_out_weight,
    attention_out_bias,
    first_hidden_weight,
    first_hidden_bias,
    second_hidden_weight,
    second_hidden_bias,
    out_grad,
):
    half, _, width = tokens.shape
    owned, _, cols = query_key_value_weight.shape
    head_size = width // HEADS
    heads_here = cols // head_size
    hidden = first_hidden_weight.shape[1]

    silu_cond, silu_back = jax.vjp(jax.nn.silu, cond.astype(F32))
    pieces = jnp.pad(
        silu_cond.astype(BF16).reshape(16, 1, owned), ((0, 0), (0, 7), (0, 128 - owned))
    )
    s_qkv = query_key_value_weight.reshape(1, owned, 3 * cols)
    small = jnp.stack(
        [
            jnp.pad(qkv_bias[0], (0, hidden - cols)),
            jnp.pad(qkv_bias[1], (0, hidden - cols)),
            first_hidden_bias,
        ]
    )
    small = jnp.pad(small, ((0, 5), (0, 0)))
    shards = [
        s_qkv,
        attention_out_weight.T.reshape(1, owned, cols),
        first_hidden_weight.reshape(1, owned, hidden),
        second_hidden_weight.T.reshape(1, owned, hidden),
    ]
    chunks = [(0, p, False) for p in columns(3 * cols, 896)] + [(1, None, False)]
    chunks += [(g, p, False) for g in (2, 3) for p in columns(hidden, 1152)]
    (
        modulation,
        silu_owned,
        fc2_bias_part,
        rows_a,
        qkv,
        attended,
        log_totals,
        branch_a,
        resid_mid,
        rows_m,
        act_low,
        slope,
        fc2_grad,
        grad_m,
        tokens_here,
        out_grad_here,
        w_qkv,
        w_proj,
        w_fc1,
        w_fc2,
    ) = forward_stage(
        pieces,
        mod_weight,
        mod_bias.astype(F32)[None],
        attention_out_bias.astype(F32)[None],
        small,
        tokens.reshape(half, width),
        out_grad.reshape(half, width),
        shards,
        head_size,
        chunks,
        2,
    )

    fc1_bias_part, fc2_out, fc1_grad, branch_m, normed_m_grad = hidden_back(
        second_hidden_bias.astype(F32)[None],
        grad_m,
        act_low,
        slope,
        rows_m,
        fc2_grad,
        w_fc2,
        w_fc1,
        columns(hidden, 768),
        4,
    )
    sums, fc1_out, proj_out, output, resid_grad, qkv_grad = attention_back(
        modulation,
        resid_mid,
        normed_m_grad,
        out_grad_here,
        branch_a,
        branch_m,
        w_proj,
        qkv,
        attended,
        log_totals,
        fc1_grad,
        [(0, p) for p in columns(hidden, 768)] + [(1, (0, cols))],
        5,
    )
    tokens_grad, qkv_out, silu_grad, mods_a, mods_b, wide, narrow = last_stage(
        modulation,
        sums,
        fc2_bias_part,
        fc1_bias_part,
        mod_weight,
        rows_a,
        qkv_grad,
        w_qkv,
        tokens_here,
        resid_grad,
        6,
    )
    mods = jnp.concatenate([mods_a[:, 0], mods_b[:, 0]], axis=1)
    mod_weight_grad = product(silu_owned[:, 0, :owned], mods, 0, 0)
    mod_bias_grad = jnp.sum(mods, axis=0, dtype=F32)
    wide, narrow = jnp.sum(wide[:, 0], axis=0), jnp.sum(narrow[:, 0], axis=0)
    step = (cols + 127) // 128 * 128
    qkv_bias_grad = jnp.stack([narrow[hidden + i * step :][:cols] for i in range(2)])
    cond_grad = silu_back(silu_grad[:, 0, :owned].reshape(1, width))[0]
    return (
        output.reshape(half, 1, width),
        tokens_grad.reshape(half, 1, width),
        cond_grad,
        mod_weight_grad,
        mod_bias_grad,
        jnp.moveaxis(qkv_out, 0, 1),
        qkv_bias_grad,
        proj_out.T,
        wide[:width],
        fc1_out,
        narrow[:hidden],
        fc2_out.T,
        wide[width:],
    )


def solution(mesh):
    shape = dict(mesh.shape)
    body = on_device_chip if shape == {"dp": 16, "tensor": 2} else on_device_general
    return jax.shard_map(
        body,
        mesh=mesh,
        in_specs=(
            P("tensor", "dp", None),
            P("dp", None),
            P("dp", None),
            P(),
            P("dp", None, "tensor"),
            P(None, "tensor"),
            P("tensor", "dp"),
            P(),
            P("dp", "tensor"),
            P("tensor"),
            P("tensor", "dp"),
            P(),
            P("tensor", "dp", None),
        ),
        out_specs=(
            P("tensor", "dp", None),
            P("tensor", "dp", None),
            P("dp", None),
            P("dp", None),
            P(),
            P("dp", None, "tensor"),
            P(None, "tensor"),
            P("tensor", "dp"),
            P(),
            P("dp", "tensor"),
            P("tensor"),
            P("tensor", "dp"),
            P(),
        ),
        check_vma=False,
    )
```

```python
import functools
import math

import jax
import jax.numpy as jnp
from jax import lax
from jax.experimental import pallas as pl
from jax.experimental.pallas import tpu as pltpu
from jax.sharding import PartitionSpec as P

HEADS = 16
MESH = pl.DeviceIdType.MESH
AXES = ("dp", "tensor")
F32 = jnp.float32
BF16 = jnp.bfloat16


def modulate(hidden, shifts, scales):
    center = hidden - jnp.mean(hidden, axis=-1, keepdims=True)
    spread = jnp.mean(center * center, axis=-1, keepdims=True)
    return center * lax.rsqrt(spread + 1e-06) * (1.0 + scales) + shifts


def gelu_tanh(values):
    return jax.nn.gelu(values, approximate=True)


def attend_forward(packed):
    queries = packed[:, 0]
    keys_all = packed[:, 1]
    values_all = packed[:, 2]
    seq_len = packed.shape[0]
    scaling = packed.shape[3] ** (-0.5)
    block_rows = min(512, seq_len)
    results = []
    log_parts = []
    for offset in range(0, seq_len, block_rows):
        query_block = queries[offset : offset + block_rows]
        scores = (
            jnp.einsum("qhe,khe->hqk", query_block, keys_all, preferred_element_type=jnp.float32)
            * scaling
        )
        highest = jnp.max(scores, axis=-1, keepdims=True)
        weights = jnp.exp(scores - highest)
        row_total = jnp.sum(weights, axis=-1, keepdims=True)
        prob_low = (weights / row_total).astype(jnp.bfloat16)
        mixture = jnp.einsum(
            "hqk,khe->qhe", prob_low, values_all, preferred_element_type=jnp.float32
        )
        results.append(mixture.reshape(block_rows, -1))
        log_parts.append((highest + jnp.log(row_total))[..., 0])
    return (jnp.concatenate(results, 0).astype(jnp.bfloat16), jnp.concatenate(log_parts, 1))


def attend_backward(inputs):
    packed, grad_out, log_totals = inputs
    queries = packed[:, 0]
    keys_all = packed[:, 1]
    values_all = packed[:, 2]
    seq_len = packed.shape[0]
    scaling = packed.shape[3] ** (-0.5)
    block_rows = min(512, seq_len)
    query_grads = []
    key_grad = jnp.zeros(keys_all.shape, jnp.float32)
    value_grad = jnp.zeros(values_all.shape, jnp.float32)
    for offset in range(0, seq_len, block_rows):
        query_block = queries[offset : offset + block_rows]
        grad_block = grad_out[offset : offset + block_rows]
        scores = (
            jnp.einsum("qhe,khe->hqk", query_block, keys_all, preferred_element_type=jnp.float32)
            * scaling
        )
        probs = jnp.exp(scores - log_totals[:, offset : offset + block_rows, None])
        prob_low = probs.astype(jnp.bfloat16)
        prob_grad = jnp.einsum(
            "qhe,khe->hqk", grad_block, values_all, preferred_element_type=jnp.float32
        )
        inner = jnp.sum(probs * prob_grad, axis=-1, keepdims=True)
        score_grad = (probs * (prob_grad - inner)).astype(jnp.bfloat16)
        query_grads.append(
            jnp.einsum("hqk,khe->qhe", score_grad, keys_all, preferred_element_type=jnp.float32)
            * scaling
        )
        key_grad = (
            key_grad
            + jnp.einsum(
                "hqk,qhe->khe", score_grad, query_block, preferred_element_type=jnp.float32
            )
            * scaling
        )
        value_grad = value_grad + jnp.einsum(
            "hqk,qhe->khe", prob_low, grad_block, preferred_element_type=jnp.float32
        )
    return jnp.stack([jnp.concatenate(query_grads, 0), key_grad, value_grad], 1).astype(
        jnp.bfloat16
    )


def on_device_general(
    tokens,
    cond,
    mod_weight,
    mod_bias,
    query_key_value_weight,
    qkv_bias,
    attention_out_weight,
    attention_out_bias,
    first_hidden_weight,
    first_hidden_bias,
    second_hidden_weight,
    second_hidden_bias,
    out_grad,
):
    w_mod, w_qkv, w_proj, w_fc1, w_fc2 = (
        lax.all_gather(mod_weight, "dp", axis=0, tiled=True),
        lax.all_gather(query_key_value_weight, "dp", axis=0, tiled=True),
        lax.all_gather(attention_out_weight, "dp", axis=1, tiled=True),
        lax.all_gather(first_hidden_weight, "dp", axis=0, tiled=True),
        lax.all_gather(second_hidden_weight, "dp", axis=1, tiled=True),
    )
    seq_local, latents, width = tokens.shape
    columns = query_key_value_weight.shape[2]
    head_size = width // HEADS
    heads_here = columns // head_size
    local_rows = seq_local * latents
    cond_wide = cond.astype(jnp.float32)
    silu_cond, silu_back = jax.vjp(jax.nn.silu, cond_wide)
    silu_low = silu_cond.astype(jnp.bfloat16)
    modulation = jnp.dot(silu_low, w_mod, preferred_element_type=jnp.float32) + mod_bias.astype(
        jnp.float32
    )
    pieces = modulation.reshape(latents, 6, width)
    hidden_in = tokens.astype(jnp.float32)
    attention_normalized, norm_a_back = jax.vjp(modulate, hidden_in, pieces[:, 0], pieces[:, 1])
    gathered_a = lax.all_gather(
        attention_normalized.astype(jnp.bfloat16), "tensor", axis=0, tiled=True
    )
    seq_len = gathered_a.shape[0]
    total_rows = seq_len * latents
    rows_a = gathered_a.reshape(total_rows, width)
    qkv_flat = w_qkv.reshape(width, 3 * columns)
    zero_row = jnp.zeros((columns,), jnp.float32)
    query_key_value_shift = jnp.stack(
        [qkv_bias[0].astype(jnp.float32), zero_row, qkv_bias[1].astype(jnp.float32)]
    )
    projected_output = (
        jnp.dot(rows_a, qkv_flat, preferred_element_type=jnp.float32).reshape(
            seq_len, latents, 3, columns
        )
        + query_key_value_shift
    )
    packed = jnp.moveaxis(projected_output.astype(jnp.bfloat16), 1, 0).reshape(
        latents, seq_len, 3, heads_here, head_size
    )
    attention_result, log_totals = lax.map(attend_forward, packed)
    attended_rows = jnp.moveaxis(attention_result, 0, 1).reshape(total_rows, columns)
    summed_a = lax.psum_scatter(
        jnp.dot(attended_rows, w_proj, preferred_element_type=jnp.float32).astype(jnp.bfloat16),
        "tensor",
        scatter_dimension=0,
        tiled=True,
    ).astype(jnp.float32)
    attention_branch = summed_a.reshape(seq_local, latents, width) + attention_out_bias.astype(
        jnp.float32
    )
    resid_mid = hidden_in + pieces[:, 2] * attention_branch
    feedforward_normalized, norm_m_back = jax.vjp(modulate, resid_mid, pieces[:, 3], pieces[:, 4])
    gathered_m = lax.all_gather(
        feedforward_normalized.astype(jnp.bfloat16), "tensor", axis=0, tiled=True
    )
    rows_m = gathered_m.reshape(total_rows, width)
    before_activation = jnp.dot(
        rows_m, w_fc1, preferred_element_type=jnp.float32
    ) + first_hidden_bias.astype(jnp.float32)
    gelu_activated, gelu_back = jax.vjp(gelu_tanh, before_activation)
    act_low = gelu_activated.astype(jnp.bfloat16)
    summed_m = lax.psum_scatter(
        jnp.dot(act_low, w_fc2, preferred_element_type=jnp.float32).astype(jnp.bfloat16),
        "tensor",
        scatter_dimension=0,
        tiled=True,
    ).astype(jnp.float32)
    feedforward_branch = summed_m.reshape(seq_local, latents, width) + second_hidden_bias.astype(
        jnp.float32
    )
    output = (resid_mid + pieces[:, 5] * feedforward_branch).astype(jnp.bfloat16)
    grad_out = out_grad.astype(jnp.float32)
    gate_m_grad = jnp.sum(grad_out * feedforward_branch, axis=0)
    grad_m_low = (grad_out * pieces[:, 5]).astype(jnp.bfloat16)
    grad_m_rows = lax.all_gather(grad_m_low, "tensor", axis=0, tiled=True).reshape(
        total_rows, width
    )
    fc2_bias_grad = jnp.sum(grad_m_rows, axis=0, dtype=jnp.float32)
    fc2_weight_grad = jnp.einsum(
        "rf,rd->fd", act_low, grad_m_rows, preferred_element_type=jnp.float32
    )
    act_grad = jnp.einsum("rd,fd->rf", grad_m_rows, w_fc2, preferred_element_type=jnp.float32)
    pre_grad = gelu_back(act_grad)[0].astype(jnp.bfloat16)
    fc1_bias_grad = jnp.sum(pre_grad, axis=0, dtype=jnp.float32)
    fc1_weight_grad = jnp.einsum("rd,rf->df", rows_m, pre_grad, preferred_element_type=jnp.float32)
    normed_m_grad = (
        lax.psum_scatter(
            jnp.einsum("rf,df->rd", pre_grad, w_fc1, preferred_element_type=jnp.float32).astype(
                jnp.bfloat16
            ),
            "tensor",
            scatter_dimension=0,
            tiled=True,
        )
        .astype(jnp.float32)
        .reshape(seq_local, latents, width)
    )
    resid_part, shift_m_grad, scale_m_grad = norm_m_back(normed_m_grad)
    resid_grad = grad_out + resid_part
    gate_a_grad = jnp.sum(resid_grad * attention_branch, axis=0)
    grad_a_low = (resid_grad * pieces[:, 2]).astype(jnp.bfloat16)
    grad_a_flat = grad_a_low.reshape(local_rows, width)
    proj_bias_part = jnp.sum(grad_a_flat, axis=0, dtype=jnp.float32)
    grad_a_rows = lax.all_gather(grad_a_low, "tensor", axis=0, tiled=True).reshape(
        total_rows, width
    )
    proj_weight_grad = jnp.einsum(
        "rc,rd->cd", attended_rows, grad_a_rows, preferred_element_type=jnp.float32
    )
    attended_grad = jnp.einsum(
        "rd,cd->rc", grad_a_rows, w_proj, preferred_element_type=jnp.float32
    ).astype(jnp.bfloat16)
    grad_packed = jnp.moveaxis(attended_grad.reshape(seq_len, latents, heads_here, head_size), 1, 0)
    qkv_grad_packed = lax.map(attend_backward, (packed, grad_packed, log_totals))
    qkv_grad_rows = jnp.moveaxis(qkv_grad_packed, 0, 1).reshape(total_rows, 3 * columns)
    bias_sums = jnp.sum(qkv_grad_rows.reshape(total_rows, 3, columns), axis=0, dtype=jnp.float32)
    qkv_bias_grad = jnp.stack([bias_sums[0], bias_sums[2]])
    qkv_weight_grad = jnp.einsum(
        "rd,rc->dc", rows_a, qkv_grad_rows, preferred_element_type=jnp.float32
    ).reshape(width, 3, columns)
    normed_a_grad = (
        lax.psum_scatter(
            jnp.einsum(
                "rc,dc->rd", qkv_grad_rows, qkv_flat, preferred_element_type=jnp.float32
            ).astype(jnp.bfloat16),
            "tensor",
            scatter_dimension=0,
            tiled=True,
        )
        .astype(jnp.float32)
        .reshape(seq_local, latents, width)
    )
    input_part, shift_a_grad, scale_a_grad = norm_a_back(normed_a_grad)
    tokens_grad = (resid_grad + input_part).astype(jnp.bfloat16)
    partial_mod = jnp.stack(
        [shift_a_grad, scale_a_grad, gate_a_grad, shift_m_grad, scale_m_grad, gate_m_grad], 1
    ).reshape(latents, 6 * width)
    mod_summed, proj_bias_grad = (
        lax.psum(partial_mod.astype(jnp.bfloat16), "tensor").astype(jnp.float32),
        lax.psum(proj_bias_part.astype(jnp.bfloat16), "tensor").astype(jnp.float32),
    )
    mod_grad_low = mod_summed.astype(jnp.bfloat16)
    silu_grad = jnp.einsum("le,de->ld", mod_grad_low, w_mod, preferred_element_type=jnp.float32)
    cond_grad = silu_back(silu_grad)[0]
    silu_every, mod_every = (
        lax.all_gather(silu_low, "dp", axis=0, tiled=True),
        lax.all_gather(mod_grad_low, "dp", axis=0, tiled=True),
    )
    owned_rows = mod_weight.shape[0]
    silu_owned = lax.dynamic_slice_in_dim(
        silu_every, lax.axis_index("dp") * owned_rows, owned_rows, 1
    )
    mod_weight_grad = jnp.einsum(
        "ld,le->de", silu_owned, mod_every, preferred_element_type=jnp.float32
    )
    mod_bias_grad = jnp.sum(mod_every, axis=0, dtype=jnp.float32)
    qkv_weight_grad, proj_weight_grad, fc1_weight_grad, fc2_weight_grad = (
        lax.psum_scatter(
            qkv_weight_grad.astype(jnp.bfloat16), "dp", scatter_dimension=0, tiled=True
        ).astype(jnp.float32),
        lax.psum_scatter(
            proj_weight_grad.astype(jnp.bfloat16), "dp", scatter_dimension=1, tiled=True
        ).astype(jnp.float32),
        lax.psum_scatter(
            fc1_weight_grad.astype(jnp.bfloat16), "dp", scatter_dimension=0, tiled=True
        ).astype(jnp.float32),
        lax.psum_scatter(
            fc2_weight_grad.astype(jnp.bfloat16), "dp", scatter_dimension=1, tiled=True
        ).astype(jnp.float32),
    )
    qkv_bias_grad, proj_bias_grad, fc1_bias_grad, fc2_bias_grad = lax.psum(
        (qkv_bias_grad, proj_bias_grad, fc1_bias_grad, fc2_bias_grad), "dp"
    )
    return (
        output,
        tokens_grad,
        cond_grad,
        mod_weight_grad,
        mod_bias_grad,
        qkv_weight_grad,
        qkv_bias_grad,
        proj_weight_grad,
        proj_bias_grad,
        fc1_weight_grad,
        fc1_bias_grad,
        fc2_weight_grad,
        fc2_bias_grad,
    )


def place():
    d = lax.axis_index("dp")
    y = lax.axis_index("tensor")
    return d, d // 4, (d // 2) % 2, d % 2, y


def neighbours(pos):
    d, z, x, c, y = pos
    sib = (z * 4 + x * 2 + (1 - c), y)
    xn = (z * 4 + (1 - x) * 2 + c, y)
    yn = (d, 1 - y)
    return sib, xn, yn


def z_peer(pos, k):
    d, z, x, c, y = pos
    return (((z + k) % 4) * 4 + x * 2 + c, y)


def z_order(z, k):
    return (z, z + 1 - 2 * (z % 2), 2 - z // 2, 3 - 3 * (z // 2))[k]


def greet(peers):
    sem = pltpu.get_barrier_semaphore()
    for peer in peers:
        pl.semaphore_signal(sem, inc=1, device_id=peer, device_id_type=MESH)
    pl.semaphore_wait(sem, len(peers))


def chip_peers(pos):
    d, z, x, c, y = pos
    across = [(z * 4 + x * 2 + 1 - c, 1 - y)]
    return list(neighbours(pos)) + across + [z_peer(pos, k) for k in (1, 2, 3)]


def remote(src, dst, send, recv, peer):
    return pltpu.make_async_remote_copy(
        src_ref=src, dst_ref=dst, send_sem=send, recv_sem=recv, device_id=peer, device_id_type=MESH
    )


Z_SENDS = (1, 2, 3)
GATHER_RECV = 24
GATHER_SEND = 32


def repeat(first, stop, action):
    def step(i, _):
        action(i)
        return 0

    lax.fori_loop(first, stop, step, 0)


class Gather:
    def __init__(self, shard, full, relay, cols, wide, recv, send, pos):
        self.wide = wide
        self.shard, self.full, self.relay, self.cols = shard, full, relay, cols
        self.recv, self.send, self.pos = recv, send, pos
        d, z, x, c, y = pos
        self.sib, self.xn, _ = neighbours(pos)
        self.far = (z * 4 + x * 2 + y, 1 - y)
        self.home, self.away = c == y, c != y

    def part(self, ref, b):
        if self.cols is None:
            return ref.at[pl.ds(b, 1)]
        return ref.at[pl.ds(b, 1), :, pl.ds(*self.cols)]

    def move(self, src, dst, s, r, peer):
        return remote(src, dst, self.send.at[s], self.recv.at[r], peer)

    def came(self, r):
        block = self.part(self.full, 0)
        self.move(block, block, 0, r, self.sib).wait_recv()

    def stay(self):
        return pltpu.make_async_copy(
            self.part(self.shard, 0), self.part(self.full, self.pos[0]), self.send.at[31]
        )

    def start(self):
        d, z, x, c, y = self.pos
        q = z * 2 + x
        own = self.part(self.shard, 0)

        @pl.when(self.home)
        def _():
            for k in Z_SENDS:
                peer = (z_order(z, k) * 4 + x * 2 + c, y)
                self.move(own, self.part(self.full, d), k, q, peer).start()
            self.move(own, self.part(self.full, d), 4, q, self.xn).start()
            self.move(own, self.part(self.full, d), 8, 8 + q, self.far).start()
            self.stay().start()

        @pl.when(self.away)
        def _():
            for k in Z_SENDS:
                peer = (z_order(z, k) * 4 + x * 2 + c, y)
                self.move(own, self.part(self.relay, q), k, q, peer).start()
            self.move(own, self.part(self.full, d), 8, 16 + q, self.far).start()
            self.move(own, self.part(self.relay, q), 4, q, self.xn).start()
            self.move(own, self.part(self.full, d), 16, 8 + q, self.sib).start()

    def from_z(self, k):
        d, z, x, c, y = self.pos
        q = z_order(z, k) * 2 + x
        dst = self.part(self.full, 2 * q + c)

        @pl.when(self.home)
        def _():
            self.came(q)
            self.move(dst, dst, 4 + k, q, self.xn).start()
            self.move(dst, dst, 8 + k, 8 + q, self.far).start()

        @pl.when(self.away)
        def _():
            self.came(q)
            src = self.part(self.relay, q)
            self.move(src, dst, 8 + k, 16 + q, self.far).start()
            self.move(src, src, 4 + k, q, self.xn).start()
            self.move(src, dst, 16 + k, 8 + q, self.sib).start()

    def from_x(self, k):
        d, z, x, c, y = self.pos
        q = z_order(z, k) * 2 + 1 - x
        dst = self.part(self.full, 2 * q + c)

        @pl.when(self.home)
        def _():
            self.came(q)
            if self.wide != 1:
                self.move(dst, dst, 12 + k, 8 + q, self.far).start()

        @pl.when(self.away)
        def _():
            self.came(q)
            if self.wide == 2:
                self.move(self.part(self.relay, q), dst, 12 + k, 16 + q, self.far).start()
            self.move(self.part(self.relay, q), dst, 20 + k, 8 + q, self.sib).start()

    def from_y(self, k):
        d, z, x, c, y = self.pos
        q = z_order(z, k) * 2 + x

        @pl.when(self.away)
        def _():
            block = self.part(self.full, 2 * q + 1 - c)
            if self.wide != 2:
                self.came(16 + q)
                self.move(block, block, 12 + k, 16 + q, self.xn).start()
            if self.wide == 1:
                block = self.part(self.full, 2 * q + c)
                self.came(8 + q)
                self.move(block, block, 24 + k, 8 + q, self.xn).start()

    def ready(self):
        d, z, x, c, y = self.pos

        @pl.when(self.home)
        def _():
            repeat(0, 8, lambda q: self.came(8 + q))
            self.stay().wait()

        @pl.when(self.away)
        def _():
            def other(k):
                self.came(16 + 2 * k + 1 - x)
                self.came(8 + 2 * k + 1 - x)
                if self.wide != 1:
                    self.came(8 + 2 * k + x)
                if self.wide == 2:
                    self.came(16 + 2 * k + x)

            repeat(0, 4, other)

    def finish(self):
        block = self.part(self.full, 0)

        def sent(s):
            self.move(block, block, s, 0, self.sib).wait_send()

        repeat(1, 12, sent)
        if self.wide != 1:
            pl.when(self.home)(lambda: repeat(12, 16, sent))
        pl.when(self.away)(lambda: repeat(12, 28 if self.wide == 1 else 24, sent))

    def early(self):
        return [functools.partial(self.from_z, k) for k in (1, 2, 3)]

    def late(self):
        steps = []
        for k in range(4):
            steps += [functools.partial(self.from_x, k), functools.partial(self.from_y, k)]
        return steps + [self.ready]


def gather_events(parts, lead=2):
    n = len(parts)
    events = [p.start for p in parts[:lead]]
    for i in range(n + 1):
        if i < n:
            events += parts[i].early()
        if i + lead < n:
            events.append(parts[i + lead].start)
        if i > 0:
            events += parts[i - 1].late()
    return events


def gather_parts(shards, fulls, relays, chunks, recv, send, pos):
    return [
        Gather(shards[g], fulls[g], relays[g], cols, wide, recv.at[i], send.at[i], pos)
        for i, (g, cols, wide) in enumerate(chunks)
    ]


def gather_sems(chunks):
    n = len(chunks)
    return [
        pltpu.SemaphoreType.DMA((n, GATHER_RECV)),
        pltpu.SemaphoreType.DMA((n, GATHER_SEND)),
    ]


def gather_shapes(shards):
    return [jax.ShapeDtypeStruct((16,) + s.shape[1:], s.dtype) for s in shards] + [
        jax.ShapeDtypeStruct((8,) + s.shape[1:], s.dtype) for s in shards
    ]


REDUCE_RECV = 27
REDUCE_SEND = 23


class Reduce:
    def __init__(self, grad, land, out, recv, send, pos, cols):
        self.grad, self.land, self.out = grad, land, out
        self.recv, self.send, self.pos, self.cols = recv, send, pos, pl.ds(*cols)
        d, z, x, c, y = pos
        self.sib, self.xn, self.yn = neighbours(pos)
        self.home, self.away = c == y, c != y

    def rows(self, b):
        return self.grad.at[pl.ds(b, 1), :, self.cols]

    def slot(self, i):
        return self.land.at[pl.ds(i, 1)]

    def push(self, src, slot, s, peer):
        return remote(src, self.slot(slot), self.send.at[s], self.recv.at[slot], peer)

    def came(self, slot):
        self.push(self.slot(slot), slot, 0, self.sib).wait_recv()

    def value(self, i, r):
        return self.land[i, r].astype(F32)

    def by_rows(self, body):
        def step(i, _):
            body(pl.ds(pl.multiple_of(i * 8, 8), 8))
            return 0

        lax.fori_loop(0, 9, step, 0)

    def first(self):
        d, z, x, c, y = self.pos

        @pl.when(self.away)
        def _():
            for column, base in ((1 - x, 0), (x, 4)):

                def step(k, _):
                    q = lax.rem(z + 1 + k, 4) * 2 + column
                    self.push(self.rows(2 * q + c), q, base + k, self.yn).start()
                    self.push(self.rows(2 * q + 1 - c), 15 + q, 8 + base + k, self.sib).start()
                    return 0

                lax.fori_loop(0, 4, step, 0)

        @pl.when(self.home)
        def _():
            for column, base in ((1 - x, 0), (x, 4)):

                def step(k, _):
                    q = lax.rem(z + 1 + k, 4) * 2 + column
                    self.push(self.rows(2 * q + 1 - c), q, base + k, self.sib).start()
                    return 0

                lax.fori_loop(0, 4, step, 0)

    def second(self, k):
        d, z, x, c, y = self.pos
        zz = (z + 1 + k) % 4
        q = zz * 2 + 1 - x

        @pl.when(self.away)
        def _():
            self.came(q)
            self.push(self.slot(q), 8 + zz, 16 + k, self.xn).start()

        @pl.when(self.home)
        def _():
            self.came(15 + q)
            self.push(self.slot(15 + q), 23 + zz, 15 + k, self.xn).start()
            b = 2 * q + c
            self.came(q)

            def add(r):
                total = self.grad[b, r, self.cols].astype(F32) + self.value(q, r)
                self.grad[b, r, self.cols] = total.astype(BF16)

            self.by_rows(add)
            self.push(self.rows(b), 8 + zz, 8 + k, self.xn).start()

    def third(self, k):
        d, z, x, c, y = self.pos
        zz = (z + 1 + k) % 4
        q = zz * 2 + x

        @pl.when(self.home)
        def _():
            self.came(15 + q)
            self.came(23 + zz)

            def add(r):
                self.land[15 + q, r] = (self.value(15 + q, r) + self.value(23 + zz, r)).astype(BF16)

            self.by_rows(add)
            self.push(self.slot(15 + q), 15 + zz, 19 + k, self.yn).start()
            if k < 3:
                b = 2 * q + c
                self.came(q)
                self.came(8 + zz)

                def add_two(r):
                    total = self.grad[b, r, self.cols].astype(F32)
                    total = total + self.value(q, r) + self.value(8 + zz, r)
                    self.grad[b, r, self.cols] = total.astype(BF16)

                self.by_rows(add_two)
                self.push(self.rows(b), 12 + k, 12 + k, (zz * 4 + x * 2 + c, y)).start()

    def fourth(self, k):
        d, z, x, c, y = self.pos
        zz = (z + 1 + k) % 4
        q = zz * 2 + x

        @pl.when(self.away)
        def _():
            self.came(q)
            self.came(8 + zz)
            self.came(15 + zz)

            def add(r):
                total = self.value(q, r) + self.value(8 + zz, r) + self.value(15 + zz, r)
                self.land[q, r] = total.astype(BF16)

            self.by_rows(add)
            self.push(self.slot(q), 12 + k, 20 + k, (zz * 4 + x * 2 + c, y)).start()

    def fifth(self):
        d, z, x, c, y = self.pos
        q = z * 2 + x
        self.came(q)
        self.came(8 + z)
        for k in range(3):
            self.came(12 + k)
        pl.when(self.away)(lambda: self.came(15 + z))

        def add(r):
            total = self.value(q, r) + self.value(8 + z, r)
            total = total + self.value(12, r) + self.value(13, r) + self.value(14, r)

            @pl.when(self.home)
            def _():
                self.out[r, self.cols] = total + self.grad[d, r, self.cols].astype(F32)

            @pl.when(self.away)
            def _():
                self.out[r, self.cols] = total + self.value(15 + z, r)

        self.by_rows(add)

    def finish(self):
        block = self.slot(0)
        repeat(0, REDUCE_SEND, lambda s: self.push(block, 0, s, self.sib).wait_send())


def reduce_events(parts, lead=1):
    n = len(parts)
    events = [p.first for p in parts[:lead]]
    for i in range(n + 3):
        if i + lead < n:
            events.append(parts[i + lead].first)
        for k in range(4):
            if i < n:
                events.append(functools.partial(parts[i].second, k))
            if 0 <= i - 1 < n:
                events.append(functools.partial(parts[i - 1].third, k))
            if 0 <= i - 2 < n and k < 3:
                events.append(functools.partial(parts[i - 2].fourth, k))
        if 0 <= i - 3 < n:
            events.append(parts[i - 3].fifth)
    return events


def reduce_scratch(chunks):
    n = len(chunks)
    return [pltpu.VMEM((27, 72, cols[1]), BF16) for _, cols in chunks] + [
        pltpu.SemaphoreType.DMA((n, REDUCE_RECV)),
        pltpu.SemaphoreType.DMA((n, REDUCE_SEND)),
    ]


class Pump:
    def __init__(self, events):
        self.events, self.next = list(events), 0

    def run(self, count=None):
        stop = len(self.events)
        if count is not None:
            stop = min(stop, self.next + max(0, count))
        for event in self.events[self.next : stop]:
            event()
        self.next = stop

    def loop(self, steps, body, count=0):
        todo = self.events[self.next :][:count]
        self.next += len(todo)

        def step(i, _):
            for j, event in enumerate(todo):
                pl.when(i == j * steps // count)(event)
            body(i)
            return 0

        lax.fori_loop(0, steps, step, 0)


def flat(value):
    return value.reshape(-1, value.shape[-1])


def product(a, b, ca, cb):
    return lax.dot_general(a, b, (((ca,), (cb,)), ((), ())), preferred_element_type=F32)


def loader(sems):
    count = iter(range(64))

    def load(src, dst):
        copy = pltpu.make_async_copy(src, dst, sems.at[next(count)])
        copy.start()
        return copy.wait

    return load


def norm_back_rows(value, g, scale_up):
    center = value - jnp.mean(value, axis=-1, keepdims=True)
    rate = lax.rsqrt(jnp.mean(center * center, axis=-1, keepdims=True) + 1e-06)
    normed = center * rate
    e = g * scale_up
    inner = jnp.mean(e * normed, axis=-1, keepdims=True)
    return rate * (e - jnp.mean(e, axis=-1, keepdims=True) - normed * inner), normed


def row_sum(value):
    return jnp.sum(value, axis=0, keepdims=True)


def last_kernel(
    mod_ref, sums_ref, fc2_bias_ref, fc1_bias_ref, w_ref,
    rows_in, dqkv_in, wqkv_in, tokens_in, resid_in,
    tgrad_ref, qkv_out, sg_ref, mods_a, mods_b, b2, b3,
    rows_ref, dqkv_ref, wqkv_ref, tokens_ref, resid_ref, tsend, half_ref,
    grad, ngrad, sent, got, v1, v1_in, v2, v2_in, sgp, land0, land1, land2,
    load_sems, s0, s1, r1, s2, r2, s3, r3, s4, r4, s5, r5, recv, send,
):
    pos = place()
    d, z, x, c, y = pos
    sib = neighbours(pos)[0]
    far = (z * 4 + x * 2 + 1 - c, 1 - y)
    lin = d * 2 + y
    half, width = tokens_ref.shape
    heads = dqkv_ref.shape[0] // 3
    load = loader(load_sems)
    ready = [load(dqkv_in, dqkv_ref), load(rows_in, rows_ref)]
    ready_late = [
        load(*pair)
        for pair in ((wqkv_in, wqkv_ref), (tokens_in, tokens_ref), (resid_in, resid_ref))
    ]
    greet([(((lin + k) % 32) // 2, (lin + k) % 2) for k in range(1, 32)])
    me = (z * 2 + x) * 2 + y
    sgp[...] = jnp.zeros_like(sgp)
    n = dqkv_ref.shape[1] * heads
    hidden = fc1_bias_ref.shape[1]
    for wait in ready:
        wait()

    half_ref[...] = jnp.zeros_like(half_ref)
    half_ref[:, :hidden] = fc1_bias_ref[...]
    ones = jnp.ones((8, 2 * half), BF16)
    for j, at in ((0, hidden), (2, hidden + (n + 127) // 128 * 128)):
        value = product(ones, flat(dqkv_ref[j * heads : (j + 1) * heads]), 1, 1)
        half_ref[:, at : at + n] = value[0:1, :]

    for i in range(6):
        early = sums_ref[i : i + 1, :] if i < 5 else fc2_bias_ref[...]
        v2[:, i * width : (i + 1) * width] = early
    swap_early = remote(v2, v2_in, s0.at[2], s0.at[3], sib)
    swap_early.start()

    @pl.when(y == c)
    def _():
        b3[me] = half_ref[...]

    def send3(q, core):
        s = q * 2 + core
        return remote(half_ref, b3.at[me], s3.at[s], r3.at[me], (s, c))

    def each3(action):
        for q in range(8):
            for core in range(2):
                pl.when(jnp.logical_or(d != q * 2 + core, y != c))(
                    functools.partial(action, q, core)
                )

    reducers = [
        Reduce(grad.at[j], land, qkv_out.at[j], recv.at[j], send.at[j], pos, (0, n))
        for j, land in enumerate((land0, land1, land2))
    ]

    def weight_grad(j, _):
        value = product(rows_ref[...], flat(dqkv_ref[pl.ds(j * heads, heads)]), 0, 1)
        grad[j] = value.reshape(grad.shape[1:]).astype(BF16)
        for i, reducer in enumerate(reducers):
            pl.when(j == i)(reducer.first)
        return 0

    lax.fori_loop(0, 3, weight_grad, 0)
    each3(lambda q, core: send3(q, core).start())
    pump = Pump(reduce_events(reducers, 3)[3:])

    def chip(k):
        m = (me + k) % 16
        return m, ((m // 2) * 2 + c, m % 2)

    def to_chip(buf, send, recv, k):
        return remote(buf.at[me], buf.at[me], send.at[k], recv.at[me], chip(k)[1])

    def from_chip(buf, send, recv, k):
        m, peer = chip(k)
        return remote(buf.at[m], buf.at[m], send.at[k], recv.at[m], peer)

    last, wide, known = (mods_a, s1, r1), (b2, s2, r2), (mods_b, s5, r5)
    swap_early.wait()
    mods_b[me] = (v2[:, : 4 * width] + v2_in[:, : 4 * width]).astype(BF16)
    b2[me] = v2[:, 4 * width :] + v2_in[:, 4 * width :]
    for k in range(1, 16):
        to_chip(*known, k).start()
        to_chip(*wide, k).start()
    for wait in ready_late:
        wait()

    tile = half // 2
    swap = remote(sent, got, s0.at[4], s0.at[5], sib)

    def into_norm(i):
        part = pl.ds(pl.multiple_of(lax.rem(i + 2, 4) * tile, tile), tile)
        value = product(flat(dqkv_ref[:, :, part]), flat(wqkv_ref[...]), 0, 1)

        @pl.when(i < 2)
        def _():
            sent[pl.ds(pl.multiple_of(i * tile, tile), tile), :] = value.astype(BF16)

        @pl.when(i >= 2)
        def _():
            ngrad[part, :] = value

        pl.when(i == 1)(lambda: swap.start())

    pump.loop(4, into_norm, 12)
    swap.wait()
    piece = half // 8
    scale = 1.0 + mod_ref[:, width : 2 * width]
    v1[...] = jnp.zeros_like(v1)

    def norm_back(i):
        part = pl.ds(pl.multiple_of(i * piece, piece), piece)
        g = ngrad[part, :] + got[part, :].astype(F32)
        back, normed = norm_back_rows(tokens_ref[part, :].astype(F32), g, scale)
        value = (resid_ref[part, :] + back).astype(BF16)

        @pl.when(y == c)
        def _():
            tgrad_ref[part, :] = value

        @pl.when(y != c)
        def _():
            tsend[part, :] = value

        v1[:, :width] += row_sum(g)
        v1[:, width : 2 * width] += row_sum(g * normed)

    pump.loop(8, norm_back, 8)
    trade = remote(tsend, tgrad_ref, s0.at[6], s0.at[7], far)
    pl.when(y != c)(lambda: trade.start())

    swap = remote(v1, v1_in, s0.at[0], s0.at[1], sib)
    swap.start()
    pump.run(2)
    swap.wait()
    mods_a[me] = (v1[...] + v1_in[...]).astype(BF16)
    for k in range(1, 16):
        to_chip(*last, k).start()

    def rows_of(buf):
        return jnp.concatenate([buf[i].astype(F32) for i in range(16)], axis=0)

    def back_of(buf, at):
        every = rows_of(buf).astype(BF16)
        return product(every, w_ref[:, at : at + every.shape[1]], 1, 1)

    pump.run(8)
    for k in range(1, 16):
        from_chip(*known, k).wait_recv()
    back = back_of(mods_b, 2 * width)
    pump.run(2)
    for k in range(1, 16):
        from_chip(*last, k).wait_recv()
    back = back + back_of(mods_a, 0)
    for i in range(16):
        sgp[i, 0:1, :72] = back[i : i + 1, :]

    def send4(k):
        m = (d + k) % 16
        return remote(sgp.at[m], sg_ref.at[d], s4.at[k], r4.at[d], (m, y))

    for k in range(1, 16):
        send4(k).start()
    sg_ref[d] = sgp[d]
    pump.run(4)
    for k in range(1, 16):
        from_chip(*wide, k).wait_recv()

    def arrive3(i):
        remote(half_ref, b3.at[i], s3.at[0], r3.at[i], sib).wait_recv()

    for i in range(16):
        pl.when(jnp.logical_or(i != me, y != c))(functools.partial(arrive3, i))
    for k in range(1, 16):
        m = (d + k) % 16
        remote(sgp.at[m], sg_ref.at[m], s4.at[k], r4.at[m], (m, y)).wait_recv()
    pump.run()
    for reducer in reducers:
        reducer.finish()
    pl.when(y != c)(lambda: trade.wait())
    each3(lambda q, core: send3(q, core).wait_send())
    for k in range(1, 16):
        for buf in (last, wide, known):
            to_chip(*buf, k).wait_send()
        send4(k).wait_send()


def last_stage(
    mod, sums, fc2_bias, fc1_bias, w_mod, rows, dqkv, w_qkv, tokens, resid, collective_id
):
    vmem, anywhere = pl.BlockSpec(memory_space=pltpu.VMEM), pl.BlockSpec(memory_space=pl.ANY)
    n = w_mod.shape[1]
    half, width = tokens.shape
    cols = dqkv.shape[0] * dqkv.shape[1] // 3
    n2, n3 = 2 * width, fc1_bias.shape[1] + 2 * ((cols + 127) // 128 * 128)
    dma = pltpu.SemaphoreType.DMA((16,))
    shape = jax.ShapeDtypeStruct
    loaded = (rows, dqkv, w_qkv, tokens, resid)
    return pl.pallas_call(
        last_kernel,
        out_shape=[
            shape((half, width), BF16),
            shape((3, 72, cols), F32),
            shape((16, 8, 128), F32),
            shape((16, 1, n // 3), BF16),
            shape((16, 1, n - n // 3), BF16),
            shape((16, 1, n2), F32),
            shape((16, 1, n3), F32),
        ],
        in_specs=[vmem] * 5 + [anywhere] * 5,
        out_specs=[vmem] * 7,
        scratch_shapes=[pltpu.VMEM(a.shape, a.dtype) for a in loaded]
        + [
            pltpu.VMEM((half, width), BF16),
            pltpu.VMEM((1, n3), F32),
            pltpu.VMEM((3, 16, 72, cols), BF16),
            pltpu.VMEM((half, width), F32),
            pltpu.VMEM((half, width), BF16),
            pltpu.VMEM((half, width), BF16),
            pltpu.VMEM((1, n // 3), F32),
            pltpu.VMEM((1, n // 3), F32),
            pltpu.VMEM((1, n), F32),
            pltpu.VMEM((1, n), F32),
            pltpu.VMEM((16, 8, 128), F32),
        ]
        + [pltpu.VMEM((27, 72, cols), BF16)] * 3
        + [pltpu.SemaphoreType.DMA((8,)), pltpu.SemaphoreType.DMA((8,))]
        + [dma] * 10
        + [
            pltpu.SemaphoreType.DMA((3, REDUCE_RECV)),
            pltpu.SemaphoreType.DMA((3, REDUCE_SEND)),
        ],
        compiler_params=pltpu.CompilerParams(
            collective_id=collective_id, has_side_effects=True, vmem_limit_bytes=64500 * 1024
        ),
    )(mod, sums, fc2_bias, fc1_bias, w_mod, *loaded)


LOG2E = math.log2(math.e)


def attention_step(qkv, out, lse, block, scale):
    heads, blocks = qkv.shape[0] // 3, qkv.shape[2] // block
    factor = scale * LOG2E

    def body(i):
        h = i // blocks
        cols = pl.ds(pl.multiple_of((i % blocks) * block, block), block)
        scores = product(qkv[heads + h], qkv[h, :, cols], 0, 0)
        top = jnp.max(scores, axis=0, keepdims=True)
        probs = jnp.exp2((scores - top) * factor)
        total = jnp.sum(probs, axis=0, keepdims=True)
        mixed = product(qkv[2 * heads + h], probs.astype(BF16), 1, 0)
        out[h, :, cols] = (mixed / total).astype(BF16)
        lse[h, :, cols] = top * factor + jnp.log2(total)

    return heads * blocks, body


GELU = math.sqrt(2 / math.pi)


def gelu_and_slope(v):
    square = v * v
    t = jnp.tanh(v * (GELU + GELU * 0.044715 * square))
    half = 0.5 * (1.0 + t)
    return v * half, half + 0.5 * v * (1.0 - t * t) * (GELU + GELU * 3 * 0.044715 * square)


def forward_kernel(
    chunks, block, scale,
    piece_ref, w_mod, mod_bias, proj_bias, small_in, tokens_in, grad_in,
    s_qkv, s_proj, s_fc1, s_fc2,
    mod, silu_ref, fc2_bias_grad,
    rows_a_out, qkv_out, attended_out, lse_out, branch_out, resid_out, rows_out, act_out,
    slope_out, fc2_grad_out, grad_m_out, tokens_out, grad_out,
    w_qkv, w_proj, w_fc1, w_fc2, relay_qkv, relay_proj, relay_1, relay_2,
    part, land, mine, other, small, tokens, out_grad,
    rows_a, qkv, out, lse, branch, resid, rows, act, slope, fc2_grad, grad_m,
    qkv_here, proj_here, weight_here, sent, got,
    s1, r1, s2, r2, sems, out_sems, recv, send,
):
    pos = place()
    d, z, x, c, y = pos
    sib, _, yn = neighbours(pos)
    far = (z * 4 + x * 2 + 1 - c, 1 - y)
    half, width = tokens.shape
    home, away = c == y, c != y
    greet([((d + k) % 16, y) for k in range(1, 16)] + [yn, far])

    stores = []

    def store(src, dst):
        copy = pltpu.make_async_copy(src, dst, out_sems.at[len(stores)])
        copy.start()
        stores.append(copy)

    def swapped(src, dst, i):
        there = remote(src, dst, sems.at[i], sems.at[i + 1], far)
        here = pltpu.make_async_copy(src, dst, sems.at[i + 1])

        def start():
            pl.when(away)(lambda: there.start())
            pl.when(home)(lambda: here.start())

        def wait():
            pl.when(away)(lambda: there.wait())
            pl.when(home)(lambda: here.wait())

        return start, wait

    def piece(k):
        to = (d + k) % 16
        return remote(piece_ref.at[to], silu_ref.at[d], s1.at[k], r1.at[d], (to, y))

    def piece_in(k):
        src = (d + k) % 16
        return remote(piece_ref.at[src], silu_ref.at[src], s1.at[k], r1.at[src], (src, y))

    for k in range(1, 16):
        piece(k).start()
    small_start, small_wait = swapped(small_in, small, 7)
    tokens_start, tokens_wait = swapped(tokens_in, tokens, 9)
    grad_start, grad_wait = swapped(grad_in, out_grad, 11)
    small_start()
    tokens_start()
    parts = gather_parts(
        [s_qkv, s_proj, s_fc1, s_fc2],
        [w_qkv, w_proj, w_fc1, w_fc2],
        [relay_qkv, relay_proj, relay_1, relay_2],
        chunks,
        recv,
        send,
        pos,
    )
    last_of = {g: parts[i].ready for i, (g, _, _) in enumerate(chunks)}
    events = gather_events(parts)
    pump = Pump(events)

    def until_ready(g):
        pump.run(events.index(last_of[g]) + 1 - pump.next)

    pump.run(6)
    silu_ref[d] = piece_ref[d]
    for k in range(1, 16):
        piece_in(k).wait_recv()
    some = jnp.concatenate(
        [silu_ref[2 * q + y].astype(F32)[0:1, :] for q in range(8)], axis=0
    ).astype(BF16)[:, :72]
    for j in range(6):
        cols = slice(j * width, (j + 1) * width)
        value = jnp.dot(some, w_mod[:, cols], preferred_element_type=F32)
        for q in range(8):
            part[q, :, cols] = value[q : q + 1, :]
    me = z * 2 + x

    def send_part(k):
        q = (me + k) % 8
        return remote(part.at[q], land.at[me], s2.at[k], r2.at[me], (q * 2 + c, y))

    def part_in(k):
        q = (me + k) % 8
        return remote(part.at[q], land.at[q], s2.at[k], r2.at[q], (q * 2 + c, y))

    for k in range(1, 8):
        send_part(k).start()
    land[me] = part[me]
    pump.run(10)
    for k in range(1, 8):
        part_in(k).wait_recv()
    total = land[0]
    for q in range(1, 8):
        total = total + land[q]
    mine[...] = total
    swap = remote(mine, other, sems.at[13], sems.at[14], sib)
    swap.start()
    pump.run(4)
    for k in range(1, 16):
        piece(k).wait_send()
    for k in range(1, 8):
        send_part(k).wait_send()
    swap.wait()
    mod[...] = mine[...] + other[...] + mod_bias[...]
    shift_a, scale_a, gate_a, shift_m, scale_m, gate_m = [
        mod[:, i * width : (i + 1) * width] for i in range(6)
    ]
    small_wait()
    tokens_wait()

    tall = half // 8

    def norm_rows(value, shift, scale_up):
        center = value - jnp.mean(value, axis=-1, keepdims=True)
        spread = jnp.mean(center * center, axis=-1, keepdims=True)
        normed = center * lax.rsqrt(spread + 1e-06) * (1.0 + scale_up) + shift
        return normed.astype(BF16)

    def first_norm(i, _):
        own = pl.ds(pl.multiple_of(i * tall, tall), tall)
        rows_a[own, :] = norm_rows(tokens[own, :].astype(F32), shift_a, scale_a)
        return 0

    lax.fori_loop(0, 8, first_norm, 0)
    share = remote(rows_a.at[:half], rows_a.at[half:], sems.at[5], sems.at[6], sib)
    share.start()
    until_ready(0)
    heads = qkv.shape[0] // 3
    cols = heads * qkv.shape[1]
    load = pltpu.make_async_copy(w_qkv, qkv_here, sems.at[0])
    load.start()
    grad_start()
    pump.run(2)
    load.wait()
    share.wait()
    store(rows_a, rows_a_out)
    store(tokens, tokens_out)
    row = lax.broadcasted_iota(jnp.int32, (8, 2 * half), 0)
    for j in range(3):
        weight = flat(qkv_here[:, :, j * cols : (j + 1) * cols])
        value = product(weight, rows_a[...], 0, 1)
        if j != 1:
            pick = jnp.where(row == j // 2, 1.0, 0.0).astype(BF16)
            value = value + product(small[:, :cols], pick, 0, 0)
        value = value.reshape((heads,) + qkv.shape[1:])
        qkv[pl.ds(j * heads, heads)] = value.astype(BF16)
        pump.run(2)
    store(qkv, qkv_out)
    steps, body = attention_step(qkv, out, lse, block, scale)
    pump.loop(steps, body, 22)
    store(out, attended_out)
    store(lse, lse_out)
    until_ready(1)

    load = pltpu.make_async_copy(w_proj, proj_here, sems.at[0])
    load.start()
    load.wait()
    tile = half // 2
    swap = remote(sent, got, sems.at[1], sems.at[2], sib)

    def project(i, _):
        part = pl.ds(pl.multiple_of(lax.rem(i + 2, 4) * tile, tile), tile)
        value = product(flat(out[:, :, part]), flat(proj_here[...]), 0, 1)

        @pl.when(i < 2)
        def _():
            sent[pl.ds(pl.multiple_of(i * tile, tile), tile), :] = value.astype(BF16)

        @pl.when(i >= 2)
        def _():
            branch[part, :] = value + proj_bias[...]

        pl.when(i == 1)(lambda: swap.start())
        return 0

    lax.fori_loop(0, 4, project, 0)
    pump.run(2)
    grad_wait()
    store(out_grad, grad_out)

    def gated(i, total):
        own = pl.ds(pl.multiple_of(i * tall, tall), tall)
        value = (out_grad[own, :].astype(F32) * gate_m).astype(BF16)
        grad_m[own, :] = value
        return total + jnp.sum(value.astype(F32), axis=0, keepdims=True)

    fc2_bias_grad[...] = lax.fori_loop(0, 8, gated, jnp.zeros((1, width), F32))
    share_m = remote(grad_m.at[:half], grad_m.at[half:], sems.at[15], sems.at[16], sib)
    share_m.start()
    swap.wait()
    share = remote(rows.at[:half], rows.at[half:], sems.at[3], sems.at[4], sib)

    def norm(i, _):
        own = pl.ds(pl.multiple_of(i * tall, tall), tall)
        total = branch[own, :] + got[own, :].astype(F32)
        branch[own, :] = total
        mid = tokens[own, :].astype(F32) + gate_a * total
        resid[own, :] = mid
        rows[own, :] = norm_rows(mid, shift_m, scale_m)
        return 0

    lax.fori_loop(0, 8, norm, 0)
    share.start()
    store(branch, branch_out)
    store(resid, resid_out)
    until_ready(2)

    load = pltpu.make_async_copy(w_fc1, weight_here, sems.at[0])
    load.start()
    load.wait()
    share.wait()
    store(rows, rows_out)
    n = 256
    hidden_steps = act.shape[1] // n

    def hidden(i):
        cols = pl.ds(pl.multiple_of(i * n, n), n)
        bias = small[:, cols].astype(F32)[2:3, :]
        value, rate = gelu_and_slope(
            product(rows[...], flat(weight_here[:, :, cols]), 1, 0) + bias
        )
        act[:, cols] = value.astype(BF16)
        slope[:, cols] = rate.astype(BF16)

    pump.loop(hidden_steps, hidden, hidden_steps)
    store(act, act_out)
    store(slope, slope_out)
    share_m.wait()
    store(grad_m, grad_m_out)

    def weight_grad(i):
        cols = pl.ds(pl.multiple_of(i * n, n), n)
        value = product(grad_m[...], act[:, cols], 0, 0)
        fc2_grad[:, :, cols] = value.reshape(fc2_grad.shape[:2] + (n,)).astype(BF16)

    pump.loop(hidden_steps, weight_grad, hidden_steps)
    store(fc2_grad, fc2_grad_out)
    pump.run()
    for p in parts:
        p.finish()
    for copy in stores:
        copy.wait()


def forward_stage(
    pieces, w_mod, mod_bias, proj_bias, small, tokens, out_grad, shards, size, chunks,
    collective_id, block=512,
):
    half, width = tokens.shape
    count = 2 * half
    owned, cols = shards[1].shape[1:]
    heads = cols // size
    hidden = shards[2].shape[2]
    n = w_mod.shape[1]
    vmem, anywhere = pl.BlockSpec(memory_space=pltpu.VMEM), pl.BlockSpec(memory_space=pl.ANY)
    shape, dma = jax.ShapeDtypeStruct, pltpu.SemaphoreType.DMA
    kept = [
        ((count, width), BF16),
        ((3 * heads, size, count), BF16),
        ((heads, size, count), BF16),
        ((heads, 1, count), F32),
        ((half, width), F32),
        ((half, width), F32),
        ((count, width), BF16),
        ((count, hidden), BF16),
        ((count, hidden), BF16),
        ((16, owned, hidden), BF16),
        ((count, width), BF16),
    ]
    swap = ((half, width), BF16)
    return pl.pallas_call(
        functools.partial(forward_kernel, chunks, block, size**-0.5),
        out_shape=[shape((1, n), F32), shape((16, 8, 128), BF16), shape((1, width), F32)]
        + [shape(*k) for k in kept + [swap, swap]]
        + gather_shapes(shards),
        in_specs=[vmem] * 5 + [anywhere] * 6,
        out_specs=[vmem] * 3 + [anywhere] * 21,
        scratch_shapes=[
            pltpu.VMEM((8, 1, n), F32),
            pltpu.VMEM((8, 1, n), F32),
            pltpu.VMEM((1, n), F32),
            pltpu.VMEM((1, n), F32),
            pltpu.VMEM(small.shape, BF16),
            pltpu.VMEM(*swap),
            pltpu.VMEM(*swap),
        ]
        + [pltpu.VMEM(*k) for k in kept]
        + [
            pltpu.VMEM((16, owned, 3 * cols), BF16),
            pltpu.VMEM((16, owned, cols), BF16),
            pltpu.VMEM((16, owned, hidden), BF16),
            pltpu.VMEM(*swap),
            pltpu.VMEM(*swap),
            dma((16,)),
            dma((16,)),
            dma((8,)),
            dma((8,)),
            dma((17,)),
            dma((13,)),
        ]
        + gather_sems(chunks),
        compiler_params=pltpu.CompilerParams(
            collective_id=collective_id, has_side_effects=True, vmem_limit_bytes=64500 * 1024
        ),
    )(pieces, w_mod, mod_bias, proj_bias, small, tokens, out_grad, *shards)[:20]


def attention_back_step(qkv, grad, out, lse, result, key_sum, value_sum, block, scale):
    heads, blocks = qkv.shape[0] // 3, qkv.shape[2] // block
    factor = scale * LOG2E

    def body(i):
        h, j = i // blocks, i % blocks
        cols = pl.ds(pl.multiple_of(j * block, block), block)
        queries, keys, values = qkv[h, :, cols], qkv[heads + h], qkv[2 * heads + h]
        grads = grad[h, :, cols]
        inner = jnp.sum(out[h, :, cols].astype(F32) * grads.astype(F32), axis=0, keepdims=True)
        probs = jnp.exp2(product(keys, queries, 0, 0) * factor - lse[h, :, cols])
        score_grad = (probs * (product(values, grads, 0, 0) - inner)).astype(BF16)
        value_part = product(grads, probs.astype(BF16), 1, 1)
        key_part = product(queries, score_grad, 1, 1)
        result[h, :, cols] = (product(keys, score_grad, 1, 0) * scale).astype(BF16)

        @pl.when(j == 0)
        def _():
            key_sum[...] = key_part
            value_sum[...] = value_part

        @pl.when(j > 0)
        def _():
            key_sum[...] += key_part
            value_sum[...] += value_part

        @pl.when(j == blocks - 1)
        def _():
            result[heads + h] = (key_sum[...] * scale).astype(BF16)
            result[2 * heads + h] = value_sum[...].astype(BF16)

    return heads * blocks, body


def hidden_back_kernel(
    chunks, bias, grad_m_in, act_in, slope_in, rows_in, fc2_grad_in, w_fc2, w_fc1,
    fc1_bias_grad, fc2_out, fc1_grad_out, branch_out, ngrad_out,
    grad_m, act, slope, rows, fc2_grad, fc1_grad, branch, ngrad,
    weight, pre_grad, sent1, got1, sent2, got2, *rest,
):
    n = len(chunks)
    lands, (sems, load_sems, recv, send) = rest[:n], rest[n:]
    pos = place()
    sib = neighbours(pos)[0]
    half, width = branch.shape
    hidden = act.shape[1]
    load = loader(load_sems)
    grad_ready = load(fc2_grad_in, fc2_grad)
    weight_ready = load(w_fc2, weight)
    m_ready = load(grad_m_in, grad_m)
    slope_ready = load(slope_in, slope)
    act_ready = load(act_in, act)
    rows_ready = load(rows_in, rows)
    greet(chip_peers(pos))
    parts = [
        Reduce(fc2_grad, lands[i], fc2_out, recv.at[i], send.at[i], pos, cols)
        for i, cols in enumerate(chunks)
    ]
    pump = Pump(reduce_events(parts))
    grad_ready()
    pump.run(2)
    weight_ready()
    m_ready()
    slope_ready()
    tile = 256

    def into_hidden(i):
        cols = pl.ds(pl.multiple_of(i * tile, tile), tile)
        value = product(grad_m[...], flat(weight[:, :, cols]), 1, 0)
        value = (value * slope[:, cols].astype(F32)).astype(BF16)
        pre_grad[:, cols] = value
        fc1_bias_grad[:, cols] = jnp.sum(value.astype(F32), axis=0, keepdims=True)

    pump.loop(hidden // tile, into_hidden, 9)

    def out_of_hidden(source, sent, own, extra):
        def body(i):
            turn = lax.rem(i + 2, 4)
            part = pl.ds(pl.multiple_of(turn * tile, tile), tile)
            value = product(source[part, :], flat(weight[...]), 1, 1)

            @pl.when(i < 2)
            def _():
                sent[pl.ds(pl.multiple_of(i * tile, tile), tile), :] = value.astype(BF16)

            @pl.when(i >= 2)
            def _():
                own[part, :] = value + extra

        return body

    swap1 = remote(sent1, got1, sems.at[1], sems.at[2], sib)
    swap2 = remote(sent2, got2, sems.at[3], sems.at[4], sib)
    act_ready()
    pump.loop(4, out_of_hidden(act, sent1, branch, bias[...]), 8)
    swap1.start()
    weight_ready = load(w_fc1, weight)
    pump.run(2)
    weight_ready()
    pump.loop(4, out_of_hidden(pre_grad, sent2, ngrad, 0.0), 8)
    swap2.start()

    def join(own, got):
        def body(i, _):
            part = pl.ds(pl.multiple_of(i * tile, tile), tile)
            own[part, :] += got[part, :].astype(F32)
            return 0

        lax.fori_loop(0, half // tile, body, 0)

    swap1.wait()
    join(branch, got1)
    stored = [load(branch, branch_out)]
    rows_ready()

    def weight_grad(i):
        cols = pl.ds(pl.multiple_of(i * tile, tile), tile)
        value = product(rows[...], pre_grad[:, cols], 0, 0)
        fc1_grad[:, :, cols] = value.reshape(fc1_grad.shape[:2] + (tile,)).astype(BF16)

    pump.loop(hidden // tile, weight_grad, 9)
    stored.append(load(fc1_grad, fc1_grad_out))
    swap2.wait()
    join(ngrad, got2)
    stored.append(load(ngrad, ngrad_out))
    pump.run()
    for p in parts:
        p.finish()
    for wait in stored:
        wait()


def hidden_back(bias, grad_m, act, slope, rows, fc2_grad, w_fc2, w_fc1, chunks, collective_id):
    vmem, anywhere = pl.BlockSpec(memory_space=pltpu.VMEM), pl.BlockSpec(memory_space=pl.ANY)
    shape = jax.ShapeDtypeStruct
    count, width = grad_m.shape
    half, hidden = count // 2, act.shape[1]
    swap = pltpu.VMEM((half, width), BF16)
    sums = pltpu.VMEM((half, width), F32)
    land = reduce_scratch([(0, cols) for cols in chunks])
    return pl.pallas_call(
        functools.partial(hidden_back_kernel, chunks),
        out_shape=[
            shape((1, hidden), F32),
            shape(fc2_grad.shape[1:], F32),
            shape(fc2_grad.shape, BF16),
            shape((half, width), F32),
            shape((half, width), F32),
        ],
        in_specs=[vmem] + [anywhere] * 7,
        out_specs=[vmem] * 2 + [anywhere] * 3,
        scratch_shapes=[
            pltpu.VMEM((count, width), BF16),
            pltpu.VMEM((count, hidden), BF16),
            pltpu.VMEM((count, hidden), BF16),
            pltpu.VMEM((count, width), BF16),
            pltpu.VMEM(fc2_grad.shape, BF16),
            pltpu.VMEM(fc2_grad.shape, BF16),
            sums,
            sums,
            pltpu.VMEM(fc2_grad.shape, BF16),
            pltpu.VMEM((count, hidden), BF16),
            swap,
            swap,
            swap,
            swap,
        ]
        + land[: len(chunks)]
        + [pltpu.SemaphoreType.DMA((5,)), pltpu.SemaphoreType.DMA((12,))]
        + land[len(chunks) :],
        compiler_params=pltpu.CompilerParams(
            collective_id=collective_id, has_side_effects=True, vmem_limit_bytes=64500 * 1024
        ),
    )(bias, grad_m, act, slope, rows, fc2_grad, w_fc2, w_fc1)


def attention_back_kernel(
    chunks, block, scale, mod, resid_in, ngrad_in, out_grad_in, branch_in, branch_m_in, w_proj_in,
    qkv_in, out_in, lse_in, fc1_grad_in,
    sums, fc1_out, proj_out, output, resid_grad_out, result_out,
    resid, ngrad, out_grad, branch, branch_m, w_proj, qkv, out, lse, fc1_grad, resid_grad, result,
    rows, grad, proj_grad, key_sum, value_sum, given, *rest,
):
    n = len(chunks)
    lands, (sems, load_sems, recv, send) = rest[:n], rest[n:]
    pos = place()
    sib = neighbours(pos)[0]
    half, width = resid.shape
    d, z, x, c, y = pos
    home, away = c == y, c != y
    far = (z * 4 + x * 2 + 1 - c, 1 - y)
    load = loader(load_sems)
    first = [load(fc1_grad_in, fc1_grad)]
    norm_ready = [
        load(*pair)
        for pair in (
            (ngrad_in, ngrad),
            (resid_in, resid),
            (out_grad_in, out_grad),
            (branch_in, branch),
            (branch_m_in, branch_m),
        )
    ]
    late = [load(w_proj_in, w_proj), load(out_in, out), load(qkv_in, qkv), load(lse_in, lse)]
    greet(chip_peers(pos))
    parts = [
        Reduce(
            (fc1_grad, proj_grad)[g],
            lands[i],
            (fc1_out, proj_out)[g],
            recv.at[i],
            send.at[i],
            pos,
            cols,
        )
        for i, (g, cols) in enumerate(chunks)
    ]
    pump = Pump(reduce_events(parts))
    for wait in first:
        wait()
    pump.run(2)
    for wait in norm_ready:
        wait()
    tall = half // 8
    gate_a, scale_m, gate_m = (mod[:, i * width : (i + 1) * width] for i in (2, 4, 5))
    scale_up = 1.0 + scale_m

    def norm(i, total):
        part = pl.ds(pl.multiple_of(i * tall, tall), tall)
        g = ngrad[part, :]
        mid = resid[part, :]
        back, normed = norm_back_rows(mid, g, scale_up)
        grads = out_grad[part, :].astype(F32)
        value = grads + back
        resid_grad[part, :] = value
        low = (value * gate_a).astype(BF16)
        rows[part, :] = low
        made = (mid + gate_m * branch_m[part, :]).astype(BF16)

        @pl.when(home)
        def _():
            output[part, :] = made

        @pl.when(away)
        def _():
            given[part, :] = made

        terms = (
            value * branch[part, :],
            g,
            g * normed,
            grads * branch_m[part, :],
            low.astype(F32),
        )
        return tuple(t + row_sum(v) for t, v in zip(total, terms))

    total = lax.fori_loop(0, 8, norm, (jnp.zeros((1, width), F32),) * 5)
    share = remote(rows.at[:half], rows.at[half:], sems.at[0], sems.at[1], sib)
    share.start()
    stored = [load(resid_grad, resid_grad_out)]
    trade = remote(given, output, sems.at[2], sems.at[3], far)
    pl.when(away)(lambda: trade.start())
    sums[...] = jnp.zeros_like(sums)
    for i in range(5):
        sums[i : i + 1, :] = total[i]
    pump.run(1)
    for wait in late:
        wait()
    share.wait()
    tile = 256

    def attended(i):
        cols = pl.ds(pl.multiple_of(i * tile, tile), tile)
        value = product(flat(w_proj[...]), rows[cols, :], 0, 1)
        grad[:, :, cols] = value.reshape(grad.shape[:2] + (tile,)).astype(BF16)

    pump.loop(2 * half // tile, attended, 4)
    value = product(rows[...], flat(out[...]), 0, 1)
    proj_grad[...] = value.reshape(proj_grad.shape).astype(BF16)
    steps, body = attention_back_step(
        qkv, grad, out, lse, result, key_sum, value_sum, block, scale
    )
    pump.loop(steps, body, 28)
    stored.append(load(result, result_out))
    pump.run()
    pl.when(away)(lambda: trade.wait())
    for p in parts:
        p.finish()
    for wait in stored:
        wait()


def attention_back(
    mod, resid, ngrad, out_grad, branch, branch_m, w_proj, qkv, out, lse, fc1_grad, chunks,
    collective_id, block=512,
):
    heads, size, count = out.shape
    half, width = resid.shape
    owned, cols = w_proj.shape[1:]
    vmem, anywhere = pl.BlockSpec(memory_space=pltpu.VMEM), pl.BlockSpec(memory_space=pl.ANY)
    shape = jax.ShapeDtypeStruct
    land = reduce_scratch(chunks)
    arrays = (resid, ngrad, out_grad, branch, branch_m, w_proj, qkv, out, lse, fc1_grad)
    made = [((half, width), F32), (qkv.shape, BF16)]
    return pl.pallas_call(
        functools.partial(attention_back_kernel, chunks, block, size**-0.5),
        out_shape=[
            shape((8, width), F32),
            shape(fc1_grad.shape[1:], F32),
            shape((owned, cols), F32),
            shape((half, width), BF16),
        ]
        + [shape(*m) for m in made],
        in_specs=[vmem] + [anywhere] * 10,
        out_specs=[vmem] * 4 + [anywhere] * 2,
        scratch_shapes=[pltpu.VMEM(a.shape, a.dtype) for a in arrays]
        + [pltpu.VMEM(*m) for m in made]
        + [
            pltpu.VMEM((count, width), BF16),
            pltpu.VMEM(out.shape, BF16),
            pltpu.VMEM((16, owned, cols), BF16),
            pltpu.VMEM((size, count), F32),
            pltpu.VMEM((size, count), F32),
            pltpu.VMEM((half, width), BF16),
        ]
        + land[: len(chunks)]
        + [pltpu.SemaphoreType.DMA((4,)), pltpu.SemaphoreType.DMA((12,))]
        + land[len(chunks) :],
        compiler_params=pltpu.CompilerParams(
            collective_id=collective_id, has_side_effects=True, vmem_limit_bytes=64500 * 1024
        ),
    )(mod, *arrays)


def columns(n, step):
    return [(i, min(step, n - i)) for i in range(0, n, step)]


def on_device_chip(
    tokens,
    cond,
    mod_weight,
    mod_bias,
    query_key_value_weight,
    qkv_bias,
    attention_out_weight,
    attention_out_bias,
    first_hidden_weight,
    first_hidden_bias,
    second_hidden_weight,
    second_hidden_bias,
    out_grad,
):
    half, _, width = tokens.shape
    owned, _, cols = query_key_value_weight.shape
    head_size = width // HEADS
    heads_here = cols // head_size
    hidden = first_hidden_weight.shape[1]

    silu_cond, silu_back = jax.vjp(jax.nn.silu, cond.astype(F32))
    pieces = jnp.pad(
        silu_cond.astype(BF16).reshape(16, 1, owned), ((0, 0), (0, 7), (0, 128 - owned))
    )
    s_qkv = query_key_value_weight.reshape(1, owned, 3 * cols)
    small = jnp.stack(
        [
            jnp.pad(qkv_bias[0], (0, hidden - cols)),
            jnp.pad(qkv_bias[1], (0, hidden - cols)),
            first_hidden_bias,
        ]
    )
    small = jnp.pad(small, ((0, 5), (0, 0)))
    shards = [
        s_qkv,
        attention_out_weight.T.reshape(1, owned, cols),
        first_hidden_weight.reshape(1, owned, hidden),
        second_hidden_weight.T.reshape(1, owned, hidden),
    ]
    chunks = [(0, p, False) for p in columns(3 * cols, 896)] + [(1, None, False)]
    chunks += [(g, p, False) for g in (2, 3) for p in columns(hidden, 1152)]
    (
        modulation,
        silu_owned,
        fc2_bias_part,
        rows_a,
        qkv,
        attended,
        log_totals,
        branch_a,
        resid_mid,
        rows_m,
        act_low,
        slope,
        fc2_grad,
        grad_m,
        tokens_here,
        out_grad_here,
        w_qkv,
        w_proj,
        w_fc1,
        w_fc2,
    ) = forward_stage(
        pieces,
        mod_weight,
        mod_bias.astype(F32)[None],
        attention_out_bias.astype(F32)[None],
        small,
        tokens.reshape(half, width),
        out_grad.reshape(half, width),
        shards,
        head_size,
        chunks,
        2,
    )

    fc1_bias_part, fc2_out, fc1_grad, branch_m, normed_m_grad = hidden_back(
        second_hidden_bias.astype(F32)[None],
        grad_m,
        act_low,
        slope,
        rows_m,
        fc2_grad,
        w_fc2,
        w_fc1,
        columns(hidden, 768),
        4,
    )
    sums, fc1_out, proj_out, output, resid_grad, qkv_grad = attention_back(
        modulation,
        resid_mid,
        normed_m_grad,
        out_grad_here,
        branch_a,
        branch_m,
        w_proj,
        qkv,
        attended,
        log_totals,
        fc1_grad,
        [(0, p) for p in columns(hidden, 768)] + [(1, (0, cols))],
        5,
    )
    tokens_grad, qkv_out, silu_grad, mods_a, mods_b, wide, narrow = last_stage(
        modulation,
        sums,
        fc2_bias_part,
        fc1_bias_part,
        mod_weight,
        rows_a,
        qkv_grad,
        w_qkv,
        tokens_here,
        resid_grad,
        6,
    )
    mods = jnp.concatenate([mods_a[:, 0], mods_b[:, 0]], axis=1)
    mod_weight_grad = product(silu_owned[:, 0, :owned], mods, 0, 0)
    mod_bias_grad = jnp.sum(mods, axis=0, dtype=F32)
    wide, narrow = jnp.sum(wide[:, 0], axis=0), jnp.sum(narrow[:, 0], axis=0)
    step = (cols + 127) // 128 * 128
    qkv_bias_grad = jnp.stack([narrow[hidden + i * step :][:cols] for i in range(2)])
    cond_grad = silu_back(silu_grad[:, 0, :owned].reshape(1, width))[0]
    return (
        output.reshape(half, 1, width),
        tokens_grad.reshape(half, 1, width),
        cond_grad,
        mod_weight_grad,
        mod_bias_grad,
        jnp.moveaxis(qkv_out, 0, 1),
        qkv_bias_grad,
        proj_out.T,
        wide[:width],
        fc1_out,
        narrow[:hidden],
        fc2_out.T,
        wide[width:],
    )


def solution(mesh):
    shape = dict(mesh.shape)
    body = on_device_chip if shape == {"dp": 16, "tensor": 2} else on_device_general
    return jax.shard_map(
        body,
        mesh=mesh,
        in_specs=(
            P("tensor", "dp", None),
            P("dp", None),
            P("dp", None),
            P(),
            P("dp", None, "tensor"),
            P(None, "tensor"),
            P("tensor", "dp"),
            P(),
            P("dp", "tensor"),
            P("tensor"),
            P("tensor", "dp"),
            P(),
            P("tensor", "dp", None),
        ),
        out_specs=(
            P("tensor", "dp", None),
            P("tensor", "dp", None),
            P("dp", None),
            P("dp", None),
            P(),
            P("dp", None, "tensor"),
            P(None, "tensor"),
            P("tensor", "dp"),
            P(),
            P("dp", "tensor"),
            P("tensor"),
            P("tensor", "dp"),
            P(),
        ),
        check_vma=False,
    )
```

```python
import functools
import math

import jax
import jax.numpy as jnp
from jax import lax
from jax.experimental import pallas as pl
from jax.experimental.pallas import tpu as pltpu
from jax.sharding import PartitionSpec as P

HEADS = 16
MESH = pl.DeviceIdType.MESH
AXES = ("dp", "tensor")
F32 = jnp.float32
BF16 = jnp.bfloat16


def modulate(hidden, shifts, scales):
    center = hidden - jnp.mean(hidden, axis=-1, keepdims=True)
    spread = jnp.mean(center * center, axis=-1, keepdims=True)
    return center * lax.rsqrt(spread + 1e-06) * (1.0 + scales) + shifts


def gelu_tanh(values):
    return jax.nn.gelu(values, approximate=True)


def attend_forward(packed):
    queries = packed[:, 0]
    keys_all = packed[:, 1]
    values_all = packed[:, 2]
    seq_len = packed.shape[0]
    scaling = packed.shape[3] ** (-0.5)
    block_rows = min(512, seq_len)
    results = []
    log_parts = []
    for offset in range(0, seq_len, block_rows):
        query_block = queries[offset : offset + block_rows]
        scores = (
            jnp.einsum("qhe,khe->hqk", query_block, keys_all, preferred_element_type=jnp.float32)
            * scaling
        )
        highest = jnp.max(scores, axis=-1, keepdims=True)
        weights = jnp.exp(scores - highest)
        row_total = jnp.sum(weights, axis=-1, keepdims=True)
        prob_low = (weights / row_total).astype(jnp.bfloat16)
        mixture = jnp.einsum(
            "hqk,khe->qhe", prob_low, values_all, preferred_element_type=jnp.float32
        )
        results.append(mixture.reshape(block_rows, -1))
        log_parts.append((highest + jnp.log(row_total))[..., 0])
    return (jnp.concatenate(results, 0).astype(jnp.bfloat16), jnp.concatenate(log_parts, 1))


def attend_backward(inputs):
    packed, grad_out, log_totals = inputs
    queries = packed[:, 0]
    keys_all = packed[:, 1]
    values_all = packed[:, 2]
    seq_len = packed.shape[0]
    scaling = packed.shape[3] ** (-0.5)
    block_rows = min(512, seq_len)
    query_grads = []
    key_grad = jnp.zeros(keys_all.shape, jnp.float32)
    value_grad = jnp.zeros(values_all.shape, jnp.float32)
    for offset in range(0, seq_len, block_rows):
        query_block = queries[offset : offset + block_rows]
        grad_block = grad_out[offset : offset + block_rows]
        scores = (
            jnp.einsum("qhe,khe->hqk", query_block, keys_all, preferred_element_type=jnp.float32)
            * scaling
        )
        probs = jnp.exp(scores - log_totals[:, offset : offset + block_rows, None])
        prob_low = probs.astype(jnp.bfloat16)
        prob_grad = jnp.einsum(
            "qhe,khe->hqk", grad_block, values_all, preferred_element_type=jnp.float32
        )
        inner = jnp.sum(probs * prob_grad, axis=-1, keepdims=True)
        score_grad = (probs * (prob_grad - inner)).astype(jnp.bfloat16)
        query_grads.append(
            jnp.einsum("hqk,khe->qhe", score_grad, keys_all, preferred_element_type=jnp.float32)
            * scaling
        )
        key_grad = (
            key_grad
            + jnp.einsum(
                "hqk,qhe->khe", score_grad, query_block, preferred_element_type=jnp.float32
            )
            * scaling
        )
        value_grad = value_grad + jnp.einsum(
            "hqk,qhe->khe", prob_low, grad_block, preferred_element_type=jnp.float32
        )
    return jnp.stack([jnp.concatenate(query_grads, 0), key_grad, value_grad], 1).astype(
        jnp.bfloat16
    )


def on_device_general(
    tokens,
    cond,
    mod_weight,
    mod_bias,
    query_key_value_weight,
    qkv_bias,
    attention_out_weight,
    attention_out_bias,
    first_hidden_weight,
    first_hidden_bias,
    second_hidden_weight,
    second_hidden_bias,
    out_grad,
):
    w_mod, w_qkv, w_proj, w_fc1, w_fc2 = (
        lax.all_gather(mod_weight, "dp", axis=0, tiled=True),
        lax.all_gather(query_key_value_weight, "dp", axis=0, tiled=True),
        lax.all_gather(attention_out_weight, "dp", axis=1, tiled=True),
        lax.all_gather(first_hidden_weight, "dp", axis=0, tiled=True),
        lax.all_gather(second_hidden_weight, "dp", axis=1, tiled=True),
    )
    seq_local, latents, width = tokens.shape
    columns = query_key_value_weight.shape[2]
    head_size = width // HEADS
    heads_here = columns // head_size
    local_rows = seq_local * latents
    cond_wide = cond.astype(jnp.float32)
    silu_cond, silu_back = jax.vjp(jax.nn.silu, cond_wide)
    silu_low = silu_cond.astype(jnp.bfloat16)
    modulation = jnp.dot(silu_low, w_mod, preferred_element_type=jnp.float32) + mod_bias.astype(
        jnp.float32
    )
    pieces = modulation.reshape(latents, 6, width)
    hidden_in = tokens.astype(jnp.float32)
    attention_normalized, norm_a_back = jax.vjp(modulate, hidden_in, pieces[:, 0], pieces[:, 1])
    gathered_a = lax.all_gather(
        attention_normalized.astype(jnp.bfloat16), "tensor", axis=0, tiled=True
    )
    seq_len = gathered_a.shape[0]
    total_rows = seq_len * latents
    rows_a = gathered_a.reshape(total_rows, width)
    qkv_flat = w_qkv.reshape(width, 3 * columns)
    zero_row = jnp.zeros((columns,), jnp.float32)
    query_key_value_shift = jnp.stack(
        [qkv_bias[0].astype(jnp.float32), zero_row, qkv_bias[1].astype(jnp.float32)]
    )
    projected_output = (
        jnp.dot(rows_a, qkv_flat, preferred_element_type=jnp.float32).reshape(
            seq_len, latents, 3, columns
        )
        + query_key_value_shift
    )
    packed = jnp.moveaxis(projected_output.astype(jnp.bfloat16), 1, 0).reshape(
        latents, seq_len, 3, heads_here, head_size
    )
    attention_result, log_totals = lax.map(attend_forward, packed)
    attended_rows = jnp.moveaxis(attention_result, 0, 1).reshape(total_rows, columns)
    summed_a = lax.psum_scatter(
        jnp.dot(attended_rows, w_proj, preferred_element_type=jnp.float32).astype(jnp.bfloat16),
        "tensor",
        scatter_dimension=0,
        tiled=True,
    ).astype(jnp.float32)
    attention_branch = summed_a.reshape(seq_local, latents, width) + attention_out_bias.astype(
        jnp.float32
    )
    resid_mid = hidden_in + pieces[:, 2] * attention_branch
    feedforward_normalized, norm_m_back = jax.vjp(modulate, resid_mid, pieces[:, 3], pieces[:, 4])
    gathered_m = lax.all_gather(
        feedforward_normalized.astype(jnp.bfloat16), "tensor", axis=0, tiled=True
    )
    rows_m = gathered_m.reshape(total_rows, width)
    before_activation = jnp.dot(
        rows_m, w_fc1, preferred_element_type=jnp.float32
    ) + first_hidden_bias.astype(jnp.float32)
    gelu_activated, gelu_back = jax.vjp(gelu_tanh, before_activation)
    act_low = gelu_activated.astype(jnp.bfloat16)
    summed_m = lax.psum_scatter(
        jnp.dot(act_low, w_fc2, preferred_element_type=jnp.float32).astype(jnp.bfloat16),
        "tensor",
        scatter_dimension=0,
        tiled=True,
    ).astype(jnp.float32)
    feedforward_branch = summed_m.reshape(seq_local, latents, width) + second_hidden_bias.astype(
        jnp.float32
    )
    output = (resid_mid + pieces[:, 5] * feedforward_branch).astype(jnp.bfloat16)
    grad_out = out_grad.astype(jnp.float32)
    gate_m_grad = jnp.sum(grad_out * feedforward_branch, axis=0)
    grad_m_low = (grad_out * pieces[:, 5]).astype(jnp.bfloat16)
    grad_m_rows = lax.all_gather(grad_m_low, "tensor", axis=0, tiled=True).reshape(
        total_rows, width
    )
    fc2_bias_grad = jnp.sum(grad_m_rows, axis=0, dtype=jnp.float32)
    fc2_weight_grad = jnp.einsum(
        "rf,rd->fd", act_low, grad_m_rows, preferred_element_type=jnp.float32
    )
    act_grad = jnp.einsum("rd,fd->rf", grad_m_rows, w_fc2, preferred_element_type=jnp.float32)
    pre_grad = gelu_back(act_grad)[0].astype(jnp.bfloat16)
    fc1_bias_grad = jnp.sum(pre_grad, axis=0, dtype=jnp.float32)
    fc1_weight_grad = jnp.einsum("rd,rf->df", rows_m, pre_grad, preferred_element_type=jnp.float32)
    normed_m_grad = (
        lax.psum_scatter(
            jnp.einsum("rf,df->rd", pre_grad, w_fc1, preferred_element_type=jnp.float32).astype(
                jnp.bfloat16
            ),
            "tensor",
            scatter_dimension=0,
            tiled=True,
        )
        .astype(jnp.float32)
        .reshape(seq_local, latents, width)
    )
    resid_part, shift_m_grad, scale_m_grad = norm_m_back(normed_m_grad)
    resid_grad = grad_out + resid_part
    gate_a_grad = jnp.sum(resid_grad * attention_branch, axis=0)
    grad_a_low = (resid_grad * pieces[:, 2]).astype(jnp.bfloat16)
    grad_a_flat = grad_a_low.reshape(local_rows, width)
    proj_bias_part = jnp.sum(grad_a_flat, axis=0, dtype=jnp.float32)
    grad_a_rows = lax.all_gather(grad_a_low, "tensor", axis=0, tiled=True).reshape(
        total_rows, width
    )
    proj_weight_grad = jnp.einsum(
        "rc,rd->cd", attended_rows, grad_a_rows, preferred_element_type=jnp.float32
    )
    attended_grad = jnp.einsum(
        "rd,cd->rc", grad_a_rows, w_proj, preferred_element_type=jnp.float32
    ).astype(jnp.bfloat16)
    grad_packed = jnp.moveaxis(attended_grad.reshape(seq_len, latents, heads_here, head_size), 1, 0)
    qkv_grad_packed = lax.map(attend_backward, (packed, grad_packed, log_totals))
    qkv_grad_rows = jnp.moveaxis(qkv_grad_packed, 0, 1).reshape(total_rows, 3 * columns)
    bias_sums = jnp.sum(qkv_grad_rows.reshape(total_rows, 3, columns), axis=0, dtype=jnp.float32)
    qkv_bias_grad = jnp.stack([bias_sums[0], bias_sums[2]])
    qkv_weight_grad = jnp.einsum(
        "rd,rc->dc", rows_a, qkv_grad_rows, preferred_element_type=jnp.float32
    ).reshape(width, 3, columns)
    normed_a_grad = (
        lax.psum_scatter(
            jnp.einsum(
                "rc,dc->rd", qkv_grad_rows, qkv_flat, preferred_element_type=jnp.float32
            ).astype(jnp.bfloat16),
            "tensor",
            scatter_dimension=0,
            tiled=True,
        )
        .astype(jnp.float32)
        .reshape(seq_local, latents, width)
    )
    input_part, shift_a_grad, scale_a_grad = norm_a_back(normed_a_grad)
    tokens_grad = (resid_grad + input_part).astype(jnp.bfloat16)
    partial_mod = jnp.stack(
        [shift_a_grad, scale_a_grad, gate_a_grad, shift_m_grad, scale_m_grad, gate_m_grad], 1
    ).reshape(latents, 6 * width)
    mod_summed, proj_bias_grad = (
        lax.psum(partial_mod.astype(jnp.bfloat16), "tensor").astype(jnp.float32),
        lax.psum(proj_bias_part.astype(jnp.bfloat16), "tensor").astype(jnp.float32),
    )
    mod_grad_low = mod_summed.astype(jnp.bfloat16)
    silu_grad = jnp.einsum("le,de->ld", mod_grad_low, w_mod, preferred_element_type=jnp.float32)
    cond_grad = silu_back(silu_grad)[0]
    silu_every, mod_every = (
        lax.all_gather(silu_low, "dp", axis=0, tiled=True),
        lax.all_gather(mod_grad_low, "dp", axis=0, tiled=True),
    )
    owned_rows = mod_weight.shape[0]
    silu_owned = lax.dynamic_slice_in_dim(
        silu_every, lax.axis_index("dp") * owned_rows, owned_rows, 1
    )
    mod_weight_grad = jnp.einsum(
        "ld,le->de", silu_owned, mod_every, preferred_element_type=jnp.float32
    )
    mod_bias_grad = jnp.sum(mod_every, axis=0, dtype=jnp.float32)
    qkv_weight_grad, proj_weight_grad, fc1_weight_grad, fc2_weight_grad = (
        lax.psum_scatter(
            qkv_weight_grad.astype(jnp.bfloat16), "dp", scatter_dimension=0, tiled=True
        ).astype(jnp.float32),
        lax.psum_scatter(
            proj_weight_grad.astype(jnp.bfloat16), "dp", scatter_dimension=1, tiled=True
        ).astype(jnp.float32),
        lax.psum_scatter(
            fc1_weight_grad.astype(jnp.bfloat16), "dp", scatter_dimension=0, tiled=True
        ).astype(jnp.float32),
        lax.psum_scatter(
            fc2_weight_grad.astype(jnp.bfloat16), "dp", scatter_dimension=1, tiled=True
        ).astype(jnp.float32),
    )
    qkv_bias_grad, proj_bias_grad, fc1_bias_grad, fc2_bias_grad = lax.psum(
        (qkv_bias_grad, proj_bias_grad, fc1_bias_grad, fc2_bias_grad), "dp"
    )
    return (
        output,
        tokens_grad,
        cond_grad,
        mod_weight_grad,
        mod_bias_grad,
        qkv_weight_grad,
        qkv_bias_grad,
        proj_weight_grad,
        proj_bias_grad,
        fc1_weight_grad,
        fc1_bias_grad,
        fc2_weight_grad,
        fc2_bias_grad,
    )


def place():
    d = lax.axis_index("dp")
    y = lax.axis_index("tensor")
    return d, d // 4, (d // 2) % 2, d % 2, y


def neighbours(pos):
    d, z, x, c, y = pos
    sib = (z * 4 + x * 2 + (1 - c), y)
    xn = (z * 4 + (1 - x) * 2 + c, y)
    yn = (d, 1 - y)
    return sib, xn, yn


def z_peer(pos, k):
    d, z, x, c, y = pos
    return (((z + k) % 4) * 4 + x * 2 + c, y)


def z_order(z, k):
    return (z, z + 1 - 2 * (z % 2), 2 - z // 2, 3 - 3 * (z // 2))[k]


def greet(peers):
    sem = pltpu.get_barrier_semaphore()
    for peer in peers:
        pl.semaphore_signal(sem, inc=1, device_id=peer, device_id_type=MESH)
    pl.semaphore_wait(sem, len(peers))


def chip_peers(pos):
    d, z, x, c, y = pos
    across = [(z * 4 + x * 2 + 1 - c, 1 - y)]
    return list(neighbours(pos)) + across + [z_peer(pos, k) for k in (1, 2, 3)]


def remote(src, dst, send, recv, peer):
    return pltpu.make_async_remote_copy(
        src_ref=src, dst_ref=dst, send_sem=send, recv_sem=recv, device_id=peer, device_id_type=MESH
    )


Z_SENDS = (1, 2, 3)
GATHER_RECV = 24
GATHER_SEND = 32


def repeat(first, stop, action):
    def step(i, _):
        action(i)
        return 0

    lax.fori_loop(first, stop, step, 0)


class Gather:
    def __init__(self, shard, full, relay, cols, wide, recv, send, pos):
        self.wide = wide
        self.shard, self.full, self.relay, self.cols = shard, full, relay, cols
        self.recv, self.send, self.pos = recv, send, pos
        d, z, x, c, y = pos
        self.sib, self.xn, _ = neighbours(pos)
        self.far = (z * 4 + x * 2 + y, 1 - y)
        self.home, self.away = c == y, c != y

    def part(self, ref, b):
        if self.cols is None:
            return ref.at[pl.ds(b, 1)]
        return ref.at[pl.ds(b, 1), :, pl.ds(*self.cols)]

    def move(self, src, dst, s, r, peer):
        return remote(src, dst, self.send.at[s], self.recv.at[r], peer)

    def came(self, r):
        block = self.part(self.full, 0)
        self.move(block, block, 0, r, self.sib).wait_recv()

    def stay(self):
        return pltpu.make_async_copy(
            self.part(self.shard, 0), self.part(self.full, self.pos[0]), self.send.at[31]
        )

    def start(self):
        d, z, x, c, y = self.pos
        q = z * 2 + x
        own = self.part(self.shard, 0)

        @pl.when(self.home)
        def _():
            for k in Z_SENDS:
                peer = (z_order(z, k) * 4 + x * 2 + c, y)
                self.move(own, self.part(self.full, d), k, q, peer).start()
            self.move(own, self.part(self.full, d), 4, q, self.xn).start()
            self.move(own, self.part(self.full, d), 8, 8 + q, self.far).start()
            self.stay().start()

        @pl.when(self.away)
        def _():
            for k in Z_SENDS:
                peer = (z_order(z, k) * 4 + x * 2 + c, y)
                self.move(own, self.part(self.relay, q), k, q, peer).start()
            self.move(own, self.part(self.full, d), 8, 16 + q, self.far).start()
            self.move(own, self.part(self.relay, q), 4, q, self.xn).start()
            self.move(own, self.part(self.full, d), 16, 8 + q, self.sib).start()

    def from_z(self, k):
        d, z, x, c, y = self.pos
        q = z_order(z, k) * 2 + x
        dst = self.part(self.full, 2 * q + c)

        @pl.when(self.home)
        def _():
            self.came(q)
            self.move(dst, dst, 4 + k, q, self.xn).start()
            self.move(dst, dst, 8 + k, 8 + q, self.far).start()

        @pl.when(self.away)
        def _():
            self.came(q)
            src = self.part(self.relay, q)
            self.move(src, dst, 8 + k, 16 + q, self.far).start()
            self.move(src, src, 4 + k, q, self.xn).start()
            self.move(src, dst, 16 + k, 8 + q, self.sib).start()

    def from_x(self, k):
        d, z, x, c, y = self.pos
        q = z_order(z, k) * 2 + 1 - x
        dst = self.part(self.full, 2 * q + c)

        @pl.when(self.home)
        def _():
            self.came(q)
            if self.wide != 1:
                self.move(dst, dst, 12 + k, 8 + q, self.far).start()

        @pl.when(self.away)
        def _():
            self.came(q)
            if self.wide == 2:
                self.move(self.part(self.relay, q), dst, 12 + k, 16 + q, self.far).start()
            self.move(self.part(self.relay, q), dst, 20 + k, 8 + q, self.sib).start()

    def from_y(self, k):
        d, z, x, c, y = self.pos
        q = z_order(z, k) * 2 + x

        @pl.when(self.away)
        def _():
            block = self.part(self.full, 2 * q + 1 - c)
            if self.wide != 2:
                self.came(16 + q)
                self.move(block, block, 12 + k, 16 + q, self.xn).start()
            if self.wide == 1:
                block = self.part(self.full, 2 * q + c)
                self.came(8 + q)
                self.move(block, block, 24 + k, 8 + q, self.xn).start()

    def ready(self):
        d, z, x, c, y = self.pos

        @pl.when(self.home)
        def _():
            repeat(0, 8, lambda q: self.came(8 + q))
            self.stay().wait()

        @pl.when(self.away)
        def _():
            def other(k):
                self.came(16 + 2 * k + 1 - x)
                self.came(8 + 2 * k + 1 - x)
                if self.wide != 1:
                    self.came(8 + 2 * k + x)
                if self.wide == 2:
                    self.came(16 + 2 * k + x)

            repeat(0, 4, other)

    def finish(self):
        block = self.part(self.full, 0)

        def sent(s):
            self.move(block, block, s, 0, self.sib).wait_send()

        repeat(1, 12, sent)
        if self.wide != 1:
            pl.when(self.home)(lambda: repeat(12, 16, sent))
        pl.when(self.away)(lambda: repeat(12, 28 if self.wide == 1 else 24, sent))

    def early(self):
        return [functools.partial(self.from_z, k) for k in (1, 2, 3)]

    def late(self):
        steps = []
        for k in range(4):
            steps += [functools.partial(self.from_x, k), functools.partial(self.from_y, k)]
        return steps + [self.ready]


def gather_events(parts, lead=2):
    n = len(parts)
    events = [p.start for p in parts[:lead]]
    for i in range(n + 1):
        if i < n:
            events += parts[i].early()
        if i + lead < n:
            events.append(parts[i + lead].start)
        if i > 0:
            events += parts[i - 1].late()
    return events


def gather_parts(shards, fulls, relays, chunks, recv, send, pos):
    return [
        Gather(shards[g], fulls[g], relays[g], cols, wide, recv.at[i], send.at[i], pos)
        for i, (g, cols, wide) in enumerate(chunks)
    ]


def gather_sems(chunks):
    n = len(chunks)
    return [
        pltpu.SemaphoreType.DMA((n, GATHER_RECV)),
        pltpu.SemaphoreType.DMA((n, GATHER_SEND)),
    ]


def gather_shapes(shards):
    return [jax.ShapeDtypeStruct((16,) + s.shape[1:], s.dtype) for s in shards] + [
        jax.ShapeDtypeStruct((8,) + s.shape[1:], s.dtype) for s in shards
    ]


REDUCE_RECV = 27
REDUCE_SEND = 23


class Reduce:
    def __init__(self, grad, land, out, recv, send, pos, cols):
        self.grad, self.land, self.out = grad, land, out
        self.recv, self.send, self.pos, self.cols = recv, send, pos, pl.ds(*cols)
        d, z, x, c, y = pos
        self.sib, self.xn, self.yn = neighbours(pos)
        self.home, self.away = c == y, c != y

    def rows(self, b):
        return self.grad.at[pl.ds(b, 1), :, self.cols]

    def slot(self, i):
        return self.land.at[pl.ds(i, 1)]

    def push(self, src, slot, s, peer):
        return remote(src, self.slot(slot), self.send.at[s], self.recv.at[slot], peer)

    def came(self, slot):
        self.push(self.slot(slot), slot, 0, self.sib).wait_recv()

    def value(self, i, r):
        return self.land[i, r].astype(F32)

    def by_rows(self, body):
        def step(i, _):
            body(pl.ds(pl.multiple_of(i * 8, 8), 8))
            return 0

        lax.fori_loop(0, 9, step, 0)

    def first(self):
        d, z, x, c, y = self.pos

        @pl.when(self.away)
        def _():
            for column, base in ((1 - x, 0), (x, 4)):

                def step(k, _):
                    q = lax.rem(z + 1 + k, 4) * 2 + column
                    self.push(self.rows(2 * q + c), q, base + k, self.yn).start()
                    self.push(self.rows(2 * q + 1 - c), 15 + q, 8 + base + k, self.sib).start()
                    return 0

                lax.fori_loop(0, 4, step, 0)

        @pl.when(self.home)
        def _():
            for column, base in ((1 - x, 0), (x, 4)):

                def step(k, _):
                    q = lax.rem(z + 1 + k, 4) * 2 + column
                    self.push(self.rows(2 * q + 1 - c), q, base + k, self.sib).start()
                    return 0

                lax.fori_loop(0, 4, step, 0)

    def second(self, k):
        d, z, x, c, y = self.pos
        zz = (z + 1 + k) % 4
        q = zz * 2 + 1 - x

        @pl.when(self.away)
        def _():
            self.came(q)
            self.push(self.slot(q), 8 + zz, 16 + k, self.xn).start()

        @pl.when(self.home)
        def _():
            self.came(15 + q)
            self.push(self.slot(15 + q), 23 + zz, 15 + k, self.xn).start()
            b = 2 * q + c
            self.came(q)

            def add(r):
                total = self.grad[b, r, self.cols].astype(F32) + self.value(q, r)
                self.grad[b, r, self.cols] = total.astype(BF16)

            self.by_rows(add)
            self.push(self.rows(b), 8 + zz, 8 + k, self.xn).start()

    def third(self, k):
        d, z, x, c, y = self.pos
        zz = (z + 1 + k) % 4
        q = zz * 2 + x

        @pl.when(self.home)
        def _():
            self.came(15 + q)
            self.came(23 + zz)

            def add(r):
                self.land[15 + q, r] = (self.value(15 + q, r) + self.value(23 + zz, r)).astype(BF16)

            self.by_rows(add)
            self.push(self.slot(15 + q), 15 + zz, 19 + k, self.yn).start()
            if k < 3:
                b = 2 * q + c
                self.came(q)
                self.came(8 + zz)

                def add_two(r):
                    total = self.grad[b, r, self.cols].astype(F32)
                    total = total + self.value(q, r) + self.value(8 + zz, r)
                    self.grad[b, r, self.cols] = total.astype(BF16)

                self.by_rows(add_two)
                self.push(self.rows(b), 12 + k, 12 + k, (zz * 4 + x * 2 + c, y)).start()

    def fourth(self, k):
        d, z, x, c, y = self.pos
        zz = (z + 1 + k) % 4
        q = zz * 2 + x

        @pl.when(self.away)
        def _():
            self.came(q)
            self.came(8 + zz)
            self.came(15 + zz)

            def add(r):
                total = self.value(q, r) + self.value(8 + zz, r) + self.value(15 + zz, r)
                self.land[q, r] = total.astype(BF16)

            self.by_rows(add)
            self.push(self.slot(q), 12 + k, 20 + k, (zz * 4 + x * 2 + c, y)).start()

    def fifth(self):
        d, z, x, c, y = self.pos
        q = z * 2 + x
        self.came(q)
        self.came(8 + z)
        for k in range(3):
            self.came(12 + k)
        pl.when(self.away)(lambda: self.came(15 + z))

        def add(r):
            total = self.value(q, r) + self.value(8 + z, r)
            total = total + self.value(12, r) + self.value(13, r) + self.value(14, r)

            @pl.when(self.home)
            def _():
                self.out[r, self.cols] = total + self.grad[d, r, self.cols].astype(F32)

            @pl.when(self.away)
            def _():
                self.out[r, self.cols] = total + self.value(15 + z, r)

        self.by_rows(add)

    def finish(self):
        block = self.slot(0)
        repeat(0, REDUCE_SEND, lambda s: self.push(block, 0, s, self.sib).wait_send())


def reduce_events(parts, lead=1):
    n = len(parts)
    events = [p.first for p in parts[:lead]]
    for i in range(n + 3):
        if i + lead < n:
            events.append(parts[i + lead].first)
        for k in range(4):
            if i < n:
                events.append(functools.partial(parts[i].second, k))
            if 0 <= i - 1 < n:
                events.append(functools.partial(parts[i - 1].third, k))
            if 0 <= i - 2 < n and k < 3:
                events.append(functools.partial(parts[i - 2].fourth, k))
        if 0 <= i - 3 < n:
            events.append(parts[i - 3].fifth)
    return events


def reduce_scratch(chunks):
    n = len(chunks)
    return [pltpu.VMEM((27, 72, cols[1]), BF16) for _, cols in chunks] + [
        pltpu.SemaphoreType.DMA((n, REDUCE_RECV)),
        pltpu.SemaphoreType.DMA((n, REDUCE_SEND)),
    ]


class Pump:
    def __init__(self, events):
        self.events, self.next = list(events), 0

    def run(self, count=None):
        stop = len(self.events)
        if count is not None:
            stop = min(stop, self.next + max(0, count))
        for event in self.events[self.next : stop]:
            event()
        self.next = stop

    def loop(self, steps, body, count=0):
        todo = self.events[self.next :][:count]
        self.next += len(todo)

        def step(i, _):
            for j, event in enumerate(todo):
                pl.when(i == j * steps // count)(event)
            body(i)
            return 0

        lax.fori_loop(0, steps, step, 0)


def flat(value):
    return value.reshape(-1, value.shape[-1])


def product(a, b, ca, cb):
    return lax.dot_general(a, b, (((ca,), (cb,)), ((), ())), preferred_element_type=F32)


def loader(sems):
    count = iter(range(64))

    def load(src, dst):
        copy = pltpu.make_async_copy(src, dst, sems.at[next(count)])
        copy.start()
        return copy.wait

    return load


def norm_back_rows(value, g, scale_up):
    center = value - jnp.mean(value, axis=-1, keepdims=True)
    rate = lax.rsqrt(jnp.mean(center * center, axis=-1, keepdims=True) + 1e-06)
    normed = center * rate
    e = g * scale_up
    inner = jnp.mean(e * normed, axis=-1, keepdims=True)
    return rate * (e - jnp.mean(e, axis=-1, keepdims=True) - normed * inner), normed


def row_sum(value):
    return jnp.sum(value, axis=0, keepdims=True)


def last_kernel(
    mod_ref, sums_ref, fc2_bias_ref, fc1_bias_ref, w_ref,
    rows_in, dqkv_in, wqkv_in, tokens_in, resid_in,
    tgrad_ref, qkv_out, sg_ref, mods_a, mods_b, b2, b3,
    rows_ref, dqkv_ref, wqkv_ref, tokens_ref, resid_ref, tsend, half_ref,
    grad, ngrad, sent, got, v1, v1_in, v2, v2_in, sgp, land0, land1, land2,
    load_sems, s0, s1, r1, s2, r2, s3, r3, s4, r4, s5, r5, recv, send,
):
    pos = place()
    d, z, x, c, y = pos
    sib = neighbours(pos)[0]
    far = (z * 4 + x * 2 + 1 - c, 1 - y)
    lin = d * 2 + y
    half, width = tokens_ref.shape
    heads = dqkv_ref.shape[0] // 3
    load = loader(load_sems)
    ready = [load(dqkv_in, dqkv_ref), load(rows_in, rows_ref)]
    ready_late = [
        load(*pair)
        for pair in ((wqkv_in, wqkv_ref), (tokens_in, tokens_ref), (resid_in, resid_ref))
    ]
    greet([(((lin + k) % 32) // 2, (lin + k) % 2) for k in range(1, 32)])
    me = (z * 2 + x) * 2 + y
    sgp[...] = jnp.zeros_like(sgp)
    n = dqkv_ref.shape[1] * heads
    hidden = fc1_bias_ref.shape[1]
    for wait in ready:
        wait()

    half_ref[...] = jnp.zeros_like(half_ref)
    half_ref[:, :hidden] = fc1_bias_ref[...]
    ones = jnp.ones((8, 2 * half), BF16)
    for j, at in ((0, hidden), (2, hidden + (n + 127) // 128 * 128)):
        value = product(ones, flat(dqkv_ref[j * heads : (j + 1) * heads]), 1, 1)
        half_ref[:, at : at + n] = value[0:1, :]

    for i in range(6):
        early = sums_ref[i : i + 1, :] if i < 5 else fc2_bias_ref[...]
        v2[:, i * width : (i + 1) * width] = early
    swap_early = remote(v2, v2_in, s0.at[2], s0.at[3], sib)
    swap_early.start()

    @pl.when(y == c)
    def _():
        b3[me] = half_ref[...]

    def send3(q, core):
        s = q * 2 + core
        return remote(half_ref, b3.at[me], s3.at[s], r3.at[me], (s, c))

    def each3(action):
        for q in range(8):
            for core in range(2):
                pl.when(jnp.logical_or(d != q * 2 + core, y != c))(
                    functools.partial(action, q, core)
                )

    reducers = [
        Reduce(grad.at[j], land, qkv_out.at[j], recv.at[j], send.at[j], pos, (0, n))
        for j, land in enumerate((land0, land1, land2))
    ]

    def weight_grad(j, _):
        value = product(rows_ref[...], flat(dqkv_ref[pl.ds(j * heads, heads)]), 0, 1)
        grad[j] = value.reshape(grad.shape[1:]).astype(BF16)
        for i, reducer in enumerate(reducers):
            pl.when(j == i)(reducer.first)
        return 0

    lax.fori_loop(0, 3, weight_grad, 0)
    each3(lambda q, core: send3(q, core).start())
    pump = Pump(reduce_events(reducers, 3)[3:])

    def chip(k):
        m = (me + k) % 16
        return m, ((m // 2) * 2 + c, m % 2)

    def to_chip(buf, send, recv, k):
        return remote(buf.at[me], buf.at[me], send.at[k], recv.at[me], chip(k)[1])

    def from_chip(buf, send, recv, k):
        m, peer = chip(k)
        return remote(buf.at[m], buf.at[m], send.at[k], recv.at[m], peer)

    last, wide, known = (mods_a, s1, r1), (b2, s2, r2), (mods_b, s5, r5)
    swap_early.wait()
    mods_b[me] = (v2[:, : 4 * width] + v2_in[:, : 4 * width]).astype(BF16)
    b2[me] = v2[:, 4 * width :] + v2_in[:, 4 * width :]
    for k in range(1, 16):
        to_chip(*known, k).start()
        to_chip(*wide, k).start()
    for wait in ready_late:
        wait()

    tile = half // 2
    swap = remote(sent, got, s0.at[4], s0.at[5], sib)

    def into_norm(i):
        part = pl.ds(pl.multiple_of(lax.rem(i + 2, 4) * tile, tile), tile)
        value = product(flat(dqkv_ref[:, :, part]), flat(wqkv_ref[...]), 0, 1)

        @pl.when(i < 2)
        def _():
            sent[pl.ds(pl.multiple_of(i * tile, tile), tile), :] = value.astype(BF16)

        @pl.when(i >= 2)
        def _():
            ngrad[part, :] = value

        pl.when(i == 1)(lambda: swap.start())

    pump.loop(4, into_norm, 12)
    swap.wait()
    piece = half // 8
    scale = 1.0 + mod_ref[:, width : 2 * width]
    v1[...] = jnp.zeros_like(v1)

    def norm_back(i):
        part = pl.ds(pl.multiple_of(i * piece, piece), piece)
        g = ngrad[part, :] + got[part, :].astype(F32)
        back, normed = norm_back_rows(tokens_ref[part, :].astype(F32), g, scale)
        value = (resid_ref[part, :] + back).astype(BF16)

        @pl.when(y == c)
        def _():
            tgrad_ref[part, :] = value

        @pl.when(y != c)
        def _():
            tsend[part, :] = value

        v1[:, :width] += row_sum(g)
        v1[:, width : 2 * width] += row_sum(g * normed)

    pump.loop(8, norm_back, 8)
    trade = remote(tsend, tgrad_ref, s0.at[6], s0.at[7], far)
    pl.when(y != c)(lambda: trade.start())

    swap = remote(v1, v1_in, s0.at[0], s0.at[1], sib)
    swap.start()
    pump.run(2)
    swap.wait()
    mods_a[me] = (v1[...] + v1_in[...]).astype(BF16)
    for k in range(1, 16):
        to_chip(*last, k).start()

    def rows_of(buf):
        return jnp.concatenate([buf[i].astype(F32) for i in range(16)], axis=0)

    def back_of(buf, at):
        every = rows_of(buf).astype(BF16)
        return product(every, w_ref[:, at : at + every.shape[1]], 1, 1)

    pump.run(8)
    for k in range(1, 16):
        from_chip(*known, k).wait_recv()
    back = back_of(mods_b, 2 * width)
    pump.run(2)
    for k in range(1, 16):
        from_chip(*last, k).wait_recv()
    back = back + back_of(mods_a, 0)
    for i in range(16):
        sgp[i, 0:1, :72] = back[i : i + 1, :]

    def send4(k):
        m = (d + k) % 16
        return remote(sgp.at[m], sg_ref.at[d], s4.at[k], r4.at[d], (m, y))

    for k in range(1, 16):
        send4(k).start()
    sg_ref[d] = sgp[d]
    pump.run(4)
    for k in range(1, 16):
        from_chip(*wide, k).wait_recv()

    def arrive3(i):
        remote(half_ref, b3.at[i], s3.at[0], r3.at[i], sib).wait_recv()

    for i in range(16):
        pl.when(jnp.logical_or(i != me, y != c))(functools.partial(arrive3, i))
    for k in range(1, 16):
        m = (d + k) % 16
        remote(sgp.at[m], sg_ref.at[m], s4.at[k], r4.at[m], (m, y)).wait_recv()
    pump.run()
    for reducer in reducers:
        reducer.finish()
    pl.when(y != c)(lambda: trade.wait())
    each3(lambda q, core: send3(q, core).wait_send())
    for k in range(1, 16):
        for buf in (last, wide, known):
            to_chip(*buf, k).wait_send()
        send4(k).wait_send()


def last_stage(
    mod, sums, fc2_bias, fc1_bias, w_mod, rows, dqkv, w_qkv, tokens, resid, collective_id
):
    vmem, anywhere = pl.BlockSpec(memory_space=pltpu.VMEM), pl.BlockSpec(memory_space=pl.ANY)
    n = w_mod.shape[1]
    half, width = tokens.shape
    cols = dqkv.shape[0] * dqkv.shape[1] // 3
    n2, n3 = 2 * width, fc1_bias.shape[1] + 2 * ((cols + 127) // 128 * 128)
    dma = pltpu.SemaphoreType.DMA((16,))
    shape = jax.ShapeDtypeStruct
    loaded = (rows, dqkv, w_qkv, tokens, resid)
    return pl.pallas_call(
        last_kernel,
        out_shape=[
            shape((half, width), BF16),
            shape((3, 72, cols), F32),
            shape((16, 8, 128), F32),
            shape((16, 1, n // 3), BF16),
            shape((16, 1, n - n // 3), BF16),
            shape((16, 1, n2), F32),
            shape((16, 1, n3), F32),
        ],
        in_specs=[vmem] * 5 + [anywhere] * 5,
        out_specs=[vmem] * 7,
        scratch_shapes=[pltpu.VMEM(a.shape, a.dtype) for a in loaded]
        + [
            pltpu.VMEM((half, width), BF16),
            pltpu.VMEM((1, n3), F32),
            pltpu.VMEM((3, 16, 72, cols), BF16),
            pltpu.VMEM((half, width), F32),
            pltpu.VMEM((half, width), BF16),
            pltpu.VMEM((half, width), BF16),
            pltpu.VMEM((1, n // 3), F32),
            pltpu.VMEM((1, n // 3), F32),
            pltpu.VMEM((1, n), F32),
            pltpu.VMEM((1, n), F32),
            pltpu.VMEM((16, 8, 128), F32),
        ]
        + [pltpu.VMEM((27, 72, cols), BF16)] * 3
        + [pltpu.SemaphoreType.DMA((8,)), pltpu.SemaphoreType.DMA((8,))]
        + [dma] * 10
        + [
            pltpu.SemaphoreType.DMA((3, REDUCE_RECV)),
            pltpu.SemaphoreType.DMA((3, REDUCE_SEND)),
        ],
        compiler_params=pltpu.CompilerParams(
            collective_id=collective_id, has_side_effects=True, vmem_limit_bytes=64500 * 1024
        ),
    )(mod, sums, fc2_bias, fc1_bias, w_mod, *loaded)


LOG2E = math.log2(math.e)


def attention_step(qkv, out, lse, block, scale):
    heads, blocks = qkv.shape[0] // 3, qkv.shape[2] // block
    factor = scale * LOG2E

    def body(i):
        h = i // blocks
        cols = pl.ds(pl.multiple_of((i % blocks) * block, block), block)
        scores = product(qkv[heads + h], qkv[h, :, cols], 0, 0)
        top = jnp.max(scores, axis=0, keepdims=True)
        probs = jnp.exp2((scores - top) * factor)
        total = jnp.sum(probs, axis=0, keepdims=True)
        mixed = product(qkv[2 * heads + h], probs.astype(BF16), 1, 0)
        out[h, :, cols] = (mixed / total).astype(BF16)
        lse[h, :, cols] = top * factor + jnp.log2(total)

    return heads * blocks, body


GELU = math.sqrt(2 / math.pi)


def gelu_and_slope(v):
    square = v * v
    t = jnp.tanh(v * (GELU + GELU * 0.044715 * square))
    half = 0.5 * (1.0 + t)
    return v * half, half + 0.5 * v * (1.0 - t * t) * (GELU + GELU * 3 * 0.044715 * square)


def forward_kernel(
    chunks, block, scale,
    piece_ref, w_mod, mod_bias, proj_bias, small_in, tokens_in, grad_in,
    s_qkv, s_proj, s_fc1, s_fc2,
    mod, silu_ref, fc2_bias_grad,
    rows_a_out, qkv_out, attended_out, lse_out, branch_out, resid_out, rows_out, act_out,
    slope_out, fc2_grad_out, grad_m_out, tokens_out, grad_out,
    w_qkv, w_proj, w_fc1, w_fc2, relay_qkv, relay_proj, relay_1, relay_2,
    part, land, mine, other, small, tokens, out_grad,
    rows_a, qkv, out, lse, branch, resid, rows, act, slope, fc2_grad, grad_m,
    qkv_here, proj_here, weight_here, sent, got,
    s1, r1, s2, r2, sems, out_sems, recv, send,
):
    pos = place()
    d, z, x, c, y = pos
    sib, _, yn = neighbours(pos)
    far = (z * 4 + x * 2 + 1 - c, 1 - y)
    half, width = tokens.shape
    home, away = c == y, c != y
    greet([((d + k) % 16, y) for k in range(1, 16)] + [yn, far])

    stores = []

    def store(src, dst):
        copy = pltpu.make_async_copy(src, dst, out_sems.at[len(stores)])
        copy.start()
        stores.append(copy)

    def swapped(src, dst, i):
        there = remote(src, dst, sems.at[i], sems.at[i + 1], far)
        here = pltpu.make_async_copy(src, dst, sems.at[i + 1])

        def start():
            pl.when(away)(lambda: there.start())
            pl.when(home)(lambda: here.start())

        def wait():
            pl.when(away)(lambda: there.wait())
            pl.when(home)(lambda: here.wait())

        return start, wait

    def piece(k):
        to = (d + k) % 16
        return remote(piece_ref.at[to], silu_ref.at[d], s1.at[k], r1.at[d], (to, y))

    def piece_in(k):
        src = (d + k) % 16
        return remote(piece_ref.at[src], silu_ref.at[src], s1.at[k], r1.at[src], (src, y))

    for k in range(1, 16):
        piece(k).start()
    small_start, small_wait = swapped(small_in, small, 7)
    tokens_start, tokens_wait = swapped(tokens_in, tokens, 9)
    grad_start, grad_wait = swapped(grad_in, out_grad, 11)
    small_start()
    tokens_start()
    parts = gather_parts(
        [s_qkv, s_proj, s_fc1, s_fc2],
        [w_qkv, w_proj, w_fc1, w_fc2],
        [relay_qkv, relay_proj, relay_1, relay_2],
        chunks,
        recv,
        send,
        pos,
    )
    last_of = {g: parts[i].ready for i, (g, _, _) in enumerate(chunks)}
    events = gather_events(parts)
    pump = Pump(events)

    def until_ready(g):
        pump.run(events.index(last_of[g]) + 1 - pump.next)

    pump.run(6)
    silu_ref[d] = piece_ref[d]
    for k in range(1, 16):
        piece_in(k).wait_recv()
    some = jnp.concatenate(
        [silu_ref[2 * q + y].astype(F32)[0:1, :] for q in range(8)], axis=0
    ).astype(BF16)[:, :72]
    for j in range(6):
        cols = slice(j * width, (j + 1) * width)
        value = jnp.dot(some, w_mod[:, cols], preferred_element_type=F32)
        for q in range(8):
            part[q, :, cols] = value[q : q + 1, :]
    me = z * 2 + x

    def send_part(k):
        q = (me + k) % 8
        return remote(part.at[q], land.at[me], s2.at[k], r2.at[me], (q * 2 + c, y))

    def part_in(k):
        q = (me + k) % 8
        return remote(part.at[q], land.at[q], s2.at[k], r2.at[q], (q * 2 + c, y))

    for k in range(1, 8):
        send_part(k).start()
    land[me] = part[me]
    pump.run(10)
    for k in range(1, 8):
        part_in(k).wait_recv()
    total = land[0]
    for q in range(1, 8):
        total = total + land[q]
    mine[...] = total
    swap = remote(mine, other, sems.at[13], sems.at[14], sib)
    swap.start()
    pump.run(4)
    for k in range(1, 16):
        piece(k).wait_send()
    for k in range(1, 8):
        send_part(k).wait_send()
    swap.wait()
    for i in range(6):
        cols = slice(i * width, (i + 1) * width)
        mod[:, cols] = mine[:, cols] + other[:, cols] + mod_bias[i : i + 1, :]
    shift_a, scale_a, gate_a, shift_m, scale_m, gate_m = [
        mod[:, i * width : (i + 1) * width] for i in range(6)
    ]
    small_wait()
    tokens_wait()

    tall = half // 8

    def norm_rows(value, shift, scale_up):
        center = value - jnp.mean(value, axis=-1, keepdims=True)
        spread = jnp.mean(center * center, axis=-1, keepdims=True)
        normed = center * lax.rsqrt(spread + 1e-06) * (1.0 + scale_up) + shift
        return normed.astype(BF16)

    def first_norm(i, _):
        own = pl.ds(pl.multiple_of(i * tall, tall), tall)
        rows_a[own, :] = norm_rows(tokens[own, :].astype(F32), shift_a, scale_a)
        return 0

    lax.fori_loop(0, 8, first_norm, 0)
    share = remote(rows_a.at[:half], rows_a.at[half:], sems.at[5], sems.at[6], sib)
    share.start()
    until_ready(0)
    heads = qkv.shape[0] // 3
    cols = heads * qkv.shape[1]
    load = pltpu.make_async_copy(w_qkv, qkv_here, sems.at[0])
    load.start()
    grad_start()
    pump.run(2)
    load.wait()
    share.wait()
    store(rows_a, rows_a_out)
    store(tokens, tokens_out)
    row = lax.broadcasted_iota(jnp.int32, (8, 2 * half), 0)
    for j in range(3):
        weight = flat(qkv_here[:, :, j * cols : (j + 1) * cols])
        value = product(weight, rows_a[...], 0, 1)
        if j != 1:
            pick = jnp.where(row == j // 2, 1.0, 0.0).astype(BF16)
            value = value + product(small[:, :cols], pick, 0, 0)
        value = value.reshape((heads,) + qkv.shape[1:])
        qkv[pl.ds(j * heads, heads)] = value.astype(BF16)
        pump.run(2)
    store(qkv, qkv_out)
    steps, body = attention_step(qkv, out, lse, block, scale)
    pump.loop(steps, body, 22)
    store(out, attended_out)
    store(lse, lse_out)
    until_ready(1)

    load = pltpu.make_async_copy(w_proj, proj_here, sems.at[0])
    load.start()
    load.wait()
    tile = half // 2
    swap = remote(sent, got, sems.at[1], sems.at[2], sib)

    def project(i, _):
        part = pl.ds(pl.multiple_of(lax.rem(i + 2, 4) * tile, tile), tile)
        value = product(flat(out[:, :, part]), flat(proj_here[...]), 0, 1)

        @pl.when(i < 2)
        def _():
            sent[pl.ds(pl.multiple_of(i * tile, tile), tile), :] = value.astype(BF16)

        @pl.when(i >= 2)
        def _():
            branch[part, :] = value + proj_bias[6:7, :]

        pl.when(i == 1)(lambda: swap.start())
        return 0

    lax.fori_loop(0, 4, project, 0)
    pump.run(2)
    grad_wait()
    store(out_grad, grad_out)

    def gated(i, total):
        own = pl.ds(pl.multiple_of(i * tall, tall), tall)
        value = (out_grad[own, :].astype(F32) * gate_m).astype(BF16)
        grad_m[own, :] = value
        return total + jnp.sum(value.astype(F32), axis=0, keepdims=True)

    fc2_bias_grad[...] = lax.fori_loop(0, 8, gated, jnp.zeros((1, width), F32))
    share_m = remote(grad_m.at[:half], grad_m.at[half:], sems.at[15], sems.at[16], sib)
    share_m.start()
    swap.wait()
    share = remote(rows.at[:half], rows.at[half:], sems.at[3], sems.at[4], sib)

    def norm(i, _):
        own = pl.ds(pl.multiple_of(i * tall, tall), tall)
        total = branch[own, :] + got[own, :].astype(F32)
        branch[own, :] = total
        mid = tokens[own, :].astype(F32) + gate_a * total
        resid[own, :] = mid
        rows[own, :] = norm_rows(mid, shift_m, scale_m)
        return 0

    lax.fori_loop(0, 8, norm, 0)
    share.start()
    store(branch, branch_out)
    store(resid, resid_out)
    until_ready(2)

    load = pltpu.make_async_copy(w_fc1, weight_here, sems.at[0])
    load.start()
    load.wait()
    share.wait()
    store(rows, rows_out)
    n = 256
    hidden_steps = act.shape[1] // n

    def hidden(i):
        cols = pl.ds(pl.multiple_of(i * n, n), n)
        bias = small[:, cols].astype(F32)[2:3, :]
        value, rate = gelu_and_slope(
            product(rows[...], flat(weight_here[:, :, cols]), 1, 0) + bias
        )
        act[:, cols] = value.astype(BF16)
        slope[:, cols] = rate.astype(BF16)

    pump.loop(hidden_steps, hidden, hidden_steps)
    store(act, act_out)
    store(slope, slope_out)
    share_m.wait()
    store(grad_m, grad_m_out)

    def weight_grad(i):
        cols = pl.ds(pl.multiple_of(i * n, n), n)
        value = product(grad_m[...], act[:, cols], 0, 0)
        fc2_grad[:, :, cols] = value.reshape(fc2_grad.shape[:2] + (n,)).astype(BF16)

    pump.loop(hidden_steps, weight_grad, hidden_steps)
    store(fc2_grad, fc2_grad_out)
    pump.run()
    for p in parts:
        p.finish()
    for copy in stores:
        copy.wait()


def forward_stage(
    pieces, w_mod, mod_bias, proj_bias, small, tokens, out_grad, shards, size, chunks,
    collective_id, block=512,
):
    half, width = tokens.shape
    count = 2 * half
    owned, cols = shards[1].shape[1:]
    heads = cols // size
    hidden = shards[2].shape[2]
    n = w_mod.shape[1]
    vmem, anywhere = pl.BlockSpec(memory_space=pltpu.VMEM), pl.BlockSpec(memory_space=pl.ANY)
    shape, dma = jax.ShapeDtypeStruct, pltpu.SemaphoreType.DMA
    kept = [
        ((count, width), BF16),
        ((3 * heads, size, count), BF16),
        ((heads, size, count), BF16),
        ((heads, 1, count), F32),
        ((half, width), F32),
        ((half, width), F32),
        ((count, width), BF16),
        ((count, hidden), BF16),
        ((count, hidden), BF16),
        ((16, owned, hidden), BF16),
        ((count, width), BF16),
    ]
    swap = ((half, width), BF16)
    return pl.pallas_call(
        functools.partial(forward_kernel, chunks, block, size**-0.5),
        out_shape=[shape((1, n), F32), shape((16, 8, 128), BF16), shape((1, width), F32)]
        + [shape(*k) for k in kept + [swap, swap]]
        + gather_shapes(shards),
        in_specs=[vmem] * 5 + [anywhere] * 6,
        out_specs=[vmem] * 3 + [anywhere] * 21,
        scratch_shapes=[
            pltpu.VMEM((8, 1, n), F32),
            pltpu.VMEM((8, 1, n), F32),
            pltpu.VMEM((1, n), F32),
            pltpu.VMEM((1, n), F32),
            pltpu.VMEM(small.shape, BF16),
            pltpu.VMEM(*swap),
            pltpu.VMEM(*swap),
        ]
        + [pltpu.VMEM(*k) for k in kept]
        + [
            pltpu.VMEM((16, owned, 3 * cols), BF16),
            pltpu.VMEM((16, owned, cols), BF16),
            pltpu.VMEM((16, owned, hidden), BF16),
            pltpu.VMEM(*swap),
            pltpu.VMEM(*swap),
            dma((16,)),
            dma((16,)),
            dma((8,)),
            dma((8,)),
            dma((17,)),
            dma((13,)),
        ]
        + gather_sems(chunks),
        compiler_params=pltpu.CompilerParams(
            collective_id=collective_id, has_side_effects=True, vmem_limit_bytes=64500 * 1024
        ),
    )(pieces, w_mod, mod_bias, proj_bias, small, tokens, out_grad, *shards)[:20]


def attention_back_step(qkv, grad, out, lse, result, key_sum, value_sum, block, scale):
    heads, blocks = qkv.shape[0] // 3, qkv.shape[2] // block
    factor = scale * LOG2E

    def body(i):
        h, j = i // blocks, i % blocks
        cols = pl.ds(pl.multiple_of(j * block, block), block)
        queries, keys, values = qkv[h, :, cols], qkv[heads + h], qkv[2 * heads + h]
        grads = grad[h, :, cols]
        inner = jnp.sum(out[h, :, cols].astype(F32) * grads.astype(F32), axis=0, keepdims=True)
        probs = jnp.exp2(product(keys, queries, 0, 0) * factor - lse[h, :, cols])
        score_grad = (probs * (product(values, grads, 0, 0) - inner)).astype(BF16)
        value_part = product(grads, probs.astype(BF16), 1, 1)
        key_part = product(queries, score_grad, 1, 1)
        result[h, :, cols] = (product(keys, score_grad, 1, 0) * scale).astype(BF16)

        @pl.when(j == 0)
        def _():
            key_sum[...] = key_part
            value_sum[...] = value_part

        @pl.when(j > 0)
        def _():
            key_sum[...] += key_part
            value_sum[...] += value_part

        @pl.when(j == blocks - 1)
        def _():
            result[heads + h] = (key_sum[...] * scale).astype(BF16)
            result[2 * heads + h] = value_sum[...].astype(BF16)

    return heads * blocks, body


def hidden_back_kernel(
    chunks, bias, grad_m_in, act_in, slope_in, rows_in, fc2_grad_in, w_fc2, w_fc1,
    fc1_bias_grad, fc2_out, fc1_grad_out, branch_out, ngrad_out,
    grad_m, act, slope, rows, fc2_grad, fc1_grad, branch, ngrad,
    weight, pre_grad, sent1, got1, sent2, got2, *rest,
):
    n = len(chunks)
    lands, (sems, load_sems, recv, send) = rest[:n], rest[n:]
    pos = place()
    sib = neighbours(pos)[0]
    half, width = branch.shape
    hidden = act.shape[1]
    load = loader(load_sems)
    grad_ready = load(fc2_grad_in, fc2_grad)
    weight_ready = load(w_fc2, weight)
    m_ready = load(grad_m_in, grad_m)
    slope_ready = load(slope_in, slope)
    act_ready = load(act_in, act)
    rows_ready = load(rows_in, rows)
    greet(chip_peers(pos))
    parts = [
        Reduce(fc2_grad, lands[i], fc2_out, recv.at[i], send.at[i], pos, cols)
        for i, cols in enumerate(chunks)
    ]
    pump = Pump(reduce_events(parts))
    grad_ready()
    pump.run(2)
    weight_ready()
    m_ready()
    slope_ready()
    tile = 256

    def into_hidden(i):
        cols = pl.ds(pl.multiple_of(i * tile, tile), tile)
        value = product(grad_m[...], flat(weight[:, :, cols]), 1, 0)
        value = (value * slope[:, cols].astype(F32)).astype(BF16)
        pre_grad[:, cols] = value
        fc1_bias_grad[:, cols] = jnp.sum(value.astype(F32), axis=0, keepdims=True)

    pump.loop(hidden // tile, into_hidden, 9)

    def out_of_hidden(source, sent, own, extra):
        def body(i):
            turn = lax.rem(i + 2, 4)
            part = pl.ds(pl.multiple_of(turn * tile, tile), tile)
            value = product(source[part, :], flat(weight[...]), 1, 1)

            @pl.when(i < 2)
            def _():
                sent[pl.ds(pl.multiple_of(i * tile, tile), tile), :] = value.astype(BF16)

            @pl.when(i >= 2)
            def _():
                own[part, :] = value + extra

        return body

    swap1 = remote(sent1, got1, sems.at[1], sems.at[2], sib)
    swap2 = remote(sent2, got2, sems.at[3], sems.at[4], sib)
    act_ready()
    pump.loop(4, out_of_hidden(act, sent1, branch, bias[7:8, :]), 8)
    swap1.start()
    weight_ready = load(w_fc1, weight)
    pump.run(2)
    weight_ready()
    pump.loop(4, out_of_hidden(pre_grad, sent2, ngrad, 0.0), 8)
    swap2.start()

    def join(own, got):
        def body(i, _):
            part = pl.ds(pl.multiple_of(i * tile, tile), tile)
            own[part, :] += got[part, :].astype(F32)
            return 0

        lax.fori_loop(0, half // tile, body, 0)

    swap1.wait()
    join(branch, got1)
    stored = [load(branch, branch_out)]
    rows_ready()

    def weight_grad(i):
        cols = pl.ds(pl.multiple_of(i * tile, tile), tile)
        value = product(rows[...], pre_grad[:, cols], 0, 0)
        fc1_grad[:, :, cols] = value.reshape(fc1_grad.shape[:2] + (tile,)).astype(BF16)

    pump.loop(hidden // tile, weight_grad, 9)
    stored.append(load(fc1_grad, fc1_grad_out))
    swap2.wait()
    join(ngrad, got2)
    stored.append(load(ngrad, ngrad_out))
    pump.run()
    for p in parts:
        p.finish()
    for wait in stored:
        wait()


def hidden_back(bias, grad_m, act, slope, rows, fc2_grad, w_fc2, w_fc1, chunks, collective_id):
    vmem, anywhere = pl.BlockSpec(memory_space=pltpu.VMEM), pl.BlockSpec(memory_space=pl.ANY)
    shape = jax.ShapeDtypeStruct
    count, width = grad_m.shape
    half, hidden = count // 2, act.shape[1]
    swap = pltpu.VMEM((half, width), BF16)
    sums = pltpu.VMEM((half, width), F32)
    land = reduce_scratch([(0, cols) for cols in chunks])
    return pl.pallas_call(
        functools.partial(hidden_back_kernel, chunks),
        out_shape=[
            shape((1, hidden), F32),
            shape(fc2_grad.shape[1:], F32),
            shape(fc2_grad.shape, BF16),
            shape((half, width), F32),
            shape((half, width), F32),
        ],
        in_specs=[vmem] + [anywhere] * 7,
        out_specs=[vmem] * 2 + [anywhere] * 3,
        scratch_shapes=[
            pltpu.VMEM((count, width), BF16),
            pltpu.VMEM((count, hidden), BF16),
            pltpu.VMEM((count, hidden), BF16),
            pltpu.VMEM((count, width), BF16),
            pltpu.VMEM(fc2_grad.shape, BF16),
            pltpu.VMEM(fc2_grad.shape, BF16),
            sums,
            sums,
            pltpu.VMEM(fc2_grad.shape, BF16),
            pltpu.VMEM((count, hidden), BF16),
            swap,
            swap,
            swap,
            swap,
        ]
        + land[: len(chunks)]
        + [pltpu.SemaphoreType.DMA((5,)), pltpu.SemaphoreType.DMA((12,))]
        + land[len(chunks) :],
        compiler_params=pltpu.CompilerParams(
            collective_id=collective_id, has_side_effects=True, vmem_limit_bytes=64500 * 1024
        ),
    )(bias, grad_m, act, slope, rows, fc2_grad, w_fc2, w_fc1)


def attention_back_kernel(
    chunks, block, scale, mod, resid_in, ngrad_in, out_grad_in, branch_in, branch_m_in, w_proj_in,
    qkv_in, out_in, lse_in, fc1_grad_in,
    sums, fc1_out, proj_out, output, resid_grad_out, result_out,
    resid, ngrad, out_grad, branch, branch_m, w_proj, qkv, out, lse, fc1_grad, resid_grad, result,
    rows, grad, proj_grad, key_sum, value_sum, given, *rest,
):
    n = len(chunks)
    lands, (sems, load_sems, recv, send) = rest[:n], rest[n:]
    pos = place()
    sib = neighbours(pos)[0]
    half, width = resid.shape
    d, z, x, c, y = pos
    home, away = c == y, c != y
    far = (z * 4 + x * 2 + 1 - c, 1 - y)
    load = loader(load_sems)
    first = [load(fc1_grad_in, fc1_grad)]
    norm_ready = [
        load(*pair)
        for pair in (
            (ngrad_in, ngrad),
            (resid_in, resid),
            (out_grad_in, out_grad),
            (branch_in, branch),
            (branch_m_in, branch_m),
        )
    ]
    late = [load(w_proj_in, w_proj), load(out_in, out), load(qkv_in, qkv), load(lse_in, lse)]
    greet(chip_peers(pos))
    parts = [
        Reduce(
            (fc1_grad, proj_grad)[g],
            lands[i],
            (fc1_out, proj_out)[g],
            recv.at[i],
            send.at[i],
            pos,
            cols,
        )
        for i, (g, cols) in enumerate(chunks)
    ]
    pump = Pump(reduce_events(parts))
    for wait in first:
        wait()
    pump.run(2)
    for wait in norm_ready:
        wait()
    tall = half // 8
    gate_a, scale_m, gate_m = (mod[:, i * width : (i + 1) * width] for i in (2, 4, 5))
    scale_up = 1.0 + scale_m

    def norm(i, total):
        part = pl.ds(pl.multiple_of(i * tall, tall), tall)
        g = ngrad[part, :]
        mid = resid[part, :]
        back, normed = norm_back_rows(mid, g, scale_up)
        grads = out_grad[part, :].astype(F32)
        value = grads + back
        resid_grad[part, :] = value
        low = (value * gate_a).astype(BF16)
        rows[part, :] = low
        made = (mid + gate_m * branch_m[part, :]).astype(BF16)

        @pl.when(home)
        def _():
            output[part, :] = made

        @pl.when(away)
        def _():
            given[part, :] = made

        terms = (
            value * branch[part, :],
            g,
            g * normed,
            grads * branch_m[part, :],
            low.astype(F32),
        )
        return tuple(t + row_sum(v) for t, v in zip(total, terms))

    total = lax.fori_loop(0, 8, norm, (jnp.zeros((1, width), F32),) * 5)
    share = remote(rows.at[:half], rows.at[half:], sems.at[0], sems.at[1], sib)
    share.start()
    stored = [load(resid_grad, resid_grad_out)]
    trade = remote(given, output, sems.at[2], sems.at[3], far)
    pl.when(away)(lambda: trade.start())
    sums[...] = jnp.zeros_like(sums)
    for i in range(5):
        sums[i : i + 1, :] = total[i]
    pump.run(1)
    for wait in late:
        wait()
    share.wait()
    tile = 256

    def attended(i):
        cols = pl.ds(pl.multiple_of(i * tile, tile), tile)
        value = product(flat(w_proj[...]), rows[cols, :], 0, 1)
        grad[:, :, cols] = value.reshape(grad.shape[:2] + (tile,)).astype(BF16)

    pump.loop(2 * half // tile, attended, 4)
    value = product(rows[...], flat(out[...]), 0, 1)
    proj_grad[...] = value.reshape(proj_grad.shape).astype(BF16)
    steps, body = attention_back_step(
        qkv, grad, out, lse, result, key_sum, value_sum, block, scale
    )
    pump.loop(steps, body, 28)
    stored.append(load(result, result_out))
    pump.run()
    pl.when(away)(lambda: trade.wait())
    for p in parts:
        p.finish()
    for wait in stored:
        wait()


def attention_back(
    mod, resid, ngrad, out_grad, branch, branch_m, w_proj, qkv, out, lse, fc1_grad, chunks,
    collective_id, block=512,
):
    heads, size, count = out.shape
    half, width = resid.shape
    owned, cols = w_proj.shape[1:]
    vmem, anywhere = pl.BlockSpec(memory_space=pltpu.VMEM), pl.BlockSpec(memory_space=pl.ANY)
    shape = jax.ShapeDtypeStruct
    land = reduce_scratch(chunks)
    arrays = (resid, ngrad, out_grad, branch, branch_m, w_proj, qkv, out, lse, fc1_grad)
    made = [((half, width), F32), (qkv.shape, BF16)]
    return pl.pallas_call(
        functools.partial(attention_back_kernel, chunks, block, size**-0.5),
        out_shape=[
            shape((8, width), F32),
            shape(fc1_grad.shape[1:], F32),
            shape((owned, cols), F32),
            shape((half, width), BF16),
        ]
        + [shape(*m) for m in made],
        in_specs=[vmem] + [anywhere] * 10,
        out_specs=[vmem] * 4 + [anywhere] * 2,
        scratch_shapes=[pltpu.VMEM(a.shape, a.dtype) for a in arrays]
        + [pltpu.VMEM(*m) for m in made]
        + [
            pltpu.VMEM((count, width), BF16),
            pltpu.VMEM(out.shape, BF16),
            pltpu.VMEM((16, owned, cols), BF16),
            pltpu.VMEM((size, count), F32),
            pltpu.VMEM((size, count), F32),
            pltpu.VMEM((half, width), BF16),
        ]
        + land[: len(chunks)]
        + [pltpu.SemaphoreType.DMA((4,)), pltpu.SemaphoreType.DMA((12,))]
        + land[len(chunks) :],
        compiler_params=pltpu.CompilerParams(
            collective_id=collective_id, has_side_effects=True, vmem_limit_bytes=64500 * 1024
        ),
    )(mod, *arrays)


def columns(n, step):
    return [(i, min(step, n - i)) for i in range(0, n, step)]


def on_device_chip(
    tokens,
    cond,
    mod_weight,
    mod_bias,
    query_key_value_weight,
    qkv_bias,
    attention_out_weight,
    attention_out_bias,
    first_hidden_weight,
    first_hidden_bias,
    second_hidden_weight,
    second_hidden_bias,
    out_grad,
):
    half, _, width = tokens.shape
    owned, _, cols = query_key_value_weight.shape
    head_size = width // HEADS
    heads_here = cols // head_size
    hidden = first_hidden_weight.shape[1]

    silu_cond, silu_back = jax.vjp(jax.nn.silu, cond.astype(F32))
    pieces = jnp.pad(
        silu_cond.astype(BF16).reshape(16, 1, owned), ((0, 0), (0, 7), (0, 128 - owned))
    )
    s_qkv = query_key_value_weight.reshape(1, owned, 3 * cols)
    biases = jnp.concatenate([mod_bias, attention_out_bias, second_hidden_bias])
    biases = biases.astype(F32).reshape(8, width)
    small = jnp.stack(
        [
            jnp.pad(qkv_bias[0], (0, hidden - cols)),
            jnp.pad(qkv_bias[1], (0, hidden - cols)),
            first_hidden_bias,
        ]
    )
    small = jnp.pad(small, ((0, 5), (0, 0)))
    shards = [
        s_qkv,
        attention_out_weight.T.reshape(1, owned, cols),
        first_hidden_weight.reshape(1, owned, hidden),
        second_hidden_weight.T.reshape(1, owned, hidden),
    ]
    chunks = [(0, p, False) for p in columns(3 * cols, 896)] + [(1, None, False)]
    chunks += [(g, p, False) for g in (2, 3) for p in columns(hidden, 1152)]
    (
        modulation,
        silu_owned,
        fc2_bias_part,
        rows_a,
        qkv,
        attended,
        log_totals,
        branch_a,
        resid_mid,
        rows_m,
        act_low,
        slope,
        fc2_grad,
        grad_m,
        tokens_here,
        out_grad_here,
        w_qkv,
        w_proj,
        w_fc1,
        w_fc2,
    ) = forward_stage(
        pieces,
        mod_weight,
        biases,
        biases,
        small,
        tokens.reshape(half, width),
        out_grad.reshape(half, width),
        shards,
        head_size,
        chunks,
        2,
    )

    fc1_bias_part, fc2_out, fc1_grad, branch_m, normed_m_grad = hidden_back(
        biases,
        grad_m,
        act_low,
        slope,
        rows_m,
        fc2_grad,
        w_fc2,
        w_fc1,
        columns(hidden, 768),
        4,
    )
    sums, fc1_out, proj_out, output, resid_grad, qkv_grad = attention_back(
        modulation,
        resid_mid,
        normed_m_grad,
        out_grad_here,
        branch_a,
        branch_m,
        w_proj,
        qkv,
        attended,
        log_totals,
        fc1_grad,
        [(0, p) for p in columns(hidden, 768)] + [(1, (0, cols))],
        5,
    )
    tokens_grad, qkv_out, silu_grad, mods_a, mods_b, wide, narrow = last_stage(
        modulation,
        sums,
        fc2_bias_part,
        fc1_bias_part,
        mod_weight,
        rows_a,
        qkv_grad,
        w_qkv,
        tokens_here,
        resid_grad,
        6,
    )
    mods = jnp.concatenate([mods_a[:, 0], mods_b[:, 0]], axis=1)
    mod_weight_grad = product(silu_owned[:, 0, :owned], mods, 0, 0)
    mod_bias_grad = jnp.sum(mods, axis=0, dtype=F32)
    wide, narrow = jnp.sum(wide[:, 0], axis=0), jnp.sum(narrow[:, 0], axis=0)
    step = (cols + 127) // 128 * 128
    qkv_bias_grad = jnp.stack([narrow[hidden + i * step :][:cols] for i in range(2)])
    cond_grad = silu_back(silu_grad[:, 0, :owned].reshape(1, width))[0]
    return (
        output.reshape(half, 1, width),
        tokens_grad.reshape(half, 1, width),
        cond_grad,
        mod_weight_grad,
        mod_bias_grad,
        jnp.moveaxis(qkv_out, 0, 1),
        qkv_bias_grad,
        proj_out.T,
        wide[:width],
        fc1_out,
        narrow[:hidden],
        fc2_out.T,
        wide[width:],
    )


def solution(mesh):
    shape = dict(mesh.shape)
    body = on_device_chip if shape == {"dp": 16, "tensor": 2} else on_device_general
    return jax.shard_map(
        body,
        mesh=mesh,
        in_specs=(
            P("tensor", "dp", None),
            P("dp", None),
            P("dp", None),
            P(),
            P("dp", None, "tensor"),
            P(None, "tensor"),
            P("tensor", "dp"),
            P(),
            P("dp", "tensor"),
            P("tensor"),
            P("tensor", "dp"),
            P(),
            P("tensor", "dp", None),
        ),
        out_specs=(
            P("tensor", "dp", None),
            P("tensor", "dp", None),
            P("dp", None),
            P("dp", None),
            P(),
            P("dp", None, "tensor"),
            P(None, "tensor"),
            P("tensor", "dp"),
            P(),
            P("dp", "tensor"),
            P("tensor"),
            P("tensor", "dp"),
            P(),
        ),
        check_vma=False,
    )
```
